32 devices in a mesh: dp: 2 (over y), row: 4 (over z), col: 4 (over x, core).
Axes of the slice: x: 2, y: 2, z: 4, core: 2. Of those that a mesh axis runs over, the one named last changes fastest.
Arguments:
- tokens_in: bfloat16 [2, 4096, 1024], P(None, ('dp', 'row'), 'col'), may hold values from -6 to 6
- segments: int32 [2, 2, 2048], P(None, 'dp'), may hold values from 0 to 31, never falling along the last dimension, each value on 1 to 1024 neighbouring positions
- gain_attn: float32 [1024], P('col'), may hold values from 0.25 to 1.75
- gain_ffn: float32 [1024], P('col'), may hold values from 0.25 to 1.75
- w_heads: bfloat16 [1024, 160], P('col', 'row'), may hold values from -0.4375 to 0.4375
- w_ranks: bfloat16 [1024, 640], P('col', 'row'), may hold values from -0.1875 to 0.1875
- w_out: bfloat16 [1024, 1024], P('row', 'col'), may hold values from -0.75 to 0.75
- w_gate: bfloat16 [1024, 2816], P('col', 'row'), may hold values from -0.1875 to 0.1875
- w_up: bfloat16 [1024, 2816], P('col', 'row'), may hold values from -0.1875 to 0.1875
- w_down: bfloat16 [2816, 1024], P('row', 'col'), may hold values from -0.21875 to 0.21875
- cotangent: bfloat16 [2, 4096, 1024], P(None, ('dp', 'row'), 'col'), may hold values from -6 to 6
Outputs:
- output: bfloat16 [2, 4096, 1024], P(None, ('dp', 'row'), 'col')
- grad_input: float32 [2, 4096, 1024], P(None, ('dp', 'row'), 'col')
- grad_gain_attn: float32 [1024], P('col')
- grad_gain_ffn: float32 [1024], P('col')
- grad_w_heads: float32 [1024, 160], P('col', 'row')
- grad_w_ranks: float32 [1024, 640], P('col', 'row')
- grad_w_out: float32 [1024, 1024], P('row', 'col')
- grad_w_gate: float32 [1024, 2816], P('col', 'row')
- grad_w_up: float32 [1024, 2816], P('col', 'row')
- grad_w_down: float32 [2816, 1024], P('row', 'col')
The draws below stay inside these ranges and needn't reach their ends.
Inputs may be any that keep to these rules, and one draw needn't show every extreme that they name: `segments`: document numbers count from 0 within each sequence of 2048 tokens, never fall, and a document holds 1 to 1024 tokens.
All inputs are finite; a program needn't handle non-finite values.
Results may differ from the reference program's by a relative error of at most 0.019.
The reference program's roundings to bfloat16 on the way count: a program that leaves them out, or rounds other values in their place, can miss the bound.
Values may be sent and summed in bfloat16 or wider, within the bound.
A program may use at most 128 MiB of HBM per device.

```python
import math
import jax
import jax.numpy as jnp
import numpy as np
from jax import lax

D = 1024
H = 16
HD = 64
RQ = 6
RK = 2
FF = 2816
LENGTH = 2048
MICRO = 2
FAC = 10
MBT = 4096
N_DP = 2


def level_of(own_key, shape, shards, low, largest):
    level, own = 1.0, jax.random.fold_in(own_key, 6)
    for position, blocks in shards:
        heights = jnp.exp(jax.random.uniform(jax.random.fold_in(own, position), (blocks,), jnp.float32, low / len(shards), largest / len(shards)))
        level = level * jnp.repeat(heights, shape[position] // blocks).reshape([-1 if axis == position else 1 for axis in range(len(shape))])
    return level


def profile(amount, total, most, lean):
    weights = [(1 << 20) // math.isqrt(standing ** lean) + 1 for standing in range(2, amount + 1)]
    rest, given = total - most - (amount - 1), [1] * (amount - 1)
    while rest > 0:
        movable = [i for i in range(amount - 1) if given[i] < most]
        mass, budget = sum([weights[i] for i in movable]), rest
        for i in movable:
            more = min(most - given[i], max(1, budget * weights[i] // mass), rest)
            given[i] = given[i] + more
            rest = rest - more
    return np.array([most] + given)


def uneven(rng, amount, total, most, skew):
    if amount == 2:
        one = jax.random.randint(rng, (), max(1, total - most), min(most, total - 1) + 1)
        return jnp.stack([one, total - one])
    tallies = jnp.asarray(profile(amount, total, most, skew), jnp.int32)
    couples = (amount - 1) // 2
    source_of, sink = tallies[1:1 + 2 * couples:2], tallies[2:2 + 2 * couples:2]
    margin = jnp.minimum(source_of - 1, most - sink)
    moved = jax.random.randint(jax.random.fold_in(rng, 1), (couples,), 0, 1 << 20) % (margin + 1)
    tallies = tallies.at[1:1 + 2 * couples:2].set(source_of - moved).at[2:2 + 2 * couples:2].set(sink + moved)
    return tallies[jax.random.permutation(jax.random.fold_in(rng, 2), amount)]


def bell_draw(own_key, shape, scale, reach, cuts=(), kind=jnp.bfloat16):
    level = level_of(own_key, shape, cuts, -0.22, 0.18) if cuts else 1.0
    values = jax.random.normal(own_key, shape, jnp.float32) * scale * level
    return jnp.minimum(jnp.maximum(values, -reach), reach).astype(kind)


def setup_inputs(seed: int = 0) -> dict:
    key_of = jax.random.split(jax.random.key(seed), 12)
    tokens_in = bell_draw(key_of[0], (MICRO, MBT, D), 1.0, 6.0, ((1, 8), (2, 4)))
    segments = jax.vmap(lambda own: jnp.searchsorted(jnp.cumsum(uneven(own, max(LENGTH // 64, 4), LENGTH, LENGTH // 2, 2)), jnp.arange(LENGTH), side="right"))(jax.random.split(key_of[1], MICRO * N_DP)).reshape((MICRO, N_DP, LENGTH)).astype(jnp.int32)
    gain_attn = jnp.clip(1.0 + 0.15 * jax.random.normal(key_of[2], (D,), jnp.float32), 0.25, 1.75)
    gain_ffn = jnp.clip(1.0 + 0.15 * jax.random.normal(key_of[3], (D,), jnp.float32), 0.25, 1.75)
    w_heads = bell_draw(key_of[4], (D, H * FAC), (D // 6) ** -0.5, 0.4375, ((0, 4), (1, 4)))
    w_ranks = bell_draw(key_of[5], (D, FAC * HD), D ** -0.5, 0.1875, ((0, 4), (1, 4)))
    w_out = bell_draw(key_of[6], (H * HD, D), (D // 16) ** -0.5, 0.75, ((0, 4), (1, 4)))
    w_gate = bell_draw(key_of[7], (D, FF), D ** -0.5, 0.1875, ((0, 4), (1, 4)))
    w_up = bell_draw(key_of[8], (D, FF), D ** -0.5, 0.1875, ((0, 4), (1, 4)))
    w_down = bell_draw(key_of[9], (FF, D), (FF // 4) ** -0.5, 0.21875, ((0, 4), (1, 4)))
    cotangent = bell_draw(key_of[10], (MICRO, MBT, D), 1.0, 6.0, ((1, 8), (2, 4)))
    return {"tokens_in": tokens_in, "segments": segments, "gain_attn": gain_attn, "gain_ffn": gain_ffn, "w_heads": w_heads, "w_ranks": w_ranks, "w_out": w_out, "w_gate": w_gate, "w_up": w_up, "w_down": w_down, "cotangent": cotangent}


@jax.custom_vjp
def low(v):
    return lax.optimization_barrier(v.astype(jnp.bfloat16)).astype(jnp.float32)

@jax.custom_vjp
def low_back(v):
    return v

def low_keep(v):
    return (low(v), None)

def low_pass(kept, grad):
    return (grad,)

def back_keep(v):
    return (v, None)

def back_low(kept, grad):
    return (low(grad),)
low.defvjp(low_keep, low_pass)
low_back.defvjp(back_keep, back_low)
norm_eps = 1e-06
rope_base = 10000.0
masked_score = -1e+30
highest = lax.Precision.HIGHEST

def rotate(values, places, direction):
    half_size = values.shape[-1] // 2
    inverse = rope_base ** (-(jnp.arange(half_size, dtype=jnp.float32) * 2.0 / values.shape[-1]))
    angles = places.astype(jnp.float32)[:, None] * inverse[None, :]
    cosine = jnp.cos(angles)[:, None, :]
    sine_term = direction * jnp.sin(angles)[:, None, :]
    first_half = values[..., :half_size]
    second_half = values[..., half_size:]
    return jnp.concatenate([first_half * cosine - second_half * sine_term, second_half * cosine + first_half * sine_term], axis=-1)

def doc_places(segment_row):
    seq_len = segment_row.shape[0]
    index_all = jnp.arange(seq_len, dtype=jnp.int32)
    change = jnp.concatenate([jnp.ones((1,), jnp.bool_), segment_row[1:] != segment_row[:-1]])
    starts = lax.cummax(jnp.where(change, index_all, 0), axis=0)
    return index_all - starts

def matmul(left, right):
    return jnp.dot(left, right, precision=highest)

def rms_norm(values, gain):
    scaling = lax.rsqrt(lax.optimization_barrier(jnp.mean(values * values, axis=-1, keepdims=True)) + norm_eps)
    return values * scaling * gain

def attend_sequence(queries, key_all, value_all, segment_row):
    seq_len = queries.shape[0]
    block_rows = min(512, seq_len)
    index_all = jnp.arange(seq_len, dtype=jnp.int32)
    scaling = queries.shape[-1] ** (-0.5)

    def one_block(block_no):
        offset = (block_no * block_rows).astype(jnp.int32)
        query_block = lax.dynamic_slice_in_dim(queries, offset, block_rows, 0)
        block_seg = lax.dynamic_slice_in_dim(segment_row, offset, block_rows, 0)
        block_idx = lax.dynamic_slice_in_dim(index_all, offset, block_rows, 0)
        scores = low_back(jnp.einsum('qhd,khd->hqk', query_block, key_all, precision=highest) * scaling)
        allowed = (block_seg[:, None] == segment_row[None, :]) & (index_all[None, :] <= block_idx[:, None])
        scores = jnp.where(allowed[None], scores, masked_score)
        probabilities = jax.nn.softmax(scores, axis=-1)
        return jnp.einsum('hqk,khd->qhd', low(probabilities), value_all, precision=highest)
    blocks = lax.map(jax.checkpoint(one_block), jnp.arange(seq_len // block_rows, dtype=jnp.int32))
    return blocks.reshape(queries.shape)

def reference(tokens_in, segments, gain_attn, gain_ffn, w_heads, w_ranks, w_out, w_gate, w_up, w_down, cotangent):
    model_width = tokens_in.shape[2]
    seq_count = segments.shape[0] * segments.shape[1]
    seq_len = segments.shape[2]
    seg_rows = segments.reshape(seq_count, seq_len)
    places = jax.vmap(doc_places)(seg_rows).reshape(-1)
    fac_count = RQ + 2 * RK

    def forward(tokens, gain_one, gain_two, heads_w, ranks_w, out_w, gate_w, up_w, down_w):
        flat = tokens.reshape(-1, model_width)
        count_all = flat.shape[0]
        h_one = low(rms_norm(flat, gain_one))
        head_part = low_back(matmul(h_one, heads_w)).reshape(count_all, H, fac_count)
        rank_part = low_back(matmul(h_one, ranks_w)).reshape(count_all, fac_count, HD)
        a_q = head_part[..., :RQ]
        a_k = low(head_part[..., RQ:RQ + RK])
        a_v = low(head_part[..., RQ + RK:])
        b_q = rotate(rank_part[:, :RQ], places, 1.0)
        b_k = low(rotate(rank_part[:, RQ:RQ + RK], places, 1.0))
        b_v = low(rank_part[:, RQ + RK:])
        queries = low(jnp.einsum('thr,tre->the', a_q, b_q, precision=highest) / RQ)
        key_all = low(jnp.einsum('thr,tre->the', a_k, b_k, precision=highest) / RK)
        value_all = low(jnp.einsum('thr,tre->the', a_v, b_v, precision=highest) / RK)
        packed = (queries.reshape(seq_count, seq_len, H, HD), key_all.reshape(seq_count, seq_len, H, HD), value_all.reshape(seq_count, seq_len, H, HD), seg_rows)
        attended = lax.map(jax.checkpoint(lambda member: attend_sequence(member[0], member[1], member[2], member[3])), packed)
        heads_out = low(low_back(attended.reshape(count_all, H * HD)))
        mixed = flat + low_back(matmul(heads_out, out_w))
        h_two = low(rms_norm(mixed, gain_two))
        gate = low_back(matmul(h_two, gate_w))
        up_vals = low_back(matmul(h_two, up_w))
        hidden = low(jax.nn.silu(gate) * up_vals)
        result = mixed + low_back(matmul(hidden, down_w))
        return result.reshape(tokens.shape)
    primals = (tokens_in.astype(jnp.float32), gain_attn, gain_ffn, w_heads.astype(jnp.float32), w_ranks.astype(jnp.float32), w_out.astype(jnp.float32), w_gate.astype(jnp.float32), w_up.astype(jnp.float32), w_down.astype(jnp.float32))
    result, pullback = jax.vjp(forward, *primals)
    grads = pullback(cotangent.astype(jnp.float32))
    return (result.astype(jnp.bfloat16), grads[0], grads[1], grads[2], grads[3], grads[4], grads[5], grads[6], grads[7], grads[8])
```

```python
import functools

import jax
import jax.numpy as jnp
from jax import lax
from jax.experimental import pallas as pl
from jax.experimental.pallas import tpu as pltpu
from jax.sharding import PartitionSpec as P

D = 1024
H = 16
HD = 64
RQ = 6
RK = 2
FAC = 10
MAX_DOC = 1024

EPS = 1e-06
ROPE = 10000.0
NEG = -1e30
BF = jnp.bfloat16
F32 = jnp.float32
LANES = 128
PAIRS = H // 2
FAC_ORDER = (6, 7, 8, 9, 0, 1, 2, 3, 4, 5)
FAC_BACK = (4, 5, 6, 7, 8, 9, 0, 1, 2, 3)
VMEM = pl.BlockSpec(memory_space=pltpu.VMEM)


def nn(a, b):
    return jnp.dot(a, b, preferred_element_type=F32)


def nt(a, b):
    return lax.dot_general(a, b, (((1,), (1,)), ((), ())), preferred_element_type=F32)


def tn(a, b):
    return lax.dot_general(a, b, (((0,), (0,)), ((), ())), preferred_element_type=F32)


def two_pass(a, b):
    high = a.astype(BF)
    low = (a - high.astype(F32)).astype(BF)
    return nn(high, b) + nn(low, b)


def lane_iota(shape):
    return lax.broadcasted_iota(jnp.int32, shape, len(shape) - 1)


def spread(rows, first, width):
    row = lax.broadcasted_iota(jnp.int32, (rows, width), 0)
    head = lax.broadcasted_iota(jnp.int32, (rows, width), 1) // HD
    return (row == head + first).astype(F32).astype(BF)


def collect(rows, width, first):
    head = lax.broadcasted_iota(jnp.int32, (rows, width), 0) // HD
    lane = lax.broadcasted_iota(jnp.int32, (rows, width), 1)
    return (lane == head + first).astype(F32).astype(BF)


def swap_halves(tile):
    lane = lane_iota(tile.shape)
    ahead = pltpu.roll(tile, LANES - HD // 2, 1)
    behind = pltpu.roll(tile, HD // 2, 1)
    return jnp.where(lane % HD < HD // 2, ahead, behind)


def double_left(tile):
    return jnp.where(lane_iota(tile.shape) < HD, tile, pltpu.roll(tile, HD, 1))


def double_right(tile):
    return jnp.where(lane_iota(tile.shape) < HD, pltpu.roll(tile, HD, 1), tile)


def params(**more):
    return pltpu.CompilerParams(vmem_limit_bytes=60 << 20, **more)


def call(body, outs, scratch=(), cost=None):
    return pl.pallas_call(
        body,
        out_shape=outs,
        scratch_shapes=scratch,
        compiler_params=params(),
        cost_estimate=cost,
    )


def cost_of(flops, moved):
    return pl.CostEstimate(flops=int(flops), bytes_accessed=int(moved), transcendentals=0)


def front_body(x_ref, gain_ref, w_ref, turn_ref, h_ref, hf_ref, bq_ref, kf_ref, q_ref):
    parts = x_ref.shape[0]
    feat = x_ref.shape[2]
    xs = [x_ref[c].astype(F32) for c in range(parts)]
    total = sum(jnp.sum(v * v, axis=1, keepdims=True) for v in xs)
    scale = lax.rsqrt(total / D + EPS)
    for c in range(parts):
        lanes = slice(c * feat, (c + 1) * feat)
        h_ref[:, lanes] = (xs[c] * scale * gain_ref[:, lanes]).astype(BF)
    both = nn(h_ref[...], w_ref[...])
    heads = both[:, FAC * HD :]
    hf_ref[...] = heads
    cosine = turn_ref[:, :LANES]
    sine = turn_ref[:, LANES:]
    for tile in range(FAC * HD // LANES):
        lanes = slice(tile * LANES, (tile + 1) * LANES)
        part = both[:, lanes]
        if tile < 4:
            part = part * cosine + swap_halves(part) * sine
        if tile < 3:
            bq_ref[:, lanes] = part
        else:
            kf_ref[:, (tile - 3) * LANES : (tile - 2) * LANES] = part.astype(BF)
    kf_ref[:, 2 * LANES :] = heads[:, : 2 * RK * H].astype(BF)
    high = heads.astype(BF)
    low = (heads - high.astype(F32)).astype(BF)
    ranks = []
    for r in range(RQ):
        tile = bq_ref[:, (r // 2) * LANES : (r // 2 + 1) * LANES]
        ranks.append(double_left(tile) if r % 2 == 0 else double_right(tile))
    width = 2 * LANES
    for p in range(D // width):
        lanes = slice(p * width, (p + 1) * width)
        acc = None
        for r in range(RQ):
            pick = spread(H * FAC, (2 * RK + r) * H + p * (width // HD), width)
            term = (nn(high, pick) + nn(low, pick)) * jnp.concatenate([ranks[r]] * 2, axis=1)
            acc = term if acc is None else acc + term
        q_ref[:, lanes] = (acc / RQ).astype(BF)


def front(x_parts, gain, w_rh, turn):
    rows = x_parts.shape[1]
    return call(
        front_body,
        (
            jax.ShapeDtypeStruct((rows, D), BF),
            jax.ShapeDtypeStruct((rows, H * FAC), F32),
            jax.ShapeDtypeStruct((rows, RQ * HD), F32),
            jax.ShapeDtypeStruct((rows, 2 * LANES + 2 * RK * H), BF),
            jax.ShapeDtypeStruct((rows, D), BF),
        ),
        cost=cost_of(2 * rows * D * 800 * 3, 6 << 20),
    )(x_parts, gain, w_rh, turn)


def mask_bias(seg_ref, keys, rows):
    seg_row = seg_ref[...].astype(F32)
    wide = jnp.broadcast_to(seg_row, (LANES, keys))
    column = wide.T
    column = jnp.concatenate([column] * (rows // LANES), axis=1)
    key_idx = lax.broadcasted_iota(jnp.int32, (keys, rows), 0)
    query_idx = lax.broadcasted_iota(jnp.int32, (keys, rows), 1) + (keys - rows)
    same = column == seg_row[:, keys - rows :]
    return jnp.where(same & (key_idx <= query_idx), 0.0, NEG)


def attend_body(q_ref, kf_ref, seg_ref, o_ref, lse_ref, k_ref, v_ref, bias_ref, dup_ref):
    rows = q_ref.shape[0]
    keys = kf_ref.shape[0]
    bias_ref[...] = mask_bias(seg_ref, keys, rows)
    for s in range(2 * RK):
        tile = kf_ref[:, (s // 2) * LANES : (s // 2 + 1) * LANES].astype(F32)
        dup_ref[s] = double_left(tile) if s % 2 == 0 else double_right(tile)

    def pair(p, carried):
        lanes = pl.ds(pl.multiple_of(p * LANES, LANES), LANES)
        weights = kf_ref[:, 2 * LANES :]
        made = []
        for kind in range(2):
            acc = None
            for s in range(RK):
                pick = spread(2 * RK * H, (kind * RK + s) * H + 2 * p, LANES)
                term = nn(weights, pick) * dup_ref[kind * RK + s]
                acc = term if acc is None else acc + term
            made.append((acc / RK).astype(BF))
        k_tile, v_tile = made
        k_ref[:, lanes] = k_tile
        v_ref[:, lanes] = v_tile
        v_turned = v_tile.astype(F32).T.astype(BF)
        q_turned = (q_ref[:, lanes].astype(F32) * HD**-0.5).T
        half = lax.broadcasted_iota(jnp.int32, q_turned.shape, 0) // HD
        outs = []
        for side in range(2):
            q_side = jnp.where(half == side, q_turned, 0.0).astype(BF)
            scores = nn(k_tile, q_side) + bias_ref[...]
            peak = jnp.max(scores, axis=0, keepdims=True)
            weight = jnp.exp(scores - peak)
            total = jnp.sum(weight, axis=0, keepdims=True)
            probs = (weight * (1.0 / total)).astype(BF)
            outs.append(nn(v_turned[side * HD : (side + 1) * HD], probs))
            lse_ref[2 * p + side] = jnp.broadcast_to(peak + jnp.log(total), (8, rows))
        o_ref[:, lanes] = jnp.concatenate(outs, axis=0).T.astype(BF)
        return carried

    lax.fori_loop(0, PAIRS, pair, 0)


def attend(q, kf_window, seg_window):
    rows = q.shape[0]
    keys = kf_window.shape[0]
    return call(
        attend_body,
        (
            jax.ShapeDtypeStruct((rows, D), BF),
            jax.ShapeDtypeStruct((H, 8, rows), F32),
            jax.ShapeDtypeStruct((keys, D), BF),
            jax.ShapeDtypeStruct((keys, D), BF),
        ),
        scratch=(pltpu.VMEM((keys, rows), F32), pltpu.VMEM((2 * RK, keys, LANES), F32)),
        cost=cost_of(2 * rows * keys * D * 16, 16 << 20),
    )(q, kf_window, seg_window)


def attend_back_body(
    q_ref, k_ref, v_ref, do_ref, lse_ref, kf_ref, seg_ref, dq_ref, dkf_ref, bias_ref, dup_ref, sum_ref, fac_ref
):
    rows = q_ref.shape[0]
    keys = kf_ref.shape[0]
    bias_ref[...] = mask_bias(seg_ref, keys, rows)
    for s in range(2 * RK):
        tile = kf_ref[:, (s // 2) * LANES : (s // 2 + 1) * LANES].astype(F32)
        dup_ref[s] = double_left(tile) if s % 2 == 0 else double_right(tile)
    sum_ref[...] = jnp.zeros_like(sum_ref)
    fac_ref[...] = jnp.zeros_like(fac_ref)

    def pair(p, carried):
        lanes = pl.ds(pl.multiple_of(p * LANES, LANES), LANES)
        k_tile = k_ref[:, lanes]
        v_tile = v_ref[:, lanes]
        k_turned = k_tile.astype(F32).T.astype(BF)
        q_tile = q_ref[:, lanes].astype(F32) * HD**-0.5
        do_tile = do_ref[:, lanes].astype(F32)
        q_turned = q_tile.T
        do_turned = do_tile.T
        half = lax.broadcasted_iota(jnp.int32, q_turned.shape, 0) // HD
        lane_half = lax.broadcasted_iota(jnp.int32, q_tile.shape, 1) // HD
        d_k = None
        d_v = None
        d_q = []
        for side in range(2):
            q_side = jnp.where(half == side, q_turned, 0.0).astype(BF)
            do_side = jnp.where(half == side, do_turned, 0.0).astype(BF)
            scores = nn(k_tile, q_side) + bias_ref[...]
            probs = jnp.exp(scores - lse_ref[2 * p + side][:1])
            d_prob = nn(v_tile, do_side)
            delta = jnp.sum(probs * d_prob, axis=0, keepdims=True)
            d_score = (probs * (d_prob - delta)).astype(BF)
            d_q.append(nn(k_turned[side * HD : (side + 1) * HD], d_score))
            q_back = jnp.where(lane_half == side, q_tile, 0.0).astype(BF)
            do_back = jnp.where(lane_half == side, do_tile, 0.0).astype(BF)
            part_k = nn(d_score, q_back)
            part_v = nn(probs.astype(BF), do_back)
            d_k = part_k if d_k is None else d_k + part_k
            d_v = part_v if d_v is None else d_v + part_v
        dq_ref[:, lanes] = jnp.concatenate(d_q, axis=0).T * HD**-0.5
        weights = kf_ref[:, 2 * LANES :]
        for kind, grad in ((0, d_k), (1, d_v)):
            for s in range(RK):
                slot = kind * RK + s
                pick = spread(2 * RK * H, slot * H + 2 * p, LANES)
                sum_ref[slot] += nn(weights, pick) * grad
                fac_ref[...] += two_pass(grad * dup_ref[slot], collect(LANES, 2 * RK * H, slot * H + 2 * p))
        return carried

    lax.fori_loop(0, PAIRS, pair, 0)
    for tile in range(2):
        first = sum_ref[2 * tile]
        second = sum_ref[2 * tile + 1]
        first = first + pltpu.roll(first, HD, 1)
        second = second + pltpu.roll(second, HD, 1)
        merged = jnp.where(lane_iota(first.shape) < HD, first, second)
        dkf_ref[:, tile * LANES : (tile + 1) * LANES] = (merged / RK).astype(BF)
    dkf_ref[:, 2 * LANES :] = (fac_ref[...] / RK).astype(BF)


def attend_back(q, k, v, d_heads, lse, kf_window, seg_window):
    rows = q.shape[0]
    keys = kf_window.shape[0]
    return call(
        attend_back_body,
        (
            jax.ShapeDtypeStruct((rows, D), F32),
            jax.ShapeDtypeStruct(kf_window.shape, BF),
        ),
        scratch=(
            pltpu.VMEM((keys, rows), F32),
            pltpu.VMEM((2 * RK, keys, LANES), F32),
            pltpu.VMEM((2 * RK, keys, LANES), F32),
            pltpu.VMEM((keys, 2 * RK * H), F32),
        ),
        cost=cost_of(2 * rows * keys * D * 40, 16 << 20),
    )(q, k, v, d_heads, lse, kf_window, seg_window)


def middle_body(
    x_ref, cot_ref, heads_ref, w_out_ref, gain_ref, w_ref,
    out_ref, d_mixed_ref, d_heads_ref, g_out_ref, g_gain_ref, g_ref,
    mixed_ref, h_ref, scale_ref, sum_ref, back_ref, cot_all_ref,
):
    step = pl.program_id(0)
    steps = pl.num_programs(0)
    parts, _, feat = x_ref.shape
    rows_of = w_out_ref.shape[0]
    head_rows = w_out_ref.shape[2]
    hidden_size = w_ref.shape[2] // 3

    def lanes_of(c):
        return slice(c * feat, (c + 1) * feat)

    @pl.when(step == 0)
    def _():
        total = None
        for c in range(parts):
            acc = x_ref[c].astype(F32)
            for r in range(rows_of):
                acc = acc + nn(heads_ref[:, r * head_rows : (r + 1) * head_rows], w_out_ref[r, c])
            mixed_ref[:, lanes_of(c)] = acc
            part = jnp.sum(acc * acc, axis=1, keepdims=True)
            total = part if total is None else total + part
            cot_all_ref[:, lanes_of(c)] = cot_ref[c]
        scale = lax.rsqrt(total / D + EPS)
        scale_ref[...] = jnp.broadcast_to(scale, scale_ref.shape)
        h_ref[...] = (mixed_ref[...] * scale * gain_ref[...]).astype(BF)
        sum_ref[...] = jnp.zeros_like(sum_ref)
        back_ref[...] = jnp.zeros_like(back_ref)

    gate = None
    up = None
    d_hidden = None
    for c in range(parts):
        h_part = h_ref[:, lanes_of(c)]
        term_g = nt(h_part, w_ref[0, c, :hidden_size])
        term_u = nt(h_part, w_ref[0, c, hidden_size : 2 * hidden_size])
        term_d = nt(cot_ref[c], w_ref[0, c, 2 * hidden_size :])
        gate = term_g if gate is None else gate + term_g
        up = term_u if up is None else up + term_u
        d_hidden = term_d if d_hidden is None else d_hidden + term_d
    sig = 1.0 / (1.0 + jnp.exp(-gate))
    silu = gate * sig
    hidden = (silu * up).astype(BF)
    d_gate = (d_hidden * up * sig * (1.0 + gate * (1.0 - sig))).astype(BF)
    d_up = (d_hidden * silu).astype(BF)
    for c in range(parts):
        sum_ref[:, lanes_of(c)] += nn(hidden, w_ref[0, c, 2 * hidden_size :])
        back_ref[:, lanes_of(c)] += nn(d_gate, w_ref[0, c, :hidden_size]) + nn(
            d_up, w_ref[0, c, hidden_size : 2 * hidden_size]
        )
    for place, (left, right) in enumerate(((d_gate, h_ref), (d_up, h_ref), (hidden, cot_all_ref))):
        grad = tn(left, right[...])
        for c in range(parts):
            g_ref[0, c, place * hidden_size : (place + 1) * hidden_size] = grad[:, lanes_of(c)].astype(BF)

    @pl.when(step == steps - 1)
    def _():
        scale = scale_ref[:, :1]
        mixed = mixed_ref[...]
        out_ref[...] = (mixed + sum_ref[...]).astype(BF)
        normed = mixed * scale
        d_h = back_ref[...]
        g_gain_ref[...] = jnp.sum(d_h * normed, axis=0, keepdims=True)
        inner = d_h * gain_ref[...]
        dot = jnp.sum(inner * normed, axis=1, keepdims=True) / D
        d_mixed = cot_all_ref[...].astype(F32) + scale * (inner - normed * dot)
        d_mixed_ref[...] = d_mixed
        low = d_mixed.astype(BF)
        grad = tn(heads_ref[...], low)
        for r in range(rows_of):
            acc = None
            for c in range(parts):
                term = nt(low[:, lanes_of(c)], w_out_ref[r, c])
                acc = term if acc is None else acc + term
                g_out_ref[r, c] = grad[r * head_rows : (r + 1) * head_rows, lanes_of(c)].astype(BF)
            d_heads_ref[:, r * head_rows : (r + 1) * head_rows] = acc.astype(BF)


def middle(x_parts, cot_parts, heads, w_out, gain, w_ffn):
    parts, rows, feat = x_parts.shape
    steps = w_ffn.shape[0]
    block = (1,) + w_ffn.shape[1:]

    def whole(shape):
        return pl.BlockSpec(shape, lambda r: (0,) * len(shape))

    outs = (
        jax.ShapeDtypeStruct((rows, D), BF),
        jax.ShapeDtypeStruct((rows, D), F32),
        jax.ShapeDtypeStruct((rows, D), BF),
        jax.ShapeDtypeStruct(w_out.shape, BF),
        jax.ShapeDtypeStruct((1, D), F32),
        jax.ShapeDtypeStruct(w_ffn.shape, BF),
    )
    return pl.pallas_call(
        middle_body,
        grid=(steps,),
        out_shape=outs,
        in_specs=[whole(a.shape) for a in (x_parts, cot_parts, heads, w_out, gain)]
        + [pl.BlockSpec(block, lambda r: (r, 0, 0, 0))],
        out_specs=[whole(a.shape) for a in outs[:-1]] + [pl.BlockSpec(block, lambda r: (r, 0, 0, 0))],
        scratch_shapes=(
            pltpu.VMEM((rows, D), F32),
            pltpu.VMEM((rows, D), BF),
            pltpu.VMEM((rows, LANES), F32),
            pltpu.VMEM((rows, D), F32),
            pltpu.VMEM((rows, D), F32),
            pltpu.VMEM((rows, D), BF),
        ),
        compiler_params=params(dimension_semantics=("arbitrary",)),
        cost_estimate=cost_of(2 * rows * 3 * 3 * D * 2816, 40 << 20),
    )(x_parts, cot_parts, heads, w_out, gain, w_ffn)


def back_body(
    dq_ref, dkf_ref, hf_ref, bq_ref, turn_ref, w_ref, h_ref, x_ref, gain_ref, d_mixed_ref,
    gi_ref, g_gain_ref, g_ref, d_ref,
):
    parts, rows, feat = x_ref.shape
    heads = hf_ref[...]
    high = heads.astype(BF)
    low = (heads - high.astype(F32)).astype(BF)
    dq = dq_ref[...] * (1.0 / RQ)
    cosine = turn_ref[:, :LANES]
    sine = turn_ref[:, LANES:]
    d_fac = jnp.zeros((rows, H * FAC), F32)
    folded = []
    for r in range(RQ):
        tile = bq_ref[:, (r // 2) * LANES : (r // 2 + 1) * LANES]
        rank = double_left(tile) if r % 2 == 0 else double_right(tile)
        first = (2 * RK + r) * H
        product = dq * jnp.concatenate([rank] * PAIRS, axis=1)
        d_fac = d_fac + two_pass(product, collect(D, H * FAC, first))
        pick = spread(H * FAC, first, D)
        terms = (nn(high, pick) + nn(low, pick)) * dq
        acc = terms[:, :LANES]
        for p in range(1, PAIRS):
            acc = acc + terms[:, p * LANES : (p + 1) * LANES]
        folded.append(acc + pltpu.roll(acc, HD, 1))
    lane = lane_iota(folded[0].shape)

    def turn_back(part):
        return part * cosine - swap_halves(part) * sine

    for tile in range(3):
        merged = jnp.where(lane < HD, folded[2 * tile], folded[2 * tile + 1])
        d_ref[:, tile * LANES : (tile + 1) * LANES] = turn_back(merged).astype(BF)
    d_ref[:, 3 * LANES : 4 * LANES] = turn_back(dkf_ref[:, :LANES].astype(F32)).astype(BF)
    d_ref[:, 4 * LANES : 5 * LANES] = dkf_ref[:, LANES : 2 * LANES].astype(BF)
    keep = 2 * RK * H
    key_fac = jnp.concatenate(
        [dkf_ref[:, 2 * LANES :].astype(F32), jnp.zeros((rows, H * FAC - keep), F32)], axis=1
    )
    d_ref[:, 5 * LANES :] = jnp.where(lane_iota(d_fac.shape) < keep, key_fac, d_fac).astype(BF)
    d_all = d_ref[...]
    d_h = nt(d_all, w_ref[...])
    g_ref[...] = tn(d_all, h_ref[...]).astype(BF)
    xs = [x_ref[c].astype(F32) for c in range(parts)]
    total = sum(jnp.sum(v * v, axis=1, keepdims=True) for v in xs)
    scale = lax.rsqrt(total / D + EPS)
    dot = None
    for c in range(parts):
        lanes = slice(c * feat, (c + 1) * feat)
        normed = xs[c] * scale
        grad = d_h[:, lanes]
        g_gain_ref[:, lanes] = jnp.sum(grad * normed, axis=0, keepdims=True)
        part = jnp.sum(grad * gain_ref[:, lanes] * normed, axis=1, keepdims=True)
        dot = part if dot is None else dot + part
    for c in range(parts):
        lanes = slice(c * feat, (c + 1) * feat)
        normed = xs[c] * scale
        gi_ref[c] = d_mixed_ref[:, lanes] + scale * (
            d_h[:, lanes] * gain_ref[:, lanes] - normed * (dot / D)
        )


def back(dq, dkf, hf, bq, turn, w_rh, h, x_parts, gain, d_mixed):
    rows = dq.shape[0]
    return call(
        back_body,
        (
            jax.ShapeDtypeStruct(x_parts.shape, F32),
            jax.ShapeDtypeStruct((1, D), F32),
            jax.ShapeDtypeStruct((w_rh.shape[1], D), BF),
        ),
        scratch=(pltpu.VMEM((rows, w_rh.shape[1]), BF),),
        cost=cost_of(2 * rows * D * 800 * 6, 12 << 20),
    )(dq, dkf, hf, bq, turn, w_rh, h, x_parts, gain, d_mixed)


def local(
    tokens_in, segments, gain_attn, gain_ffn, w_heads, w_ranks, w_out, w_gate, w_up, w_down, cotangent
):
    n_row = lax.axis_size("row")
    n_col = lax.axis_size("col")
    row = lax.axis_index("row")
    col = lax.axis_index("col")
    micro, row_tokens, feat = tokens_in.shape
    subs = n_col // micro
    rows = row_tokens // subs
    length = row_tokens * n_row
    head_local = w_heads.shape[1] // FAC
    rank_local = w_ranks.shape[1]
    ffn_local = w_gate.shape[1]
    out_local = w_out.shape[0]
    block = row * subs + col % subs
    past = min(-(-(MAX_DOC - 1) // rows), n_row * subs - 1)
    keys = (past + 1) * rows

    heads_t = jnp.transpose(w_heads.reshape(feat, head_local, FAC), (2, 1, 0))
    heads_t = heads_t[jnp.array(FAC_ORDER)].reshape(FAC * head_local, feat)
    attn_local = jnp.concatenate([w_ranks.T, heads_t, w_out], axis=0)
    ffn_block = jnp.concatenate([w_gate.T, w_up.T, w_down], axis=0)
    attn_all = lax.all_gather(attn_local, ("row", "col"), axis=0)
    ffn_all = lax.all_gather(ffn_block, ("row", "col"), axis=0)
    ffn_all = ffn_all.reshape(n_row, n_col, 3 * ffn_local, feat)
    attn_all = attn_all.reshape(n_row, n_col, attn_local.shape[0], feat)
    ranks_full = jnp.transpose(attn_all[:, :, :rank_local], (1, 3, 0, 2)).reshape(D, n_row * rank_local)
    heads_full = attn_all[:, :, rank_local : rank_local + FAC * head_local]
    heads_full = heads_full.reshape(n_row, n_col, FAC, head_local, feat)
    heads_full = jnp.transpose(heads_full, (1, 4, 2, 0, 3)).reshape(D, FAC * H)
    w_rh = jnp.concatenate([ranks_full, heads_full], axis=1)
    w_out_all = attn_all[:, :, rank_local + FAC * head_local :]
    gain_one = lax.all_gather(gain_attn, "col", axis=0, tiled=True).reshape(1, D)
    gain_two = lax.all_gather(gain_ffn, "col", axis=0, tiled=True).reshape(1, D)

    def own_tokens(values):
        return lax.all_to_all(values.reshape(n_col, rows, feat), "col", 0, 0, tiled=True)

    x_parts = own_tokens(tokens_in)
    cot_parts = own_tokens(cotangent)

    seg_row = lax.dynamic_index_in_dim(segments, col // subs, 0, keepdims=False)
    padded = jnp.concatenate([jnp.full((1, past * rows), -1, jnp.int32), seg_row], axis=1)
    seg_window = lax.dynamic_slice_in_dim(padded, block * rows, keys, 1)
    own_seg = seg_window[0, past * rows :]
    key_idx = jnp.arange(keys, dtype=jnp.int32)
    query_idx = jnp.arange(rows, dtype=jnp.int32) + past * rows
    before = (own_seg[:, None] == seg_window) & (key_idx[None, :] < query_idx[:, None])
    places = jnp.sum(before.astype(jnp.int32), axis=1)
    inverse = ROPE ** (-(jnp.arange(HD // 2, dtype=F32) * 2.0 / HD))
    angles = places.astype(F32)[:, None] * inverse[None, :]
    cosine = jnp.cos(angles)
    sine = jnp.sin(angles)
    turn = jnp.concatenate([cosine] * 4 + [-sine, sine, -sine, sine], axis=1)

    h_one, head_fac, bq_rot, key_fac, queries = front(x_parts, gain_one, w_rh, turn)

    groups = [[m * subs + s for s in range(subs)] for m in range(micro)]
    gathered = lax.all_gather(key_fac, "row", axis=0)
    gathered = lax.all_gather(gathered, "col", axis=1, axis_index_groups=groups)
    gathered = gathered.reshape(length, key_fac.shape[1])
    padded = jnp.concatenate([jnp.zeros((past * rows, key_fac.shape[1]), BF), gathered], axis=0)
    kf_window = lax.dynamic_slice_in_dim(padded, block * rows, keys, 0)

    heads_out, lse, key_all, value_all = attend(queries, kf_window, seg_window)
    out_own, d_mixed, d_heads, g_out, g_gain_two, g_ffn = middle(
        x_parts, cot_parts, heads_out, w_out_all, gain_two, ffn_all
    )
    d_q, d_kf = attend_back(queries, key_all, value_all, d_heads, lse, kf_window, seg_window)

    spread_kf = lax.dynamic_update_slice_in_dim(jnp.zeros_like(padded), d_kf, block * rows, 0)[past * rows :]
    spread_kf = spread_kf.reshape(n_row, subs, rows, -1)
    own_kf = lax.psum_scatter(spread_kf, "row", scatter_dimension=0, tiled=False)
    own_kf = lax.psum_scatter(own_kf, "col", scatter_dimension=0, tiled=False, axis_index_groups=groups)

    gi_parts, g_gain_one, g_rh = back(
        d_q, own_kf, head_fac, bq_rot, turn, w_rh, h_one, x_parts, gain_one, d_mixed
    )

    out_parts = jnp.transpose(out_own.reshape(rows, n_col, feat), (1, 0, 2))
    output = lax.all_to_all(out_parts, "col", 0, 0, tiled=True).reshape(tokens_in.shape)
    grad_input = lax.all_to_all(gi_parts, "col", 0, 0, tiled=True).reshape(tokens_in.shape)

    g_ranks = g_rh[: FAC * HD].reshape(n_row, rank_local, n_col, feat)
    g_heads = g_rh[FAC * HD :].reshape(FAC, n_row, head_local, n_col, feat)
    g_ranks = jnp.transpose(g_ranks, (0, 2, 1, 3))
    g_heads = jnp.transpose(g_heads, (1, 3, 0, 2, 4)).reshape(n_row, n_col, FAC * head_local, feat)
    g_attn = jnp.concatenate([g_ranks, g_heads, g_out], axis=2)

    def total(values):
        values = values.reshape((n_row * n_col,) + values.shape[2:])
        part = lax.psum_scatter(values, ("row", "col"), scatter_dimension=0, tiled=False)
        return lax.psum(part, "dp").astype(F32)

    g_ffn = total(g_ffn)
    g_attn = total(g_attn)
    gains = jnp.concatenate([g_gain_one, g_gain_two], axis=0)
    gains = lax.psum(gains, ("dp", "row", "col"))
    gains = lax.dynamic_slice_in_dim(gains, col * feat, feat, 1)
    own_heads = g_attn[rank_local : rank_local + FAC * head_local].reshape(FAC, head_local, feat)
    own_heads = jnp.transpose(own_heads[jnp.array(FAC_BACK)], (2, 1, 0)).reshape(w_heads.shape)
    return (
        output,
        grad_input,
        gains[0],
        gains[1],
        own_heads,
        g_attn[:rank_local].T,
        g_attn[rank_local + FAC * head_local :],
        g_ffn[:ffn_local].T,
        g_ffn[ffn_local : 2 * ffn_local].T,
        g_ffn[2 * ffn_local :],
    )


def solution(mesh):
    tokens = P(None, ("dp", "row"), "col")
    both = P("col", "row")
    turned = P("row", "col")
    gain = P("col")
    return jax.shard_map(
        local,
        mesh=mesh,
        in_specs=(tokens, P(None, "dp", None), gain, gain, both, both, turned, both, both, turned, tokens),
        out_specs=(tokens, tokens, gain, gain, both, both, turned, both, both, turned),
        check_vma=False,
    )
```

```python
import functools

import jax
import jax.numpy as jnp
from jax import lax
from jax.experimental import pallas as pl
from jax.experimental.pallas import tpu as pltpu
from jax.sharding import PartitionSpec as P

D = 1024
H = 16
HD = 64
RQ = 6
RK = 2
FAC = 10
MAX_DOC = 1024

EPS = 1e-06
ROPE = 10000.0
NEG = -1e30
BF = jnp.bfloat16
F32 = jnp.float32
LANES = 128
PAIRS = H // 2
FAC_ORDER = (6, 7, 8, 9, 0, 1, 2, 3, 4, 5)
FAC_BACK = (4, 5, 6, 7, 8, 9, 0, 1, 2, 3)
VMEM = pl.BlockSpec(memory_space=pltpu.VMEM)


def nn(a, b):
    return jnp.dot(a, b, preferred_element_type=F32)


def nt(a, b):
    return lax.dot_general(a, b, (((1,), (1,)), ((), ())), preferred_element_type=F32)


def tn(a, b):
    return lax.dot_general(a, b, (((0,), (0,)), ((), ())), preferred_element_type=F32)


def two_pass(a, b):
    high = a.astype(BF)
    low = (a - high.astype(F32)).astype(BF)
    return nn(high, b) + nn(low, b)


def lane_iota(shape):
    return lax.broadcasted_iota(jnp.int32, shape, len(shape) - 1)


def spread(rows, first, width):
    row = lax.broadcasted_iota(jnp.int32, (rows, width), 0)
    head = lax.broadcasted_iota(jnp.int32, (rows, width), 1) // HD
    return (row == head + first).astype(F32).astype(BF)


def collect(rows, width, first):
    head = lax.broadcasted_iota(jnp.int32, (rows, width), 0) // HD
    lane = lax.broadcasted_iota(jnp.int32, (rows, width), 1)
    return (lane == head + first).astype(F32).astype(BF)


def swap_halves(tile):
    lane = lane_iota(tile.shape)
    ahead = pltpu.roll(tile, LANES - HD // 2, 1)
    behind = pltpu.roll(tile, HD // 2, 1)
    return jnp.where(lane % HD < HD // 2, ahead, behind)


def double_left(tile):
    return jnp.where(lane_iota(tile.shape) < HD, tile, pltpu.roll(tile, HD, 1))


def double_right(tile):
    return jnp.where(lane_iota(tile.shape) < HD, pltpu.roll(tile, HD, 1), tile)


def params(**more):
    return pltpu.CompilerParams(vmem_limit_bytes=60 << 20, **more)


def call(body, outs, scratch=(), cost=None):
    return pl.pallas_call(
        body,
        out_shape=outs,
        scratch_shapes=scratch,
        compiler_params=params(),
        cost_estimate=cost,
    )


def cost_of(flops, moved):
    return pl.CostEstimate(flops=int(flops), bytes_accessed=int(moved), transcendentals=0)


def front_body(x_ref, gain_ref, w_ref, turn_ref, h_ref, hf_ref, bq_ref, kf_ref, q_ref):
    parts = x_ref.shape[0]
    feat = x_ref.shape[2]
    xs = [x_ref[c].astype(F32) for c in range(parts)]
    total = sum(jnp.sum(v * v, axis=1, keepdims=True) for v in xs)
    scale = lax.rsqrt(total / D + EPS)
    for c in range(parts):
        lanes = slice(c * feat, (c + 1) * feat)
        h_ref[:, lanes] = (xs[c] * scale * gain_ref[:, lanes]).astype(BF)
    both = nn(h_ref[...], w_ref[...])
    heads = both[:, FAC * HD :]
    hf_ref[...] = heads
    cosine = turn_ref[:, :LANES]
    sine = turn_ref[:, LANES:]
    for tile in range(FAC * HD // LANES):
        lanes = slice(tile * LANES, (tile + 1) * LANES)
        part = both[:, lanes]
        if tile < 4:
            part = part * cosine + swap_halves(part) * sine
        if tile < 3:
            bq_ref[:, lanes] = part
        else:
            kf_ref[:, (tile - 3) * LANES : (tile - 2) * LANES] = part.astype(BF)
    kf_ref[:, 2 * LANES :] = heads[:, : 2 * RK * H].astype(BF)
    high = heads.astype(BF)
    low = (heads - high.astype(F32)).astype(BF)
    ranks = []
    for r in range(RQ):
        tile = bq_ref[:, (r // 2) * LANES : (r // 2 + 1) * LANES]
        ranks.append(double_left(tile) if r % 2 == 0 else double_right(tile))
    width = 2 * LANES
    for p in range(D // width):
        lanes = slice(p * width, (p + 1) * width)
        acc = None
        for r in range(RQ):
            pick = spread(H * FAC, (2 * RK + r) * H + p * (width // HD), width)
            term = (nn(high, pick) + nn(low, pick)) * jnp.concatenate([ranks[r]] * 2, axis=1)
            acc = term if acc is None else acc + term
        q_ref[:, lanes] = (acc / RQ).astype(BF)


def front(x_parts, gain, w_rh, turn):
    rows = x_parts.shape[1]
    return call(
        front_body,
        (
            jax.ShapeDtypeStruct((rows, D), BF),
            jax.ShapeDtypeStruct((rows, H * FAC), F32),
            jax.ShapeDtypeStruct((rows, RQ * HD), F32),
            jax.ShapeDtypeStruct((rows, 2 * LANES + 2 * RK * H), BF),
            jax.ShapeDtypeStruct((rows, D), BF),
        ),
        cost=cost_of(2 * rows * D * 800 * 3, 6 << 20),
    )(x_parts, gain, w_rh, turn)


def mask_bias(seg_ref, keys, rows):
    seg_row = seg_ref[...].astype(F32)
    wide = jnp.broadcast_to(seg_row, (LANES, keys))
    column = wide.T
    column = jnp.concatenate([column] * (rows // LANES), axis=1)
    key_idx = lax.broadcasted_iota(jnp.int32, (keys, rows), 0)
    query_idx = lax.broadcasted_iota(jnp.int32, (keys, rows), 1) + (keys - rows)
    same = column == seg_row[:, keys - rows :]
    return jnp.where(same & (key_idx <= query_idx), 0.0, NEG)


def attend_body(q_ref, kf_ref, seg_ref, o_ref, lse_ref, k_ref, v_ref, bias_ref, dup_ref):
    rows = q_ref.shape[0]
    keys = kf_ref.shape[0]
    bias_ref[...] = mask_bias(seg_ref, keys, rows)
    for s in range(2 * RK):
        tile = kf_ref[:, (s // 2) * LANES : (s // 2 + 1) * LANES].astype(F32)
        dup_ref[s] = double_left(tile) if s % 2 == 0 else double_right(tile)

    def pair(p, carried):
        lanes = pl.ds(pl.multiple_of(p * LANES, LANES), LANES)
        weights = kf_ref[:, 2 * LANES :]
        made = []
        for kind in range(2):
            acc = None
            for s in range(RK):
                pick = spread(2 * RK * H, (kind * RK + s) * H + 2 * p, LANES)
                term = nn(weights, pick) * dup_ref[kind * RK + s]
                acc = term if acc is None else acc + term
            made.append((acc / RK).astype(BF))
        k_tile, v_tile = made
        k_ref[:, lanes] = k_tile
        v_ref[:, lanes] = v_tile
        v_turned = v_tile.astype(F32).T.astype(BF)
        q_turned = (q_ref[:, lanes].astype(F32) * HD**-0.5).T
        half = lax.broadcasted_iota(jnp.int32, q_turned.shape, 0) // HD
        outs = []
        for side in range(2):
            q_side = jnp.where(half == side, q_turned, 0.0).astype(BF)
            scores = nn(k_tile, q_side) + bias_ref[...]
            peak = jnp.max(scores, axis=0, keepdims=True)
            weight = jnp.exp(scores - peak)
            total = jnp.sum(weight, axis=0, keepdims=True)
            probs = (weight * (1.0 / total)).astype(BF)
            outs.append(nn(v_turned[side * HD : (side + 1) * HD], probs))
            lse_ref[2 * p + side] = jnp.broadcast_to(peak + jnp.log(total), (8, rows))
        o_ref[:, lanes] = jnp.concatenate(outs, axis=0).T.astype(BF)
        return carried

    lax.fori_loop(0, PAIRS, pair, 0)


def attend(q, kf_window, seg_window):
    rows = q.shape[0]
    keys = kf_window.shape[0]
    return call(
        attend_body,
        (
            jax.ShapeDtypeStruct((rows, D), BF),
            jax.ShapeDtypeStruct((H, 8, rows), F32),
            jax.ShapeDtypeStruct((keys, D), BF),
            jax.ShapeDtypeStruct((keys, D), BF),
        ),
        scratch=(pltpu.VMEM((keys, rows), F32), pltpu.VMEM((2 * RK, keys, LANES), F32)),
        cost=cost_of(2 * rows * keys * D * 16, 16 << 20),
    )(q, kf_window, seg_window)


def attend_back_body(
    q_ref, k_ref, v_ref, do_ref, lse_ref, kf_ref, seg_ref, dq_ref, dkf_ref, bias_ref, dup_ref, sum_ref, fac_ref
):
    rows = q_ref.shape[0]
    keys = kf_ref.shape[0]
    bias_ref[...] = mask_bias(seg_ref, keys, rows)
    for s in range(2 * RK):
        tile = kf_ref[:, (s // 2) * LANES : (s // 2 + 1) * LANES].astype(F32)
        dup_ref[s] = double_left(tile) if s % 2 == 0 else double_right(tile)
    sum_ref[...] = jnp.zeros_like(sum_ref)
    fac_ref[...] = jnp.zeros_like(fac_ref)

    def pair(p, carried):
        lanes = pl.ds(pl.multiple_of(p * LANES, LANES), LANES)
        k_tile = k_ref[:, lanes]
        v_tile = v_ref[:, lanes]
        k_turned = k_tile.astype(F32).T.astype(BF)
        q_tile = q_ref[:, lanes].astype(F32) * HD**-0.5
        do_tile = do_ref[:, lanes].astype(F32)
        q_turned = q_tile.T
        do_turned = do_tile.T
        half = lax.broadcasted_iota(jnp.int32, q_turned.shape, 0) // HD
        lane_half = lax.broadcasted_iota(jnp.int32, q_tile.shape, 1) // HD
        d_k = None
        d_v = None
        d_q = []
        for side in range(2):
            q_side = jnp.where(half == side, q_turned, 0.0).astype(BF)
            do_side = jnp.where(half == side, do_turned, 0.0).astype(BF)
            scores = nn(k_tile, q_side) + bias_ref[...]
            probs = jnp.exp(scores - lse_ref[2 * p + side][:1])
            d_prob = nn(v_tile, do_side)
            delta = jnp.sum(probs * d_prob, axis=0, keepdims=True)
            d_score = (probs * (d_prob - delta)).astype(BF)
            d_q.append(nn(k_turned[side * HD : (side + 1) * HD], d_score))
            q_back = jnp.where(lane_half == side, q_tile, 0.0).astype(BF)
            do_back = jnp.where(lane_half == side, do_tile, 0.0).astype(BF)
            part_k = nn(d_score, q_back)
            part_v = nn(probs.astype(BF), do_back)
            d_k = part_k if d_k is None else d_k + part_k
            d_v = part_v if d_v is None else d_v + part_v
        dq_ref[:, lanes] = jnp.concatenate(d_q, axis=0).T * HD**-0.5
        weights = kf_ref[:, 2 * LANES :]
        for kind, grad in ((0, d_k), (1, d_v)):
            for s in range(RK):
                slot = kind * RK + s
                pick = spread(2 * RK * H, slot * H + 2 * p, LANES)
                sum_ref[slot] += nn(weights, pick) * grad
                fac_ref[...] += two_pass(grad * dup_ref[slot], collect(LANES, 2 * RK * H, slot * H + 2 * p))
        return carried

    lax.fori_loop(0, PAIRS, pair, 0)
    for tile in range(2):
        first = sum_ref[2 * tile]
        second = sum_ref[2 * tile + 1]
        first = first + pltpu.roll(first, HD, 1)
        second = second + pltpu.roll(second, HD, 1)
        merged = jnp.where(lane_iota(first.shape) < HD, first, second)
        dkf_ref[:, tile * LANES : (tile + 1) * LANES] = (merged / RK).astype(BF)
    dkf_ref[:, 2 * LANES :] = (fac_ref[...] / RK).astype(BF)


def attend_back(q, k, v, d_heads, lse, kf_window, seg_window):
    rows = q.shape[0]
    keys = kf_window.shape[0]
    return call(
        attend_back_body,
        (
            jax.ShapeDtypeStruct((rows, D), F32),
            jax.ShapeDtypeStruct(kf_window.shape, BF),
        ),
        scratch=(
            pltpu.VMEM((keys, rows), F32),
            pltpu.VMEM((2 * RK, keys, LANES), F32),
            pltpu.VMEM((2 * RK, keys, LANES), F32),
            pltpu.VMEM((keys, 2 * RK * H), F32),
        ),
        cost=cost_of(2 * rows * keys * D * 40, 16 << 20),
    )(q, k, v, d_heads, lse, kf_window, seg_window)


MESH = pl.DeviceIdType.MESH
ANY = pl.BlockSpec(memory_space=pl.ANY)


class Mover:
    def __init__(self, send_sem, recv_sem):
        self.send_sem = send_sem
        self.recv_sem = recv_sem
        self.used = 0

    def copy(self, source, target, **place):
        index = self.used
        self.used += 1
        return pltpu.make_async_remote_copy(
            src_ref=source,
            dst_ref=target,
            send_sem=self.send_sem.at[index],
            recv_sem=self.recv_sem.at[index],
            device_id=place,
            device_id_type=MESH,
        )


def greet(partners):
    barrier = pltpu.get_barrier_semaphore()
    count = 0
    for present, place in partners:
        if present is None:
            pl.semaphore_signal(barrier, inc=1, device_id=place, device_id_type=MESH)
            count = count + 1
        else:

            @pl.when(present)
            def _():
                pl.semaphore_signal(barrier, inc=1, device_id=place, device_id_type=MESH)

            count = count + present.astype(jnp.int32)
    pl.semaphore_wait(barrier, count)


def neighbours():
    col = lax.axis_index("col")
    core = col + 1 - 2 * lax.rem(col, 2)
    across = lax.rem(col + 2, 4)
    return col, core, across


def comm_params(ident):
    return params(collective_id=ident, has_side_effects=True)


GATHER_CHUNKS = 4


def col_gather_body(x_ref, out_ref, send_sem, recv_sem, local_sem):
    col, core, across = neighbours()
    greet([(None, {"col": core}), (None, {"col": across})])
    mover = Mover(send_sem, recv_sem)
    size = x_ref.shape[0] // GATHER_CHUNKS
    rows = [pl.ds(k * size, size) for k in range(GATHER_CHUNKS)]
    far = [mover.copy(x_ref.at[r], out_ref.at[col, r], col=across) for r in rows]
    for c in far:
        c.start()
    near = mover.copy(x_ref, out_ref.at[col], col=core)
    near.start()
    own = pltpu.make_async_copy(x_ref, out_ref.at[col], local_sem)
    own.start()
    passed = []
    for k, r in enumerate(rows):
        far[k].wait_recv()
        c = mover.copy(out_ref.at[across, r], out_ref.at[across, r], col=core)
        c.start()
        passed.append(c)
    for c in far:
        c.wait_send()
    near.wait()
    own.wait()
    for c in passed:
        c.wait()


def col_gather(x, ident):
    count = 2 * GATHER_CHUNKS + 1
    return pl.pallas_call(
        col_gather_body,
        out_shape=jax.ShapeDtypeStruct((4,) + x.shape, x.dtype),
        in_specs=[ANY],
        out_specs=ANY,
        scratch_shapes=[
            pltpu.SemaphoreType.DMA((count,)),
            pltpu.SemaphoreType.DMA((count,)),
            pltpu.SemaphoreType.DMA,
        ],
        compiler_params=comm_params(ident),
        cost_estimate=cost_of(0, 3 << 20),
    )(x)


REDUCE_CHUNKS = 4


def col_reduce_body(
    dh_ref, out_ref, dh_sum_ref, out_sum_ref, near_ref, far_ref, pair_ref, send_sem, recv_sem
):
    col, core, across = neighbours()
    cross = lax.rem(core + 2, 4)
    greet([(None, {"col": core}), (None, {"col": across})])
    mover = Mover(send_sem, recv_sem)
    size = dh_ref.shape[1] // REDUCE_CHUNKS
    near = []
    for index, source in enumerate((dh_ref, out_ref)):
        pieces = []
        for k in range(REDUCE_CHUNKS):
            rows = pl.ds(k * size, size)
            c = mover.copy(source.at[cross, rows], near_ref.at[index, 1, rows], col=core)
            c.start()
            pieces.append(c)
        mine = mover.copy(source.at[core], near_ref.at[index, 0], col=core)
        mine.start()
        near.append((pieces, mine))
    far = []
    for index, source in enumerate((dh_ref, out_ref)):
        for k in range(REDUCE_CHUNKS):
            rows = pl.ds(k * size, size)
            near[index][0][k].wait_recv()
            pair_ref[index, rows] = (
                source[across, rows].astype(F32) + near_ref[index, 1, rows].astype(F32)
            ).astype(BF)
            c = mover.copy(pair_ref.at[index, rows], far_ref.at[index, rows], col=across)
            c.start()
            far.append(c)
    for index, (source, target) in enumerate(((dh_ref, dh_sum_ref), (out_ref, out_sum_ref))):
        near[index][1].wait_recv()
        for k in range(REDUCE_CHUNKS):
            rows = pl.ds(k * size, size)
            far[index * REDUCE_CHUNKS + k].wait_recv()
            target[rows] = (
                source[col, rows].astype(F32)
                + near_ref[index, 0, rows].astype(F32)
                + far_ref[index, rows].astype(F32)
            )
    for pieces, mine in near:
        for c in pieces:
            c.wait_send()
        mine.wait_send()
    for c in far:
        c.wait_send()


def col_reduce(dh_parts, out_parts):
    rows = dh_parts.shape[1]
    count = 2 * (2 * REDUCE_CHUNKS + 1)
    total = jax.ShapeDtypeStruct((rows, D), F32)
    return pl.pallas_call(
        col_reduce_body,
        out_shape=(total, total),
        in_specs=[VMEM, VMEM],
        out_specs=(VMEM, VMEM),
        scratch_shapes=[
            pltpu.VMEM((2, 2, rows, D), BF),
            pltpu.VMEM((2, rows, D), BF),
            pltpu.VMEM((2, rows, D), BF),
            pltpu.SemaphoreType.DMA((count,)),
            pltpu.SemaphoreType.DMA((count,)),
        ],
        compiler_params=comm_params(2),
        cost_estimate=cost_of(0, 6 << 20),
    )(dh_parts, out_parts)


def row_partners(row, n_row, core):
    return [
        (None, {"col": core}),
        (row + 1 < n_row, {"row": row + 1}),
        (row + 2 < n_row, {"row": row + 2}),
        (row >= 1, {"row": row - 1}),
        (row >= 2, {"row": row - 2}),
    ]


def window_body(n_row, x_ref, zero_ref, win_ref, send_sem, recv_sem, local_sem):
    row = lax.axis_index("row")
    col, core, _ = neighbours()
    side = lax.rem(col, 2)
    greet(row_partners(row, n_row, core))
    mover = Mover(send_sem, recv_sem)
    one = mover.copy(x_ref, win_ref.at[2], row=row + 1)
    two = mover.copy(x_ref, win_ref.at[0], row=row + 2)
    near = mover.copy(x_ref, win_ref.at[3], col=core)
    pass_one = mover.copy(win_ref.at[2], win_ref.at[1 + 2 * side], col=core)
    pass_two = mover.copy(win_ref.at[0], win_ref.at[1], col=core)
    has_one = row >= 1
    has_two = row >= 2

    @pl.when(row + 1 < n_row)
    def _():
        one.start()

    @pl.when(row + 2 < n_row)
    def _():
        two.start()

    @pl.when(side == 0)
    def _():
        near.start()

    own = pltpu.make_async_copy(x_ref, win_ref.at[4], local_sem.at[0])
    own.start()

    def fill(slot):
        return pltpu.make_async_copy(zero_ref, win_ref.at[slot], local_sem.at[slot + 1])

    for absent, slots in (
        (jnp.logical_not(has_two), (0,)),
        (jnp.logical_and(jnp.logical_not(has_two), side == 0), (1,)),
        (jnp.logical_and(jnp.logical_not(has_one), side == 1), (1,)),
        (jnp.logical_not(has_one), (2,)),
        (jnp.logical_and(jnp.logical_not(has_one), side == 0), (3,)),
    ):

        @pl.when(absent)
        def _():
            for slot in slots:
                c = fill(slot)
                c.start()
                c.wait()

    @pl.when(has_one)
    def _():
        one.wait_recv()
        pass_one.start()

    @pl.when(has_two)
    def _():
        two.wait_recv()

    sends_two = jnp.logical_and(has_two, side == 1)
    takes_two = jnp.logical_and(has_two, side == 0)

    @pl.when(sends_two)
    def _():
        pass_two.start()

    @pl.when(has_one)
    def _():
        pass_one.wait_recv()
        pass_one.wait_send()

    @pl.when(takes_two)
    def _():
        pass_two.wait_recv()

    @pl.when(sends_two)
    def _():
        pass_two.wait_send()

    @pl.when(side == 1)
    def _():
        near.wait_recv()

    @pl.when(side == 0)
    def _():
        near.wait_send()

    @pl.when(row + 1 < n_row)
    def _():
        one.wait_send()

    @pl.when(row + 2 < n_row)
    def _():
        two.wait_send()

    own.wait()


def window(x, n_row):
    zero = jnp.zeros(x.shape, x.dtype)
    return pl.pallas_call(
        functools.partial(window_body, n_row),
        out_shape=jax.ShapeDtypeStruct((5,) + x.shape, x.dtype),
        in_specs=[ANY, ANY],
        out_specs=ANY,
        scratch_shapes=[
            pltpu.SemaphoreType.DMA((5,)),
            pltpu.SemaphoreType.DMA((5,)),
            pltpu.SemaphoreType.DMA((6,)),
        ],
        compiler_params=comm_params(3),
        cost_estimate=cost_of(0, 1 << 20),
    )(x, zero)


def window_back_body(n_row, win_ref, sum_ref, near_ref, send_ref, far_ref, send_sem, recv_sem):
    row = lax.axis_index("row")
    col, core, _ = neighbours()
    side = lax.rem(col, 2)
    greet(row_partners(row, n_row, core))
    mover = Mover(send_sem, recv_sem)
    first = mover.copy(win_ref.at[1], near_ref.at[0], col=core)
    second = mover.copy(win_ref.at[3], near_ref.at[1], col=core)
    first.start()
    second.start()
    one = mover.copy(send_ref.at[0], far_ref.at[0], row=row - 1)
    two = mover.copy(send_ref.at[1], far_ref.at[1], row=row - 2)
    first.wait_recv()
    second.wait_recv()
    zero = jnp.zeros(near_ref.shape[1:], F32)
    low = near_ref[0].astype(F32)
    high = near_ref[1].astype(F32)
    left = side == 0
    send_ref[0] = (win_ref[2].astype(F32) + jnp.where(left, low, high)).astype(BF)
    send_ref[1] = (win_ref[0].astype(F32) + jnp.where(left, zero, low)).astype(BF)

    @pl.when(row >= 1)
    def _():
        one.start()

    @pl.when(row >= 2)
    def _():
        two.start()

    sum_ref[...] = win_ref[4].astype(F32) + jnp.where(left, high, zero)

    @pl.when(row + 1 < n_row)
    def _():
        one.wait_recv()
        sum_ref[...] += far_ref[0].astype(F32)

    @pl.when(row + 2 < n_row)
    def _():
        two.wait_recv()
        sum_ref[...] += far_ref[1].astype(F32)

    first.wait_send()
    second.wait_send()

    @pl.when(row >= 1)
    def _():
        one.wait_send()

    @pl.when(row >= 2)
    def _():
        two.wait_send()


def window_back(win, n_row):
    shape = win.shape[1:]
    return pl.pallas_call(
        functools.partial(window_back_body, n_row),
        out_shape=jax.ShapeDtypeStruct(shape, F32),
        in_specs=[VMEM],
        out_specs=VMEM,
        scratch_shapes=[
            pltpu.VMEM((2,) + shape, BF),
            pltpu.VMEM((2,) + shape, BF),
            pltpu.VMEM((2,) + shape, BF),
            pltpu.SemaphoreType.DMA((4,)),
            pltpu.SemaphoreType.DMA((4,)),
        ],
        compiler_params=comm_params(4),
        cost_estimate=cost_of(0, 1 << 20),
    )(win)


def mixing_body(x_ref, heads_ref, w_out_ref, gain_ref, mixed_ref, h_ref):
    parts, _, feat = x_ref.shape
    rows_of = w_out_ref.shape[0]
    head_rows = w_out_ref.shape[2]
    total = None
    for c in range(parts):
        lanes = slice(c * feat, (c + 1) * feat)
        acc = x_ref[c].astype(F32)
        for r in range(rows_of):
            acc = acc + nn(heads_ref[:, r * head_rows : (r + 1) * head_rows], w_out_ref[r, c])
        mixed_ref[:, lanes] = acc
        part = jnp.sum(acc * acc, axis=1, keepdims=True)
        total = part if total is None else total + part
    scale = lax.rsqrt(total / D + EPS)
    h_ref[...] = (mixed_ref[...] * scale * gain_ref[...]).astype(BF)


def mixing(x_parts, heads, w_out, gain):
    rows = heads.shape[0]
    return call(
        mixing_body,
        (jax.ShapeDtypeStruct((rows, D), F32), jax.ShapeDtypeStruct((rows, D), BF)),
        cost=cost_of(2 * rows * D * D, 5 << 20),
    )(x_parts, heads, w_out, gain)


def ffn_body(pieces, split, *refs):
    h_ref, cot_ref = refs[:2]
    w_refs = refs[2 : 2 + pieces]
    outs = refs[2 + pieces :]
    out_ref, back_ref = outs[:2]
    if split:
        keep_ref, send_ref, down_ref = outs[2:5]
        w_ref, dg_ref, du_ref, hid_ref, sems = outs[5:]
    else:
        g_ref = outs[2]
        w_ref, dg_ref, du_ref, hid_ref, sems = outs[3:]
    parts, rows, _ = h_ref.shape
    copies = []
    if split:
        dp = lax.axis_index("dp")
        units = w_refs[0].shape[1]
        wide = D // 2
        copies.append(pltpu.make_async_copy(w_refs[0], w_ref.at[:, pl.ds(0, units)], sems.at[0]))
        for k in range(1, pieces):
            slot = 1 + (k - 1) % 3
            first = dp if k <= 3 else 1 - dp
            lanes = pl.ds(pl.multiple_of(first * wide, wide), wide)
            copies.append(
                pltpu.make_async_copy(
                    w_refs[k], w_ref.at[:, pl.ds(slot * units, units), lanes], sems.at[k]
                )
            )
    else:
        copies.append(pltpu.make_async_copy(w_refs[0], w_ref, sems.at[0]))
    for c in copies:
        c.start()
    for c in copies:
        c.wait()

    def block(t, carried):
        gate = nt(h_ref[t], w_ref[0])
        up = nt(h_ref[t], w_ref[1])
        d_hidden = nt(cot_ref[t], w_ref[2])
        sig = 1.0 / (1.0 + jnp.exp(-gate))
        silu = gate * sig
        hidden = (silu * up).astype(BF)
        d_gate = (d_hidden * up * sig * (1.0 + gate * (1.0 - sig))).astype(BF)
        d_up = (d_hidden * silu).astype(BF)
        place = pl.ds(pl.multiple_of(t * rows, rows), rows)
        hid_ref[place] = hidden
        dg_ref[place] = d_gate
        du_ref[place] = d_up
        out_ref[t] = nn(hidden, w_ref[2]).astype(BF)
        back_ref[t] = (nn(d_gate, w_ref[0]) + nn(d_up, w_ref[1])).astype(BF)
        return carried

    lax.fori_loop(0, parts, block, 0)
    h_all = h_ref[...].reshape(parts * rows, D)
    cot_all = cot_ref[...].reshape(parts * rows, D)
    for place, (left, right) in enumerate(((dg_ref, h_all), (du_ref, h_all), (hid_ref, cot_all))):
        grad = tn(left[...], right)
        if not split:
            g_ref[place] = grad.astype(BF)
        elif place == 2:
            for k in range(down_ref.shape[0]):
                down_ref[k] = grad[k * units : (k + 1) * units].astype(BF)
        else:
            low = grad[:, :wide].astype(BF)
            high = grad[:, wide:].astype(BF)
            keep_ref[place] = jnp.where(dp == 0, low, high)
            send_ref[place] = jnp.where(dp == 0, high, low)


def ffn(h_all, cot_all, pieces, units, split):
    parts, rows, _ = h_all.shape
    tokens = parts * rows
    outs = [jax.ShapeDtypeStruct((parts, rows, D), BF)] * 2
    if split:
        outs += [jax.ShapeDtypeStruct((2, units, D // 2), BF)] * 2
        outs += [jax.ShapeDtypeStruct((4, units // 4, D), BF)]
    else:
        outs += [jax.ShapeDtypeStruct((3, units, D), BF)]
    return pl.pallas_call(
        functools.partial(ffn_body, len(pieces), split),
        out_shape=tuple(outs),
        in_specs=[VMEM, VMEM] + [ANY] * len(pieces),
        scratch_shapes=[
            pltpu.VMEM((3, units, D), BF),
            pltpu.VMEM((tokens, units), BF),
            pltpu.VMEM((tokens, units), BF),
            pltpu.VMEM((tokens, units), BF),
            pltpu.SemaphoreType.DMA((len(pieces),)),
        ],
        compiler_params=params(),
        cost_estimate=cost_of(2 * tokens * 9 * D * units, 20 << 20),
    )(h_all, cot_all, *pieces)


def unmix_body(
    mixed_ref, cot_ref, dh_ref, out_sum_ref, heads_ref, w_out_ref, gain_ref,
    out_ref, d_mixed_ref, d_heads_ref, g_out_ref, g_gain_ref,
):
    parts, _, feat = cot_ref.shape
    rows_of = w_out_ref.shape[0]
    head_rows = w_out_ref.shape[2]
    mixed = mixed_ref[...]
    scale = lax.rsqrt(jnp.sum(mixed * mixed, axis=1, keepdims=True) / D + EPS)
    normed = mixed * scale
    d_h = dh_ref[...]
    g_gain_ref[...] = jnp.sum(d_h * normed, axis=0, keepdims=True)
    inner = d_h * gain_ref[...]
    dot = jnp.sum(inner * normed, axis=1, keepdims=True) / D
    cot = jnp.concatenate([cot_ref[c] for c in range(parts)], axis=1).astype(F32)
    d_mixed = cot + scale * (inner - normed * dot)
    d_mixed_ref[...] = d_mixed
    low = d_mixed.astype(BF)
    grad = tn(heads_ref[...], low)
    for c in range(parts):
        out_ref[c] = (mixed[:, c * feat : (c + 1) * feat] + out_sum_ref[:, c * feat : (c + 1) * feat]).astype(BF)
    for r in range(rows_of):
        acc = None
        for c in range(parts):
            lanes = slice(c * feat, (c + 1) * feat)
            term = nt(low[:, lanes], w_out_ref[r, c])
            acc = term if acc is None else acc + term
            g_out_ref[r, c] = grad[r * head_rows : (r + 1) * head_rows, lanes].astype(BF)
        d_heads_ref[:, r * head_rows : (r + 1) * head_rows] = acc.astype(BF)


def unmix(mixed, cot_parts, dh, out_sum, heads, w_out, gain):
    rows = heads.shape[0]
    return call(
        unmix_body,
        (
            jax.ShapeDtypeStruct(cot_parts.shape, BF),
            jax.ShapeDtypeStruct((rows, D), F32),
            jax.ShapeDtypeStruct((rows, D), BF),
            jax.ShapeDtypeStruct(w_out.shape, BF),
            jax.ShapeDtypeStruct((1, D), F32),
        ),
        cost=cost_of(4 * rows * D * D, 10 << 20),
    )(mixed, cot_parts, dh, out_sum, heads, w_out, gain)


def back_body(
    dq_ref, dkf_ref, hf_ref, bq_ref, turn_ref, w_ref, h_ref, x_ref, gain_ref, d_mixed_ref,
    gi_ref, g_gain_ref, g_ref, d_ref,
):
    parts, rows, feat = x_ref.shape
    heads = hf_ref[...]
    high = heads.astype(BF)
    low = (heads - high.astype(F32)).astype(BF)
    dq = dq_ref[...] * (1.0 / RQ)
    cosine = turn_ref[:, :LANES]
    sine = turn_ref[:, LANES:]
    d_fac = jnp.zeros((rows, H * FAC), F32)
    folded = []
    for r in range(RQ):
        tile = bq_ref[:, (r // 2) * LANES : (r // 2 + 1) * LANES]
        rank = double_left(tile) if r % 2 == 0 else double_right(tile)
        first = (2 * RK + r) * H
        product = dq * jnp.concatenate([rank] * PAIRS, axis=1)
        d_fac = d_fac + two_pass(product, collect(D, H * FAC, first))
        pick = spread(H * FAC, first, D)
        terms = (nn(high, pick) + nn(low, pick)) * dq
        acc = terms[:, :LANES]
        for p in range(1, PAIRS):
            acc = acc + terms[:, p * LANES : (p + 1) * LANES]
        folded.append(acc + pltpu.roll(acc, HD, 1))
    lane = lane_iota(folded[0].shape)

    def turn_back(part):
        return part * cosine - swap_halves(part) * sine

    for tile in range(3):
        merged = jnp.where(lane < HD, folded[2 * tile], folded[2 * tile + 1])
        d_ref[:, tile * LANES : (tile + 1) * LANES] = turn_back(merged).astype(BF)
    d_ref[:, 3 * LANES : 4 * LANES] = turn_back(dkf_ref[:, :LANES].astype(F32)).astype(BF)
    d_ref[:, 4 * LANES : 5 * LANES] = dkf_ref[:, LANES : 2 * LANES].astype(BF)
    keep = 2 * RK * H
    key_fac = jnp.concatenate(
        [dkf_ref[:, 2 * LANES :].astype(F32), jnp.zeros((rows, H * FAC - keep), F32)], axis=1
    )
    d_ref[:, 5 * LANES :] = jnp.where(lane_iota(d_fac.shape) < keep, key_fac, d_fac).astype(BF)
    d_all = d_ref[...]
    d_h = nt(d_all, w_ref[...])
    g_ref[...] = tn(d_all, h_ref[...]).astype(BF)
    xs = [x_ref[c].astype(F32) for c in range(parts)]
    total = sum(jnp.sum(v * v, axis=1, keepdims=True) for v in xs)
    scale = lax.rsqrt(total / D + EPS)
    dot = None
    for c in range(parts):
        lanes = slice(c * feat, (c + 1) * feat)
        normed = xs[c] * scale
        grad = d_h[:, lanes]
        g_gain_ref[:, lanes] = jnp.sum(grad * normed, axis=0, keepdims=True)
        part = jnp.sum(grad * gain_ref[:, lanes] * normed, axis=1, keepdims=True)
        dot = part if dot is None else dot + part
    for c in range(parts):
        lanes = slice(c * feat, (c + 1) * feat)
        normed = xs[c] * scale
        gi_ref[c] = d_mixed_ref[:, lanes] + scale * (
            d_h[:, lanes] * gain_ref[:, lanes] - normed * (dot / D)
        )


def back(dq, dkf, hf, bq, turn, w_rh, h, x_parts, gain, d_mixed):
    rows = dq.shape[0]
    return call(
        back_body,
        (
            jax.ShapeDtypeStruct(x_parts.shape, F32),
            jax.ShapeDtypeStruct((1, D), F32),
            jax.ShapeDtypeStruct((w_rh.shape[1], D), BF),
        ),
        scratch=(pltpu.VMEM((rows, w_rh.shape[1]), BF),),
        cost=cost_of(2 * rows * D * 800 * 6, 12 << 20),
    )(dq, dkf, hf, bq, turn, w_rh, h, x_parts, gain, d_mixed)


def local(
    tokens_in, segments, gain_attn, gain_ffn, w_heads, w_ranks, w_out, w_gate, w_up, w_down, cotangent
):
    n_row = lax.axis_size("row")
    n_col = lax.axis_size("col")
    row = lax.axis_index("row")
    col = lax.axis_index("col")
    micro, row_tokens, feat = tokens_in.shape
    subs = n_col // micro
    rows = row_tokens // subs
    length = row_tokens * n_row
    head_local = w_heads.shape[1] // FAC
    rank_local = w_ranks.shape[1]
    ffn_local = w_gate.shape[1]
    out_local = w_out.shape[0]
    block = row * subs + col % subs
    past = min(-(-(MAX_DOC - 1) // rows), n_row * subs - 1)
    keys = (past + 1) * rows

    fast = n_col == 4 and n_row == 4 and lax.axis_size("dp") == 2 and micro == 2 and past == 4

    heads_t = jnp.transpose(w_heads.reshape(feat, head_local, FAC), (2, 1, 0))
    heads_t = heads_t[jnp.array(FAC_ORDER)].reshape(FAC * head_local, feat)
    attn_local = jnp.concatenate([w_ranks.T, heads_t, w_out], axis=0)
    attn_all = lax.all_gather(attn_local, ("row", "col"), axis=0)
    attn_all = attn_all.reshape(n_row, n_col, attn_local.shape[0], feat)
    ranks_full = jnp.transpose(attn_all[:, :, :rank_local], (1, 3, 0, 2)).reshape(D, n_row * rank_local)
    heads_full = attn_all[:, :, rank_local : rank_local + FAC * head_local]
    heads_full = heads_full.reshape(n_row, n_col, FAC, head_local, feat)
    heads_full = jnp.transpose(heads_full, (1, 4, 2, 0, 3)).reshape(D, FAC * H)
    w_rh = jnp.concatenate([ranks_full, heads_full], axis=1)
    w_out_all = attn_all[:, :, rank_local + FAC * head_local :]
    gain_one = lax.all_gather(gain_attn, "col", axis=0, tiled=True).reshape(1, D)
    gain_two = lax.all_gather(gain_ffn, "col", axis=0, tiled=True).reshape(1, D)

    part = ffn_local // n_col
    units = part * n_row
    w_ffn = jnp.stack([w_gate.T, w_up.T, w_down]).reshape(3, n_col, part, feat)
    w_ffn = lax.all_to_all(jnp.transpose(w_ffn, (1, 0, 2, 3)), "col", 0, 0, tiled=True)
    w_ffn = jnp.transpose(w_ffn, (1, 2, 0, 3)).reshape(3, part, D)

    def row_swap(values, k):
        return lax.ppermute(values, "row", [(r, r ^ k) for r in range(n_row)])

    def dp_swap(values):
        return lax.ppermute(values, "dp", [(0, 1), (1, 0)])

    if fast:
        dp = lax.axis_index("dp")
        half = lax.dynamic_slice_in_dim(w_ffn, dp * (D // 2), D // 2, 2)
        first = [row_swap(half, k) for k in range(1, n_row)]
        pieces = [w_ffn] + first + [dp_swap(v) for v in first]
    else:
        pieces = [jnp.transpose(lax.all_gather(w_ffn, "row", axis=0), (1, 0, 2, 3)).reshape(3, units, D)]

    def own_tokens(values):
        return lax.all_to_all(values.reshape(n_col, rows, feat), "col", 0, 0, tiled=True)

    x_parts = own_tokens(tokens_in)
    cot_parts = own_tokens(cotangent)
    cot_own = jnp.transpose(cot_parts, (1, 0, 2)).reshape(rows, D)

    seg_row = lax.dynamic_index_in_dim(segments, col // subs, 0, keepdims=False)
    padded = jnp.concatenate([jnp.full((1, past * rows), -1, jnp.int32), seg_row], axis=1)
    seg_window = lax.dynamic_slice_in_dim(padded, block * rows, keys, 1)
    own_seg = seg_window[0, past * rows :]
    key_idx = jnp.arange(keys, dtype=jnp.int32)
    query_idx = jnp.arange(rows, dtype=jnp.int32) + past * rows
    before = (own_seg[:, None] == seg_window) & (key_idx[None, :] < query_idx[:, None])
    places = jnp.sum(before.astype(jnp.int32), axis=1)
    inverse = ROPE ** (-(jnp.arange(HD // 2, dtype=F32) * 2.0 / HD))
    angles = places.astype(F32)[:, None] * inverse[None, :]
    cosine = jnp.cos(angles)
    sine = jnp.sin(angles)
    turn = jnp.concatenate([cosine] * 4 + [-sine, sine, -sine, sine], axis=1)

    h_one, head_fac, bq_rot, key_fac, queries = front(x_parts, gain_one, w_rh, turn)

    groups = [[m * subs + s for s in range(subs)] for m in range(micro)]
    if fast:
        kf_window = window(key_fac, n_row).reshape(keys, -1)
    else:
        gathered = lax.all_gather(key_fac, "row", axis=0)
        gathered = lax.all_gather(gathered, "col", axis=1, axis_index_groups=groups)
        gathered = gathered.reshape(length, key_fac.shape[1])
        padded_kf = jnp.concatenate([jnp.zeros((past * rows, key_fac.shape[1]), BF), gathered], axis=0)
        kf_window = lax.dynamic_slice_in_dim(padded_kf, block * rows, keys, 0)

    heads_out, lse, key_all, value_all = attend(queries, kf_window, seg_window)
    mixed, h_two = mixing(x_parts, heads_out, w_out_all, gain_two)

    if fast:
        cot_all = col_gather(cot_own, 5)
        h_all = col_gather(h_two, 1)
    else:
        cot_all = lax.all_gather(cot_own, "col", axis=0)
        h_all = lax.all_gather(h_two, "col", axis=0)
    out_part, dh_part, *g_parts = ffn(h_all, cot_all, pieces, units, fast)
    if fast:
        dh_sum, out_sum = col_reduce(dh_part, out_part)
    else:
        dh_sum = lax.psum_scatter(dh_part, "col", scatter_dimension=0, tiled=False).astype(F32)
        out_sum = lax.psum_scatter(out_part, "col", scatter_dimension=0, tiled=False).astype(F32)
    out_parts, d_mixed, d_heads, g_out, g_gain_two = unmix(
        mixed, cot_parts, dh_sum, out_sum, heads_out, w_out_all, gain_two
    )
    d_q, d_kf = attend_back(queries, key_all, value_all, d_heads, lse, kf_window, seg_window)

    if fast:
        own_kf = window_back(d_kf.reshape(past + 1, rows, -1), n_row)
    else:
        spread_kf = jnp.zeros((past * rows + length, d_kf.shape[1]), BF)
        spread_kf = lax.dynamic_update_slice_in_dim(spread_kf, d_kf, block * rows, 0)[past * rows :]
        spread_kf = spread_kf.reshape(n_row, subs, rows, -1)
        own_kf = lax.psum_scatter(spread_kf, "row", scatter_dimension=0, tiled=False)
        own_kf = lax.psum_scatter(own_kf, "col", scatter_dimension=0, tiled=False, axis_index_groups=groups)

    gi_parts, g_gain_one, g_rh = back(
        d_q, own_kf, head_fac, bq_rot, turn, w_rh, h_one, x_parts, gain_one, d_mixed
    )

    output = lax.all_to_all(out_parts, "col", 0, 0, tiled=True).reshape(tokens_in.shape)
    grad_input = lax.all_to_all(gi_parts, "col", 0, 0, tiled=True).reshape(tokens_in.shape)

    def add(*values):
        total = values[0].astype(F32)
        for v in values[1:]:
            total = total + v.astype(F32)
        return total.astype(BF)

    if fast:
        keep, send, down = g_parts
        both = add(keep, dp_swap(send)).reshape(2, n_row, part, D // 2)
        low = add(down[0], *[row_swap(down[k], k) for k in range(1, n_row)])
        both = add(both[:, 0], *[row_swap(both[:, k], k) for k in range(1, n_row)])
        other = dp_swap(both)
        both = jnp.where(dp == 0, jnp.concatenate([both, other], 2), jnp.concatenate([other, both], 2))
        low = add(low, dp_swap(low))
        g_ffn = jnp.concatenate([both, low[None]], axis=0)
    else:
        g_ffn = g_parts[0].reshape(3, n_row, part, D)
        g_ffn = lax.psum_scatter(g_ffn, "row", scatter_dimension=1, tiled=False)
        g_ffn = lax.psum(g_ffn, "dp")
    g_ffn = jnp.transpose(g_ffn.reshape(3, part, n_col, feat), (2, 0, 1, 3))
    g_ffn = lax.all_to_all(g_ffn, "col", 0, 0, tiled=True)
    g_ffn = jnp.transpose(g_ffn, (1, 0, 2, 3)).reshape(3, ffn_local, feat).astype(F32)

    g_ranks = g_rh[: FAC * HD].reshape(n_row, rank_local, n_col, feat)
    g_heads = g_rh[FAC * HD :].reshape(FAC, n_row, head_local, n_col, feat)
    g_ranks = jnp.transpose(g_ranks, (0, 2, 1, 3))
    g_heads = jnp.transpose(g_heads, (1, 3, 0, 2, 4)).reshape(n_row, n_col, FAC * head_local, feat)
    g_rh = jnp.concatenate([g_ranks, g_heads], axis=2)

    def total(values):
        if fast:
            place = [
                lax.dynamic_index_in_dim(values.reshape(n_row, 2, 2, *values.shape[2:]), (col + k) % 2, 2, False)
                for k in range(2)
            ]
            values = add(place[0], lax.ppermute(place[1], "col", [(c, c ^ 1) for c in range(4)]))
            place = [lax.dynamic_index_in_dim(values, (col // 2 + k) % 2, 1, False) for k in range(2)]
            values = add(place[0], lax.ppermute(place[1], "col", [(c, c ^ 2) for c in range(4)]))
            place = [lax.dynamic_index_in_dim(values, row ^ k, 0, False) for k in range(n_row)]
            values = add(place[0], *[row_swap(place[k], k) for k in range(1, n_row)])
            return add(values, dp_swap(values)).astype(F32)
        values = values.reshape((n_row * n_col,) + values.shape[2:])
        part = lax.psum_scatter(values, ("row", "col"), scatter_dimension=0, tiled=False)
        return lax.psum(part, "dp").astype(F32)

    g_out = total(g_out)
    g_rh = total(g_rh)
    gains = jnp.concatenate([g_gain_one, g_gain_two], axis=0)
    gains = lax.psum(gains, ("dp", "row", "col"))
    gains = lax.dynamic_slice_in_dim(gains, col * feat, feat, 1)
    own_heads = g_rh[rank_local:].reshape(FAC, head_local, feat)
    own_heads = jnp.transpose(own_heads[jnp.array(FAC_BACK)], (2, 1, 0)).reshape(w_heads.shape)
    return (
        output,
        grad_input,
        gains[0],
        gains[1],
        own_heads,
        g_rh[:rank_local].T,
        g_out,
        g_ffn[0].T,
        g_ffn[1].T,
        g_ffn[2],
    )


def solution(mesh):
    tokens = P(None, ("dp", "row"), "col")
    both = P("col", "row")
    turned = P("row", "col")
    gain = P("col")
    return jax.shard_map(
        local,
        mesh=mesh,
        in_specs=(tokens, P(None, "dp", None), gain, gain, both, both, turned, both, both, turned, tokens),
        out_specs=(tokens, tokens, gain, gain, both, both, turned, both, both, turned),
        check_vma=False,
    )
```

```python
import functools

import jax
import jax.numpy as jnp
from jax import lax
from jax.experimental import pallas as pl
from jax.experimental.pallas import tpu as pltpu
from jax.sharding import PartitionSpec as P

D = 1024
H = 16
HD = 64
RQ = 6
RK = 2
FAC = 10
MAX_DOC = 1024

EPS = 1e-06
ROPE = 10000.0
NEG = -1e30
BF = jnp.bfloat16
F32 = jnp.float32
LANES = 128
PAIRS = H // 2
FAC_ORDER = (6, 7, 8, 9, 0, 1, 2, 3, 4, 5)
FAC_BACK = (4, 5, 6, 7, 8, 9, 0, 1, 2, 3)
VMEM = pl.BlockSpec(memory_space=pltpu.VMEM)


def nn(a, b):
    return jnp.dot(a, b, preferred_element_type=F32)


def nt(a, b):
    return lax.dot_general(a, b, (((1,), (1,)), ((), ())), preferred_element_type=F32)


def tn(a, b):
    return lax.dot_general(a, b, (((0,), (0,)), ((), ())), preferred_element_type=F32)


def two_pass(a, b):
    high = a.astype(BF)
    low = (a - high.astype(F32)).astype(BF)
    return nn(high, b) + nn(low, b)


def lane_iota(shape):
    return lax.broadcasted_iota(jnp.int32, shape, len(shape) - 1)


def spread(rows, first, width):
    row = lax.broadcasted_iota(jnp.int32, (rows, width), 0)
    head = lax.broadcasted_iota(jnp.int32, (rows, width), 1) // HD
    return (row == head + first).astype(F32).astype(BF)


def collect(rows, width, first):
    head = lax.broadcasted_iota(jnp.int32, (rows, width), 0) // HD
    lane = lax.broadcasted_iota(jnp.int32, (rows, width), 1)
    return (lane == head + first).astype(F32).astype(BF)


GROUP = 4
GROUP_COLS = 48
RANK_COLS = FAC * HD
HEAD_COLS = H // GROUP * GROUP_COLS
ALL_COLS = RANK_COLS + HEAD_COLS


def factor_place(head, j):
    return head // GROUP * GROUP_COLS + j * GROUP + head % GROUP


def head_spread(j, first_head, width):
    row = lax.broadcasted_iota(jnp.int32, (HEAD_COLS, width), 0)
    head = lax.broadcasted_iota(jnp.int32, (HEAD_COLS, width), 1) // HD + first_head
    return (row == factor_place(head, j)).astype(F32).astype(BF)


def head_collect(j):
    head = lax.broadcasted_iota(jnp.int32, (D, HEAD_COLS), 0) // HD
    lane = lax.broadcasted_iota(jnp.int32, (D, HEAD_COLS), 1)
    return (lane == factor_place(head, j)).astype(F32).astype(BF)


def key_columns():
    row = lax.broadcasted_iota(jnp.int32, (HEAD_COLS, 2 * RK * H), 0)
    lane = lax.broadcasted_iota(jnp.int32, (HEAD_COLS, 2 * RK * H), 1)
    return (row == factor_place(lane % H, lane // H)).astype(F32).astype(BF)


def swap_halves(tile):
    lane = lane_iota(tile.shape)
    ahead = pltpu.roll(tile, LANES - HD // 2, 1)
    behind = pltpu.roll(tile, HD // 2, 1)
    return jnp.where(lane % HD < HD // 2, ahead, behind)


def double_left(tile):
    return jnp.where(lane_iota(tile.shape) < HD, tile, pltpu.roll(tile, HD, 1))


def double_right(tile):
    return jnp.where(lane_iota(tile.shape) < HD, pltpu.roll(tile, HD, 1), tile)


def params(**more):
    return pltpu.CompilerParams(vmem_limit_bytes=60 << 20, **more)


def call(body, outs, scratch=(), cost=None):
    return pl.pallas_call(
        body,
        out_shape=outs,
        scratch_shapes=scratch,
        compiler_params=params(),
        cost_estimate=cost,
    )


def cost_of(flops, moved):
    return pl.CostEstimate(flops=int(flops), bytes_accessed=int(moved), transcendentals=0)


MESH = pl.DeviceIdType.MESH
ANY = pl.BlockSpec(memory_space=pl.ANY)


class Mover:
    def __init__(self, send_sem, recv_sem):
        self.send_sem = send_sem
        self.recv_sem = recv_sem
        self.used = 0

    def copy(self, source, target, **place):
        index = self.used
        self.used += 1
        return pltpu.make_async_remote_copy(
            src_ref=source,
            dst_ref=target,
            send_sem=self.send_sem.at[index],
            recv_sem=self.recv_sem.at[index],
            device_id=place,
            device_id_type=MESH,
        )


def greet(partners):
    barrier = pltpu.get_barrier_semaphore()
    count = 0
    for present, place in partners:
        if present is None:
            pl.semaphore_signal(barrier, inc=1, device_id=place, device_id_type=MESH)
            count = count + 1
        else:

            @pl.when(present)
            def _():
                pl.semaphore_signal(barrier, inc=1, device_id=place, device_id_type=MESH)

            count = count + present.astype(jnp.int32)
    pl.semaphore_wait(barrier, count)


def neighbours():
    col = lax.axis_index("col")
    core = col + 1 - 2 * lax.rem(col, 2)
    across = lax.rem(col + 2, 4)
    return col, core, across


def square():
    dp = lax.axis_index("dp")
    x = lax.axis_index("col") // 2
    return dp, (dp * 2 + x, dp * 2 + 1 - x, (1 - dp) * 2 + x, (1 - dp) * 2 + 1 - x)


def comm_params(ident):
    return params(collective_id=ident, has_side_effects=True)


def start_body(tok_ref, w_ref, gain_ref, ffn_ref, x_ref, wall_ref, gains_ref, parts_ref, send_sem, recv_sem, local_sem):
    row = lax.axis_index("row")
    col, core, across = neighbours()
    cross = lax.rem(core + 2, 4)
    rows = [lax.rem(row + k, 4) for k in range(4)]
    back = [lax.rem(row + 4 - k, 4) for k in range(4)]
    greet([(None, {"col": c}) for c in (core, across, cross)] + [(None, {"row": r}) for r in rows[1:]])
    mover = Mover(send_sem, recv_sem)
    started = []

    def go(source, target, **place):
        c = mover.copy(source, target, **place)
        c.start()
        started.append(c)
        return c

    down = [None] + [go(w_ref, wall_ref.at[row, col], row=rows[k]) for k in range(1, 4)]
    sides = [go(w_ref, wall_ref.at[row, col], col=across)]
    cores = [go(w_ref, wall_ref.at[row, col], col=core)]
    rest = []
    for c in (across, cross, core):
        rest.append(go(gain_ref, gains_ref.at[col], col=c))
        rest.append(go(tok_ref.at[c], x_ref.at[col], col=c))
    for c in (across, cross, core):
        rest.append(go(ffn_ref.at[c], parts_ref.at[col], col=c))
    own = [
        pltpu.make_async_copy(w_ref, wall_ref.at[row, col], local_sem.at[0]),
        pltpu.make_async_copy(gain_ref, gains_ref.at[col], local_sem.at[1]),
        pltpu.make_async_copy(tok_ref.at[col], x_ref.at[col], local_sem.at[2]),
        pltpu.make_async_copy(ffn_ref.at[col], parts_ref.at[col], local_sem.at[3]),
    ]
    for c in own:
        c.start()
    for k in range(1, 4):
        down[k].wait_recv()
        block = wall_ref.at[back[k], col]
        sides.append(go(block, block, col=across))
        cores.append(go(block, block, col=core))
    passed = []
    for k in range(4):
        sides[k].wait_recv()
        block = wall_ref.at[back[k], across]
        passed.append(go(block, block, col=core))
    for c in cores + rest + passed:
        c.wait_recv()
    for c in started:
        c.wait_send()
    for c in own:
        c.wait()


def start(tok, w_own, gains, ffn_own):
    count = 24
    return pl.pallas_call(
        start_body,
        out_shape=(
            jax.ShapeDtypeStruct(tok.shape, tok.dtype),
            jax.ShapeDtypeStruct((4, 4) + w_own.shape, BF),
            jax.ShapeDtypeStruct((4,) + gains.shape, F32),
            jax.ShapeDtypeStruct(ffn_own.shape, BF),
        ),
        in_specs=[ANY] * 4,
        out_specs=(ANY,) * 4,
        scratch_shapes=[
            pltpu.SemaphoreType.DMA((count,)),
            pltpu.SemaphoreType.DMA((count,)),
            pltpu.SemaphoreType.DMA((4,)),
        ],
        compiler_params=comm_params(1),
        cost_estimate=cost_of(0, 8 << 20),
    )(tok, w_own, gains, ffn_own)


class AttendCopies:
    def __init__(self, w_ref, cot_ref, rows_ref, near_ref, send_sem, recv_sem, local_sem):
        row = lax.axis_index("row")
        col, core, across = neighbours()
        dp, spots = square()
        mover = Mover(send_sem, recv_sem)
        self.left = row >= 1
        self.right = row <= 2
        self.both = jnp.logical_and(self.left, self.right)
        self.from_left = row >= 2
        self.from_right = row <= 1
        self.partners = [
            (self.right, {"row": row + 1}),
            (self.left, {"row": row - 1}),
            (None, {"col": across}),
            (None, {"dp": 1 - dp}),
            (None, {"dp": 1 - dp, "col": across}),
        ]
        self.to_right = mover.copy(w_ref, rows_ref.at[row], row=row + 1)
        self.to_left = mover.copy(w_ref, rows_ref.at[row], row=row - 1)
        self.pass_right = mover.copy(rows_ref.at[row - 1], rows_ref.at[row - 1], row=row + 1)
        self.pass_left = mover.copy(rows_ref.at[row + 1], rows_ref.at[row + 1], row=row - 1)
        target = near_ref.at[spots[0]]
        self.cots = [
            mover.copy(cot_ref, target, col=across),
            mover.copy(cot_ref, target, dp=1 - dp),
            mover.copy(cot_ref, target, dp=1 - dp, col=across),
        ]
        self.own = [
            pltpu.make_async_copy(w_ref, rows_ref.at[row], local_sem.at[0]),
            pltpu.make_async_copy(cot_ref, target, local_sem.at[1]),
        ]

    def first(self):
        greet(self.partners)
        pl.when(self.right)(self.to_right.start)
        pl.when(self.left)(self.to_left.start)
        for c in self.cots + self.own:
            c.start()

    def second(self):
        pl.when(self.left)(self.to_right.wait_recv)
        pl.when(self.right)(self.to_left.wait_recv)
        pl.when(self.both)(self.pass_right.start)
        pl.when(self.both)(self.pass_left.start)

    def last(self):
        pl.when(self.right)(self.to_right.wait_send)
        pl.when(self.left)(self.to_left.wait_send)
        pl.when(self.both)(self.pass_right.wait_send)
        pl.when(self.both)(self.pass_left.wait_send)
        pl.when(self.from_left)(self.pass_right.wait_recv)
        pl.when(self.from_right)(self.pass_left.wait_recv)
        for c in self.cots + self.own:
            c.wait()


class BackCopies:
    def __init__(self, parts_ref, grads_ref, out_ref, got_ref, send_sem, recv_sem, local_sem):
        row = lax.axis_index("row")
        col, core, across = neighbours()
        cross = lax.rem(core + 2, 4)
        mover = Mover(send_sem, recv_sem)
        nxt, prv = lax.rem(row + 1, 4), lax.rem(row + 3, 4)
        self.partners = [(None, {"col": c}) for c in (core, across, cross)]
        self.partners += [(None, {"row": nxt}), (None, {"row": prv})]
        self.copies = [
            mover.copy(grads_ref.at[nxt], got_ref.at[0], row=nxt),
            mover.copy(grads_ref.at[prv], got_ref.at[1], row=prv),
        ]
        self.copies += [mover.copy(parts_ref.at[c], out_ref.at[col], col=c) for c in (across, cross, core)]
        self.own = pltpu.make_async_copy(parts_ref.at[col], out_ref.at[col], local_sem)

    def first(self):
        greet(self.partners)
        for c in self.copies:
            c.start()
        self.own.start()

    def last(self):
        for c in self.copies:
            c.wait()
        self.own.wait()


def gather_body(h_ref, cot_ref, rows_ref, near_ref, far_ref, cot_far_ref, last_ref, send_sem, recv_sem, local_sem):
    row = lax.axis_index("row")
    col, core, across = neighbours()
    dp, (me, on_x, on_y, on_both) = square()
    goes_right = row == 2
    goes_left = row == 1
    comes_left = row == 3
    comes_right = row == 0
    greet(
        [
            (None, {"col": core}),
            (None, {"col": across}),
            (None, {"dp": 1 - dp}),
            (row <= 2, {"row": row + 1}),
            (row >= 1, {"row": row - 1}),
        ]
    )
    mover = Mover(send_sem, recv_sem)
    half = h_ref.shape[0] // 2
    top, low = pl.ds(0, half), pl.ds(half, half)
    started = []

    def go(source, target, **place):
        c = mover.copy(source, target, **place)
        c.start()
        started.append(c)
        return c

    x_low = go(h_ref.at[low], near_ref.at[me, low], col=across)
    y_top = go(h_ref.at[top], near_ref.at[me, top], dp=1 - dp)
    x_top = go(h_ref.at[top], near_ref.at[me, top], col=across)
    y_low = go(h_ref.at[low], near_ref.at[me, low], dp=1 - dp)
    arriving = [go(h_ref, far_ref.at[me], col=core)]
    own = pltpu.make_async_copy(h_ref, near_ref.at[me], local_sem)
    own.start()
    right = mover.copy(rows_ref.at[row - 2], last_ref, row=row + 1)
    left = mover.copy(rows_ref.at[row + 2], last_ref, row=row - 1)
    pl.when(goes_right)(right.start)
    pl.when(goes_left)(left.start)
    for k in range(4):
        arriving.append(go(cot_ref.at[k], cot_far_ref.at[k], col=core))
    x_low.wait_recv()
    both_low = go(near_ref.at[on_x, low], near_ref.at[on_x, low], dp=1 - dp)
    y_top.wait_recv()
    both_top = go(near_ref.at[on_y, top], near_ref.at[on_y, top], col=across)
    x_top.wait_recv()
    arriving.append(go(near_ref.at[on_x], far_ref.at[on_x], col=core))
    y_low.wait_recv()
    arriving.append(go(near_ref.at[on_y], far_ref.at[on_y], col=core))
    both_low.wait_recv()
    both_top.wait_recv()
    arriving.append(go(near_ref.at[on_both], far_ref.at[on_both], col=core))
    for c in arriving:
        c.wait_recv()
    for c in started:
        c.wait_send()
    own.wait()
    pl.when(comes_left)(right.wait_recv)
    pl.when(comes_right)(left.wait_recv)
    pl.when(goes_right)(right.wait_send)
    pl.when(goes_left)(left.wait_send)


def gather(h, cot_near, w_rows):
    count = 16
    return pl.pallas_call(
        gather_body,
        out_shape=(
            jax.ShapeDtypeStruct((4,) + h.shape, BF),
            jax.ShapeDtypeStruct((4,) + h.shape, BF),
            jax.ShapeDtypeStruct(cot_near.shape, BF),
            jax.ShapeDtypeStruct(w_rows.shape[1:], BF),
        ),
        in_specs=[ANY] * 3,
        out_specs=(ANY,) * 4,
        scratch_shapes=[
            pltpu.SemaphoreType.DMA((count,)),
            pltpu.SemaphoreType.DMA((count,)),
            pltpu.SemaphoreType.DMA,
        ],
        compiler_params=comm_params(4),
        cost_estimate=cost_of(0, 12 << 20),
    )(h, cot_near, w_rows)


class SquareSum:
    def __init__(self, mover, part_ref, got_ref, pair_ref, diag_ref, far_ref):
        self.mover = mover
        self.part_ref = part_ref
        self.got_ref = got_ref
        self.pair_ref = pair_ref
        self.diag_ref = diag_ref
        self.far_ref = far_ref
        self.half = part_ref.shape[2] // 2
        self.started = []

    def go(self, source, target, **place):
        c = self.mover.copy(source, target, **place)
        c.start()
        self.started.append(c)
        return c

    def near(self, core, order):
        self.order = order
        self.cores = {}
        for name in (3, 1, 2, 0):
            spot = order[name]
            self.cores[name] = self.go(self.part_ref.at[1, spot], self.got_ref.at[spot], col=core)

    def add_pair(self, name):
        self.cores[name].wait_recv()
        spot = self.order[name]
        self.pair_ref[spot] = (self.part_ref[0, spot].astype(F32) + self.got_ref[spot].astype(F32)).astype(BF)

    def send(self, dp, across):
        me, on_x, on_y, on_both = self.order
        top, low = pl.ds(0, self.half), pl.ds(self.half, self.half)
        self.add_pair(3)
        d_top = self.go(self.pair_ref.at[on_both, top], self.diag_ref.at[0], col=across)
        d_low = self.go(self.pair_ref.at[on_both, low], self.diag_ref.at[1], dp=1 - dp)
        self.add_pair(1)
        self.far = [self.go(self.pair_ref.at[on_x, top], self.far_ref.at[0, top], col=across)]
        self.add_pair(2)
        self.far.append(self.go(self.pair_ref.at[on_y, low], self.far_ref.at[1, low], dp=1 - dp))
        self.add_pair(0)
        d_top.wait_recv()
        self.pair_ref[on_y, top] = (
            self.pair_ref[on_y, top].astype(F32) + self.diag_ref[0].astype(F32)
        ).astype(BF)
        self.far.append(self.go(self.pair_ref.at[on_y, top], self.far_ref.at[1, top], dp=1 - dp))
        d_low.wait_recv()
        self.pair_ref[on_x, low] = (
            self.pair_ref[on_x, low].astype(F32) + self.diag_ref[1].astype(F32)
        ).astype(BF)
        self.far.append(self.go(self.pair_ref.at[on_x, low], self.far_ref.at[0, low], col=across))

    def total(self):
        for c in self.far:
            c.wait_recv()
        return self.pair_ref[self.order[0]].astype(F32) + self.far_ref[0].astype(F32) + self.far_ref[1].astype(F32)

    def end(self):
        for c in self.started:
            c.wait_send()


def row_partners(row, n_row, core):
    return [
        (None, {"col": core}),
        (row + 1 < n_row, {"row": row + 1}),
        (row + 2 < n_row, {"row": row + 2}),
        (row >= 1, {"row": row - 1}),
        (row >= 2, {"row": row - 2}),
    ]


def window_body(n_row, x_ref, zero_ref, win_ref, send_sem, recv_sem, local_sem):
    row = lax.axis_index("row")
    col, core, _ = neighbours()
    side = lax.rem(col, 2)
    greet(row_partners(row, n_row, core))
    mover = Mover(send_sem, recv_sem)
    one = mover.copy(x_ref, win_ref.at[2], row=row + 1)
    two = mover.copy(x_ref, win_ref.at[0], row=row + 2)
    near = mover.copy(x_ref, win_ref.at[3], col=core)
    pass_one = mover.copy(win_ref.at[2], win_ref.at[1 + 2 * side], col=core)
    pass_two = mover.copy(win_ref.at[0], win_ref.at[1], col=core)
    has_one = row >= 1
    has_two = row >= 2

    @pl.when(row + 1 < n_row)
    def _():
        one.start()

    @pl.when(row + 2 < n_row)
    def _():
        two.start()

    @pl.when(side == 0)
    def _():
        near.start()

    own = pltpu.make_async_copy(x_ref, win_ref.at[4], local_sem.at[0])
    own.start()

    def fill(slot):
        return pltpu.make_async_copy(zero_ref, win_ref.at[slot], local_sem.at[slot + 1])

    for absent, slots in (
        (jnp.logical_not(has_two), (0,)),
        (jnp.logical_and(jnp.logical_not(has_two), side == 0), (1,)),
        (jnp.logical_and(jnp.logical_not(has_one), side == 1), (1,)),
        (jnp.logical_not(has_one), (2,)),
        (jnp.logical_and(jnp.logical_not(has_one), side == 0), (3,)),
    ):

        @pl.when(absent)
        def _():
            for slot in slots:
                c = fill(slot)
                c.start()
                c.wait()

    @pl.when(has_one)
    def _():
        one.wait_recv()
        pass_one.start()

    @pl.when(has_two)
    def _():
        two.wait_recv()

    sends_two = jnp.logical_and(has_two, side == 1)
    takes_two = jnp.logical_and(has_two, side == 0)

    @pl.when(sends_two)
    def _():
        pass_two.start()

    @pl.when(has_one)
    def _():
        pass_one.wait_recv()
        pass_one.wait_send()

    @pl.when(takes_two)
    def _():
        pass_two.wait_recv()

    @pl.when(sends_two)
    def _():
        pass_two.wait_send()

    @pl.when(side == 1)
    def _():
        near.wait_recv()

    @pl.when(side == 0)
    def _():
        near.wait_send()

    @pl.when(row + 1 < n_row)
    def _():
        one.wait_send()

    @pl.when(row + 2 < n_row)
    def _():
        two.wait_send()

    own.wait()


def window(x, n_row):
    zero = jnp.zeros(x.shape, x.dtype)
    return pl.pallas_call(
        functools.partial(window_body, n_row),
        out_shape=jax.ShapeDtypeStruct((5,) + x.shape, x.dtype),
        in_specs=[ANY, ANY],
        out_specs=ANY,
        scratch_shapes=[
            pltpu.SemaphoreType.DMA((5,)),
            pltpu.SemaphoreType.DMA((5,)),
            pltpu.SemaphoreType.DMA((6,)),
        ],
        compiler_params=comm_params(2),
        cost_estimate=cost_of(0, 1 << 20),
    )(x, zero)


def window_back_body(n_row, win_ref, sum_ref, near_ref, send_ref, far_ref, send_sem, recv_sem):
    row = lax.axis_index("row")
    col, core, _ = neighbours()
    side = lax.rem(col, 2)
    greet(row_partners(row, n_row, core))
    mover = Mover(send_sem, recv_sem)
    first = mover.copy(win_ref.at[1], near_ref.at[0], col=core)
    second = mover.copy(win_ref.at[3], near_ref.at[1], col=core)
    first.start()
    second.start()
    one = mover.copy(send_ref.at[0], far_ref.at[0], row=row - 1)
    two = mover.copy(send_ref.at[1], far_ref.at[1], row=row - 2)
    first.wait_recv()
    second.wait_recv()
    zero = jnp.zeros(near_ref.shape[1:], F32)
    low = near_ref[0].astype(F32)
    high = near_ref[1].astype(F32)
    left = side == 0
    send_ref[0] = (win_ref[2].astype(F32) + jnp.where(left, low, high)).astype(BF)
    send_ref[1] = (win_ref[0].astype(F32) + jnp.where(left, zero, low)).astype(BF)

    @pl.when(row >= 1)
    def _():
        one.start()

    @pl.when(row >= 2)
    def _():
        two.start()

    sum_ref[...] = win_ref[4].astype(F32) + jnp.where(left, high, zero)

    @pl.when(row + 1 < n_row)
    def _():
        one.wait_recv()
        sum_ref[...] += far_ref[0].astype(F32)

    @pl.when(row + 2 < n_row)
    def _():
        two.wait_recv()
        sum_ref[...] += far_ref[1].astype(F32)

    first.wait_send()
    second.wait_send()

    @pl.when(row >= 1)
    def _():
        one.wait_send()

    @pl.when(row >= 2)
    def _():
        two.wait_send()


def window_back(win, n_row):
    shape = win.shape[1:]
    return pl.pallas_call(
        functools.partial(window_back_body, n_row),
        out_shape=jax.ShapeDtypeStruct(shape, F32),
        in_specs=[VMEM],
        out_specs=VMEM,
        scratch_shapes=[
            pltpu.VMEM((2,) + shape, BF),
            pltpu.VMEM((2,) + shape, BF),
            pltpu.VMEM((2,) + shape, BF),
            pltpu.SemaphoreType.DMA((4,)),
            pltpu.SemaphoreType.DMA((4,)),
        ],
        compiler_params=comm_params(7),
        cost_estimate=cost_of(0, 1 << 20),
    )(win)


def front_body(x_ref, gain_ref, blocks_ref, turn_ref, h_ref, hf_ref, bq_ref, kf_ref, q_ref, w_ref):
    parts = x_ref.shape[0]
    feat = x_ref.shape[2]
    n_row = blocks_ref.shape[0]
    ranks_each = RANK_COLS // n_row
    xs = [x_ref[c].astype(F32) for c in range(parts)]
    total = sum(jnp.sum(v * v, axis=1, keepdims=True) for v in xs)
    scale = lax.rsqrt(total / D + EPS)
    for c in range(parts):
        lanes = slice(c * feat, (c + 1) * feat)
        h_ref[:, lanes] = (xs[c] * scale * gain_ref[c, :1]).astype(BF)
        for r in range(n_row):
            w_ref[r * ranks_each : (r + 1) * ranks_each, lanes] = blocks_ref[r, c, :ranks_each]
            w_ref[RANK_COLS + r * GROUP_COLS : RANK_COLS + (r + 1) * GROUP_COLS, lanes] = blocks_ref[
                r, c, ranks_each:
            ]
    both = nt(h_ref[...], w_ref[...])
    heads = both[:, RANK_COLS:]
    hf_ref[...] = heads
    cosine = turn_ref[:, :LANES]
    sine = turn_ref[:, LANES:]
    for tile in range(RANK_COLS // LANES):
        lanes = slice(tile * LANES, (tile + 1) * LANES)
        part = both[:, lanes]
        if tile < 4:
            part = part * cosine + swap_halves(part) * sine
        if tile < 3:
            bq_ref[:, lanes] = part
        else:
            kf_ref[:, (tile - 3) * LANES : (tile - 2) * LANES] = part.astype(BF)
    high = heads.astype(BF)
    low = (heads - high.astype(F32)).astype(BF)
    kf_ref[:, 2 * LANES :] = nn(high, key_columns()).astype(BF)
    ranks = []
    for r in range(RQ):
        tile = bq_ref[:, (r // 2) * LANES : (r // 2 + 1) * LANES]
        ranks.append(double_left(tile) if r % 2 == 0 else double_right(tile))
    width = 2 * LANES
    for p in range(D // width):
        lanes = slice(p * width, (p + 1) * width)
        acc = None
        for r in range(RQ):
            pick = head_spread(2 * RK + r, p * (width // HD), width)
            term = (nn(high, pick) + nn(low, pick)) * jnp.concatenate([ranks[r]] * 2, axis=1)
            acc = term if acc is None else acc + term
        q_ref[:, lanes] = (acc / RQ).astype(BF)


def front(x_parts, gains, blocks, turn):
    rows = x_parts.shape[1]
    return call(
        front_body,
        (
            jax.ShapeDtypeStruct((rows, D), BF),
            jax.ShapeDtypeStruct((rows, HEAD_COLS), F32),
            jax.ShapeDtypeStruct((rows, RQ * HD), F32),
            jax.ShapeDtypeStruct((rows, 2 * LANES + 2 * RK * H), BF),
            jax.ShapeDtypeStruct((rows, D), BF),
            jax.ShapeDtypeStruct((ALL_COLS, D), BF),
        ),
        cost=cost_of(2 * rows * D * 800 * 3, 6 << 20),
    )(x_parts, gains, blocks, turn)


def mask_bias(seg_ref, keys, rows):
    seg_row = seg_ref[...].astype(F32)
    wide = jnp.broadcast_to(seg_row, (LANES, keys))
    column = wide.T
    column = jnp.concatenate([column] * (rows // LANES), axis=1)
    key_idx = lax.broadcasted_iota(jnp.int32, (keys, rows), 0)
    query_idx = lax.broadcasted_iota(jnp.int32, (keys, rows), 1) + (keys - rows)
    same = column == seg_row[:, keys - rows :]
    return jnp.where(same & (key_idx <= query_idx), 0.0, NEG)


def attend_body(fast, q_ref, kf_ref, seg_ref, *refs):
    if fast:
        w_ref, cot_ref, o_ref, lse_ref, k_ref, v_ref, w_rows_ref, cot_near_ref = refs[:8]
        bias_ref, dup_ref, send_sem, recv_sem, local_sem = refs[8:]
        side_work = AttendCopies(w_ref, cot_ref, w_rows_ref, cot_near_ref, send_sem, recv_sem, local_sem)
        side_work.first()
    else:
        o_ref, lse_ref, k_ref, v_ref, bias_ref, dup_ref = refs
    rows = q_ref.shape[0]
    keys = kf_ref.shape[0]
    bias_ref[...] = mask_bias(seg_ref, keys, rows)
    for s in range(2 * RK):
        tile = kf_ref[:, (s // 2) * LANES : (s // 2 + 1) * LANES].astype(F32)
        dup_ref[s] = double_left(tile) if s % 2 == 0 else double_right(tile)

    def pair(p, carried):
        lanes = pl.ds(pl.multiple_of(p * LANES, LANES), LANES)
        weights = kf_ref[:, 2 * LANES :]
        made = []
        for kind in range(2):
            acc = None
            for s in range(RK):
                pick = spread(2 * RK * H, (kind * RK + s) * H + 2 * p, LANES)
                term = nn(weights, pick) * dup_ref[kind * RK + s]
                acc = term if acc is None else acc + term
            made.append((acc / RK).astype(BF))
        k_tile, v_tile = made
        k_ref[:, lanes] = k_tile
        v_ref[:, lanes] = v_tile
        v_turned = v_tile.astype(F32).T.astype(BF)
        q_turned = (q_ref[:, lanes].astype(F32) * HD**-0.5).T
        half = lax.broadcasted_iota(jnp.int32, q_turned.shape, 0) // HD
        outs = []
        for side in range(2):
            q_side = jnp.where(half == side, q_turned, 0.0).astype(BF)
            scores = nn(k_tile, q_side) + bias_ref[...]
            peak = jnp.max(scores, axis=0, keepdims=True)
            weight = jnp.exp(scores - peak)
            total = jnp.sum(weight, axis=0, keepdims=True)
            probs = (weight * (1.0 / total)).astype(BF)
            outs.append(nn(v_turned[side * HD : (side + 1) * HD], probs))
            lse_ref[2 * p + side] = jnp.broadcast_to(peak + jnp.log(total), (8, rows))
        o_ref[:, lanes] = jnp.concatenate(outs, axis=0).T.astype(BF)
        return carried

    if fast:
        lax.fori_loop(0, 5, pair, 0)
        side_work.second()
        lax.fori_loop(5, PAIRS, pair, 0)
        side_work.last()
    else:
        lax.fori_loop(0, PAIRS, pair, 0)


def attend(q, kf_window, seg_window, w_own=None, cot=None):
    rows = q.shape[0]
    keys = kf_window.shape[0]
    fast = w_own is not None
    outs = [
        jax.ShapeDtypeStruct((rows, D), BF),
        jax.ShapeDtypeStruct((H, 8, rows), F32),
        jax.ShapeDtypeStruct((keys, D), BF),
        jax.ShapeDtypeStruct((keys, D), BF),
    ]
    scratch = [pltpu.VMEM((keys, rows), F32), pltpu.VMEM((2 * RK, keys, LANES), F32)]
    in_specs, out_specs, more = [VMEM] * 3, [VMEM] * 4, []
    if fast:
        outs += [jax.ShapeDtypeStruct((4,) + w_own.shape, BF), jax.ShapeDtypeStruct((4,) + cot.shape, BF)]
        in_specs += [ANY] * 2
        out_specs += [ANY] * 2
        more = [w_own, cot]
        scratch += [
            pltpu.SemaphoreType.DMA((7,)),
            pltpu.SemaphoreType.DMA((7,)),
            pltpu.SemaphoreType.DMA((2,)),
        ]
    return pl.pallas_call(
        functools.partial(attend_body, fast),
        out_shape=tuple(outs),
        in_specs=in_specs,
        out_specs=tuple(out_specs),
        scratch_shapes=scratch,
        compiler_params=comm_params(3) if fast else params(),
        cost_estimate=cost_of(2 * rows * keys * D * 16, 16 << 20),
    )(q, kf_window, seg_window, *more)


def attend_back_body(fast, q_ref, k_ref, v_ref, do_ref, lse_ref, kf_ref, seg_ref, *refs):
    if fast:
        parts_ref, grads_ref, dq_ref, dkf_ref, out_ref, got_ref = refs[:6]
        bias_ref, dup_ref, sum_ref, fac_ref, send_sem, recv_sem, local_sem = refs[6:]
        side_work = BackCopies(parts_ref, grads_ref, out_ref, got_ref, send_sem, recv_sem, local_sem)
        side_work.first()
    else:
        dq_ref, dkf_ref, bias_ref, dup_ref, sum_ref, fac_ref = refs
    rows = q_ref.shape[0]
    keys = kf_ref.shape[0]
    bias_ref[...] = mask_bias(seg_ref, keys, rows)
    for s in range(2 * RK):
        tile = kf_ref[:, (s // 2) * LANES : (s // 2 + 1) * LANES].astype(F32)
        dup_ref[s] = double_left(tile) if s % 2 == 0 else double_right(tile)
    sum_ref[...] = jnp.zeros_like(sum_ref)
    fac_ref[...] = jnp.zeros_like(fac_ref)

    def pair(p, carried):
        lanes = pl.ds(pl.multiple_of(p * LANES, LANES), LANES)
        k_tile = k_ref[:, lanes]
        v_tile = v_ref[:, lanes]
        k_turned = k_tile.astype(F32).T.astype(BF)
        q_tile = q_ref[:, lanes].astype(F32) * HD**-0.5
        do_tile = do_ref[:, lanes].astype(F32)
        q_turned = q_tile.T
        do_turned = do_tile.T
        half = lax.broadcasted_iota(jnp.int32, q_turned.shape, 0) // HD
        lane_half = lax.broadcasted_iota(jnp.int32, q_tile.shape, 1) // HD
        d_k = None
        d_v = None
        d_q = []
        for side in range(2):
            q_side = jnp.where(half == side, q_turned, 0.0).astype(BF)
            do_side = jnp.where(half == side, do_turned, 0.0).astype(BF)
            scores = nn(k_tile, q_side) + bias_ref[...]
            probs = jnp.exp(scores - lse_ref[2 * p + side][:1])
            d_prob = nn(v_tile, do_side)
            delta = jnp.sum(probs * d_prob, axis=0, keepdims=True)
            d_score = (probs * (d_prob - delta)).astype(BF)
            d_q.append(nn(k_turned[side * HD : (side + 1) * HD], d_score))
            q_back = jnp.where(lane_half == side, q_tile, 0.0).astype(BF)
            do_back = jnp.where(lane_half == side, do_tile, 0.0).astype(BF)
            part_k = nn(d_score, q_back)
            part_v = nn(probs.astype(BF), do_back)
            d_k = part_k if d_k is None else d_k + part_k
            d_v = part_v if d_v is None else d_v + part_v
        dq_ref[:, lanes] = jnp.concatenate(d_q, axis=0).T * HD**-0.5
        weights = kf_ref[:, 2 * LANES :]
        for kind, grad in ((0, d_k), (1, d_v)):
            for s in range(RK):
                slot = kind * RK + s
                pick = spread(2 * RK * H, slot * H + 2 * p, LANES)
                sum_ref[slot] += nn(weights, pick) * grad
                fac_ref[...] += two_pass(grad * dup_ref[slot], collect(LANES, 2 * RK * H, slot * H + 2 * p))
        return carried

    lax.fori_loop(0, PAIRS, pair, 0)
    for tile in range(2):
        first = sum_ref[2 * tile]
        second = sum_ref[2 * tile + 1]
        first = first + pltpu.roll(first, HD, 1)
        second = second + pltpu.roll(second, HD, 1)
        merged = jnp.where(lane_iota(first.shape) < HD, first, second)
        dkf_ref[:, tile * LANES : (tile + 1) * LANES] = (merged / RK).astype(BF)
    dkf_ref[:, 2 * LANES :] = (fac_ref[...] / RK).astype(BF)
    if fast:
        side_work.last()


def attend_back(q, k, v, d_heads, lse, kf_window, seg_window, out_parts=None, grads=None):
    rows = q.shape[0]
    keys = kf_window.shape[0]
    fast = grads is not None
    outs = [jax.ShapeDtypeStruct((rows, D), F32), jax.ShapeDtypeStruct(kf_window.shape, BF)]
    scratch = [
        pltpu.VMEM((keys, rows), F32),
        pltpu.VMEM((2 * RK, keys, LANES), F32),
        pltpu.VMEM((2 * RK, keys, LANES), F32),
        pltpu.VMEM((keys, 2 * RK * H), F32),
    ]
    in_specs, out_specs, more = [VMEM] * 7, [VMEM] * 2, []
    if fast:
        outs += [
            jax.ShapeDtypeStruct(out_parts.shape, BF),
            jax.ShapeDtypeStruct((2,) + grads.shape[1:], BF),
        ]
        in_specs += [ANY] * 2
        out_specs += [ANY] * 2
        more = [out_parts, grads]
        scratch += [
            pltpu.SemaphoreType.DMA((5,)),
            pltpu.SemaphoreType.DMA((5,)),
            pltpu.SemaphoreType.DMA,
        ]
    return pl.pallas_call(
        functools.partial(attend_back_body, fast),
        out_shape=tuple(outs),
        in_specs=in_specs,
        out_specs=tuple(out_specs),
        scratch_shapes=scratch,
        compiler_params=comm_params(6) if fast else params(),
        cost_estimate=cost_of(2 * rows * keys * D * 40, 16 << 20),
    )(q, k, v, d_heads, lse, kf_window, seg_window, *more)


def mixing_body(x_ref, heads_ref, w_out_ref, gain_ref, mixed_ref, h_ref):
    parts, _, feat = x_ref.shape
    rows_of = w_out_ref.shape[0]
    head_rows = w_out_ref.shape[2]
    total = None
    for c in range(parts):
        lanes = slice(c * feat, (c + 1) * feat)
        acc = x_ref[c].astype(F32)
        for r in range(rows_of):
            acc = acc + nn(heads_ref[:, r * head_rows : (r + 1) * head_rows], w_out_ref[r, c])
        mixed_ref[:, lanes] = acc
        part = jnp.sum(acc * acc, axis=1, keepdims=True)
        total = part if total is None else total + part
    scale = lax.rsqrt(total / D + EPS)
    for c in range(parts):
        lanes = slice(c * feat, (c + 1) * feat)
        h_ref[:, lanes] = (mixed_ref[:, lanes] * scale * gain_ref[c, 1:2]).astype(BF)


def mixing(x_parts, heads, w_out, gains):
    rows = heads.shape[0]
    return call(
        mixing_body,
        (jax.ShapeDtypeStruct((rows, D), F32), jax.ShapeDtypeStruct((rows, D), BF)),
        cost=cost_of(2 * rows * D * D, 5 << 20),
    )(x_parts, heads, w_out, gains)


def ffn_steps(blocks, h_at, cot_at, w_ref, hid_ref, dg_ref, du_ref, out_at, back_at):
    def block(t, carried):
        h = h_at(t)[...]
        gate = nt(h, w_ref[0])
        up = nt(h, w_ref[1])
        d_hidden = nt(cot_at(t)[...], w_ref[2])
        sig = 1.0 / (1.0 + jnp.exp(-gate))
        silu = gate * sig
        hidden = (silu * up).astype(BF)
        d_gate = (d_hidden * up * sig * (1.0 + gate * (1.0 - sig))).astype(BF)
        d_up = (d_hidden * silu).astype(BF)
        rows = h.shape[0]
        place = pl.ds(pl.multiple_of(t * rows, rows), rows)
        hid_ref[place] = hidden
        dg_ref[place] = d_gate
        du_ref[place] = d_up
        out_at(t)[...] = nn(hidden, w_ref[2]).astype(BF)
        back_at(t)[...] = (nn(d_gate, w_ref[0]) + nn(d_up, w_ref[1])).astype(BF)
        return carried

    lax.fori_loop(0, blocks, block, 0)


def ffn_body(h_ref, cot_ref, w_ref, out_ref, back_ref, g_ref, hid_ref, dg_ref, du_ref):
    parts, rows, _ = h_ref.shape
    ffn_steps(
        parts, lambda t: h_ref.at[t], lambda t: cot_ref.at[t], w_ref, hid_ref, dg_ref, du_ref,
        lambda t: out_ref.at[t], lambda t: back_ref.at[t],
    )
    h_all = h_ref[...].reshape(parts * rows, D)
    cot_all = cot_ref[...].reshape(parts * rows, D)
    for place, (left, right) in enumerate(((dg_ref, h_all), (du_ref, h_all), (hid_ref, cot_all))):
        g_ref[place] = tn(left[...], right).astype(BF)


def ffn(h_all, cot_all, w):
    parts, rows, _ = h_all.shape
    units = w.shape[1]
    return call(
        ffn_body,
        (
            jax.ShapeDtypeStruct(h_all.shape, BF),
            jax.ShapeDtypeStruct(h_all.shape, BF),
            jax.ShapeDtypeStruct(w.shape, BF),
        ),
        scratch=[pltpu.VMEM((parts * rows, units), BF)] * 3,
        cost=cost_of(2 * parts * rows * 9 * D * units, 20 << 20),
    )(h_all, cot_all, w)


def ffn_square_body(
    near_ref, far_ref, cot_near_ref, cot_far_ref, rows_ref, last_ref,
    out_ref, back_ref, g_ref, cot_own_ref,
    w_ref, h_ref, cot_ref, hid_ref, dg_ref, du_ref, w_sem, h_sem, cot_sem,
):
    row = lax.axis_index("row")
    col = lax.axis_index("col")
    _, spots = square()
    core = lax.rem(col, 2)
    parts, _, units, feat = rows_ref.shape[1:]
    rows = near_ref.shape[1]
    waits = []
    for r in range(4):
        is_last = jnp.logical_or(jnp.logical_and(row == 3, r == 0), jnp.logical_and(row == 0, r == 3))
        for c in range(parts):
            target = w_ref.at[:, pl.ds(r * units, units), pl.ds(c * feat, feat)]
            kept = pltpu.make_async_copy(rows_ref.at[r, c], target, w_sem.at[r, c])
            late = pltpu.make_async_copy(last_ref.at[c], target, w_sem.at[r, c])
            pl.when(jnp.logical_not(is_last))(kept.start)
            pl.when(is_last)(late.start)
            waits.append(kept)
    for side, source in ((0, near_ref), (1, far_ref)):
        c = pltpu.make_async_copy(source, h_ref.at[side], h_sem.at[side])
        c.start()
        waits.append(c)
    for side, source in ((0, cot_near_ref), (1, cot_far_ref)):
        from_core = lax.rem(core + side, 2)
        for q in range(4):
            lanes = pl.ds(pl.multiple_of((q % 2 * 2 + from_core) * feat, feat), feat)
            for c in range(4):
                to = lax.rem(core + c, 2)
                copy = pltpu.make_async_copy(
                    source.at[q, pl.ds(c * rows, rows)],
                    cot_ref.at[to, q // 2 * 2 + c // 2, :, lanes],
                    cot_sem.at[side, q, c],
                )
                copy.start()
                waits.append(copy)
    for c in waits:
        c.wait()
    cot_own_ref[...] = cot_ref[0, spots[0]]
    ffn_steps(
        8, lambda t: h_ref.at[t // 4, lax.rem(t, 4)], lambda t: cot_ref.at[t // 4, lax.rem(t, 4)],
        w_ref, hid_ref, dg_ref, du_ref,
        lambda t: out_ref.at[t // 4, lax.rem(t, 4)], lambda t: back_ref.at[t // 4, lax.rem(t, 4)],
    )
    h_all = h_ref[...].reshape(8 * rows, D)
    cot_all = cot_ref[...].reshape(8 * rows, D)
    for place, (left, right) in enumerate(((dg_ref, h_all), (du_ref, h_all), (hid_ref, cot_all))):
        grad = tn(left[...], right)
        for r in range(4):
            g_ref[r, place] = grad[r * units : (r + 1) * units].astype(BF)


def ffn_square(near, far, cot_near, cot_far, w_rows, w_last):
    rows = near.shape[1]
    units = w_rows.shape[3]
    both = jax.ShapeDtypeStruct((2, 4, rows, D), BF)
    return pl.pallas_call(
        ffn_square_body,
        out_shape=(
            both,
            both,
            jax.ShapeDtypeStruct((4, 3, units, D), BF),
            jax.ShapeDtypeStruct((rows, D), BF),
        ),
        in_specs=[ANY] * 6,
        out_specs=(VMEM,) * 4,
        scratch_shapes=[
            pltpu.VMEM((3, 4 * units, D), BF),
            pltpu.VMEM((2, 4, rows, D), BF),
            pltpu.VMEM((2, 4, rows, D), BF),
        ]
        + [pltpu.VMEM((8 * rows, 4 * units), BF)] * 3
        + [
            pltpu.SemaphoreType.DMA((4, 4)),
            pltpu.SemaphoreType.DMA((2,)),
            pltpu.SemaphoreType.DMA((2, 4, 4)),
        ],
        compiler_params=params(),
        cost_estimate=cost_of(2 * 8 * rows * 9 * D * 4 * units, 24 << 20),
    )(near, far, cot_near, cot_far, w_rows, w_last)


def unmix_math(
    mixed_ref, cot_ref, d_h, heads_ref, w_out_ref, gain_ref, d_mixed_ref, d_heads_ref, g_out_ref, g_gain_ref
):
    rows_of, parts, head_rows, feat = w_out_ref.shape
    mixed = mixed_ref[...]
    scale = lax.rsqrt(jnp.sum(mixed * mixed, axis=1, keepdims=True) / D + EPS)
    normed = mixed * scale
    g_gain_ref[...] = jnp.sum(d_h * normed, axis=0, keepdims=True)
    gain = jnp.concatenate([gain_ref[c, 1:2] for c in range(parts)], axis=1)
    inner = d_h * gain
    dot = jnp.sum(inner * normed, axis=1, keepdims=True) / D
    d_mixed = cot_ref[...].astype(F32) + scale * (inner - normed * dot)
    d_mixed_ref[...] = d_mixed
    low = d_mixed.astype(BF)
    grad = tn(heads_ref[...], low)
    for r in range(rows_of):
        acc = None
        for c in range(parts):
            lanes = slice(c * feat, (c + 1) * feat)
            term = nt(low[:, lanes], w_out_ref[r, c])
            acc = term if acc is None else acc + term
            g_out_ref[r, c] = grad[r * head_rows : (r + 1) * head_rows, lanes].astype(BF)
        d_heads_ref[:, r * head_rows : (r + 1) * head_rows] = acc.astype(BF)


def write_output(mixed_ref, total, out_ref):
    parts, _, feat = out_ref.shape
    for c in range(parts):
        lanes = slice(c * feat, (c + 1) * feat)
        out_ref[c] = (mixed_ref[:, lanes] + total[:, lanes]).astype(BF)


def unmix_body(
    dh_ref, sum_ref, mixed_ref, cot_ref, heads_ref, w_out_ref, gain_ref,
    out_ref, d_mixed_ref, d_heads_ref, g_out_ref, g_gain_ref,
):
    unmix_math(
        mixed_ref, cot_ref, dh_ref[...], heads_ref, w_out_ref, gain_ref,
        d_mixed_ref, d_heads_ref, g_out_ref, g_gain_ref,
    )
    write_output(mixed_ref, sum_ref[...], out_ref)


def unmix_square_body(
    dh_ref, sum_ref, mixed_ref, cot_ref, heads_ref, w_out_ref, gain_ref, g_ref,
    out_ref, d_mixed_ref, d_heads_ref, g_out_ref, g_gain_ref, got_ref,
    near_ref, pair_ref, diag_ref, far_ref, send_sem, recv_sem,
):
    row = lax.axis_index("row")
    col, core, across = neighbours()
    dp, spots = square()
    third = lax.rem(row + 2, 4)
    greet(
        [(None, {"col": core}), (None, {"col": across}), (None, {"dp": 1 - dp}), (None, {"row": third})]
    )
    mover = Mover(send_sem, recv_sem)
    sums = [
        SquareSum(mover, part, near_ref.at[k], pair_ref.at[k], diag_ref.at[k], far_ref.at[k])
        for k, part in enumerate((dh_ref, sum_ref))
    ]
    for one in sums:
        one.near(core, spots)
    grads = mover.copy(g_ref.at[third], got_ref, row=third)
    grads.start()
    for one in sums:
        one.send(dp, across)
    unmix_math(
        mixed_ref, cot_ref, sums[0].total(), heads_ref, w_out_ref, gain_ref,
        d_mixed_ref, d_heads_ref, g_out_ref, g_gain_ref,
    )
    write_output(mixed_ref, sums[1].total(), out_ref)
    for one in sums:
        one.end()
    grads.wait()


def unmix(dh, out_sum, mixed, cot_own, heads, w_out, gains, grads=None):
    rows = heads.shape[0]
    parts, feat = w_out.shape[1], w_out.shape[3]
    outs = [
        jax.ShapeDtypeStruct((parts, rows, feat), BF),
        jax.ShapeDtypeStruct((rows, D), F32),
        jax.ShapeDtypeStruct((rows, D), BF),
        jax.ShapeDtypeStruct(w_out.shape, BF),
        jax.ShapeDtypeStruct((1, D), F32),
    ]
    cost = cost_of(4 * rows * D * D, 18 << 20)
    if grads is None:
        return call(unmix_body, tuple(outs), cost=cost)(dh, out_sum, mixed, cot_own, heads, w_out, gains)
    count = 2 * 10 + 1
    return pl.pallas_call(
        unmix_square_body,
        out_shape=tuple(outs) + (jax.ShapeDtypeStruct(grads.shape[1:], BF),),
        in_specs=[VMEM] * 7 + [ANY],
        out_specs=(VMEM,) * 5 + (ANY,),
        scratch_shapes=[
            pltpu.VMEM((2, 4, rows, D), BF),
            pltpu.VMEM((2, 4, rows, D), BF),
            pltpu.VMEM((2, 2, rows // 2, D), BF),
            pltpu.VMEM((2, 2, rows, D), BF),
            pltpu.SemaphoreType.DMA((count,)),
            pltpu.SemaphoreType.DMA((count,)),
        ],
        compiler_params=comm_params(5),
        cost_estimate=cost,
    )(dh, out_sum, mixed, cot_own, heads, w_out, gains, grads)


def back_body(
    fast, dq_ref, dkf_ref, hf_ref, bq_ref, turn_ref, w_ref, h_ref, x_ref, gain_ref, d_mixed_ref, g_two_ref, *refs
):
    if fast:
        g_own_ref, g_mid_ref, g_ends_ref, gi_ref, g_ref, cols_ref, d_ref, send_ref, send_sem, recv_sem = refs
        row = lax.axis_index("row")
        col, core, across = neighbours()
        cross = lax.rem(core + 2, 4)
        greet([(None, {"col": c}) for c in (core, across, cross)])
        mover = Mover(send_sem, recv_sem)
        width = x_ref.shape[2]
        for place in range(3):
            total = (
                g_own_ref[row, place].astype(F32)
                + g_mid_ref[place].astype(F32)
                + g_ends_ref[0, place].astype(F32)
                + g_ends_ref[1, place].astype(F32)
            ).astype(BF)
            for c in range(4):
                send_ref[c, place] = total[:, c * width : (c + 1) * width]
        copies = [mover.copy(send_ref.at[c], cols_ref.at[col], col=c) for c in (across, cross, core)]
        for c in copies:
            c.start()
        cols_ref[col] = send_ref[col]
    else:
        gi_ref, g_ref, d_ref = refs
    parts, rows, feat = x_ref.shape
    heads = hf_ref[...]
    high = heads.astype(BF)
    low = (heads - high.astype(F32)).astype(BF)
    dq = dq_ref[...] * (1.0 / RQ)
    cosine = turn_ref[:, :LANES]
    sine = turn_ref[:, LANES:]
    d_fac = jnp.zeros((rows, HEAD_COLS), F32)
    folded = []
    for r in range(RQ):
        tile = bq_ref[:, (r // 2) * LANES : (r // 2 + 1) * LANES]
        rank = double_left(tile) if r % 2 == 0 else double_right(tile)
        product = dq * jnp.concatenate([rank] * PAIRS, axis=1)
        d_fac = d_fac + two_pass(product, head_collect(2 * RK + r))
        pick = head_spread(2 * RK + r, 0, D)
        terms = (nn(high, pick) + nn(low, pick)) * dq
        acc = terms[:, :LANES]
        for p in range(1, PAIRS):
            acc = acc + terms[:, p * LANES : (p + 1) * LANES]
        folded.append(acc + pltpu.roll(acc, HD, 1))
    lane = lane_iota(folded[0].shape)

    def turn_back(part):
        return part * cosine - swap_halves(part) * sine

    for tile in range(3):
        merged = jnp.where(lane < HD, folded[2 * tile], folded[2 * tile + 1])
        d_ref[:, tile * LANES : (tile + 1) * LANES] = turn_back(merged).astype(BF)
    d_ref[:, 3 * LANES : 4 * LANES] = turn_back(dkf_ref[:, :LANES].astype(F32)).astype(BF)
    d_ref[:, 4 * LANES : 5 * LANES] = dkf_ref[:, LANES : 2 * LANES].astype(BF)
    key_low = dkf_ref[:, 2 * LANES :].astype(BF)
    d_fac = d_fac.astype(BF).astype(F32) + nt(key_low, key_columns())
    d_ref[:, RANK_COLS:] = d_fac.astype(BF)
    d_all = d_ref[...]
    d_h = nn(d_all, w_ref[...])
    xs = [x_ref[c].astype(F32) for c in range(parts)]
    total = sum(jnp.sum(v * v, axis=1, keepdims=True) for v in xs)
    scale = lax.rsqrt(total / D + EPS)
    dot = None
    gains = []
    for c in range(parts):
        lanes = slice(c * feat, (c + 1) * feat)
        normed = xs[c] * scale
        grad = d_h[:, lanes]
        gains.append(jnp.sum(grad * normed, axis=0, keepdims=True))
        part = jnp.sum(grad * gain_ref[c, :1] * normed, axis=1, keepdims=True)
        dot = part if dot is None else dot + part
    for c in range(parts):
        lanes = slice(c * feat, (c + 1) * feat)
        normed = xs[c] * scale
        gi_ref[c] = d_mixed_ref[:, lanes] + scale * (
            d_h[:, lanes] * gain_ref[c, :1] - normed * (dot / D)
        )
    grad = tn(d_all, h_ref[...])
    n_row = g_ref.shape[0]
    ranks_each = RANK_COLS // n_row
    used = FAC * GROUP
    for c in range(parts):
        lanes = slice(c * feat, (c + 1) * feat)
        tail = jnp.concatenate(
            [gains[c], g_two_ref[:, lanes], jnp.zeros((GROUP_COLS - used - 2, feat), F32)], axis=0
        )
        for r in range(n_row):
            first = RANK_COLS + r * GROUP_COLS
            g_ref[r, c, :ranks_each] = grad[r * ranks_each : (r + 1) * ranks_each, lanes].astype(BF)
            g_ref[r, c, ranks_each:] = jnp.concatenate([grad[first : first + used, lanes], tail], axis=0).astype(BF)
    if fast:
        for c in copies:
            c.wait()


def back(dq, dkf, hf, bq, turn, w_rh, h, x_parts, gains, d_mixed, g_two, n_row, grads=None):
    rows = dq.shape[0]
    parts, _, feat = x_parts.shape
    each = RANK_COLS // n_row + GROUP_COLS
    outs = [jax.ShapeDtypeStruct(x_parts.shape, F32), jax.ShapeDtypeStruct((n_row, parts, each, feat), BF)]
    scratch = [pltpu.VMEM((rows, ALL_COLS), BF)]
    more = []
    fast = grads is not None
    if fast:
        units = grads[0].shape[2]
        cols = (4, 3, units, feat)
        outs.append(jax.ShapeDtypeStruct(cols, BF))
        more = list(grads)
        scratch += [
            pltpu.VMEM(cols, BF),
            pltpu.SemaphoreType.DMA((3,)),
            pltpu.SemaphoreType.DMA((3,)),
        ]
    return pl.pallas_call(
        functools.partial(back_body, fast),
        out_shape=tuple(outs),
        in_specs=[VMEM] * (11 + len(more)),
        out_specs=(VMEM,) * len(outs),
        scratch_shapes=scratch,
        compiler_params=comm_params(8) if fast else params(),
        cost_estimate=cost_of(2 * rows * D * 800 * 6, 12 << 20),
    )(dq, dkf, hf, bq, turn, w_rh, h, x_parts, gains, d_mixed, g_two, *more)


def finish_body(
    g_ref, gi_ref, cols_ref, out_ref,
    grad_ref, gi_all_ref, cols_other_ref, out_other_ref,
    near_ref, pair_ref, far_ref, side_ref, down_ref, last_ref, end_ref, send_sem, recv_sem, local_sem,
):
    row = lax.axis_index("row")
    col, core, across = neighbours()
    cross = lax.rem(core + 2, 4)
    dp = lax.axis_index("dp")
    x, mine = col // 2, lax.rem(col, 2)
    rows = [lax.rem(row + k, 4) for k in range(4)]
    greet(
        [(None, {"col": c}) for c in (core, across, cross)]
        + [(None, {"row": r}) for r in rows[1:]]
        + [(None, {"dp": 1 - dp})]
    )
    mover = Mover(send_sem, recv_sem)
    started = []

    def go(source, target, **place):
        c = mover.copy(source, target, **place)
        c.start()
        started.append(c)
        return c

    first = [go(g_ref.at[r, (1 - x) * 2 + 1 - mine], near_ref.at[0, r], col=core) for r in range(4)]
    second = [go(g_ref.at[r, x * 2 + 1 - mine], near_ref.at[1, r], col=core) for r in range(4)]
    rest = [
        go(cols_ref, cols_other_ref, dp=1 - dp),
        go(out_ref, out_other_ref, dp=1 - dp),
    ]
    sides = []
    for r in range(4):
        first[r].wait_recv()
        pair_ref[r] = (g_ref[r, (1 - x) * 2 + mine].astype(F32) + near_ref[0, r].astype(F32)).astype(BF)
        sides.append(go(pair_ref.at[r], side_ref.at[r], col=across))
    for c in (across, cross, core):
        rest.append(go(gi_ref.at[c], gi_all_ref.at[col], col=c))
    own = pltpu.make_async_copy(gi_ref.at[col], gi_all_ref.at[col], local_sem)
    own.start()
    for r in range(4):
        second[r].wait_recv()
        sides[r].wait_recv()
        far_ref[r] = (
            g_ref[r, x * 2 + mine].astype(F32) + near_ref[1, r].astype(F32) + side_ref[r].astype(F32)
        ).astype(BF)
    downs = [go(far_ref.at[rows[k]], down_ref.at[k - 1], row=rows[k]) for k in range(1, 4)]
    total = far_ref[row].astype(F32)
    for k in range(3):
        downs[k].wait_recv()
        total = total + down_ref[k].astype(F32)
    last_ref[...] = total.astype(BF)
    end = go(last_ref, end_ref, dp=1 - dp)
    end.wait_recv()
    grad_ref[...] = last_ref[...].astype(F32) + end_ref[...].astype(F32)
    for c in rest:
        c.wait_recv()
    for c in started:
        c.wait_send()
    own.wait()


def finish(g, gi_parts, cols, g_out):
    block = g.shape[2:]
    count = 8 + 2 + 4 + 3 + 3 + 1
    return pl.pallas_call(
        finish_body,
        out_shape=(
            jax.ShapeDtypeStruct(block, F32),
            jax.ShapeDtypeStruct(gi_parts.shape, gi_parts.dtype),
            jax.ShapeDtypeStruct(cols.shape, BF),
            jax.ShapeDtypeStruct(g_out.shape, BF),
        ),
        in_specs=[VMEM, ANY, ANY, ANY],
        out_specs=(VMEM, ANY, ANY, ANY),
        scratch_shapes=[
            pltpu.VMEM((2, 4) + block, BF),
            pltpu.VMEM((4,) + block, BF),
            pltpu.VMEM((4,) + block, BF),
            pltpu.VMEM((4,) + block, BF),
            pltpu.VMEM((3,) + block, BF),
            pltpu.VMEM(block, BF),
            pltpu.VMEM(block, BF),
            pltpu.SemaphoreType.DMA((count,)),
            pltpu.SemaphoreType.DMA((count,)),
            pltpu.SemaphoreType.DMA,
        ],
        compiler_params=comm_params(9),
        cost_estimate=cost_of(0, 10 << 20),
    )(g, gi_parts, cols, g_out)


def local(
    tokens_in, segments, gain_attn, gain_ffn, w_heads, w_ranks, w_out, w_gate, w_up, w_down, cotangent
):
    n_row = lax.axis_size("row")
    n_col = lax.axis_size("col")
    row = lax.axis_index("row")
    col = lax.axis_index("col")
    micro, row_tokens, feat = tokens_in.shape
    subs = n_col // micro
    rows = row_tokens // subs
    length = row_tokens * n_row
    head_local = w_heads.shape[1] // FAC
    rank_local = w_ranks.shape[1]
    ffn_local = w_gate.shape[1]
    out_local = w_out.shape[0]
    block = row * subs + col % subs
    past = min(-(-(MAX_DOC - 1) // rows), n_row * subs - 1)
    keys = (past + 1) * rows

    dp_count = lax.axis_size("dp")
    fast = n_col == 4 and n_row == 4 and dp_count == 2 and micro == 2 and past == 4

    heads_t = jnp.transpose(w_heads.reshape(feat, head_local, FAC), (2, 1, 0))
    heads_t = heads_t[jnp.array(FAC_ORDER)].reshape(FAC * head_local, feat)
    pad = jnp.zeros((GROUP_COLS - FAC * head_local, feat), BF)
    w_own = jnp.concatenate([w_ranks.T, heads_t, pad], axis=0)
    gains_own = jnp.concatenate([gain_attn[None], gain_ffn[None], jnp.zeros((6, feat), F32)], axis=0)
    tokens = tokens_in.reshape(n_col, rows, feat)
    if fast:
        dp = lax.axis_index("dp")
        part = ffn_local // (2 * n_col)
        units = -(-part // 16) * 16
        ffn_own = jnp.stack([w_gate.T, w_up.T, w_down]).reshape(3, 2, n_col, part, feat)
        ffn_own = jnp.transpose(lax.dynamic_index_in_dim(ffn_own, dp, 1, False), (1, 0, 2, 3))
        ffn_own = jnp.pad(ffn_own, ((0, 0), (0, 0), (0, units - part), (0, 0)))
        x_parts, w_blocks, gains, ffn_parts = start(tokens, w_own, gains_own, ffn_own)
        w_out, x_parts = lax.optimization_barrier((w_out, x_parts))
    else:
        part = ffn_local // n_col
        units = part * n_row
        w_ffn = jnp.stack([w_gate.T, w_up.T, w_down]).reshape(3, n_col, part, feat)
        w_ffn = lax.all_to_all(jnp.transpose(w_ffn, (1, 0, 2, 3)), "col", 0, 0, tiled=True)
        w_ffn = jnp.transpose(w_ffn, (1, 2, 0, 3)).reshape(3, part, D)
        w_ffn = jnp.transpose(lax.all_gather(w_ffn, "row", axis=0), (1, 0, 2, 3)).reshape(3, units, D)
        w_blocks = lax.all_gather(w_own, ("row", "col"), axis=0).reshape((n_row, n_col) + w_own.shape)
        gains = lax.all_gather(gains_own, "col", axis=0)
        x_parts = lax.all_to_all(tokens, "col", 0, 0, tiled=True)
    w_out_all = lax.all_gather(w_out, ("row", "col"), axis=0).reshape((n_row, n_col) + w_out.shape)

    seg_row = lax.dynamic_index_in_dim(segments, col // subs, 0, keepdims=False)
    padded = jnp.concatenate([jnp.full((1, past * rows), -1, jnp.int32), seg_row], axis=1)
    seg_window = lax.dynamic_slice_in_dim(padded, block * rows, keys, 1)
    own_seg = seg_window[0, past * rows :]
    key_idx = jnp.arange(keys, dtype=jnp.int32)
    query_idx = jnp.arange(rows, dtype=jnp.int32) + past * rows
    before = (own_seg[:, None] == seg_window) & (key_idx[None, :] < query_idx[:, None])
    places = jnp.sum(before.astype(jnp.int32), axis=1)
    inverse = ROPE ** (-(jnp.arange(HD // 2, dtype=F32) * 2.0 / HD))
    angles = places.astype(F32)[:, None] * inverse[None, :]
    cosine = jnp.cos(angles)
    sine = jnp.sin(angles)
    turn = jnp.concatenate([cosine] * 4 + [-sine, sine, -sine, sine], axis=1)

    h_one, head_fac, bq_rot, key_fac, queries, w_rh = front(x_parts, gains, w_blocks, turn)

    groups = [[m * subs + s for s in range(subs)] for m in range(micro)]
    if fast:
        kf_window = window(key_fac, n_row).reshape(keys, -1)
        cot_rows = cotangent.reshape(micro * row_tokens, feat)
        heads_out, lse, key_all, value_all, w_rows, cot_near = attend(
            queries, kf_window, seg_window, ffn_parts, cot_rows
        )
        mixed, h_two = mixing(x_parts, heads_out, w_out_all, gains)
        h_near, h_far, cot_far, w_last = gather(h_two, cot_near, w_rows)
        out_part, dh_part, g_rows, cot_own = ffn_square(h_near, h_far, cot_near, cot_far, w_rows, w_last)
        out_parts, d_mixed, d_heads, g_out, g_gain_two, g_mid = unmix(
            dh_part, out_part, mixed, cot_own, heads_out, w_out_all, gains, g_rows
        )
        d_q, d_kf, output, g_ends = attend_back(
            queries, key_all, value_all, d_heads, lse, kf_window, seg_window, out_parts, g_rows
        )
        own_kf = window_back(d_kf.reshape(past + 1, rows, -1), n_row)
        g_out = lax.psum_scatter(
            g_out.reshape((n_row * n_col,) + w_out.shape), ("row", "col"), scatter_dimension=0, tiled=False
        )
        own_kf, g_out = lax.optimization_barrier((own_kf, g_out))
        gi_parts, g_rh, g_cols = back(
            d_q, own_kf, head_fac, bq_rot, turn, w_rh, h_one, x_parts, gains, d_mixed, g_gain_two, n_row,
            (g_rows, g_mid, g_ends),
        )
        g_rh, grad_input, cols_other, out_other = finish(g_rh, gi_parts, g_cols, g_out)
        g_out = g_out.astype(F32) + out_other.astype(F32)
        g_ffn = jnp.where(dp == 0, jnp.stack([g_cols, cols_other]), jnp.stack([cols_other, g_cols]))
        g_ffn = jnp.transpose(g_ffn[:, :, :, :part], (2, 0, 1, 3, 4)).reshape(3, ffn_local, feat).astype(F32)
    else:
        gathered = lax.all_gather(key_fac, "row", axis=0)
        gathered = lax.all_gather(gathered, "col", axis=1, axis_index_groups=groups)
        gathered = gathered.reshape(length, key_fac.shape[1])
        padded_kf = jnp.concatenate([jnp.zeros((past * rows, key_fac.shape[1]), BF), gathered], axis=0)
        kf_window = lax.dynamic_slice_in_dim(padded_kf, block * rows, keys, 0)
        heads_out, lse, key_all, value_all = attend(queries, kf_window, seg_window)
        mixed, h_two = mixing(x_parts, heads_out, w_out_all, gains)
        cot_own = lax.all_to_all(cotangent.reshape(n_col, rows, feat), "col", 0, 0, tiled=True)
        cot_own = jnp.transpose(cot_own, (1, 0, 2)).reshape(rows, D)
        cot_all = lax.all_gather(cot_own, "col", axis=0)
        h_all = lax.all_gather(h_two, "col", axis=0)
        out_part, dh_part, g_ffn = ffn(h_all, cot_all, w_ffn)
        dh_sum = lax.psum_scatter(dh_part, "col", scatter_dimension=0, tiled=False).astype(F32)
        out_sum = lax.psum_scatter(out_part, "col", scatter_dimension=0, tiled=False).astype(F32)
        out_parts, d_mixed, d_heads, g_out, g_gain_two = unmix(
            dh_sum, out_sum, mixed, cot_own, heads_out, w_out_all, gains
        )
        d_q, d_kf = attend_back(queries, key_all, value_all, d_heads, lse, kf_window, seg_window)
        spread_kf = jnp.zeros((past * rows + length, d_kf.shape[1]), BF)
        spread_kf = lax.dynamic_update_slice_in_dim(spread_kf, d_kf, block * rows, 0)[past * rows :]
        spread_kf = spread_kf.reshape(n_row, subs, rows, -1)
        own_kf = lax.psum_scatter(spread_kf, "row", scatter_dimension=0, tiled=False)
        own_kf = lax.psum_scatter(own_kf, "col", scatter_dimension=0, tiled=False, axis_index_groups=groups)
        gi_parts, g_rh = back(
            d_q, own_kf, head_fac, bq_rot, turn, w_rh, h_one, x_parts, gains, d_mixed, g_gain_two, n_row
        )
        output = lax.all_to_all(out_parts, "col", 0, 0, tiled=True)
        grad_input = lax.all_to_all(gi_parts, "col", 0, 0, tiled=True)
        g_ffn = lax.psum_scatter(g_ffn.reshape(3, n_row, part, D), "row", scatter_dimension=1, tiled=False)
        g_ffn = jnp.transpose(lax.psum(g_ffn, "dp").reshape(3, part, n_col, feat), (2, 0, 1, 3))
        g_ffn = lax.all_to_all(g_ffn, "col", 0, 0, tiled=True)
        g_ffn = jnp.transpose(g_ffn, (1, 0, 2, 3)).reshape(3, ffn_local, feat).astype(F32)

        def total(values):
            values = values.reshape((n_row * n_col,) + values.shape[2:])
            values = lax.psum_scatter(values, ("row", "col"), scatter_dimension=0, tiled=False)
            return lax.psum(values, "dp").astype(F32)

        g_out = total(g_out)
        g_rh = total(g_rh)

    used = rank_local + FAC * head_local
    own_heads = g_rh[rank_local:used].reshape(FAC, head_local, feat)
    own_heads = jnp.transpose(own_heads[jnp.array(FAC_BACK)], (2, 1, 0)).reshape(w_heads.shape)
    return (
        output.reshape(tokens_in.shape),
        grad_input.reshape(tokens_in.shape),
        g_rh[used],
        g_rh[used + 1],
        own_heads,
        g_rh[:rank_local].T,
        g_out,
        g_ffn[0].T,
        g_ffn[1].T,
        g_ffn[2],
    )


def solution(mesh):
    tokens = P(None, ("dp", "row"), "col")
    both = P("col", "row")
    turned = P("row", "col")
    gain = P("col")
    return jax.shard_map(
        local,
        mesh=mesh,
        in_specs=(tokens, P(None, "dp", None), gain, gain, both, both, turned, both, both, turned, tokens),
        out_specs=(tokens, tokens, gain, gain, both, both, turned, both, both, turned),
        check_vma=False,
    )
```

```python
import functools

import jax
import jax.numpy as jnp
from jax import lax
from jax.experimental import pallas as pl
from jax.experimental.pallas import tpu as pltpu
from jax.sharding import PartitionSpec as P

D = 1024
H = 16
HD = 64
RQ = 6
RK = 2
FAC = 10
MAX_DOC = 1024

EPS = 1e-06
ROPE = 10000.0
NEG = -1e30
BF = jnp.bfloat16
F32 = jnp.float32
LANES = 128
PAIRS = H // 2
FAC_ORDER = (6, 7, 8, 9, 0, 1, 2, 3, 4, 5)
FAC_BACK = (4, 5, 6, 7, 8, 9, 0, 1, 2, 3)
VMEM = pl.BlockSpec(memory_space=pltpu.VMEM)


def nn(a, b):
    return jnp.dot(a, b, preferred_element_type=F32)


def nt(a, b):
    return lax.dot_general(a, b, (((1,), (1,)), ((), ())), preferred_element_type=F32)


def tn(a, b):
    return lax.dot_general(a, b, (((0,), (0,)), ((), ())), preferred_element_type=F32)


def two_pass(a, b):
    high = a.astype(BF)
    low = (a - high.astype(F32)).astype(BF)
    return nn(high, b) + nn(low, b)


def lane_iota(shape):
    return lax.broadcasted_iota(jnp.int32, shape, len(shape) - 1)


def spread(rows, first, width):
    row = lax.broadcasted_iota(jnp.int32, (rows, width), 0)
    head = lax.broadcasted_iota(jnp.int32, (rows, width), 1) // HD
    return (row == head + first).astype(F32).astype(BF)


def collect(rows, width, first):
    head = lax.broadcasted_iota(jnp.int32, (rows, width), 0) // HD
    lane = lax.broadcasted_iota(jnp.int32, (rows, width), 1)
    return (lane == head + first).astype(F32).astype(BF)


GROUP = 4
GROUP_COLS = 48
RANK_COLS = FAC * HD
HEAD_COLS = H // GROUP * GROUP_COLS
ALL_COLS = RANK_COLS + HEAD_COLS


def factor_place(head, j):
    return head // GROUP * GROUP_COLS + j * GROUP + head % GROUP


def head_spread(j, first_head, width):
    row = lax.broadcasted_iota(jnp.int32, (HEAD_COLS, width), 0)
    head = lax.broadcasted_iota(jnp.int32, (HEAD_COLS, width), 1) // HD + first_head
    return (row == factor_place(head, j)).astype(F32).astype(BF)


def head_collect(j):
    head = lax.broadcasted_iota(jnp.int32, (D, HEAD_COLS), 0) // HD
    lane = lax.broadcasted_iota(jnp.int32, (D, HEAD_COLS), 1)
    return (lane == factor_place(head, j)).astype(F32).astype(BF)


def key_columns():
    row = lax.broadcasted_iota(jnp.int32, (HEAD_COLS, LANES), 0)
    lane = lax.broadcasted_iota(jnp.int32, (HEAD_COLS, LANES), 1)
    taken = (row == factor_place(lane % H, lane // H)) & (lane < 2 * RK * H)
    return taken.astype(F32).astype(BF)


def swap_halves(tile):
    lane = lane_iota(tile.shape)
    ahead = pltpu.roll(tile, LANES - HD // 2, 1)
    behind = pltpu.roll(tile, HD // 2, 1)
    return jnp.where(lane % HD < HD // 2, ahead, behind)


def double_left(tile):
    return jnp.where(lane_iota(tile.shape) < HD, tile, pltpu.roll(tile, HD, 1))


def double_right(tile):
    return jnp.where(lane_iota(tile.shape) < HD, pltpu.roll(tile, HD, 1), tile)


def params(**more):
    return pltpu.CompilerParams(vmem_limit_bytes=60 << 20, **more)


def call(body, outs, scratch=(), cost=None):
    return pl.pallas_call(
        body,
        out_shape=outs,
        scratch_shapes=scratch,
        compiler_params=params(),
        cost_estimate=cost,
    )


def cost_of(flops, moved):
    return pl.CostEstimate(flops=int(flops), bytes_accessed=int(moved), transcendentals=0)


MESH = pl.DeviceIdType.MESH
ANY = pl.BlockSpec(memory_space=pl.ANY)


class Mover:
    def __init__(self, send_sem, recv_sem):
        self.send_sem = send_sem
        self.recv_sem = recv_sem
        self.used = 0

    def copy(self, source, target, **place):
        index = self.used
        self.used += 1
        return pltpu.make_async_remote_copy(
            src_ref=source,
            dst_ref=target,
            send_sem=self.send_sem.at[index],
            recv_sem=self.recv_sem.at[index],
            device_id=place,
            device_id_type=MESH,
        )


def greet(partners):
    barrier = pltpu.get_barrier_semaphore()
    count = 0
    for present, place in partners:
        if present is None:
            pl.semaphore_signal(barrier, inc=1, device_id=place, device_id_type=MESH)
            count = count + 1
        else:

            @pl.when(present)
            def _():
                pl.semaphore_signal(barrier, inc=1, device_id=place, device_id_type=MESH)

            count = count + present.astype(jnp.int32)
    pl.semaphore_wait(barrier, count)


def neighbours():
    col = lax.axis_index("col")
    core = col + 1 - 2 * lax.rem(col, 2)
    across = lax.rem(col + 2, 4)
    return col, core, across


def square():
    dp = lax.axis_index("dp")
    x = lax.axis_index("col") // 2
    return dp, (dp * 2 + x, dp * 2 + 1 - x, (1 - dp) * 2 + x, (1 - dp) * 2 + 1 - x)


def comm_params(ident):
    return params(collective_id=ident, has_side_effects=True)


class AttendCopies:
    def __init__(self, w_ref, cot_ref, rows_ref, near_ref, mixes_ref, send_sem, recv_sem):
        row = lax.axis_index("row")
        col, core, across = neighbours()
        dp, (me, on_x, on_y, _) = square()
        mover = Mover(send_sem, recv_sem)
        self.left = row >= 1
        self.right = row <= 2
        self.both = jnp.logical_and(self.left, self.right)
        self.from_left = row >= 2
        self.from_right = row <= 1
        self.partners = [
            (self.right, {"row": row + 1}),
            (self.left, {"row": row - 1}),
            (None, {"col": across}),
            (None, {"col": core}),
            (None, {"dp": 1 - dp}),
        ]
        self.to_right = mover.copy(w_ref, rows_ref.at[row], row=row + 1)
        self.to_left = mover.copy(w_ref, rows_ref.at[row], row=row - 1)
        self.pass_right = mover.copy(rows_ref.at[row - 1], rows_ref.at[row - 1], row=row + 1)
        self.pass_left = mover.copy(rows_ref.at[row + 1], rows_ref.at[row + 1], row=row - 1)
        half = cot_ref.shape[0] // 2
        top, low = pl.ds(0, half), pl.ds(half, half)
        self.cots = [
            mover.copy(cot_ref.at[low], near_ref.at[me, low], col=across),
            mover.copy(cot_ref.at[top], near_ref.at[me, top], dp=1 - dp),
            mover.copy(cot_ref.at[top], near_ref.at[me, top], col=across),
            mover.copy(cot_ref.at[low], near_ref.at[me, low], dp=1 - dp),
        ]
        self.relays = [
            mover.copy(near_ref.at[on_x, low], near_ref.at[on_x, low], dp=1 - dp),
            mover.copy(near_ref.at[on_y, top], near_ref.at[on_y, top], col=across),
        ]
        self.mixes = []
        for r in range(4):
            for c in (col, across):
                self.mixes.append(mover.copy(mixes_ref.at[r, c], mixes_ref.at[r, c], col=core))

    def first(self):
        greet(self.partners)
        pl.when(self.right)(self.to_right.start)
        pl.when(self.left)(self.to_left.start)
        for c in self.cots + self.mixes:
            c.start()

    def second(self):
        for c in self.cots[:2]:
            c.wait_recv()
        for c in self.relays:
            c.start()
        pl.when(self.left)(self.to_right.wait_recv)
        pl.when(self.right)(self.to_left.wait_recv)
        pl.when(self.both)(self.pass_right.start)
        pl.when(self.both)(self.pass_left.start)

    def last(self):
        pl.when(self.right)(self.to_right.wait_send)
        pl.when(self.left)(self.to_left.wait_send)
        pl.when(self.both)(self.pass_right.wait_send)
        pl.when(self.both)(self.pass_left.wait_send)
        pl.when(self.from_left)(self.pass_right.wait_recv)
        pl.when(self.from_right)(self.pass_left.wait_recv)
        for c in self.cots[:2]:
            c.wait_send()
        for c in self.cots[2:] + self.relays + self.mixes:
            c.wait()


class BackCopies:
    def __init__(self, refs, sems):
        (
            self.pair_ref, self.mixed_ref, self.rows_ref, self.hop_ref, self.g_out_ref,
            self.out_ref, self.ends_ref, self.part_ref,
            self.relay_ref, self.diag_ref, self.far_ref, self.send_ref,
            self.right_ref, self.left_ref, self.got_ref,
            self.near_ref, self.side_ref, self.across_ref,
        ) = refs
        send_sem, recv_sem, local_sem = sems
        self.row = row = lax.axis_index("row")
        self.col, core, across = col, _, _ = neighbours()
        cross = lax.rem(core + 2, 4)
        self.dp, self.spots = dp, (me, on_x, on_y, on_both) = square()
        mover = Mover(send_sem, recv_sem)
        self.x, self.mine = x, mine = col // 2, lax.rem(col, 2)
        self.partners = [(None, {"col": c}) for c in (core, across, cross)]
        self.partners += [(None, {"dp": 1 - dp}), (row <= 2, {"row": row + 1}), (row >= 1, {"row": row - 1})]
        half = self.pair_ref.shape[1] // 2
        self.top, self.low = top, low = pl.ds(0, half), pl.ds(half, half)
        y = 1 - dp
        self.diag = [
            mover.copy(self.pair_ref.at[on_both, top], self.diag_ref.at[0], col=across),
            mover.copy(self.pair_ref.at[on_both, low], self.diag_ref.at[1], dp=y),
        ]
        self.far = [
            mover.copy(self.pair_ref.at[on_x, top], self.far_ref.at[0, top], col=across),
            mover.copy(self.pair_ref.at[on_y, low], self.far_ref.at[1, low], dp=y),
            mover.copy(self.relay_ref.at[0], self.far_ref.at[1, top], dp=y),
            mover.copy(self.relay_ref.at[1], self.far_ref.at[0, low], col=across),
        ]
        self.out = [mover.copy(self.send_ref.at[c], self.out_ref.at[col], col=c) for c in (across, cross, core)]
        self.own = pltpu.make_async_copy(self.send_ref.at[col], self.out_ref.at[col], local_sem)
        self.hop_right = [
            mover.copy(self.right_ref.at[k], target, row=row + 1)
            for k, target in ((0, self.got_ref.at[0]), (1, self.ends_ref.at[0]))
        ]
        self.hop_left = [
            mover.copy(self.left_ref.at[k], target, row=row - 1)
            for k, target in ((0, self.got_ref.at[1]), (1, self.ends_ref.at[1]))
        ]
        self.cores = [
            mover.copy(self.g_out_ref.at[r, k * 2 + 1 - mine], self.near_ref.at[k, r], col=core)
            for k in range(2)
            for r in range(4)
        ]
        self.sides = [mover.copy(self.side_ref.at[r], self.across_ref.at[r], col=across) for r in range(4)]

    def first(self):
        row = self.row
        greet(self.partners)
        for c in self.diag + self.far[:2] + self.cores:
            c.start()
        hop = self.hop_ref[...].astype(F32)
        ahead = self.rows_ref[jnp.minimum(row + 2, 3)].astype(F32)
        self.right_ref[0] = jnp.where(row == 1, ahead + hop, ahead).astype(BF)
        behind = self.rows_ref[jnp.maximum(row - 2, 0)].astype(F32)
        self.left_ref[0] = jnp.where(row == 2, behind + hop, behind).astype(BF)
        pl.when(row <= 1)(self.hop_right[0].start)
        pl.when(row >= 2)(self.hop_left[0].start)

    def second(self):
        row = self.row
        me, on_x, on_y, on_both = self.spots
        middle = jnp.logical_and(row >= 1, row <= 2)
        for k, (spot, rows) in enumerate(((on_y, self.top), (on_x, self.low))):
            self.diag[k].wait_recv()
            self.relay_ref[k] = (self.pair_ref[spot, rows].astype(F32) + self.diag_ref[k].astype(F32)).astype(BF)
            self.far[2 + k].start()
        pl.when(middle)(self.hop_right[0].wait_recv)
        pl.when(middle)(self.hop_left[0].wait_recv)
        ahead = self.rows_ref[jnp.minimum(row + 1, 3)].astype(F32)
        behind = self.rows_ref[jnp.maximum(row - 1, 0)].astype(F32)
        self.right_ref[1] = jnp.where(row >= 1, ahead + self.got_ref[0].astype(F32), ahead).astype(BF)
        self.left_ref[1] = jnp.where(row <= 2, behind + self.got_ref[1].astype(F32), behind).astype(BF)
        pl.when(row <= 2)(self.hop_right[1].start)
        pl.when(row >= 1)(self.hop_left[1].start)
        for c in self.cores:
            c.wait_recv()
        for r in range(4):
            self.side_ref[r] = (
                self.g_out_ref[r, (1 - self.x) * 2 + self.mine].astype(F32)
                + self.near_ref[1 - self.x, r].astype(F32)
            ).astype(BF)
            self.sides[r].start()

    def third(self):
        for c in self.far:
            c.wait_recv()
        feat = self.send_ref.shape[2]
        for c in range(4):
            lanes = slice(c * feat, (c + 1) * feat)
            self.send_ref[c] = (
                self.mixed_ref[:, lanes]
                + self.pair_ref[self.spots[0], :, lanes].astype(F32)
                + self.far_ref[0, :, lanes].astype(F32)
                + self.far_ref[1, :, lanes].astype(F32)
            ).astype(BF)
        for c in self.out:
            c.start()
        self.own.start()

    def last(self):
        row = self.row
        for r in range(4):
            self.sides[r].wait_recv()
            self.part_ref[r] = (
                self.g_out_ref[r, self.x * 2 + self.mine].astype(F32)
                + self.near_ref[self.x, r].astype(F32)
                + self.across_ref[r].astype(F32)
            ).astype(BF)
        for c in self.out:
            c.wait()
        self.own.wait()
        for c in self.diag + self.far + self.cores + self.sides:
            c.wait_send()
        pl.when(row >= 1)(self.hop_right[1].wait_recv)
        pl.when(row <= 2)(self.hop_left[1].wait_recv)
        pl.when(row <= 1)(self.hop_right[0].wait_send)
        pl.when(row >= 2)(self.hop_left[0].wait_send)
        pl.when(row <= 2)(self.hop_right[1].wait_send)
        pl.when(row >= 1)(self.hop_left[1].wait_send)


def row_partners(row, n_row, core):
    return [
        (None, {"col": core}),
        (row + 1 < n_row, {"row": row + 1}),
        (row + 2 < n_row, {"row": row + 2}),
        (row >= 1, {"row": row - 1}),
        (row >= 2, {"row": row - 2}),
    ]


def window_back_body(n_row, win_ref, sum_ref, near_ref, send_ref, far_ref, send_sem, recv_sem):
    row = lax.axis_index("row")
    col, core, _ = neighbours()
    side = lax.rem(col, 2)
    greet(row_partners(row, n_row, core))
    mover = Mover(send_sem, recv_sem)
    first = mover.copy(win_ref.at[1], near_ref.at[0], col=core)
    second = mover.copy(win_ref.at[3], near_ref.at[1], col=core)
    first.start()
    second.start()
    one = mover.copy(send_ref.at[0], far_ref.at[0], row=row - 1)
    two = mover.copy(send_ref.at[1], far_ref.at[1], row=row - 2)
    first.wait_recv()
    second.wait_recv()
    zero = jnp.zeros(near_ref.shape[1:], F32)
    low = near_ref[0].astype(F32)
    high = near_ref[1].astype(F32)
    left = side == 0
    send_ref[0] = (win_ref[2].astype(F32) + jnp.where(left, low, high)).astype(BF)
    send_ref[1] = (win_ref[0].astype(F32) + jnp.where(left, zero, low)).astype(BF)

    @pl.when(row >= 1)
    def _():
        one.start()

    @pl.when(row >= 2)
    def _():
        two.start()

    sum_ref[...] = win_ref[4].astype(F32) + jnp.where(left, high, zero)

    @pl.when(row + 1 < n_row)
    def _():
        one.wait_recv()
        sum_ref[...] += far_ref[0].astype(F32)

    @pl.when(row + 2 < n_row)
    def _():
        two.wait_recv()
        sum_ref[...] += far_ref[1].astype(F32)

    first.wait_send()
    second.wait_send()

    @pl.when(row >= 1)
    def _():
        one.wait_send()

    @pl.when(row >= 2)
    def _():
        two.wait_send()


def window_back(win, n_row):
    shape = win.shape[1:]
    return pl.pallas_call(
        functools.partial(window_back_body, n_row),
        out_shape=jax.ShapeDtypeStruct(shape, F32),
        in_specs=[VMEM],
        out_specs=VMEM,
        scratch_shapes=[
            pltpu.VMEM((2,) + shape, BF),
            pltpu.VMEM((2,) + shape, BF),
            pltpu.VMEM((2,) + shape, BF),
            pltpu.SemaphoreType.DMA((4,)),
            pltpu.SemaphoreType.DMA((4,)),
        ],
        compiler_params=comm_params(7),
        cost_estimate=cost_of(0, 1 << 20),
    )(win)


def first_norm(x_ref, gain_ref, h_ref):
    parts = x_ref.shape[0]
    feat = x_ref.shape[2]
    xs = [x_ref[c].astype(F32) for c in range(parts)]
    total = sum(jnp.sum(v * v, axis=1, keepdims=True) for v in xs)
    scale = lax.rsqrt(total / D + EPS)
    for c in range(parts):
        lanes = slice(c * feat, (c + 1) * feat)
        h_ref[:, lanes] = (xs[c] * scale * gain_ref[c, :1]).astype(BF)


def place_factor_weights(blocks_ref, w_ref):
    n_row, parts, _, feat = blocks_ref.shape
    ranks_each = RANK_COLS // n_row
    for c in range(parts):
        lanes = slice(c * feat, (c + 1) * feat)
        for r in range(n_row):
            w_ref[r * ranks_each : (r + 1) * ranks_each, lanes] = blocks_ref[r, c, :ranks_each]
            w_ref[RANK_COLS + r * GROUP_COLS : RANK_COLS + (r + 1) * GROUP_COLS, lanes] = blocks_ref[
                r, c, ranks_each:
            ]


def make_factors(h_ref, w_ref, turn_ref, hf_ref, bq_ref, kf_ref):
    both = nt(h_ref[...], w_ref[...])
    heads = both[:, RANK_COLS:]
    hf_ref[...] = heads
    cosine = turn_ref[:, :LANES]
    sine = turn_ref[:, LANES:]
    for tile in range(RANK_COLS // LANES):
        lanes = slice(tile * LANES, (tile + 1) * LANES)
        part = both[:, lanes]
        if tile < 4:
            part = part * cosine + swap_halves(part) * sine
        if tile < 3:
            bq_ref[:, lanes] = part
        else:
            kf_ref[:, (tile - 3) * LANES : (tile - 2) * LANES] = part.astype(BF)
    kf_ref[:, 2 * LANES :] = nn(heads.astype(BF), key_columns()).astype(BF)


def make_queries(hf_ref, bq_ref, q_ref):
    heads = hf_ref[...]
    high = heads.astype(BF)
    low = (heads - high.astype(F32)).astype(BF)
    ranks = []
    for r in range(RQ):
        tile = bq_ref[:, (r // 2) * LANES : (r // 2 + 1) * LANES]
        ranks.append(double_left(tile) if r % 2 == 0 else double_right(tile))
    width = 2 * LANES
    for p in range(D // width):
        lanes = slice(p * width, (p + 1) * width)
        acc = None
        for r in range(RQ):
            pick = head_spread(2 * RK + r, p * (width // HD), width)
            term = (nn(high, pick) + nn(low, pick)) * jnp.concatenate([ranks[r]] * 2, axis=1)
            acc = term if acc is None else acc + term
        q_ref[:, lanes] = (acc / RQ).astype(BF)


def front_body(x_ref, gain_ref, blocks_ref, turn_ref, h_ref, hf_ref, bq_ref, kf_ref, q_ref, w_ref):
    first_norm(x_ref, gain_ref, h_ref)
    place_factor_weights(blocks_ref, w_ref)
    make_factors(h_ref, w_ref, turn_ref, hf_ref, bq_ref, kf_ref)
    make_queries(hf_ref, bq_ref, q_ref)


def head_body(
    tok_ref, w_own_ref, gain_ref, ffn_ref, mix_ref, turn_ref,
    x_ref, gains_ref, parts_ref, mixes_ref, h_ref, hf_ref, bq_ref, q_ref, w_ref, win_ref,
    blocks_ref, send_sem, recv_sem,
):
    row = lax.axis_index("row")
    col, core, across = neighbours()
    cross = lax.rem(core + 2, 4)
    side = lax.rem(col, 2)
    rows = [lax.rem(row + k, 4) for k in range(4)]
    back = [lax.rem(row + 4 - k, 4) for k in range(4)]
    greet([(None, {"col": c}) for c in (core, across, cross)] + [(None, {"row": r}) for r in rows[1:]])
    mover = Mover(send_sem, recv_sem)
    started = []

    def go(source, target, **place):
        c = mover.copy(source, target, **place)
        c.start()
        started.append(c)
        return c

    down = [None] + [go(w_own_ref, blocks_ref.at[row, col], row=rows[k]) for k in range(1, 4)]
    sides = [go(w_own_ref, blocks_ref.at[row, col], col=across)]
    cores = [go(w_own_ref, blocks_ref.at[row, col], col=core)]
    toks = []
    rest = []
    for c in (across, cross, core):
        toks.append(go(gain_ref, gains_ref.at[col], col=c))
        toks.append(go(tok_ref.at[c], x_ref.at[col], col=c))
    for c in (across, cross, core):
        rest.append(go(ffn_ref.at[c], parts_ref.at[col], col=c))
    mix_down = [None] + [go(mix_ref, mixes_ref.at[row, col], row=rows[k]) for k in range(1, 4)]
    blocks_ref[row, col] = w_own_ref[...]
    gains_ref[col] = gain_ref[...]
    x_ref[col] = tok_ref[col]
    parts_ref[col] = ffn_ref[col]
    mixes_ref[row, col] = mix_ref[...]
    zero = jnp.zeros(win_ref.shape[1:], BF)
    has_one = row >= 1
    has_two = row >= 2
    for absent, slot in (
        (jnp.logical_not(has_two), 0),
        (jnp.logical_and(jnp.logical_not(has_two), side == 0), 1),
        (jnp.logical_and(jnp.logical_not(has_one), side == 1), 1),
        (jnp.logical_not(has_one), 2),
        (jnp.logical_and(jnp.logical_not(has_one), side == 0), 3),
    ):

        @pl.when(absent)
        def _():
            win_ref[slot] = zero

    for k in range(1, 4):
        down[k].wait_recv()
        block = blocks_ref.at[back[k], col]
        sides.append(go(block, block, col=across))
        cores.append(go(block, block, col=core))
    for c in toks:
        c.wait_recv()
    first_norm(x_ref, gains_ref, h_ref)
    passed = []
    for k in range(4):
        sides[k].wait_recv()
        block = blocks_ref.at[back[k], across]
        passed.append(go(block, block, col=core))
    for c in cores + passed:
        c.wait_recv()
    for k in range(4):
        if k > 0:
            mix_down[k].wait_recv()
        block = mixes_ref.at[back[k], col]
        rest.append(go(block, block, col=across))
    place_factor_weights(blocks_ref, w_ref)
    make_factors(h_ref, w_ref, turn_ref, hf_ref, bq_ref, win_ref.at[4])

    own = win_ref.at[4]
    one = mover.copy(own, win_ref.at[2], row=row + 1)
    two = mover.copy(own, win_ref.at[0], row=row + 2)
    near = mover.copy(own, win_ref.at[3], col=core)
    pass_one = mover.copy(win_ref.at[2], win_ref.at[1 + 2 * side], col=core)
    pass_two = mover.copy(win_ref.at[0], win_ref.at[1], col=core)
    sends_two = jnp.logical_and(has_two, side == 1)
    takes_two = jnp.logical_and(has_two, side == 0)
    pl.when(row <= 2)(one.start)
    pl.when(row <= 1)(two.start)
    pl.when(side == 0)(near.start)
    make_queries(hf_ref, bq_ref, q_ref)

    @pl.when(has_one)
    def _():
        one.wait_recv()
        pass_one.start()

    @pl.when(has_two)
    def _():
        two.wait_recv()

    pl.when(sends_two)(pass_two.start)

    @pl.when(has_one)
    def _():
        pass_one.wait_recv()
        pass_one.wait_send()

    pl.when(takes_two)(pass_two.wait_recv)
    pl.when(sends_two)(pass_two.wait_send)
    pl.when(side == 1)(near.wait_recv)
    pl.when(side == 0)(near.wait_send)
    pl.when(row <= 2)(one.wait_send)
    pl.when(row <= 1)(two.wait_send)
    for c in rest:
        c.wait_recv()
    for c in started:
        c.wait_send()


def head(tok, w_own, gains, ffn_own, w_out, turn):
    rows, feat = tok.shape[1:]
    count = 3 + 4 + 4 + 6 + 3 + 3 + 4 + 4 + 5
    return pl.pallas_call(
        head_body,
        out_shape=(
            jax.ShapeDtypeStruct(tok.shape, BF),
            jax.ShapeDtypeStruct((4,) + gains.shape, F32),
            jax.ShapeDtypeStruct(ffn_own.shape, BF),
            jax.ShapeDtypeStruct((4, 4) + w_out.shape, BF),
            jax.ShapeDtypeStruct((rows, D), BF),
            jax.ShapeDtypeStruct((rows, HEAD_COLS), F32),
            jax.ShapeDtypeStruct((rows, RQ * HD), F32),
            jax.ShapeDtypeStruct((rows, D), BF),
            jax.ShapeDtypeStruct((ALL_COLS, D), BF),
            jax.ShapeDtypeStruct((5, rows, 3 * LANES), BF),
        ),
        in_specs=[VMEM] * 6,
        out_specs=(VMEM,) * 10,
        scratch_shapes=[
            pltpu.VMEM((4, 4) + w_own.shape, BF),
            pltpu.SemaphoreType.DMA((count,)),
            pltpu.SemaphoreType.DMA((count,)),
        ],
        compiler_params=comm_params(1),
        cost_estimate=cost_of(2 * rows * D * 800 * 3, 14 << 20),
    )(tok, w_own, gains, ffn_own, w_out, turn)


def front(x_parts, gains, blocks, turn):
    rows = x_parts.shape[1]
    return call(
        front_body,
        (
            jax.ShapeDtypeStruct((rows, D), BF),
            jax.ShapeDtypeStruct((rows, HEAD_COLS), F32),
            jax.ShapeDtypeStruct((rows, RQ * HD), F32),
            jax.ShapeDtypeStruct((rows, 3 * LANES), BF),
            jax.ShapeDtypeStruct((rows, D), BF),
            jax.ShapeDtypeStruct((ALL_COLS, D), BF),
        ),
        cost=cost_of(2 * rows * D * 800 * 3, 6 << 20),
    )(x_parts, gains, blocks, turn)


def mask_bias(seg_ref, keys, rows):
    seg_row = seg_ref[...].astype(F32)
    wide = jnp.broadcast_to(seg_row, (LANES, keys))
    column = wide.T
    column = jnp.concatenate([column] * (rows // LANES), axis=1)
    key_idx = lax.broadcasted_iota(jnp.int32, (keys, rows), 0)
    query_idx = lax.broadcasted_iota(jnp.int32, (keys, rows), 1) + (keys - rows)
    same = column == seg_row[:, keys - rows :]
    return jnp.where(same & (key_idx <= query_idx), 0.0, NEG)


def attend_body(fast, q_ref, kf_ref, seg_ref, *refs):
    if fast:
        w_ref, cot_ref, _, o_ref, lse_ref, k_ref, v_ref, w_rows_ref, cot_near_ref, mixes_ref = refs[:10]
        bias_ref, dup_ref, send_sem, recv_sem = refs[10:]
        side_work = AttendCopies(w_ref, cot_ref, w_rows_ref, cot_near_ref, mixes_ref, send_sem, recv_sem)
        side_work.first()
    else:
        o_ref, lse_ref, k_ref, v_ref, bias_ref, dup_ref = refs
    rows = q_ref.shape[0]
    keys = kf_ref.shape[0]
    bias_ref[...] = mask_bias(seg_ref, keys, rows)
    for s in range(2 * RK):
        tile = kf_ref[:, (s // 2) * LANES : (s // 2 + 1) * LANES].astype(F32)
        dup_ref[s] = double_left(tile) if s % 2 == 0 else double_right(tile)

    def pair(p, carried):
        lanes = pl.ds(pl.multiple_of(p * LANES, LANES), LANES)
        weights = kf_ref[:, 2 * LANES :]
        made = []
        for kind in range(2):
            acc = None
            for s in range(RK):
                pick = spread(LANES, (kind * RK + s) * H + 2 * p, LANES)
                term = nn(weights, pick) * dup_ref[kind * RK + s]
                acc = term if acc is None else acc + term
            made.append((acc / RK).astype(BF))
        k_tile, v_tile = made
        k_ref[:, lanes] = k_tile
        v_ref[:, lanes] = v_tile
        v_turned = v_tile.astype(F32).T.astype(BF)
        q_turned = (q_ref[:, lanes].astype(F32) * HD**-0.5).T
        half = lax.broadcasted_iota(jnp.int32, q_turned.shape, 0) // HD
        outs = []
        for side in range(2):
            q_side = jnp.where(half == side, q_turned, 0.0).astype(BF)
            scores = nn(k_tile, q_side) + bias_ref[...]
            peak = jnp.max(scores, axis=0, keepdims=True)
            weight = jnp.exp(scores - peak)
            total = jnp.sum(weight, axis=0, keepdims=True)
            probs = (weight * (1.0 / total)).astype(BF)
            outs.append(nn(v_turned[side * HD : (side + 1) * HD], probs))
            lse_ref[2 * p + side] = jnp.broadcast_to(peak + jnp.log(total), (8, rows))
        o_ref[:, lanes] = jnp.concatenate(outs, axis=0).T.astype(BF)
        return carried

    if fast:
        lax.fori_loop(0, 5, pair, 0)
        side_work.second()
        lax.fori_loop(5, PAIRS, pair, 0)
        side_work.last()
    else:
        lax.fori_loop(0, PAIRS, pair, 0)


def attend(q, kf_window, seg_window, w_own=None, cot=None, mixes=None):
    rows = q.shape[0]
    keys = kf_window.shape[0]
    fast = w_own is not None
    outs = [
        jax.ShapeDtypeStruct((rows, D), BF),
        jax.ShapeDtypeStruct((H, 8, rows), F32),
        jax.ShapeDtypeStruct((keys, D), BF),
        jax.ShapeDtypeStruct((keys, D), BF),
    ]
    scratch = [pltpu.VMEM((keys, rows), F32), pltpu.VMEM((2 * RK, keys, LANES), F32)]
    in_specs, out_specs, more = [VMEM] * 3, [VMEM] * 4, []
    if fast:
        outs += [
            jax.ShapeDtypeStruct((4,) + w_own.shape, BF),
            jax.ShapeDtypeStruct((4,) + cot.shape, BF),
            jax.ShapeDtypeStruct(mixes.shape, BF),
        ]
        in_specs += [ANY] * 3
        out_specs += [ANY] * 3
        more = [w_own, cot, mixes]
        scratch += [
            pltpu.SemaphoreType.DMA((18,)),
            pltpu.SemaphoreType.DMA((18,)),
        ]
    return pl.pallas_call(
        functools.partial(attend_body, fast),
        out_shape=tuple(outs),
        in_specs=in_specs,
        out_specs=tuple(out_specs),
        scratch_shapes=scratch,
        input_output_aliases={5: 6} if fast else {},
        compiler_params=comm_params(3) if fast else params(),
        cost_estimate=cost_of(2 * rows * keys * D * 16, 16 << 20),
    )(q, kf_window, seg_window, *more)


def attend_back_body(fast, q_ref, k_ref, v_ref, do_ref, lse_ref, kf_ref, seg_ref, *refs):
    if fast:
        dq_ref, dkf_ref = refs[5:7]
        bias_ref, dup_ref, sum_ref, fac_ref = refs[10:14]
        side_work = BackCopies(refs[:5] + refs[7:10] + refs[14:24], refs[24:])
        side_work.first()
    else:
        dq_ref, dkf_ref, bias_ref, dup_ref, sum_ref, fac_ref = refs
    rows = q_ref.shape[0]
    keys = kf_ref.shape[0]
    bias_ref[...] = mask_bias(seg_ref, keys, rows)
    for s in range(2 * RK):
        tile = kf_ref[:, (s // 2) * LANES : (s // 2 + 1) * LANES].astype(F32)
        dup_ref[s] = double_left(tile) if s % 2 == 0 else double_right(tile)
    sum_ref[...] = jnp.zeros_like(sum_ref)
    fac_ref[...] = jnp.zeros_like(fac_ref)

    def pair(p, carried):
        lanes = pl.ds(pl.multiple_of(p * LANES, LANES), LANES)
        k_tile = k_ref[:, lanes]
        v_tile = v_ref[:, lanes]
        k_turned = k_tile.astype(F32).T.astype(BF)
        q_tile = q_ref[:, lanes].astype(F32) * HD**-0.5
        do_tile = do_ref[:, lanes].astype(F32)
        q_turned = q_tile.T
        do_turned = do_tile.T
        half = lax.broadcasted_iota(jnp.int32, q_turned.shape, 0) // HD
        lane_half = lax.broadcasted_iota(jnp.int32, q_tile.shape, 1) // HD
        d_k = None
        d_v = None
        d_q = []
        for side in range(2):
            q_side = jnp.where(half == side, q_turned, 0.0).astype(BF)
            do_side = jnp.where(half == side, do_turned, 0.0).astype(BF)
            scores = nn(k_tile, q_side) + bias_ref[...]
            probs = jnp.exp(scores - lse_ref[2 * p + side][:1])
            d_prob = nn(v_tile, do_side)
            delta = jnp.sum(probs * d_prob, axis=0, keepdims=True)
            d_score = (probs * (d_prob - delta)).astype(BF)
            d_q.append(nn(k_turned[side * HD : (side + 1) * HD], d_score))
            q_back = jnp.where(lane_half == side, q_tile, 0.0).astype(BF)
            do_back = jnp.where(lane_half == side, do_tile, 0.0).astype(BF)
            part_k = nn(d_score, q_back)
            part_v = nn(probs.astype(BF), do_back)
            d_k = part_k if d_k is None else d_k + part_k
            d_v = part_v if d_v is None else d_v + part_v
        dq_ref[:, lanes] = jnp.concatenate(d_q, axis=0).T * HD**-0.5
        weights = kf_ref[:, 2 * LANES :]
        for kind, grad in ((0, d_k), (1, d_v)):
            for s in range(RK):
                slot = kind * RK + s
                pick = spread(LANES, slot * H + 2 * p, LANES)
                sum_ref[slot] += nn(weights, pick) * grad
                fac_ref[...] += two_pass(grad * dup_ref[slot], collect(LANES, LANES, slot * H + 2 * p))
        return carried

    if fast:
        lax.fori_loop(0, 4, pair, 0)
        side_work.second()
        lax.fori_loop(4, 6, pair, 0)
        side_work.third()
        lax.fori_loop(6, PAIRS, pair, 0)
    else:
        lax.fori_loop(0, PAIRS, pair, 0)
    for tile in range(2):
        first = sum_ref[2 * tile]
        second = sum_ref[2 * tile + 1]
        first = first + pltpu.roll(first, HD, 1)
        second = second + pltpu.roll(second, HD, 1)
        merged = jnp.where(lane_iota(first.shape) < HD, first, second)
        dkf_ref[:, tile * LANES : (tile + 1) * LANES] = (merged / RK).astype(BF)
    dkf_ref[:, 2 * LANES :] = (fac_ref[...] / RK).astype(BF)
    if fast:
        side_work.last()


def attend_back(q, k, v, d_heads, lse, kf_window, seg_window, *more):
    rows = q.shape[0]
    keys = kf_window.shape[0]
    fast = len(more) > 0
    outs = [jax.ShapeDtypeStruct((rows, D), F32), jax.ShapeDtypeStruct(kf_window.shape, BF)]
    scratch = [
        pltpu.VMEM((keys, rows), F32),
        pltpu.VMEM((2 * RK, keys, LANES), F32),
        pltpu.VMEM((2 * RK, keys, LANES), F32),
        pltpu.VMEM((keys, LANES), F32),
    ]
    in_specs, out_specs = [VMEM] * (7 + len(more)), [VMEM] * 2
    if fast:
        grads, g_out = more[2], more[4]
        parts, feat = g_out.shape[1], g_out.shape[3]
        block, hop = g_out.shape[2:], grads.shape[1:]
        outs += [
            jax.ShapeDtypeStruct((parts, rows, feat), BF),
            jax.ShapeDtypeStruct((2,) + hop, BF),
            jax.ShapeDtypeStruct((4,) + block, BF),
        ]
        out_specs += [ANY, ANY, VMEM]
        scratch += [
            pltpu.VMEM((2, rows // 2, D), BF),
            pltpu.VMEM((2, rows // 2, D), BF),
            pltpu.VMEM((2, rows, D), BF),
            pltpu.VMEM((parts, rows, feat), BF),
            pltpu.VMEM((2,) + hop, BF),
            pltpu.VMEM((2,) + hop, BF),
            pltpu.VMEM((2,) + hop, BF),
            pltpu.VMEM((2, 4) + block, BF),
            pltpu.VMEM((4,) + block, BF),
            pltpu.VMEM((4,) + block, BF),
            pltpu.SemaphoreType.DMA((25,)),
            pltpu.SemaphoreType.DMA((25,)),
            pltpu.SemaphoreType.DMA,
        ]
    return pl.pallas_call(
        functools.partial(attend_back_body, fast),
        out_shape=tuple(outs),
        in_specs=in_specs,
        out_specs=tuple(out_specs),
        scratch_shapes=scratch,
        compiler_params=comm_params(6) if fast else params(),
        cost_estimate=cost_of(2 * rows * keys * D * 40, 16 << 20),
    )(q, k, v, d_heads, lse, kf_window, seg_window, *more)


def mixing_body(x_ref, heads_ref, w_out_ref, gain_ref, mixed_ref, h_ref):
    parts, _, feat = x_ref.shape
    rows_of = w_out_ref.shape[0]
    head_rows = w_out_ref.shape[2]
    total = None
    for c in range(parts):
        lanes = slice(c * feat, (c + 1) * feat)
        acc = x_ref[c].astype(F32)
        for r in range(rows_of):
            acc = acc + nn(heads_ref[:, r * head_rows : (r + 1) * head_rows], w_out_ref[r, c])
        mixed_ref[:, lanes] = acc
        part = jnp.sum(acc * acc, axis=1, keepdims=True)
        total = part if total is None else total + part
    scale = lax.rsqrt(total / D + EPS)
    for c in range(parts):
        lanes = slice(c * feat, (c + 1) * feat)
        h_ref[:, lanes] = (mixed_ref[:, lanes] * scale * gain_ref[c, 1:2]).astype(BF)


def mixing(x_parts, heads, w_out, gains):
    rows = heads.shape[0]
    return call(
        mixing_body,
        (jax.ShapeDtypeStruct((rows, D), F32), jax.ShapeDtypeStruct((rows, D), BF)),
        cost=cost_of(2 * rows * D * D, 5 << 20),
    )(x_parts, heads, w_out, gains)


def ffn_steps(blocks, h_at, cot_at, w_ref, hid_ref, dg_ref, du_ref, out_at, back_at):
    def block(t, carried):
        h = h_at(t)[...]
        gate = nt(h, w_ref[0])
        up = nt(h, w_ref[1])
        d_hidden = nt(cot_at(t)[...], w_ref[2])
        sig = 1.0 / (1.0 + jnp.exp(-gate))
        silu = gate * sig
        hidden = (silu * up).astype(BF)
        d_gate = (d_hidden * up * sig * (1.0 + gate * (1.0 - sig))).astype(BF)
        d_up = (d_hidden * silu).astype(BF)
        rows = h.shape[0]
        place = pl.ds(pl.multiple_of(t * rows, rows), rows)
        hid_ref[place] = hidden
        dg_ref[place] = d_gate
        du_ref[place] = d_up
        out_at(t)[...] = nn(hidden, w_ref[2]).astype(BF)
        back_at(t)[...] = (nn(d_gate, w_ref[0]) + nn(d_up, w_ref[1])).astype(BF)
        return carried

    lax.fori_loop(0, blocks, block, 0)


def ffn_body(h_ref, cot_ref, w_ref, out_ref, back_ref, g_ref, hid_ref, dg_ref, du_ref):
    parts, rows, _ = h_ref.shape
    ffn_steps(
        parts, lambda t: h_ref.at[t], lambda t: cot_ref.at[t], w_ref, hid_ref, dg_ref, du_ref,
        lambda t: out_ref.at[t], lambda t: back_ref.at[t],
    )
    h_all = h_ref[...].reshape(parts * rows, D)
    cot_all = cot_ref[...].reshape(parts * rows, D)
    for place, (left, right) in enumerate(((dg_ref, h_all), (du_ref, h_all), (hid_ref, cot_all))):
        g_ref[place] = tn(left[...], right).astype(BF)


def ffn(h_all, cot_all, w):
    parts, rows, _ = h_all.shape
    units = w.shape[1]
    return call(
        ffn_body,
        (
            jax.ShapeDtypeStruct(h_all.shape, BF),
            jax.ShapeDtypeStruct(h_all.shape, BF),
            jax.ShapeDtypeStruct(w.shape, BF),
        ),
        scratch=[pltpu.VMEM((parts * rows, units), BF)] * 3,
        cost=cost_of(2 * parts * rows * 9 * D * units, 20 << 20),
    )(h_all, cot_all, w)


def unmix_math(
    mixed_ref, cot_ref, d_h, heads_ref, w_out_ref, gain_ref, d_mixed_ref, d_heads_ref, g_out_ref, g_gain_ref
):
    rows_of, parts, head_rows, feat = w_out_ref.shape
    mixed = mixed_ref[...]
    scale = lax.rsqrt(jnp.sum(mixed * mixed, axis=1, keepdims=True) / D + EPS)
    normed = mixed * scale
    g_gain_ref[...] = jnp.sum(d_h * normed, axis=0, keepdims=True)
    gain = jnp.concatenate([gain_ref[c, 1:2] for c in range(parts)], axis=1)
    inner = d_h * gain
    dot = jnp.sum(inner * normed, axis=1, keepdims=True) / D
    d_mixed = cot_ref[...].astype(F32) + scale * (inner - normed * dot)
    d_mixed_ref[...] = d_mixed
    low = d_mixed.astype(BF)
    grad = tn(heads_ref[...], low)
    for r in range(rows_of):
        acc = None
        for c in range(parts):
            lanes = slice(c * feat, (c + 1) * feat)
            term = nt(low[:, lanes], w_out_ref[r, c])
            acc = term if acc is None else acc + term
            g_out_ref[r, c] = grad[r * head_rows : (r + 1) * head_rows, lanes].astype(BF)
        d_heads_ref[:, r * head_rows : (r + 1) * head_rows] = acc.astype(BF)


def write_output(mixed_ref, total, out_ref):
    parts, _, feat = out_ref.shape
    for c in range(parts):
        lanes = slice(c * feat, (c + 1) * feat)
        out_ref[c] = (mixed_ref[:, lanes] + total[:, lanes]).astype(BF)


def unmix_body(
    dh_ref, sum_ref, mixed_ref, cot_ref, heads_ref, w_out_ref, gain_ref,
    out_ref, d_mixed_ref, d_heads_ref, g_out_ref, g_gain_ref,
):
    unmix_math(
        mixed_ref, cot_ref, dh_ref[...], heads_ref, w_out_ref, gain_ref,
        d_mixed_ref, d_heads_ref, g_out_ref, g_gain_ref,
    )
    write_output(mixed_ref, sum_ref[...], out_ref)


def middle_body(
    x_ref, heads_ref, w_out_ref, gain_ref, cot_own_ref, cot_in_ref, w_own_ref, rows_ref,
    mixed_ref, d_mixed_ref, d_heads_ref, g_out_ref, g_gain_ref, g_ref, out_pair_ref, hop_ref,
    w_ref, h_ref, cot_ref, hid_ref, dg_ref, du_ref, back_ref, fwd_ref, back_got_ref, fwd_got_ref,
    pair_ref, diag_ref, far_ref, send_sem, recv_sem, w_sem, cot_sem,
):
    row = lax.axis_index("row")
    col, core, across = neighbours()
    dp, (me, on_x, on_y, on_both) = square()
    x, mine = col // 2, lax.rem(col, 2)
    y = 1 - dp
    parts, rows, feat = x_ref.shape
    units = rows_ref.shape[3]
    greet(
        [
            (None, {"col": core}),
            (None, {"col": across}),
            (None, {"dp": y}),
            (row <= 2, {"row": row + 1}),
            (row >= 1, {"row": row - 1}),
        ]
    )
    mover = Mover(send_sem, recv_sem)

    def w_place(r, c):
        return w_ref.at[:, pl.ds(pl.multiple_of(r * units, units), units), pl.ds(c * feat, feat)]

    last = []
    for c in range(4):
        right = mover.copy(rows_ref.at[0, c], w_place(0, c), row=row + 1)
        left = mover.copy(rows_ref.at[3, c], w_place(3, c), row=row - 1)
        pl.when(row == 2)(right.start)
        pl.when(row == 1)(left.start)
        last.append((right, left))
    local = []
    for k in range(4):
        r = lax.rem(row + k, 4)
        here = {1: row != 3, 3: row != 0}.get(k)
        for c in range(4):
            source = w_own_ref.at[c] if k == 0 else rows_ref.at[r, c]
            copy = pltpu.make_async_copy(source, w_place(r, c), w_sem.at[k, c])
            if here is None:
                copy.start()
            else:
                pl.when(here)(copy.start)
            local.append((here, copy))
    cots = []
    for k in range(4):
        from_x = lax.rem(x + k % 2, 2)
        from_dp = lax.rem(dp + k // 2, 2)
        lanes = pl.ds(pl.multiple_of((from_x * 2 + mine) * feat, feat), feat)
        for c in range(4):
            part = pl.ds(c * rows, rows)
            source = cot_own_ref.at[part] if k == 0 else cot_in_ref.at[from_dp * 2 + from_x, part]
            spot = from_dp * 2 + c // 2
            copy = pltpu.make_async_copy(source, cot_ref.at[lax.rem(mine + c, 2), spot, :, lanes], cot_sem.at[k, c])
            copy.start()
            local.append((None, copy))
            sent = mover.copy(source, cot_ref.at[lax.rem(mine + c + 1, 2), spot, :, lanes], col=core)
            sent.start()
            cots.append(sent)

    total = None
    for c in range(parts):
        lanes = slice(c * feat, (c + 1) * feat)
        acc = x_ref[c].astype(F32)
        for r in range(4):
            acc = acc + nn(heads_ref[:, r * feat : (r + 1) * feat], w_out_ref[r, c])
        mixed_ref[:, lanes] = acc
        part = jnp.sum(acc * acc, axis=1, keepdims=True)
        total = part if total is None else total + part
    scale = lax.rsqrt(total / D + EPS)
    for c in range(parts):
        lanes = slice(c * feat, (c + 1) * feat)
        h_ref[0, me, :, lanes] = (mixed_ref[:, lanes] * scale * gain_ref[c, 1:2]).astype(BF)

    half = rows // 2
    top, low = pl.ds(0, half), pl.ds(half, half)

    def h_copy(spot, part=None, side=0, **place):
        source = h_ref.at[0, spot] if part is None else h_ref.at[0, spot, part]
        target = h_ref.at[side, spot] if part is None else h_ref.at[side, spot, part]
        return mover.copy(source, target, **place)

    x_low = h_copy(me, low, col=across)
    y_top = h_copy(me, top, dp=y)
    x_top = h_copy(me, top, col=across)
    y_low = h_copy(me, low, dp=y)
    near = h_copy(me, None, 1, col=core)
    both_low = h_copy(on_x, low, dp=y)
    both_top = h_copy(on_y, top, col=across)
    near_x = h_copy(on_x, None, 1, col=core)
    near_y = h_copy(on_y, None, 1, col=core)
    near_both = h_copy(on_both, None, 1, col=core)
    for c in (x_low, y_top, near, x_top, y_low):
        c.start()
    names = (me, on_x, on_y, on_both)
    back_near = [mover.copy(back_ref.at[1, s], back_got_ref.at[s], col=core) for s in names]
    fwd_near = [mover.copy(fwd_ref.at[1, s], fwd_got_ref.at[s], col=core) for s in names]
    diag = [
        mover.copy(pair_ref.at[on_both, top], diag_ref.at[0], col=across),
        mover.copy(pair_ref.at[on_both, low], diag_ref.at[1], dp=y),
    ]
    far = [
        mover.copy(pair_ref.at[on_x, top], far_ref.at[0, top], col=across),
        mover.copy(pair_ref.at[on_y, low], far_ref.at[1, low], dp=y),
        mover.copy(pair_ref.at[on_y, top], far_ref.at[1, top], dp=y),
        mover.copy(pair_ref.at[on_x, low], far_ref.at[0, low], col=across),
    ]

    def add_pair(k):
        back_near[k].wait_recv()
        s = names[k]
        pair_ref[s] = (back_ref[0, s].astype(F32) + back_got_ref[s].astype(F32)).astype(BF)

    for here, copy in local:
        if here is None:
            copy.wait()
        else:
            pl.when(here)(copy.wait)
    for c in cots:
        c.wait_recv()
    for right, left in last:
        pl.when(row == 3)(right.wait_recv)
        pl.when(row == 0)(left.wait_recv)

    def block(t, carried):
        @pl.when(t == 1)
        def _():
            near.wait_recv()

        @pl.when(t == 2)
        def _():
            x_low.wait_recv()
            both_low.start()
            y_top.wait_recv()
            both_top.start()
            x_top.wait_recv()
            near_x.start()

        @pl.when(t == 3)
        def _():
            near_x.wait_recv()
            y_low.wait_recv()
            near_y.start()

        @pl.when(t == 5)
        def _():
            near_y.wait_recv()

        @pl.when(t == 6)
        def _():
            both_low.wait_recv()
            both_top.wait_recv()
            near_both.start()
            add_pair(1)
            far[0].start()

        @pl.when(t == 7)
        def _():
            near_both.wait_recv()
            add_pair(2)
            far[1].start()

        name, side = t // 2, lax.rem(t, 2)
        spot = lax.rem(dp + name // 2, 2) * 2 + lax.rem(x + lax.rem(name, 2), 2)
        h = h_ref[side, spot]
        gate = nt(h, w_ref[0])
        up = nt(h, w_ref[1])
        d_hidden = nt(cot_ref[side, spot], w_ref[2])
        sig = 1.0 / (1.0 + jnp.exp(-gate))
        silu = gate * sig
        hidden = (silu * up).astype(BF)
        d_gate = (d_hidden * up * sig * (1.0 + gate * (1.0 - sig))).astype(BF)
        d_up = (d_hidden * silu).astype(BF)
        place = pl.ds(pl.multiple_of((side * 4 + spot) * rows, rows), rows)
        hid_ref[place] = hidden
        dg_ref[place] = d_gate
        du_ref[place] = d_up
        back_ref[side, spot] = (nn(d_gate, w_ref[0]) + nn(d_up, w_ref[1])).astype(BF)
        fwd_ref[side, spot] = nn(hidden, w_ref[2]).astype(BF)
        for k in range(4):

            @pl.when(t == 2 * k + 1)
            def _():
                back_near[k].start()
                fwd_near[k].start()

        return carried

    lax.fori_loop(0, 8, block, 0)
    add_pair(3)
    for c in diag:
        c.start()

    def gradient(place, left, right):
        grad = tn(left[...], right[...].reshape(8 * rows, D))
        for r in range(4):
            g_ref[r, place] = grad[r * units : (r + 1) * units].astype(BF)

    gradient(0, dg_ref, h_ref)
    gradient(1, du_ref, h_ref)
    for k, (s, part) in enumerate(((on_y, top), (on_x, low))):
        if k == 1:
            far[0].wait_send()
        else:
            far[1].wait_send()
        diag[k].wait_recv()
        pair_ref[s, part] = (pair_ref[s, part].astype(F32) + diag_ref[k].astype(F32)).astype(BF)
        far[2 + k].start()
    gradient(2, hid_ref, cot_ref)
    hop_right = mover.copy(g_ref.at[3], hop_ref, row=row + 1)
    hop_left = mover.copy(g_ref.at[0], hop_ref, row=row - 1)
    pl.when(row == 0)(hop_right.start)
    pl.when(row == 3)(hop_left.start)
    for k, s in enumerate(names):
        fwd_near[k].wait_recv()
        out_pair_ref[s] = (fwd_ref[0, s].astype(F32) + fwd_got_ref[s].astype(F32)).astype(BF)
    add_pair(0)
    for c in far:
        c.wait_recv()
    d_h = pair_ref[me].astype(F32) + far_ref[0].astype(F32) + far_ref[1].astype(F32)
    unmix_math(
        mixed_ref, cot_ref.at[0, me], d_h, heads_ref, w_out_ref, gain_ref,
        d_mixed_ref, d_heads_ref, g_out_ref, g_gain_ref,
    )
    for c in cots + [x_low, y_top, x_top, y_low, near, both_low, both_top, near_x, near_y, near_both]:
        c.wait_send()
    for c in back_near + fwd_near + diag + far[2:]:
        c.wait_send()
    for right, left in last:
        pl.when(row == 2)(right.wait_send)
        pl.when(row == 1)(left.wait_send)
    pl.when(row == 0)(hop_right.wait_send)
    pl.when(row == 3)(hop_left.wait_send)
    pl.when(row == 1)(hop_right.wait_recv)
    pl.when(row == 2)(hop_left.wait_recv)


def middle(x_parts, heads, w_out, gains, cot_own, cot_near, w_own, w_rows):
    parts, rows, feat = x_parts.shape
    units = w_rows.shape[3]
    count = 8 + 16 + 10 + 8 + 6 + 2
    square_of = pltpu.VMEM((2, 4, rows, D), BF)
    hidden_of = pltpu.VMEM((8 * rows, 4 * units), BF)
    quarter = pltpu.VMEM((4, rows, D), BF)
    return pl.pallas_call(
        middle_body,
        out_shape=(
            jax.ShapeDtypeStruct((rows, D), F32),
            jax.ShapeDtypeStruct((rows, D), F32),
            jax.ShapeDtypeStruct((rows, D), BF),
            jax.ShapeDtypeStruct(w_out.shape, BF),
            jax.ShapeDtypeStruct((1, D), F32),
            jax.ShapeDtypeStruct((4, 3, units, D), BF),
            jax.ShapeDtypeStruct((4, rows, D), BF),
            jax.ShapeDtypeStruct((3, units, D), BF),
        ),
        in_specs=[VMEM] * 4 + [ANY] * 4,
        out_specs=(VMEM,) * 7 + (ANY,),
        scratch_shapes=[pltpu.VMEM((3, 4 * units, D), BF), square_of, square_of]
        + [hidden_of] * 3
        + [square_of, square_of, quarter, quarter, quarter]
        + [
            pltpu.VMEM((2, rows // 2, D), BF),
            pltpu.VMEM((2, rows, D), BF),
            pltpu.SemaphoreType.DMA((count,)),
            pltpu.SemaphoreType.DMA((count,)),
            pltpu.SemaphoreType.DMA((4, 4)),
            pltpu.SemaphoreType.DMA((4, 4)),
        ],
        compiler_params=comm_params(4),
        cost_estimate=cost_of(2 * 8 * rows * 9 * D * 4 * units, 24 << 20),
    )(x_parts, heads, w_out, gains, cot_own, cot_near, w_own, w_rows)


def unmix(dh, out_sum, mixed, cot_own, heads, w_out, gains):
    rows = heads.shape[0]
    parts, feat = w_out.shape[1], w_out.shape[3]
    outs = (
        jax.ShapeDtypeStruct((parts, rows, feat), BF),
        jax.ShapeDtypeStruct((rows, D), F32),
        jax.ShapeDtypeStruct((rows, D), BF),
        jax.ShapeDtypeStruct(w_out.shape, BF),
        jax.ShapeDtypeStruct((1, D), F32),
    )
    return call(unmix_body, outs, cost=cost_of(4 * rows * D * D, 18 << 20))(
        dh, out_sum, mixed, cot_own, heads, w_out, gains
    )


def back_body(
    fast, dq_ref, dkf_ref, hf_ref, bq_ref, turn_ref, w_ref, h_ref, x_ref, gain_ref, d_mixed_ref, g_two_ref, *refs
):
    if fast:
        g_rows_ref, g_ends_ref, g_part_ref, gi_ref, g_ref, cols_ref, mix_ref = refs[:7]
        d_ref, own_ref, send_ref, got_ref, send_sem, recv_sem, local_sem = refs[7:]
        row = lax.axis_index("row")
        col, core, across = neighbours()
        cross = lax.rem(core + 2, 4)
        own = pltpu.make_async_copy(g_rows_ref.at[row], own_ref, local_sem)
        own.start()
        others = [lax.rem(row + k, 4) for k in range(1, 4)]
        greet([(None, {"col": c}) for c in (core, across, cross)] + [(None, {"row": r}) for r in others])
        mover = Mover(send_sem, recv_sem)
        mixes = [mover.copy(g_part_ref.at[r], got_ref.at[k], row=r) for k, r in enumerate(others)]
        for c in mixes:
            c.start()
        width = x_ref.shape[2]
        own.wait()
        for place in range(3):
            total = own_ref[place].astype(F32)
            total = total + jnp.where(row >= 1, g_ends_ref[0, place].astype(F32), 0.0)
            total = (total + jnp.where(row <= 2, g_ends_ref[1, place].astype(F32), 0.0)).astype(BF)
            for c in range(4):
                send_ref[c, place] = total[:, c * width : (c + 1) * width]
        copies = [mover.copy(send_ref.at[c], cols_ref.at[col], col=c) for c in (across, cross, core)]
        for c in copies:
            c.start()
        cols_ref[col] = send_ref[col]
    else:
        gi_ref, g_ref, d_ref = refs
    parts, rows, feat = x_ref.shape
    heads = hf_ref[...]
    high = heads.astype(BF)
    low = (heads - high.astype(F32)).astype(BF)
    dq = dq_ref[...] * (1.0 / RQ)
    cosine = turn_ref[:, :LANES]
    sine = turn_ref[:, LANES:]
    d_fac = jnp.zeros((rows, HEAD_COLS), F32)
    folded = []
    for r in range(RQ):
        tile = bq_ref[:, (r // 2) * LANES : (r // 2 + 1) * LANES]
        rank = double_left(tile) if r % 2 == 0 else double_right(tile)
        product = dq * jnp.concatenate([rank] * PAIRS, axis=1)
        d_fac = d_fac + two_pass(product, head_collect(2 * RK + r))
        pick = head_spread(2 * RK + r, 0, D)
        terms = (nn(high, pick) + nn(low, pick)) * dq
        acc = terms[:, :LANES]
        for p in range(1, PAIRS):
            acc = acc + terms[:, p * LANES : (p + 1) * LANES]
        folded.append(acc + pltpu.roll(acc, HD, 1))
    lane = lane_iota(folded[0].shape)

    def turn_back(part):
        return part * cosine - swap_halves(part) * sine

    for tile in range(3):
        merged = jnp.where(lane < HD, folded[2 * tile], folded[2 * tile + 1])
        d_ref[:, tile * LANES : (tile + 1) * LANES] = turn_back(merged).astype(BF)
    d_ref[:, 3 * LANES : 4 * LANES] = turn_back(dkf_ref[:, :LANES].astype(F32)).astype(BF)
    d_ref[:, 4 * LANES : 5 * LANES] = dkf_ref[:, LANES : 2 * LANES].astype(BF)
    key_low = dkf_ref[:, 2 * LANES :].astype(BF)
    d_fac = d_fac.astype(BF).astype(F32) + nt(key_low, key_columns())
    d_ref[:, RANK_COLS:] = d_fac.astype(BF)
    d_all = d_ref[...]
    d_h = nn(d_all, w_ref[...])
    xs = [x_ref[c].astype(F32) for c in range(parts)]
    total = sum(jnp.sum(v * v, axis=1, keepdims=True) for v in xs)
    scale = lax.rsqrt(total / D + EPS)
    dot = None
    gains = []
    for c in range(parts):
        lanes = slice(c * feat, (c + 1) * feat)
        normed = xs[c] * scale
        grad = d_h[:, lanes]
        gains.append(jnp.sum(grad * normed, axis=0, keepdims=True))
        part = jnp.sum(grad * gain_ref[c, :1] * normed, axis=1, keepdims=True)
        dot = part if dot is None else dot + part
    for c in range(parts):
        lanes = slice(c * feat, (c + 1) * feat)
        normed = xs[c] * scale
        gi_ref[c] = d_mixed_ref[:, lanes] + scale * (
            d_h[:, lanes] * gain_ref[c, :1] - normed * (dot / D)
        )
    grad = tn(d_all, h_ref[...])
    n_row = g_ref.shape[0]
    ranks_each = RANK_COLS // n_row
    used = FAC * GROUP
    for c in range(parts):
        lanes = slice(c * feat, (c + 1) * feat)
        tail = jnp.concatenate(
            [gains[c], g_two_ref[:, lanes], jnp.zeros((GROUP_COLS - used - 2, feat), F32)], axis=0
        )
        for r in range(n_row):
            first = RANK_COLS + r * GROUP_COLS
            g_ref[r, c, :ranks_each] = grad[r * ranks_each : (r + 1) * ranks_each, lanes].astype(BF)
            g_ref[r, c, ranks_each:] = jnp.concatenate([grad[first : first + used, lanes], tail], axis=0).astype(BF)
    if fast:
        total = g_part_ref[row].astype(F32)
        for k, c in enumerate(mixes):
            c.wait_recv()
            total = total + got_ref[k].astype(F32)
        mix_ref[...] = total.astype(BF)
        for c in mixes:
            c.wait_send()
        for c in copies:
            c.wait()


def back(dq, dkf, hf, bq, turn, w_rh, h, x_parts, gains, d_mixed, g_two, n_row, grads=None):
    rows = dq.shape[0]
    parts, _, feat = x_parts.shape
    each = RANK_COLS // n_row + GROUP_COLS
    outs = [jax.ShapeDtypeStruct(x_parts.shape, F32), jax.ShapeDtypeStruct((n_row, parts, each, feat), BF)]
    scratch = [pltpu.VMEM((rows, ALL_COLS), BF)]
    more = []
    fast = grads is not None
    if fast:
        units = grads[0].shape[2]
        cols = (4, 3, units, feat)
        block = grads[2].shape[1:]
        outs += [jax.ShapeDtypeStruct(cols, BF), jax.ShapeDtypeStruct(block, BF)]
        more = list(grads)
        scratch += [
            pltpu.VMEM((3, units, D), BF),
            pltpu.VMEM(cols, BF),
            pltpu.VMEM((3,) + block, BF),
            pltpu.SemaphoreType.DMA((6,)),
            pltpu.SemaphoreType.DMA((6,)),
            pltpu.SemaphoreType.DMA,
        ]
    return pl.pallas_call(
        functools.partial(back_body, fast),
        out_shape=tuple(outs),
        in_specs=[VMEM] * 11 + ([ANY, VMEM, VMEM] if fast else []),
        out_specs=(VMEM,) * len(outs),
        scratch_shapes=scratch,
        compiler_params=comm_params(8) if fast else params(),
        cost_estimate=cost_of(2 * rows * D * 800 * 6, 12 << 20),
    )(dq, dkf, hf, bq, turn, w_rh, h, x_parts, gains, d_mixed, g_two, *more)


def finish_body(
    g_ref, gi_ref, cols_ref, out_ref,
    grad_ref, gi_all_ref, cols_other_ref, out_other_ref,
    near_ref, pair_ref, far_ref, side_ref, down_ref, last_ref, end_ref, send_sem, recv_sem, local_sem,
):
    row = lax.axis_index("row")
    col, core, across = neighbours()
    cross = lax.rem(core + 2, 4)
    dp = lax.axis_index("dp")
    x, mine = col // 2, lax.rem(col, 2)
    rows = [lax.rem(row + k, 4) for k in range(4)]
    greet(
        [(None, {"col": c}) for c in (core, across, cross)]
        + [(None, {"row": r}) for r in rows[1:]]
        + [(None, {"dp": 1 - dp})]
    )
    mover = Mover(send_sem, recv_sem)
    started = []

    def go(source, target, **place):
        c = mover.copy(source, target, **place)
        c.start()
        started.append(c)
        return c

    first = [go(g_ref.at[r, (1 - x) * 2 + 1 - mine], near_ref.at[0, r], col=core) for r in range(4)]
    second = [go(g_ref.at[r, x * 2 + 1 - mine], near_ref.at[1, r], col=core) for r in range(4)]
    rest = [
        go(cols_ref, cols_other_ref, dp=1 - dp),
        go(out_ref, out_other_ref, dp=1 - dp),
    ]
    sides = []
    for r in range(4):
        first[r].wait_recv()
        pair_ref[r] = (g_ref[r, (1 - x) * 2 + mine].astype(F32) + near_ref[0, r].astype(F32)).astype(BF)
        sides.append(go(pair_ref.at[r], side_ref.at[r], col=across))
    for c in (across, cross, core):
        rest.append(go(gi_ref.at[c], gi_all_ref.at[col], col=c))
    own = pltpu.make_async_copy(gi_ref.at[col], gi_all_ref.at[col], local_sem)
    own.start()
    for r in range(4):
        second[r].wait_recv()
        sides[r].wait_recv()
        far_ref[r] = (
            g_ref[r, x * 2 + mine].astype(F32) + near_ref[1, r].astype(F32) + side_ref[r].astype(F32)
        ).astype(BF)
    downs = [go(far_ref.at[rows[k]], down_ref.at[k - 1], row=rows[k]) for k in range(1, 4)]
    total = far_ref[row].astype(F32)
    for k in range(3):
        downs[k].wait_recv()
        total = total + down_ref[k].astype(F32)
    last_ref[...] = total.astype(BF)
    end = go(last_ref, end_ref, dp=1 - dp)
    end.wait_recv()
    grad_ref[...] = last_ref[...].astype(F32) + end_ref[...].astype(F32)
    for c in rest:
        c.wait_recv()
    for c in started:
        c.wait_send()
    own.wait()


def finish(g, gi_parts, cols, g_out):
    block = g.shape[2:]
    count = 8 + 2 + 4 + 3 + 3 + 1
    return pl.pallas_call(
        finish_body,
        out_shape=(
            jax.ShapeDtypeStruct(block, F32),
            jax.ShapeDtypeStruct(gi_parts.shape, gi_parts.dtype),
            jax.ShapeDtypeStruct(cols.shape, BF),
            jax.ShapeDtypeStruct(g_out.shape, BF),
        ),
        in_specs=[VMEM, VMEM, ANY, ANY],
        out_specs=(VMEM, ANY, ANY, ANY),
        scratch_shapes=[
            pltpu.VMEM((2, 4) + block, BF),
            pltpu.VMEM((4,) + block, BF),
            pltpu.VMEM((4,) + block, BF),
            pltpu.VMEM((4,) + block, BF),
            pltpu.VMEM((3,) + block, BF),
            pltpu.VMEM(block, BF),
            pltpu.VMEM(block, BF),
            pltpu.SemaphoreType.DMA((count,)),
            pltpu.SemaphoreType.DMA((count,)),
            pltpu.SemaphoreType.DMA,
        ],
        compiler_params=comm_params(9),
        cost_estimate=cost_of(0, 10 << 20),
    )(g, gi_parts, cols, g_out)


def local(
    tokens_in, segments, gain_attn, gain_ffn, w_heads, w_ranks, w_out, w_gate, w_up, w_down, cotangent
):
    n_row = lax.axis_size("row")
    n_col = lax.axis_size("col")
    row = lax.axis_index("row")
    col = lax.axis_index("col")
    micro, row_tokens, feat = tokens_in.shape
    subs = n_col // micro
    rows = row_tokens // subs
    length = row_tokens * n_row
    head_local = w_heads.shape[1] // FAC
    rank_local = w_ranks.shape[1]
    ffn_local = w_gate.shape[1]
    out_local = w_out.shape[0]
    block = row * subs + col % subs
    past = min(-(-(MAX_DOC - 1) // rows), n_row * subs - 1)
    keys = (past + 1) * rows

    dp_count = lax.axis_size("dp")
    fast = n_col == 4 and n_row == 4 and dp_count == 2 and micro == 2 and past == 4

    heads_t = jnp.transpose(w_heads.reshape(feat, head_local, FAC), (2, 1, 0))
    heads_t = heads_t[jnp.array(FAC_ORDER)].reshape(FAC * head_local, feat)
    pad = jnp.zeros((GROUP_COLS - FAC * head_local, feat), BF)
    w_own = jnp.concatenate([w_ranks.T, heads_t, pad], axis=0)
    gains_own = jnp.concatenate([gain_attn[None], gain_ffn[None], jnp.zeros((6, feat), F32)], axis=0)
    tokens = tokens_in.reshape(n_col, rows, feat)
    if fast:
        dp = lax.axis_index("dp")
        part = ffn_local // (2 * n_col)
        units = -(-part // 16) * 16
        ffn_own = jnp.stack([w_gate.T, w_up.T, w_down]).reshape(3, 2, n_col, part, feat)
        ffn_own = jnp.transpose(lax.dynamic_index_in_dim(ffn_own, dp, 1, False), (1, 0, 2, 3))
        ffn_own = jnp.pad(ffn_own, ((0, 0), (0, 0), (0, units - part), (0, 0)))
    else:
        part = ffn_local // n_col
        units = part * n_row
        w_ffn = jnp.stack([w_gate.T, w_up.T, w_down]).reshape(3, n_col, part, feat)
        w_ffn = lax.all_to_all(jnp.transpose(w_ffn, (1, 0, 2, 3)), "col", 0, 0, tiled=True)
        w_ffn = jnp.transpose(w_ffn, (1, 2, 0, 3)).reshape(3, part, D)
        w_ffn = jnp.transpose(lax.all_gather(w_ffn, "row", axis=0), (1, 0, 2, 3)).reshape(3, units, D)
        w_blocks = lax.all_gather(w_own, ("row", "col"), axis=0).reshape((n_row, n_col) + w_own.shape)
        gains = lax.all_gather(gains_own, "col", axis=0)
        x_parts = lax.all_to_all(tokens, "col", 0, 0, tiled=True)
        w_out_all = lax.all_gather(w_out, ("row", "col"), axis=0).reshape((n_row, n_col) + w_out.shape)

    seg_row = lax.dynamic_index_in_dim(segments, col // subs, 0, keepdims=False)
    padded = jnp.concatenate([jnp.full((1, past * rows), -1, jnp.int32), seg_row], axis=1)
    seg_window = lax.dynamic_slice_in_dim(padded, block * rows, keys, 1)
    own_seg = seg_window[0, past * rows :]
    key_idx = jnp.arange(keys, dtype=jnp.int32)
    query_idx = jnp.arange(rows, dtype=jnp.int32) + past * rows
    before = (own_seg[:, None] == seg_window) & (key_idx[None, :] < query_idx[:, None])
    places = jnp.sum(before.astype(jnp.int32), axis=1)
    inverse = ROPE ** (-(jnp.arange(HD // 2, dtype=F32) * 2.0 / HD))
    angles = places.astype(F32)[:, None] * inverse[None, :]
    cosine = jnp.cos(angles)
    sine = jnp.sin(angles)
    turn = jnp.concatenate([cosine] * 4 + [-sine, sine, -sine, sine], axis=1)

    groups = [[m * subs + s for s in range(subs)] for m in range(micro)]
    if fast:
        x_parts, gains, ffn_parts, mixes, h_one, head_fac, bq_rot, queries, w_rh, kf_window = head(
            tokens, w_own, gains_own, ffn_own, w_out, turn
        )
        kf_window = kf_window.reshape(keys, -1)
        cot_rows = cotangent.reshape(micro * row_tokens, feat)
        heads_out, lse, key_all, value_all, w_rows, cot_near, mixes = attend(
            queries, kf_window, seg_window, ffn_parts, cot_rows, mixes
        )
        mixed, d_mixed, d_heads, g_out, g_gain_two, g_rows, out_pair, hop = middle(
            x_parts, heads_out, mixes, gains, cot_rows, cot_near, ffn_parts, w_rows
        )
        d_q, d_kf, output, g_ends, g_part = attend_back(
            queries, key_all, value_all, d_heads, lse, kf_window, seg_window, out_pair, mixed, g_rows, hop, g_out
        )
        own_kf = window_back(d_kf.reshape(past + 1, rows, -1), n_row)
        gi_parts, g_rh, g_cols, g_out = back(
            d_q, own_kf, head_fac, bq_rot, turn, w_rh, h_one, x_parts, gains, d_mixed, g_gain_two, n_row,
            (g_rows, g_ends, g_part),
        )
        g_rh, grad_input, cols_other, out_other = finish(g_rh, gi_parts, g_cols, g_out)
        g_out = g_out.astype(F32) + out_other.astype(F32)
        g_ffn = jnp.where(dp == 0, jnp.stack([g_cols, cols_other]), jnp.stack([cols_other, g_cols]))
        g_ffn = jnp.transpose(g_ffn[:, :, :, :part], (2, 0, 1, 3, 4)).reshape(3, ffn_local, feat).astype(F32)
    else:
        h_one, head_fac, bq_rot, key_fac, queries, w_rh = front(x_parts, gains, w_blocks, turn)
        gathered = lax.all_gather(key_fac, "row", axis=0)
        gathered = lax.all_gather(gathered, "col", axis=1, axis_index_groups=groups)
        gathered = gathered.reshape(length, key_fac.shape[1])
        padded_kf = jnp.concatenate([jnp.zeros((past * rows, key_fac.shape[1]), BF), gathered], axis=0)
        kf_window = lax.dynamic_slice_in_dim(padded_kf, block * rows, keys, 0)
        heads_out, lse, key_all, value_all = attend(queries, kf_window, seg_window)
        mixed, h_two = mixing(x_parts, heads_out, w_out_all, gains)
        cot_own = lax.all_to_all(cotangent.reshape(n_col, rows, feat), "col", 0, 0, tiled=True)
        cot_own = jnp.transpose(cot_own, (1, 0, 2)).reshape(rows, D)
        cot_all = lax.all_gather(cot_own, "col", axis=0)
        h_all = lax.all_gather(h_two, "col", axis=0)
        out_part, dh_part, g_ffn = ffn(h_all, cot_all, w_ffn)
        dh_sum = lax.psum_scatter(dh_part, "col", scatter_dimension=0, tiled=False).astype(F32)
        out_sum = lax.psum_scatter(out_part, "col", scatter_dimension=0, tiled=False).astype(F32)
        out_parts, d_mixed, d_heads, g_out, g_gain_two = unmix(
            dh_sum, out_sum, mixed, cot_own, heads_out, w_out_all, gains
        )
        d_q, d_kf = attend_back(queries, key_all, value_all, d_heads, lse, kf_window, seg_window)
        spread_kf = jnp.zeros((past * rows + length, d_kf.shape[1]), BF)
        spread_kf = lax.dynamic_update_slice_in_dim(spread_kf, d_kf, block * rows, 0)[past * rows :]
        spread_kf = spread_kf.reshape(n_row, subs, rows, -1)
        own_kf = lax.psum_scatter(spread_kf, "row", scatter_dimension=0, tiled=False)
        own_kf = lax.psum_scatter(own_kf, "col", scatter_dimension=0, tiled=False, axis_index_groups=groups)
        gi_parts, g_rh = back(
            d_q, own_kf, head_fac, bq_rot, turn, w_rh, h_one, x_parts, gains, d_mixed, g_gain_two, n_row
        )
        output = lax.all_to_all(out_parts, "col", 0, 0, tiled=True)
        grad_input = lax.all_to_all(gi_parts, "col", 0, 0, tiled=True)
        g_ffn = lax.psum_scatter(g_ffn.reshape(3, n_row, part, D), "row", scatter_dimension=1, tiled=False)
        g_ffn = jnp.transpose(lax.psum(g_ffn, "dp").reshape(3, part, n_col, feat), (2, 0, 1, 3))
        g_ffn = lax.all_to_all(g_ffn, "col", 0, 0, tiled=True)
        g_ffn = jnp.transpose(g_ffn, (1, 0, 2, 3)).reshape(3, ffn_local, feat).astype(F32)

        def total(values):
            values = values.reshape((n_row * n_col,) + values.shape[2:])
            values = lax.psum_scatter(values, ("row", "col"), scatter_dimension=0, tiled=False)
            return lax.psum(values, "dp").astype(F32)

        g_out = total(g_out)
        g_rh = total(g_rh)

    used = rank_local + FAC * head_local
    own_heads = g_rh[rank_local:used].reshape(FAC, head_local, feat)
    own_heads = jnp.transpose(own_heads[jnp.array(FAC_BACK)], (2, 1, 0)).reshape(w_heads.shape)
    return (
        output.reshape(tokens_in.shape),
        grad_input.reshape(tokens_in.shape),
        g_rh[used],
        g_rh[used + 1],
        own_heads,
        g_rh[:rank_local].T,
        g_out,
        g_ffn[0].T,
        g_ffn[1].T,
        g_ffn[2],
    )


def solution(mesh):
    tokens = P(None, ("dp", "row"), "col")
    both = P("col", "row")
    turned = P("row", "col")
    gain = P("col")
    return jax.shard_map(
        local,
        mesh=mesh,
        in_specs=(tokens, P(None, "dp", None), gain, gain, both, both, turned, both, both, turned, tokens),
        out_specs=(tokens, tokens, gain, gain, both, both, turned, both, both, turned),
        check_vma=False,
    )
```

```python
import functools

import jax
import jax.numpy as jnp
from jax import lax
from jax.experimental import pallas as pl
from jax.experimental.pallas import tpu as pltpu
from jax.sharding import PartitionSpec as P

D = 1024
H = 16
HD = 64
RQ = 6
RK = 2
FAC = 10
MAX_DOC = 1024

EPS = 1e-06
ROPE = 10000.0
NEG = -1e30
BF = jnp.bfloat16
F32 = jnp.float32
LANES = 128
PAIRS = H // 2
FAC_ORDER = (6, 7, 8, 9, 0, 1, 2, 3, 4, 5)
FAC_BACK = (4, 5, 6, 7, 8, 9, 0, 1, 2, 3)
VMEM = pl.BlockSpec(memory_space=pltpu.VMEM)


def nn(a, b):
    return jnp.dot(a, b, preferred_element_type=F32)


def nt(a, b):
    return lax.dot_general(a, b, (((1,), (1,)), ((), ())), preferred_element_type=F32)


def tn(a, b):
    return lax.dot_general(a, b, (((0,), (0,)), ((), ())), preferred_element_type=F32)


def two_pass(a, b):
    high = a.astype(BF)
    low = (a - high.astype(F32)).astype(BF)
    return nn(high, b) + nn(low, b)


def lane_iota(shape):
    return lax.broadcasted_iota(jnp.int32, shape, len(shape) - 1)


def spread(rows, first, width):
    row = lax.broadcasted_iota(jnp.int32, (rows, width), 0)
    head = lax.broadcasted_iota(jnp.int32, (rows, width), 1) // HD
    return (row == head + first).astype(F32).astype(BF)


def collect(rows, width, first):
    head = lax.broadcasted_iota(jnp.int32, (rows, width), 0) // HD
    lane = lax.broadcasted_iota(jnp.int32, (rows, width), 1)
    return (lane == head + first).astype(F32).astype(BF)


GROUP = 4
GROUP_COLS = 48
RANK_COLS = FAC * HD
HEAD_COLS = H // GROUP * GROUP_COLS
ALL_COLS = RANK_COLS + HEAD_COLS


def factor_place(head, j):
    return head // GROUP * GROUP_COLS + j * GROUP + head % GROUP


def head_spread(j, first_head, width):
    row = lax.broadcasted_iota(jnp.int32, (HEAD_COLS, width), 0)
    head = lax.broadcasted_iota(jnp.int32, (HEAD_COLS, width), 1) // HD + first_head
    return (row == factor_place(head, j)).astype(F32).astype(BF)


def head_collect(j):
    head = lax.broadcasted_iota(jnp.int32, (D, HEAD_COLS), 0) // HD
    lane = lax.broadcasted_iota(jnp.int32, (D, HEAD_COLS), 1)
    return (lane == factor_place(head, j)).astype(F32).astype(BF)


def key_columns():
    row = lax.broadcasted_iota(jnp.int32, (HEAD_COLS, LANES), 0)
    lane = lax.broadcasted_iota(jnp.int32, (HEAD_COLS, LANES), 1)
    taken = (row == factor_place(lane % H, lane // H)) & (lane < 2 * RK * H)
    return taken.astype(F32).astype(BF)


def swap_halves(tile):
    lane = lane_iota(tile.shape)
    ahead = pltpu.roll(tile, LANES - HD // 2, 1)
    behind = pltpu.roll(tile, HD // 2, 1)
    return jnp.where(lane % HD < HD // 2, ahead, behind)


def double_left(tile):
    return jnp.where(lane_iota(tile.shape) < HD, tile, pltpu.roll(tile, HD, 1))


def double_right(tile):
    return jnp.where(lane_iota(tile.shape) < HD, pltpu.roll(tile, HD, 1), tile)


def params(**more):
    return pltpu.CompilerParams(vmem_limit_bytes=60 << 20, **more)


def call(body, outs, scratch=(), cost=None):
    return pl.pallas_call(
        body,
        out_shape=outs,
        scratch_shapes=scratch,
        compiler_params=params(),
        cost_estimate=cost,
    )


def cost_of(flops, moved):
    return pl.CostEstimate(flops=int(flops), bytes_accessed=int(moved), transcendentals=0)


MESH = pl.DeviceIdType.MESH
ANY = pl.BlockSpec(memory_space=pl.ANY)


class Mover:
    def __init__(self, send_sem, recv_sem):
        self.send_sem = send_sem
        self.recv_sem = recv_sem
        self.used = 0

    def copy(self, source, target, **place):
        index = self.used
        self.used += 1
        return pltpu.make_async_remote_copy(
            src_ref=source,
            dst_ref=target,
            send_sem=self.send_sem.at[index],
            recv_sem=self.recv_sem.at[index],
            device_id=place,
            device_id_type=MESH,
        )


def greet(partners):
    barrier = pltpu.get_barrier_semaphore()
    count = 0
    for present, place in partners:
        if present is None:
            pl.semaphore_signal(barrier, inc=1, device_id=place, device_id_type=MESH)
            count = count + 1
        else:

            @pl.when(present)
            def _():
                pl.semaphore_signal(barrier, inc=1, device_id=place, device_id_type=MESH)

            count = count + present.astype(jnp.int32)
    pl.semaphore_wait(barrier, count)


def neighbours():
    col = lax.axis_index("col")
    core = col + 1 - 2 * lax.rem(col, 2)
    across = lax.rem(col + 2, 4)
    return col, core, across


def square():
    dp = lax.axis_index("dp")
    x = lax.axis_index("col") // 2
    return dp, (dp * 2 + x, dp * 2 + 1 - x, (1 - dp) * 2 + x, (1 - dp) * 2 + 1 - x)


def comm_params(ident):
    return params(collective_id=ident, has_side_effects=True)


class AttendCopies:
    def __init__(self, w_ref, cot_ref, rows_ref, near_ref, mixes_ref, send_sem, recv_sem):
        row = lax.axis_index("row")
        col, core, across = neighbours()
        dp, (me, on_x, on_y, _) = square()
        mover = Mover(send_sem, recv_sem)
        self.left = row >= 1
        self.right = row <= 2
        self.both = jnp.logical_and(self.left, self.right)
        self.from_left = row >= 2
        self.from_right = row <= 1
        self.partners = [
            (self.right, {"row": row + 1}),
            (self.left, {"row": row - 1}),
            (None, {"col": across}),
            (None, {"col": core}),
            (None, {"dp": 1 - dp}),
        ]
        self.to_right = mover.copy(w_ref, rows_ref.at[row], row=row + 1)
        self.to_left = mover.copy(w_ref, rows_ref.at[row], row=row - 1)
        self.pass_right = mover.copy(rows_ref.at[row - 1], rows_ref.at[row - 1], row=row + 1)
        self.pass_left = mover.copy(rows_ref.at[row + 1], rows_ref.at[row + 1], row=row - 1)
        half = cot_ref.shape[0] // 2
        top, low = pl.ds(0, half), pl.ds(half, half)
        self.cots = [
            mover.copy(cot_ref.at[low], near_ref.at[me, low], col=across),
            mover.copy(cot_ref.at[top], near_ref.at[me, top], dp=1 - dp),
            mover.copy(cot_ref.at[top], near_ref.at[me, top], col=across),
            mover.copy(cot_ref.at[low], near_ref.at[me, low], dp=1 - dp),
        ]
        self.relays = [
            mover.copy(near_ref.at[on_x, low], near_ref.at[on_x, low], dp=1 - dp),
            mover.copy(near_ref.at[on_y, top], near_ref.at[on_y, top], col=across),
        ]
        self.mixes = []
        for r in range(4):
            for c in (col, across):
                self.mixes.append(mover.copy(mixes_ref.at[r, c], mixes_ref.at[r, c], col=core))

    def first(self):
        greet(self.partners)
        pl.when(self.right)(self.to_right.start)
        pl.when(self.left)(self.to_left.start)
        for c in self.cots + self.mixes:
            c.start()

    def second(self):
        for c in self.cots[:2]:
            c.wait_recv()
        for c in self.relays:
            c.start()
        pl.when(self.left)(self.to_right.wait_recv)
        pl.when(self.right)(self.to_left.wait_recv)
        pl.when(self.both)(self.pass_right.start)
        pl.when(self.both)(self.pass_left.start)

    def last(self):
        pl.when(self.right)(self.to_right.wait_send)
        pl.when(self.left)(self.to_left.wait_send)
        pl.when(self.both)(self.pass_right.wait_send)
        pl.when(self.both)(self.pass_left.wait_send)
        pl.when(self.from_left)(self.pass_right.wait_recv)
        pl.when(self.from_right)(self.pass_left.wait_recv)
        for c in self.cots[:2]:
            c.wait_send()
        for c in self.cots[2:] + self.relays + self.mixes:
            c.wait()


class BackCopies:
    def __init__(self, refs, sems):
        (
            self.pair_ref, self.mixed_ref, self.rows_ref, self.g_out_ref,
            self.out_ref, self.ends_ref, self.part_ref,
            self.relay_ref, self.diag_ref, self.far_ref, self.send_ref,
            self.right_ref, self.left_ref, self.got_ref,
            self.near_ref, self.side_ref, self.across_ref,
            self.pieces_ref, self.mine_ref, self.rows_in_ref, self.g_in_ref,
        ) = refs
        send_sem, recv_sem, local_sem = sems
        self.row = row = lax.axis_index("row")
        self.col, core, across = col, _, _ = neighbours()
        cross = lax.rem(core + 2, 4)
        self.dp, self.spots = dp, (me, on_x, on_y, on_both) = square()
        mover = Mover(send_sem, recv_sem)
        self.x, self.mine = x, mine = col // 2, lax.rem(col, 2)
        self.partners = [(None, {"col": c}) for c in (core, across, cross)]
        self.partners += [(None, {"dp": 1 - dp}), (row <= 2, {"row": row + 1}), (row >= 1, {"row": row - 1})]
        half = self.pair_ref.shape[1] // 2
        top, low = pl.ds(0, half), pl.ds(half, half)
        y = 1 - dp
        self.diag = [
            mover.copy(self.pair_ref.at[on_both, top], self.diag_ref.at[0], col=across),
            mover.copy(self.pair_ref.at[on_both, low], self.diag_ref.at[1], dp=y),
        ]
        self.far = [
            mover.copy(self.pair_ref.at[on_x, top], self.far_ref.at[0, top], col=across),
            mover.copy(self.pair_ref.at[on_y, low], self.far_ref.at[1, low], dp=y),
            mover.copy(self.relay_ref.at[0], self.far_ref.at[1, top], dp=y),
            mover.copy(self.relay_ref.at[1], self.far_ref.at[0, low], col=across),
        ]
        self.out = [mover.copy(self.send_ref.at[c], self.out_ref.at[col], col=c) for c in (across, cross, core)]
        self.own = pltpu.make_async_copy(self.send_ref.at[col], self.out_ref.at[col], local_sem.at[0])
        self.hop_right = [
            mover.copy(self.rows_ref.at[3], self.got_ref.at[0], row=row + 1),
            mover.copy(self.right_ref.at[0], self.got_ref.at[1], row=row + 1),
            mover.copy(self.right_ref.at[1], self.ends_ref.at[0], row=row + 1),
        ]
        self.hop_left = [
            mover.copy(self.rows_ref.at[0], self.got_ref.at[0], row=row - 1),
            mover.copy(self.left_ref.at[0], self.got_ref.at[2], row=row - 1),
            mover.copy(self.left_ref.at[1], self.ends_ref.at[1], row=row - 1),
        ]
        self.cores = [
            mover.copy(self.g_out_ref.at[r, k * 2 + 1 - mine], self.near_ref.at[k, r], col=core)
            for k in range(2)
            for r in range(4)
        ]
        self.sides = [mover.copy(self.side_ref.at[r], self.across_ref.at[r], col=across) for r in range(4)]
        self.loads = [
            pltpu.make_async_copy(self.pair_ref.at[on_y, top], self.pieces_ref.at[0], local_sem.at[1]),
            pltpu.make_async_copy(self.pair_ref.at[on_x, low], self.pieces_ref.at[1], local_sem.at[2]),
            pltpu.make_async_copy(self.pair_ref.at[me], self.mine_ref, local_sem.at[3]),
            pltpu.make_async_copy(self.rows_ref, self.rows_in_ref, local_sem.at[4]),
        ]
        self.g_loads = [
            pltpu.make_async_copy(
                self.g_out_ref.at[r, lax.rem(x + k, 2) * 2 + mine], self.g_in_ref.at[k, r], local_sem.at[5 + 4 * k + r]
            )
            for k in range(2)
            for r in range(4)
        ]

    def first(self):
        row = self.row
        greet(self.partners)
        for c in self.diag + self.far[:2] + self.cores:
            c.start()
        pl.when(row == 0)(self.hop_right[0].start)
        pl.when(row == 3)(self.hop_left[0].start)
        for c in self.loads + self.g_loads:
            c.start()

    def cross_x(self):
        for c in self.g_loads:
            c.wait()
        for c in self.cores:
            c.wait_recv()
        for r in range(4):
            self.side_ref[r] = (
                self.g_in_ref[1, r].astype(F32) + self.near_ref[1 - self.x, r].astype(F32)
            ).astype(BF)
            self.sides[r].start()

    def second(self):
        row = self.row
        for c in self.loads:
            c.wait()
        pl.when(row == 1)(self.hop_right[0].wait_recv)
        pl.when(row == 2)(self.hop_left[0].wait_recv)
        hop = self.got_ref[0].astype(F32)
        ahead = self.rows_in_ref[jnp.minimum(row + 2, 3)].astype(F32)
        self.right_ref[0] = jnp.where(row == 1, ahead + hop, ahead).astype(BF)
        behind = self.rows_in_ref[jnp.maximum(row - 2, 0)].astype(F32)
        self.left_ref[0] = jnp.where(row == 2, behind + hop, behind).astype(BF)
        pl.when(row <= 1)(self.hop_right[1].start)
        pl.when(row >= 2)(self.hop_left[1].start)
        for k in range(2):
            self.diag[k].wait_recv()
            self.relay_ref[k] = (self.pieces_ref[k].astype(F32) + self.diag_ref[k].astype(F32)).astype(BF)
            self.far[2 + k].start()

    def third(self):
        row = self.row
        middle = jnp.logical_and(row >= 1, row <= 2)
        pl.when(middle)(self.hop_right[1].wait_recv)
        pl.when(middle)(self.hop_left[1].wait_recv)
        ahead = self.rows_in_ref[jnp.minimum(row + 1, 3)].astype(F32)
        behind = self.rows_in_ref[jnp.maximum(row - 1, 0)].astype(F32)
        self.right_ref[1] = jnp.where(row >= 1, ahead + self.got_ref[1].astype(F32), ahead).astype(BF)
        self.left_ref[1] = jnp.where(row <= 2, behind + self.got_ref[2].astype(F32), behind).astype(BF)
        pl.when(row <= 2)(self.hop_right[2].start)
        pl.when(row >= 1)(self.hop_left[2].start)
        for c in self.far:
            c.wait_recv()
        feat = self.send_ref.shape[2]
        for c in range(4):
            lanes = slice(c * feat, (c + 1) * feat)
            self.send_ref[c] = (
                self.mixed_ref[:, lanes]
                + self.mine_ref[:, lanes].astype(F32)
                + self.far_ref[0, :, lanes].astype(F32)
                + self.far_ref[1, :, lanes].astype(F32)
            ).astype(BF)
        for c in self.out:
            c.start()
        self.own.start()

    def last(self):
        row = self.row
        for r in range(4):
            self.sides[r].wait_recv()
            self.part_ref[r] = (
                self.g_in_ref[0, r].astype(F32)
                + self.near_ref[self.x, r].astype(F32)
                + self.across_ref[r].astype(F32)
            ).astype(BF)
        for c in self.out:
            c.wait()
        self.own.wait()
        for c in self.diag + self.far + self.cores + self.sides:
            c.wait_send()
        pl.when(row == 0)(self.hop_right[0].wait_send)
        pl.when(row == 3)(self.hop_left[0].wait_send)
        pl.when(row <= 1)(self.hop_right[1].wait_send)
        pl.when(row >= 2)(self.hop_left[1].wait_send)
        pl.when(row <= 2)(self.hop_right[2].wait_send)
        pl.when(row >= 1)(self.hop_left[2].wait_send)
        pl.when(row >= 1)(self.hop_right[2].wait_recv)
        pl.when(row <= 2)(self.hop_left[2].wait_recv)


def first_norm(x_ref, gain_ref, h_ref):
    parts = x_ref.shape[0]
    feat = x_ref.shape[2]
    xs = [x_ref[c].astype(F32) for c in range(parts)]
    total = sum(jnp.sum(v * v, axis=1, keepdims=True) for v in xs)
    scale = lax.rsqrt(total / D + EPS)
    for c in range(parts):
        lanes = slice(c * feat, (c + 1) * feat)
        h_ref[:, lanes] = (xs[c] * scale * gain_ref[c, :1]).astype(BF)


def place_factor_weights(blocks_ref, w_ref):
    n_row, parts, _, feat = blocks_ref.shape
    ranks_each = RANK_COLS // n_row
    for c in range(parts):
        lanes = slice(c * feat, (c + 1) * feat)
        for r in range(n_row):
            w_ref[r * ranks_each : (r + 1) * ranks_each, lanes] = blocks_ref[r, c, :ranks_each]
            w_ref[RANK_COLS + r * GROUP_COLS : RANK_COLS + (r + 1) * GROUP_COLS, lanes] = blocks_ref[
                r, c, ranks_each:
            ]


def make_factors(h_ref, w_ref, turn_ref, hf_ref, bq_ref, kf_ref):
    both = nt(h_ref[...], w_ref[...])
    heads = both[:, RANK_COLS:]
    hf_ref[...] = heads
    cosine = turn_ref[:, :LANES]
    sine = turn_ref[:, LANES:]
    for tile in range(RANK_COLS // LANES):
        lanes = slice(tile * LANES, (tile + 1) * LANES)
        part = both[:, lanes]
        if tile < 4:
            part = part * cosine + swap_halves(part) * sine
        if tile < 3:
            bq_ref[:, lanes] = part
        else:
            kf_ref[:, (tile - 3) * LANES : (tile - 2) * LANES] = part.astype(BF)
    kf_ref[:, 2 * LANES :] = nn(heads.astype(BF), key_columns()).astype(BF)


def make_queries(hf_ref, bq_ref, q_ref):
    heads = hf_ref[...]
    high = heads.astype(BF)
    low = (heads - high.astype(F32)).astype(BF)
    ranks = []
    for r in range(RQ):
        tile = bq_ref[:, (r // 2) * LANES : (r // 2 + 1) * LANES]
        ranks.append(double_left(tile) if r % 2 == 0 else double_right(tile))
    width = 2 * LANES
    for p in range(D // width):
        lanes = slice(p * width, (p + 1) * width)
        acc = None
        for r in range(RQ):
            pick = head_spread(2 * RK + r, p * (width // HD), width)
            term = (nn(high, pick) + nn(low, pick)) * jnp.concatenate([ranks[r]] * 2, axis=1)
            acc = term if acc is None else acc + term
        q_ref[:, lanes] = (acc / RQ).astype(BF)


def front_body(x_ref, gain_ref, blocks_ref, turn_ref, h_ref, hf_ref, bq_ref, kf_ref, q_ref, w_ref):
    first_norm(x_ref, gain_ref, h_ref)
    place_factor_weights(blocks_ref, w_ref)
    make_factors(h_ref, w_ref, turn_ref, hf_ref, bq_ref, kf_ref)
    make_queries(hf_ref, bq_ref, q_ref)


def head_body(
    tok_ref, w_own_ref, gain_ref, ffn_ref, mix_ref, turn_ref,
    x_ref, gains_ref, parts_ref, mixes_ref, h_ref, hf_ref, bq_ref, q_ref, w_ref, win_ref,
    blocks_ref, send_sem, recv_sem,
):
    row = lax.axis_index("row")
    col, core, across = neighbours()
    cross = lax.rem(core + 2, 4)
    side = lax.rem(col, 2)
    rows = [lax.rem(row + k, 4) for k in range(4)]
    back = [lax.rem(row + 4 - k, 4) for k in range(4)]
    greet([(None, {"col": c}) for c in (core, across, cross)] + [(None, {"row": r}) for r in rows[1:]])
    mover = Mover(send_sem, recv_sem)
    started = []

    def go(source, target, **place):
        c = mover.copy(source, target, **place)
        c.start()
        started.append(c)
        return c

    down = [None] + [go(w_own_ref, blocks_ref.at[row, col], row=rows[k]) for k in range(1, 4)]
    sides = [go(w_own_ref, blocks_ref.at[row, col], col=across)]
    cores = [go(w_own_ref, blocks_ref.at[row, col], col=core)]
    toks = []
    rest = []
    for c in (across, cross, core):
        toks.append(go(gain_ref, gains_ref.at[col], col=c))
        toks.append(go(tok_ref.at[c], x_ref.at[col], col=c))
    mix_down = [None] + [go(mix_ref, mixes_ref.at[row, col], row=rows[k]) for k in range(1, 4)]
    blocks_ref[row, col] = w_own_ref[...]
    gains_ref[col] = gain_ref[...]
    x_ref[col] = tok_ref[col]
    parts_ref[col] = ffn_ref[col]
    mixes_ref[row, col] = mix_ref[...]
    zero = jnp.zeros(win_ref.shape[1:], BF)
    has_one = row >= 1
    has_two = row >= 2
    for absent, slot in (
        (jnp.logical_not(has_two), 0),
        (jnp.logical_and(jnp.logical_not(has_two), side == 0), 1),
        (jnp.logical_and(jnp.logical_not(has_one), side == 1), 1),
        (jnp.logical_not(has_one), 2),
        (jnp.logical_and(jnp.logical_not(has_one), side == 0), 3),
    ):

        @pl.when(absent)
        def _():
            win_ref[slot] = zero

    for k in range(1, 4):
        down[k].wait_recv()
        block = blocks_ref.at[back[k], col]
        sides.append(go(block, block, col=across))
        cores.append(go(block, block, col=core))
    for c in (across, cross, core):
        rest.append(go(ffn_ref.at[c], parts_ref.at[col], col=c))
    for c in toks:
        c.wait_recv()
    first_norm(x_ref, gains_ref, h_ref)
    passed = []
    for k in range(4):
        sides[k].wait_recv()
        block = blocks_ref.at[back[k], across]
        passed.append(go(block, block, col=core))
    for c in cores + passed:
        c.wait_recv()
    for k in range(4):
        if k > 0:
            mix_down[k].wait_recv()
        block = mixes_ref.at[back[k], col]
        rest.append(go(block, block, col=across))
    place_factor_weights(blocks_ref, w_ref)
    make_factors(h_ref, w_ref, turn_ref, hf_ref, bq_ref, win_ref.at[4])

    own = win_ref.at[4]
    one = mover.copy(own, win_ref.at[2], row=row + 1)
    two = mover.copy(win_ref.at[2], win_ref.at[0], row=row + 1)
    near = mover.copy(own, win_ref.at[3], col=core)
    pass_one = mover.copy(win_ref.at[2], win_ref.at[1 + 2 * side], col=core)
    pass_two = mover.copy(win_ref.at[0], win_ref.at[1], col=core)
    hands_on = jnp.logical_and(has_one, row <= 2)
    sends_two = jnp.logical_and(has_two, side == 1)
    takes_two = jnp.logical_and(has_two, side == 0)
    pl.when(row <= 2)(one.start)
    pl.when(side == 0)(near.start)

    @pl.when(has_one)
    def _():
        one.wait_recv()
        pass_one.start()

    pl.when(hands_on)(two.start)
    make_queries(hf_ref, bq_ref, q_ref)

    @pl.when(has_two)
    def _():
        two.wait_recv()

    pl.when(sends_two)(pass_two.start)

    @pl.when(has_one)
    def _():
        pass_one.wait_recv()
        pass_one.wait_send()

    pl.when(takes_two)(pass_two.wait_recv)
    pl.when(sends_two)(pass_two.wait_send)
    pl.when(side == 1)(near.wait_recv)
    pl.when(side == 0)(near.wait_send)
    pl.when(row <= 2)(one.wait_send)
    pl.when(hands_on)(two.wait_send)
    for c in rest:
        c.wait_recv()
    for c in started:
        c.wait_send()


def head(tok, w_own, gains, ffn_own, w_out, turn):
    rows, feat = tok.shape[1:]
    count = 3 + 4 + 4 + 6 + 3 + 3 + 4 + 4 + 5
    return pl.pallas_call(
        head_body,
        out_shape=(
            jax.ShapeDtypeStruct(tok.shape, BF),
            jax.ShapeDtypeStruct((4,) + gains.shape, F32),
            jax.ShapeDtypeStruct(ffn_own.shape, BF),
            jax.ShapeDtypeStruct((4, 4) + w_out.shape, BF),
            jax.ShapeDtypeStruct((rows, D), BF),
            jax.ShapeDtypeStruct((rows, HEAD_COLS), F32),
            jax.ShapeDtypeStruct((rows, RQ * HD), F32),
            jax.ShapeDtypeStruct((rows, D), BF),
            jax.ShapeDtypeStruct((ALL_COLS, D), BF),
            jax.ShapeDtypeStruct((5, rows, 3 * LANES), BF),
        ),
        in_specs=[VMEM] * 6,
        out_specs=(VMEM,) * 10,
        scratch_shapes=[
            pltpu.VMEM((4, 4) + w_own.shape, BF),
            pltpu.SemaphoreType.DMA((count,)),
            pltpu.SemaphoreType.DMA((count,)),
        ],
        compiler_params=comm_params(1),
        cost_estimate=cost_of(2 * rows * D * 800 * 3, 14 << 20),
    )(tok, w_own, gains, ffn_own, w_out, turn)


def front(x_parts, gains, blocks, turn):
    rows = x_parts.shape[1]
    return call(
        front_body,
        (
            jax.ShapeDtypeStruct((rows, D), BF),
            jax.ShapeDtypeStruct((rows, HEAD_COLS), F32),
            jax.ShapeDtypeStruct((rows, RQ * HD), F32),
            jax.ShapeDtypeStruct((rows, 3 * LANES), BF),
            jax.ShapeDtypeStruct((rows, D), BF),
            jax.ShapeDtypeStruct((ALL_COLS, D), BF),
        ),
        cost=cost_of(2 * rows * D * 800 * 3, 6 << 20),
    )(x_parts, gains, blocks, turn)


def mask_bias(seg_ref, keys, rows):
    seg_row = seg_ref[...].astype(F32)
    wide = jnp.broadcast_to(seg_row, (LANES, keys))
    column = wide.T
    column = jnp.concatenate([column] * (rows // LANES), axis=1)
    key_idx = lax.broadcasted_iota(jnp.int32, (keys, rows), 0)
    query_idx = lax.broadcasted_iota(jnp.int32, (keys, rows), 1) + (keys - rows)
    same = column == seg_row[:, keys - rows :]
    return jnp.where(same & (key_idx <= query_idx), 0.0, NEG)


def attend_body(fast, q_ref, kf_ref, seg_ref, *refs):
    if fast:
        w_ref, cot_ref, _, o_ref, lse_ref, k_ref, v_ref, w_rows_ref, cot_near_ref, mixes_ref = refs[:10]
        bias_ref, dup_ref, send_sem, recv_sem = refs[10:]
        side_work = AttendCopies(w_ref, cot_ref, w_rows_ref, cot_near_ref, mixes_ref, send_sem, recv_sem)
        side_work.first()
    else:
        o_ref, lse_ref, k_ref, v_ref, bias_ref, dup_ref = refs
    rows = q_ref.shape[0]
    keys = kf_ref.shape[0]
    bias_ref[...] = mask_bias(seg_ref, keys, rows)
    for s in range(2 * RK):
        tile = kf_ref[:, (s // 2) * LANES : (s // 2 + 1) * LANES].astype(F32)
        dup_ref[s] = double_left(tile) if s % 2 == 0 else double_right(tile)

    def pair(p, carried):
        if fast:
            pl.when(p == 4)(side_work.second)
        lanes = pl.ds(pl.multiple_of(p * LANES, LANES), LANES)
        weights = kf_ref[:, 2 * LANES :]
        made = []
        for kind in range(2):
            acc = None
            for s in range(RK):
                pick = spread(LANES, (kind * RK + s) * H + 2 * p, LANES)
                term = nn(weights, pick) * dup_ref[kind * RK + s]
                acc = term if acc is None else acc + term
            made.append((acc / RK).astype(BF))
        k_tile, v_tile = made
        k_ref[:, lanes] = k_tile
        v_ref[:, lanes] = v_tile
        v_turned = v_tile.astype(F32).T.astype(BF)
        q_turned = (q_ref[:, lanes].astype(F32) * HD**-0.5).T
        half = lax.broadcasted_iota(jnp.int32, q_turned.shape, 0) // HD
        outs = []
        for side in range(2):
            q_side = jnp.where(half == side, q_turned, 0.0).astype(BF)
            scores = nn(k_tile, q_side) + bias_ref[...]
            peak = jnp.max(scores, axis=0, keepdims=True)
            weight = jnp.exp(scores - peak)
            total = jnp.sum(weight, axis=0, keepdims=True)
            probs = (weight * (1.0 / total)).astype(BF)
            outs.append(nn(v_turned[side * HD : (side + 1) * HD], probs))
            lse_ref[2 * p + side] = jnp.broadcast_to(peak + jnp.log(total), (8, rows))
        o_ref[:, lanes] = jnp.concatenate(outs, axis=0).T.astype(BF)
        return carried

    lax.fori_loop(0, PAIRS, pair, 0)
    if fast:
        side_work.last()


def attend(q, kf_window, seg_window, w_own=None, cot=None, mixes=None):
    rows = q.shape[0]
    keys = kf_window.shape[0]
    fast = w_own is not None
    outs = [
        jax.ShapeDtypeStruct((rows, D), BF),
        jax.ShapeDtypeStruct((H, 8, rows), F32),
        jax.ShapeDtypeStruct((keys, D), BF),
        jax.ShapeDtypeStruct((keys, D), BF),
    ]
    scratch = [pltpu.VMEM((keys, rows), F32), pltpu.VMEM((2 * RK, keys, LANES), F32)]
    in_specs, out_specs, more = [VMEM] * 3, [VMEM] * 4, []
    if fast:
        outs += [
            jax.ShapeDtypeStruct((4,) + w_own.shape, BF),
            jax.ShapeDtypeStruct((4,) + cot.shape, BF),
            jax.ShapeDtypeStruct(mixes.shape, BF),
        ]
        in_specs += [ANY] * 3
        out_specs += [ANY] * 3
        more = [w_own, cot, mixes]
        scratch += [
            pltpu.SemaphoreType.DMA((18,)),
            pltpu.SemaphoreType.DMA((18,)),
        ]
    return pl.pallas_call(
        functools.partial(attend_body, fast),
        out_shape=tuple(outs),
        in_specs=in_specs,
        out_specs=tuple(out_specs),
        scratch_shapes=scratch,
        input_output_aliases={5: 6} if fast else {},
        compiler_params=comm_params(3) if fast else params(),
        cost_estimate=cost_of(2 * rows * keys * D * 16, 16 << 20),
    )(q, kf_window, seg_window, *more)


def attend_back_body(fast, q_ref, k_ref, v_ref, do_ref, lse_ref, kf_ref, seg_ref, *refs):
    if fast:
        dq_ref, dkf_ref = refs[4:6]
        bias_ref, dup_ref, sum_ref, fac_ref = refs[9:13]
        side_work = BackCopies(refs[:4] + refs[6:9] + refs[13:27], refs[27:])
        side_work.first()
    else:
        dq_ref, dkf_ref, bias_ref, dup_ref, sum_ref, fac_ref = refs
    rows = q_ref.shape[0]
    keys = kf_ref.shape[0]
    bias_ref[...] = mask_bias(seg_ref, keys, rows)
    for s in range(2 * RK):
        tile = kf_ref[:, (s // 2) * LANES : (s // 2 + 1) * LANES].astype(F32)
        dup_ref[s] = double_left(tile) if s % 2 == 0 else double_right(tile)
    sum_ref[...] = jnp.zeros_like(sum_ref)
    fac_ref[...] = jnp.zeros_like(fac_ref)

    def pair(p, carried):
        if fast:
            pl.when(p == 1)(side_work.cross_x)
            pl.when(p == 3)(side_work.second)
            pl.when(p == 6)(side_work.third)
        lanes = pl.ds(pl.multiple_of(p * LANES, LANES), LANES)
        k_tile = k_ref[:, lanes]
        v_tile = v_ref[:, lanes]
        k_turned = k_tile.astype(F32).T.astype(BF)
        q_tile = q_ref[:, lanes].astype(F32) * HD**-0.5
        do_tile = do_ref[:, lanes].astype(F32)
        q_turned = q_tile.T
        do_turned = do_tile.T
        half = lax.broadcasted_iota(jnp.int32, q_turned.shape, 0) // HD
        lane_half = lax.broadcasted_iota(jnp.int32, q_tile.shape, 1) // HD
        d_k = None
        d_v = None
        d_q = []
        for side in range(2):
            q_side = jnp.where(half == side, q_turned, 0.0).astype(BF)
            do_side = jnp.where(half == side, do_turned, 0.0).astype(BF)
            scores = nn(k_tile, q_side) + bias_ref[...]
            probs = jnp.exp(scores - lse_ref[2 * p + side][:1])
            d_prob = nn(v_tile, do_side)
            delta = jnp.sum(probs * d_prob, axis=0, keepdims=True)
            d_score = (probs * (d_prob - delta)).astype(BF)
            d_q.append(nn(k_turned[side * HD : (side + 1) * HD], d_score))
            q_back = jnp.where(lane_half == side, q_tile, 0.0).astype(BF)
            do_back = jnp.where(lane_half == side, do_tile, 0.0).astype(BF)
            part_k = nn(d_score, q_back)
            part_v = nn(probs.astype(BF), do_back)
            d_k = part_k if d_k is None else d_k + part_k
            d_v = part_v if d_v is None else d_v + part_v
        dq_ref[:, lanes] = jnp.concatenate(d_q, axis=0).T * HD**-0.5
        weights = kf_ref[:, 2 * LANES :]
        for kind, grad in ((0, d_k), (1, d_v)):
            for s in range(RK):
                slot = kind * RK + s
                pick = spread(LANES, slot * H + 2 * p, LANES)
                sum_ref[slot] += nn(weights, pick) * grad
                fac_ref[...] += two_pass(grad * dup_ref[slot], collect(LANES, LANES, slot * H + 2 * p))
        return carried

    lax.fori_loop(0, PAIRS, pair, 0)
    for tile in range(2):
        first = sum_ref[2 * tile]
        second = sum_ref[2 * tile + 1]
        first = first + pltpu.roll(first, HD, 1)
        second = second + pltpu.roll(second, HD, 1)
        merged = jnp.where(lane_iota(first.shape) < HD, first, second)
        dkf_ref[:, tile * LANES : (tile + 1) * LANES] = (merged / RK).astype(BF)
    dkf_ref[:, 2 * LANES :] = (fac_ref[...] / RK).astype(BF)
    if fast:
        side_work.last()


def attend_back(q, k, v, d_heads, lse, kf_window, seg_window, *more):
    rows = q.shape[0]
    keys = kf_window.shape[0]
    fast = len(more) > 0
    outs = [jax.ShapeDtypeStruct((rows, D), F32), jax.ShapeDtypeStruct(kf_window.shape, BF)]
    scratch = [
        pltpu.VMEM((keys, rows), F32),
        pltpu.VMEM((2 * RK, keys, LANES), F32),
        pltpu.VMEM((2 * RK, keys, LANES), F32),
        pltpu.VMEM((keys, LANES), F32),
    ]
    in_specs, out_specs = [VMEM] * 7, [VMEM] * 2
    if fast:
        in_specs += [ANY, VMEM, ANY, ANY]
        grads, g_out = more[2], more[3]
        parts, feat = g_out.shape[1], g_out.shape[3]
        block, hop = g_out.shape[2:], grads.shape[1:]
        outs += [
            jax.ShapeDtypeStruct((parts, rows, feat), BF),
            jax.ShapeDtypeStruct((2,) + hop, BF),
            jax.ShapeDtypeStruct((4,) + block, BF),
        ]
        out_specs += [ANY, ANY, VMEM]
        scratch += [
            pltpu.VMEM((2, rows // 2, D), BF),
            pltpu.VMEM((2, rows // 2, D), BF),
            pltpu.VMEM((2, rows, D), BF),
            pltpu.VMEM((parts, rows, feat), BF),
            pltpu.VMEM((2,) + hop, BF),
            pltpu.VMEM((2,) + hop, BF),
            pltpu.VMEM((3,) + hop, BF),
            pltpu.VMEM((2, 4) + block, BF),
            pltpu.VMEM((4,) + block, BF),
            pltpu.VMEM((4,) + block, BF),
            pltpu.VMEM((2, rows // 2, D), BF),
            pltpu.VMEM((rows, D), BF),
            pltpu.VMEM(grads.shape, BF),
            pltpu.VMEM((2, 4) + block, BF),
            pltpu.SemaphoreType.DMA((27,)),
            pltpu.SemaphoreType.DMA((27,)),
            pltpu.SemaphoreType.DMA((13,)),
        ]
    return pl.pallas_call(
        functools.partial(attend_back_body, fast),
        out_shape=tuple(outs),
        in_specs=in_specs,
        out_specs=tuple(out_specs),
        scratch_shapes=scratch,
        compiler_params=comm_params(6) if fast else params(),
        cost_estimate=cost_of(2 * rows * keys * D * 40, 16 << 20),
    )(q, k, v, d_heads, lse, kf_window, seg_window, *more)


def mixing_body(x_ref, heads_ref, w_out_ref, gain_ref, mixed_ref, h_ref):
    parts, _, feat = x_ref.shape
    rows_of = w_out_ref.shape[0]
    head_rows = w_out_ref.shape[2]
    total = None
    for c in range(parts):
        lanes = slice(c * feat, (c + 1) * feat)
        acc = x_ref[c].astype(F32)
        for r in range(rows_of):
            acc = acc + nn(heads_ref[:, r * head_rows : (r + 1) * head_rows], w_out_ref[r, c])
        mixed_ref[:, lanes] = acc
        part = jnp.sum(acc * acc, axis=1, keepdims=True)
        total = part if total is None else total + part
    scale = lax.rsqrt(total / D + EPS)
    for c in range(parts):
        lanes = slice(c * feat, (c + 1) * feat)
        h_ref[:, lanes] = (mixed_ref[:, lanes] * scale * gain_ref[c, 1:2]).astype(BF)


def mixing(x_parts, heads, w_out, gains):
    rows = heads.shape[0]
    return call(
        mixing_body,
        (jax.ShapeDtypeStruct((rows, D), F32), jax.ShapeDtypeStruct((rows, D), BF)),
        cost=cost_of(2 * rows * D * D, 5 << 20),
    )(x_parts, heads, w_out, gains)


def ffn_steps(blocks, h_at, cot_at, w_ref, hid_ref, dg_ref, du_ref, out_at, back_at):
    def block(t, carried):
        h = h_at(t)[...]
        gate = nt(h, w_ref[0])
        up = nt(h, w_ref[1])
        d_hidden = nt(cot_at(t)[...], w_ref[2])
        sig = 1.0 / (1.0 + jnp.exp(-gate))
        silu = gate * sig
        hidden = (silu * up).astype(BF)
        d_gate = (d_hidden * up * sig * (1.0 + gate * (1.0 - sig))).astype(BF)
        d_up = (d_hidden * silu).astype(BF)
        rows = h.shape[0]
        place = pl.ds(pl.multiple_of(t * rows, rows), rows)
        hid_ref[place] = hidden
        dg_ref[place] = d_gate
        du_ref[place] = d_up
        out_at(t)[...] = nn(hidden, w_ref[2]).astype(BF)
        back_at(t)[...] = (nn(d_gate, w_ref[0]) + nn(d_up, w_ref[1])).astype(BF)
        return carried

    lax.fori_loop(0, blocks, block, 0)


def ffn_body(h_ref, cot_ref, w_ref, out_ref, back_ref, g_ref, hid_ref, dg_ref, du_ref):
    parts, rows, _ = h_ref.shape
    ffn_steps(
        parts, lambda t: h_ref.at[t], lambda t: cot_ref.at[t], w_ref, hid_ref, dg_ref, du_ref,
        lambda t: out_ref.at[t], lambda t: back_ref.at[t],
    )
    h_all = h_ref[...].reshape(parts * rows, D)
    cot_all = cot_ref[...].reshape(parts * rows, D)
    for place, (left, right) in enumerate(((dg_ref, h_all), (du_ref, h_all), (hid_ref, cot_all))):
        g_ref[place] = tn(left[...], right).astype(BF)


def ffn(h_all, cot_all, w):
    parts, rows, _ = h_all.shape
    units = w.shape[1]
    return call(
        ffn_body,
        (
            jax.ShapeDtypeStruct(h_all.shape, BF),
            jax.ShapeDtypeStruct(h_all.shape, BF),
            jax.ShapeDtypeStruct(w.shape, BF),
        ),
        scratch=[pltpu.VMEM((parts * rows, units), BF)] * 3,
        cost=cost_of(2 * parts * rows * 9 * D * units, 20 << 20),
    )(h_all, cot_all, w)


def unmix_math(
    mixed_ref, cot_ref, d_h, heads_ref, w_out_ref, gain_ref, d_mixed_ref, d_heads_ref, g_out_ref, g_gain_ref
):
    rows_of, parts, head_rows, feat = w_out_ref.shape
    mixed = mixed_ref[...]
    scale = lax.rsqrt(jnp.sum(mixed * mixed, axis=1, keepdims=True) / D + EPS)
    normed = mixed * scale
    g_gain_ref[...] = jnp.sum(d_h * normed, axis=0, keepdims=True)
    gain = jnp.concatenate([gain_ref[c, 1:2] for c in range(parts)], axis=1)
    inner = d_h * gain
    dot = jnp.sum(inner * normed, axis=1, keepdims=True) / D
    d_mixed = cot_ref[...].astype(F32) + scale * (inner - normed * dot)
    d_mixed_ref[...] = d_mixed
    low = d_mixed.astype(BF)
    grad = tn(heads_ref[...], low)
    for r in range(rows_of):
        acc = None
        for c in range(parts):
            lanes = slice(c * feat, (c + 1) * feat)
            term = nt(low[:, lanes], w_out_ref[r, c])
            acc = term if acc is None else acc + term
            g_out_ref[r, c] = grad[r * head_rows : (r + 1) * head_rows, lanes].astype(BF)
        d_heads_ref[:, r * head_rows : (r + 1) * head_rows] = acc.astype(BF)


def write_output(mixed_ref, total, out_ref):
    parts, _, feat = out_ref.shape
    for c in range(parts):
        lanes = slice(c * feat, (c + 1) * feat)
        out_ref[c] = (mixed_ref[:, lanes] + total[:, lanes]).astype(BF)


def unmix_body(
    dh_ref, sum_ref, mixed_ref, cot_ref, heads_ref, w_out_ref, gain_ref,
    out_ref, d_mixed_ref, d_heads_ref, g_out_ref, g_gain_ref,
):
    unmix_math(
        mixed_ref, cot_ref, dh_ref[...], heads_ref, w_out_ref, gain_ref,
        d_mixed_ref, d_heads_ref, g_out_ref, g_gain_ref,
    )
    write_output(mixed_ref, sum_ref[...], out_ref)


def middle_body(
    x_ref, heads_ref, w_out_ref, gain_ref, cot_own_ref, cot_in_ref, w_own_ref, rows_ref,
    mixed_ref, d_mixed_ref, d_heads_ref, g_out_ref, g_gain_ref, g_ref, out_pair_ref,
    w_ref, h_ref, cot_ref, hid_ref, dg_ref, du_ref, back_ref, fwd_ref, back_got_ref, fwd_got_ref,
    pair_ref, diag_ref, far_ref, send_sem, recv_sem, w_sem, cot_sem,
):
    row = lax.axis_index("row")
    col, core, across = neighbours()
    dp, (me, on_x, on_y, on_both) = square()
    x, mine = col // 2, lax.rem(col, 2)
    y = 1 - dp
    parts, rows, feat = x_ref.shape
    units = rows_ref.shape[3]
    greet(
        [
            (None, {"col": core}),
            (None, {"col": across}),
            (None, {"dp": y}),
            (row <= 2, {"row": row + 1}),
            (row >= 1, {"row": row - 1}),
        ]
    )
    mover = Mover(send_sem, recv_sem)

    def w_place(r, c):
        return w_ref.at[:, pl.ds(pl.multiple_of(r * units, units), units), pl.ds(c * feat, feat)]

    last = []
    for c in range(4):
        right = mover.copy(rows_ref.at[0, c], w_place(0, c), row=row + 1)
        left = mover.copy(rows_ref.at[3, c], w_place(3, c), row=row - 1)
        pl.when(row == 2)(right.start)
        pl.when(row == 1)(left.start)
        last.append((right, left))
    local = []
    for k in range(4):
        r = lax.rem(row + k, 4)
        here = {1: row != 3, 3: row != 0}.get(k)
        for c in range(4):
            source = w_own_ref.at[c] if k == 0 else rows_ref.at[r, c]
            copy = pltpu.make_async_copy(source, w_place(r, c), w_sem.at[k, c])
            if here is None:
                copy.start()
            else:
                pl.when(here)(copy.start)
            local.append((here, copy))
    cots = []
    for k in range(4):
        from_x = lax.rem(x + k % 2, 2)
        from_dp = lax.rem(dp + k // 2, 2)
        lanes = pl.ds(pl.multiple_of((from_x * 2 + mine) * feat, feat), feat)
        for c in range(4):
            part = pl.ds(c * rows, rows)
            source = cot_own_ref.at[part] if k == 0 else cot_in_ref.at[from_dp * 2 + from_x, part]
            spot = from_dp * 2 + c // 2
            copy = pltpu.make_async_copy(source, cot_ref.at[lax.rem(mine + c, 2), spot, :, lanes], cot_sem.at[k, c])
            copy.start()
            local.append((None, copy))
            sent = mover.copy(source, cot_ref.at[lax.rem(mine + c + 1, 2), spot, :, lanes], col=core)
            sent.start()
            cots.append(sent)

    total = None
    for c in range(parts):
        lanes = slice(c * feat, (c + 1) * feat)
        acc = x_ref[c].astype(F32)
        for r in range(4):
            acc = acc + nn(heads_ref[:, r * feat : (r + 1) * feat], w_out_ref[r, c])
        mixed_ref[:, lanes] = acc
        part = jnp.sum(acc * acc, axis=1, keepdims=True)
        total = part if total is None else total + part
    scale = lax.rsqrt(total / D + EPS)
    for c in range(parts):
        lanes = slice(c * feat, (c + 1) * feat)
        h_ref[0, me, :, lanes] = (mixed_ref[:, lanes] * scale * gain_ref[c, 1:2]).astype(BF)

    half = rows // 2
    top, low = pl.ds(0, half), pl.ds(half, half)

    def h_copy(spot, part=None, side=0, **place):
        source = h_ref.at[0, spot] if part is None else h_ref.at[0, spot, part]
        target = h_ref.at[side, spot] if part is None else h_ref.at[side, spot, part]
        return mover.copy(source, target, **place)

    x_low = h_copy(me, low, col=across)
    y_top = h_copy(me, top, dp=y)
    x_top = h_copy(me, top, col=across)
    y_low = h_copy(me, low, dp=y)
    near = h_copy(me, None, 1, col=core)
    both_low = h_copy(on_x, low, dp=y)
    both_top = h_copy(on_y, top, col=across)
    near_first = [h_copy(on_x, low, 1, col=core), h_copy(on_y, top, 1, col=core)]
    near_second = [h_copy(on_x, top, 1, col=core), h_copy(on_y, low, 1, col=core)]
    near_both = h_copy(on_both, None, 1, col=core)
    for c in (x_low, y_top, near, x_top, y_low):
        c.start()
    steps = (
        ((me, top), (me, low)),
        ((on_x, low), (on_y, top)),
        ((on_x, top), (on_y, low)),
        ((on_both, top), (on_both, low)),
    )
    back_near = [[mover.copy(back_ref.at[1, s, p], back_got_ref.at[s, p], col=core) for s, p in two] for two in steps]
    fwd_near = [[mover.copy(fwd_ref.at[1, s, p], fwd_got_ref.at[s, p], col=core) for s, p in two] for two in steps]
    diag = [
        mover.copy(pair_ref.at[on_both, top], diag_ref.at[0], col=across),
        mover.copy(pair_ref.at[on_both, low], diag_ref.at[1], dp=y),
    ]
    far = [
        mover.copy(pair_ref.at[on_x, top], far_ref.at[0, top], col=across),
        mover.copy(pair_ref.at[on_y, low], far_ref.at[1, low], dp=y),
        mover.copy(pair_ref.at[on_y, top], far_ref.at[1, top], dp=y),
        mover.copy(pair_ref.at[on_x, low], far_ref.at[0, low], col=across),
    ]

    def add_pair(k):
        for (s, p), c in zip(steps[k], back_near[k]):
            c.wait_recv()
            pair_ref[s, p] = (back_ref[0, s, p].astype(F32) + back_got_ref[s, p].astype(F32)).astype(BF)

    for here, copy in local:
        if here is None:
            copy.wait()
        else:
            pl.when(here)(copy.wait)
    for c in cots:
        c.wait_recv()
    for right, left in last:
        pl.when(row == 3)(right.wait_recv)
        pl.when(row == 0)(left.wait_recv)

    def block(t, carried):
        @pl.when(t == 1)
        def _():
            near.wait_recv()

        @pl.when(t == 2)
        def _():
            x_low.wait_recv()
            both_low.start()
            near_first[0].start()
            y_top.wait_recv()
            both_top.start()
            near_first[1].start()

        @pl.when(t == 3)
        def _():
            for c in near_first:
                c.wait_recv()

        @pl.when(t == 4)
        def _():
            x_top.wait_recv()
            near_second[0].start()
            y_low.wait_recv()
            near_second[1].start()

        @pl.when(t == 5)
        def _():
            for c in near_second:
                c.wait_recv()
            add_pair(1)

        @pl.when(t == 6)
        def _():
            both_low.wait_recv()
            both_top.wait_recv()
            near_both.start()

        @pl.when(t == 7)
        def _():
            near_both.wait_recv()
            add_pair(2)
            far[0].start()
            far[1].start()

        name, side = t // 2, lax.rem(t, 2)
        first_dp = lax.rem(dp + jnp.where(name == 3, 1, 0), 2)
        first_x = lax.rem(x + jnp.where(name >= 1, 1, 0), 2)
        first = first_dp * 2 + first_x
        other_dp = lax.rem(dp + jnp.where(name >= 1, 1, 0), 2)
        other_x = lax.rem(x + jnp.where(name == 3, 1, 0), 2)
        other = other_dp * 2 + other_x
        first_rows = pl.ds(pl.multiple_of(jnp.where(name == 1, half, 0), half), half)
        other_rows = pl.ds(pl.multiple_of(jnp.where(name == 1, 0, half), half), half)
        h = jnp.concatenate([h_ref[side, first, first_rows], h_ref[side, other, other_rows]], axis=0)
        cot = jnp.concatenate([cot_ref[side, first, first_rows], cot_ref[side, other, other_rows]], axis=0)
        gate = nt(h, w_ref[0])
        up = nt(h, w_ref[1])
        d_hidden = nt(cot, w_ref[2])
        sig = 1.0 / (1.0 + jnp.exp(-gate))
        silu = gate * sig
        hidden = (silu * up).astype(BF)
        d_gate = (d_hidden * up * sig * (1.0 + gate * (1.0 - sig))).astype(BF)
        d_up = (d_hidden * silu).astype(BF)
        back = (nn(d_gate, w_ref[0]) + nn(d_up, w_ref[1])).astype(BF)
        fwd = nn(hidden, w_ref[2]).astype(BF)
        for spot, part, cut in ((first, first_rows, slice(0, half)), (other, other_rows, slice(half, rows))):
            start = jnp.where(part.start == 0, 0, half)
            place = pl.ds(pl.multiple_of((side * 4 + spot) * rows + start, half), half)
            hid_ref[place] = hidden[cut]
            dg_ref[place] = d_gate[cut]
            du_ref[place] = d_up[cut]
            back_ref[side, spot, part] = back[cut]
            fwd_ref[side, spot, part] = fwd[cut]
        for k in range(4):

            @pl.when(t == 2 * k + 1)
            def _():
                for c in back_near[k] + fwd_near[k]:
                    c.start()

        return carried

    lax.fori_loop(0, 8, block, 0)
    add_pair(3)
    for c in diag:
        c.start()

    def gradient(place, left, right):
        grad = tn(left[...], right[...].reshape(8 * rows, D))
        for r in range(4):
            g_ref[r, place] = grad[r * units : (r + 1) * units].astype(BF)

    gradient(0, dg_ref, h_ref)
    gradient(1, du_ref, h_ref)
    for k, (s, part) in enumerate(((on_y, top), (on_x, low))):
        if k == 1:
            far[0].wait_send()
        else:
            far[1].wait_send()
        diag[k].wait_recv()
        pair_ref[s, part] = (pair_ref[s, part].astype(F32) + diag_ref[k].astype(F32)).astype(BF)
        far[2 + k].start()
    gradient(2, hid_ref, cot_ref)
    for two, copies in zip(steps, fwd_near):
        for (s, p), c in zip(two, copies):
            c.wait_recv()
            out_pair_ref[s, p] = (fwd_ref[0, s, p].astype(F32) + fwd_got_ref[s, p].astype(F32)).astype(BF)
    add_pair(0)
    for c in far:
        c.wait_recv()
    d_h = pair_ref[me].astype(F32) + far_ref[0].astype(F32) + far_ref[1].astype(F32)
    unmix_math(
        mixed_ref, cot_ref.at[0, me], d_h, heads_ref, w_out_ref, gain_ref,
        d_mixed_ref, d_heads_ref, g_out_ref, g_gain_ref,
    )
    for c in cots + [x_low, y_top, x_top, y_low, near, both_low, both_top, near_both] + near_first + near_second:
        c.wait_send()
    for two in back_near + fwd_near:
        for c in two:
            c.wait_send()
    for c in diag + far[2:]:
        c.wait_send()
    for right, left in last:
        pl.when(row == 2)(right.wait_send)
        pl.when(row == 1)(left.wait_send)


def middle(x_parts, heads, w_out, gains, cot_own, cot_near, w_own, w_rows):
    parts, rows, feat = x_parts.shape
    units = w_rows.shape[3]
    count = 8 + 16 + 12 + 16 + 6
    square_of = pltpu.VMEM((2, 4, rows, D), BF)
    hidden_of = pltpu.VMEM((8 * rows, 4 * units), BF)
    quarter = pltpu.VMEM((4, rows, D), BF)
    return pl.pallas_call(
        middle_body,
        out_shape=(
            jax.ShapeDtypeStruct((rows, D), F32),
            jax.ShapeDtypeStruct((rows, D), F32),
            jax.ShapeDtypeStruct((rows, D), BF),
            jax.ShapeDtypeStruct(w_out.shape, BF),
            jax.ShapeDtypeStruct((1, D), F32),
            jax.ShapeDtypeStruct((4, 3, units, D), BF),
            jax.ShapeDtypeStruct((4, rows, D), BF),
        ),
        in_specs=[VMEM] * 4 + [ANY] * 4,
        out_specs=(VMEM,) * 7,
        scratch_shapes=[pltpu.VMEM((3, 4 * units, D), BF), square_of, square_of]
        + [hidden_of] * 3
        + [square_of, square_of, quarter, quarter, quarter]
        + [
            pltpu.VMEM((2, rows // 2, D), BF),
            pltpu.VMEM((2, rows, D), BF),
            pltpu.SemaphoreType.DMA((count,)),
            pltpu.SemaphoreType.DMA((count,)),
            pltpu.SemaphoreType.DMA((4, 4)),
            pltpu.SemaphoreType.DMA((4, 4)),
        ],
        compiler_params=comm_params(4),
        cost_estimate=cost_of(2 * 8 * rows * 9 * D * 4 * units, 24 << 20),
    )(x_parts, heads, w_out, gains, cot_own, cot_near, w_own, w_rows)


def unmix(dh, out_sum, mixed, cot_own, heads, w_out, gains):
    rows = heads.shape[0]
    parts, feat = w_out.shape[1], w_out.shape[3]
    outs = (
        jax.ShapeDtypeStruct((parts, rows, feat), BF),
        jax.ShapeDtypeStruct((rows, D), F32),
        jax.ShapeDtypeStruct((rows, D), BF),
        jax.ShapeDtypeStruct(w_out.shape, BF),
        jax.ShapeDtypeStruct((1, D), F32),
    )
    return call(unmix_body, outs, cost=cost_of(4 * rows * D * D, 18 << 20))(
        dh, out_sum, mixed, cot_own, heads, w_out, gains
    )


def query_grads(ranks_taken, dq, high, low, bq_ref):
    fac = None
    folded = []
    for r in ranks_taken:
        tile = bq_ref[:, (r // 2) * LANES : (r // 2 + 1) * LANES]
        rank = double_left(tile) if r % 2 == 0 else double_right(tile)
        product = dq * jnp.concatenate([rank] * PAIRS, axis=1)
        term = two_pass(product, head_collect(2 * RK + r))
        fac = term if fac is None else fac + term
        pick = head_spread(2 * RK + r, 0, D)
        terms = (nn(high, pick) + nn(low, pick)) * dq
        acc = terms[:, :LANES]
        for p in range(1, PAIRS):
            acc = acc + terms[:, p * LANES : (p + 1) * LANES]
        folded.append(acc + pltpu.roll(acc, HD, 1))
    return fac, folded


def turned_back(part, turn_ref):
    return part * turn_ref[:, :LANES] - swap_halves(part) * turn_ref[:, LANES:]


def put_query_grads(folded, first, turn_ref, d_ref):
    lane = lane_iota(folded[0].shape)
    for k in range(len(folded) // 2):
        merged = jnp.where(lane < HD, folded[2 * k], folded[2 * k + 1])
        tile = first // 2 + k
        d_ref[:, tile * LANES : (tile + 1) * LANES] = turned_back(merged, turn_ref).astype(BF)


def put_key_grads(dkf, fac, turn_ref, d_ref):
    d_ref[:, 3 * LANES : 4 * LANES] = turned_back(dkf[:, :LANES], turn_ref).astype(BF)
    d_ref[:, 4 * LANES : 5 * LANES] = dkf[:, LANES : 2 * LANES].astype(BF)
    fac = fac.astype(BF).astype(F32) + nt(dkf[:, 2 * LANES :].astype(BF), key_columns())
    d_ref[:, RANK_COLS:] = fac.astype(BF)


def factor_weight_grads(d_ref, h_ref, gains, g_two_ref, g_ref):
    n_row, parts, _, feat = g_ref.shape
    grad = tn(d_ref[...], h_ref[...])
    ranks_each = RANK_COLS // n_row
    used = FAC * GROUP
    for c in range(parts):
        lanes = slice(c * feat, (c + 1) * feat)
        tail = jnp.concatenate(
            [gains[c], g_two_ref[:, lanes], jnp.zeros((GROUP_COLS - used - 2, feat), F32)], axis=0
        )
        for r in range(n_row):
            first = RANK_COLS + r * GROUP_COLS
            g_ref[r, c, :ranks_each] = grad[r * ranks_each : (r + 1) * ranks_each, lanes].astype(BF)
            g_ref[r, c, ranks_each:] = jnp.concatenate([grad[first : first + used, lanes], tail], axis=0).astype(BF)


def first_norm_back(d_h, x_ref, gain_ref, d_mixed_ref, gi_ref):
    parts, _, feat = x_ref.shape
    xs = [x_ref[c].astype(F32) for c in range(parts)]
    total = sum(jnp.sum(v * v, axis=1, keepdims=True) for v in xs)
    scale = lax.rsqrt(total / D + EPS)
    dot = None
    gains = []
    for c in range(parts):
        normed = xs[c] * scale
        grad = d_h[:, c * feat : (c + 1) * feat]
        gains.append(jnp.sum(grad * normed, axis=0, keepdims=True))
        part = jnp.sum(grad * gain_ref[c, :1] * normed, axis=1, keepdims=True)
        dot = part if dot is None else dot + part
    for c in range(parts):
        lanes = slice(c * feat, (c + 1) * feat)
        normed = xs[c] * scale
        total = d_mixed_ref[:, lanes] + scale * (d_h[:, lanes] * gain_ref[c, :1] - normed * (dot / D))
        gi_ref[c] = total.astype(gi_ref.dtype)
    return gains


def back_body(
    dq_ref, dkf_ref, hf_ref, bq_ref, turn_ref, w_ref, h_ref, x_ref, gain_ref, d_mixed_ref, g_two_ref,
    gi_ref, g_ref, d_ref,
):
    heads = hf_ref[...]
    high = heads.astype(BF)
    low = (heads - high.astype(F32)).astype(BF)
    fac, folded = query_grads(range(RQ), dq_ref[...] * (1.0 / RQ), high, low, bq_ref)
    put_query_grads(folded, 0, turn_ref, d_ref)
    put_key_grads(dkf_ref[...].astype(F32), fac, turn_ref, d_ref)
    gains = first_norm_back(nn(d_ref[...], w_ref[...]), x_ref, gain_ref, d_mixed_ref, gi_ref)
    factor_weight_grads(d_ref, h_ref, gains, g_two_ref, g_ref)


def back(dq, dkf, hf, bq, turn, w_rh, h, x_parts, gains, d_mixed, g_two, n_row):
    rows = dq.shape[0]
    parts, _, feat = x_parts.shape
    each = RANK_COLS // n_row + GROUP_COLS
    return call(
        back_body,
        (jax.ShapeDtypeStruct(x_parts.shape, F32), jax.ShapeDtypeStruct((n_row, parts, each, feat), BF)),
        scratch=[pltpu.VMEM((rows, ALL_COLS), BF)],
        cost=cost_of(2 * rows * D * 800 * 6, 12 << 20),
    )(dq, dkf, hf, bq, turn, w_rh, h, x_parts, gains, d_mixed, g_two)


def tail_body(
    win_ref, dq_ref, hf_ref, bq_ref, turn_ref, w_ref, h_ref, x_ref, gain_ref, d_mixed_ref, g_two_ref,
    rows_ref, ends_ref, part_ref,
    grad_ref, gi_all_ref, cols_ref, cols_other_ref, mix_ref, mix_other_ref,
    d_ref, gi_ref, wnear_ref, wsend_ref, wfar_ref, rows_own_ref, cols_send_ref, mix_got_ref,
    g_ref, near_ref, pair_ref, far_ref, side_ref, down_ref, last_ref, end_ref,
    send_sem, recv_sem, local_sem,
):
    row = lax.axis_index("row")
    col, core, across = neighbours()
    cross = lax.rem(core + 2, 4)
    dp = lax.axis_index("dp")
    x, mine = col // 2, lax.rem(col, 2)
    y = 1 - dp
    order = [lax.rem(row + k, 4) for k in (1, 2, 3, 0)]
    greet(
        [(None, {"col": c}) for c in (core, across, cross)]
        + [(None, {"row": r}) for r in order[:3]]
        + [(None, {"dp": y})]
    )
    mover = Mover(send_sem, recv_sem)
    started = []

    def go(source, target, **place):
        c = mover.copy(source, target, **place)
        c.start()
        started.append(c)
        return c

    rows_own = pltpu.make_async_copy(rows_ref.at[row], rows_own_ref, local_sem.at[1])
    rows_own.start()

    near_one = go(win_ref.at[1], wnear_ref.at[0], col=core)
    near_two = go(win_ref.at[3], wnear_ref.at[1], col=core)
    one = mover.copy(wsend_ref.at[0], wfar_ref.at[0], row=row - 1)
    two = mover.copy(wsend_ref.at[1], wfar_ref.at[1], row=row - 1)
    hands_on = jnp.logical_and(row >= 1, row <= 2)
    left = mine == 0
    heads = hf_ref[...]
    high = heads.astype(BF)
    low = (heads - high.astype(F32)).astype(BF)
    dq = dq_ref[...] * (1.0 / RQ)
    near_one.wait_recv()
    near_two.wait_recv()
    zero = jnp.zeros(wnear_ref.shape[1:], F32)
    from_low = wnear_ref[0].astype(F32)
    from_high = wnear_ref[1].astype(F32)
    wsend_ref[1] = (win_ref[0].astype(F32) + jnp.where(left, zero, from_low)).astype(BF)
    pl.when(row >= 2)(two.start)

    width = x_ref.shape[2]
    rows_own.wait()
    for place in range(3):
        total = rows_own_ref[place].astype(F32)
        total = total + jnp.where(row >= 1, ends_ref[0, place].astype(F32), 0.0)
        total = (total + jnp.where(row <= 2, ends_ref[1, place].astype(F32), 0.0)).astype(BF)
        for c in range(4):
            cols_send_ref[c, place] = total[:, c * width : (c + 1) * width]
    columns = [go(cols_send_ref.at[c], cols_ref.at[col], col=c) for c in (across, cross, core)]
    cols_ref[col] = cols_send_ref[col]
    rest = [go(cols_ref.at[col], cols_other_ref.at[col], dp=y)]

    fac, folded = query_grads(range(0, 4), dq, high, low, bq_ref)
    put_query_grads(folded, 0, turn_ref, d_ref)
    sent_on = win_ref[2].astype(F32) + jnp.where(left, from_low, from_high)
    pl.when(hands_on)(two.wait_recv)
    wsend_ref[0] = jnp.where(hands_on, sent_on + wfar_ref[1].astype(F32), sent_on).astype(BF)
    pl.when(row >= 1)(one.start)

    mixes = [go(part_ref.at[order[k]], mix_got_ref.at[k], row=order[k]) for k in range(3)]

    fac_more, folded = query_grads(range(4, RQ), dq, high, low, bq_ref)
    put_query_grads(folded, 4, turn_ref, d_ref)
    for c, source in zip(columns, (across, cross, core)):
        c.wait_recv()
        rest.append(go(cols_ref.at[source], cols_other_ref.at[source], dp=y))
    d_kf = win_ref[4].astype(F32) + jnp.where(left, from_high, zero)
    pl.when(row <= 2)(one.wait_recv)
    d_kf = jnp.where(row <= 2, d_kf + wfar_ref[0].astype(F32), d_kf)
    put_key_grads(d_kf, fac + fac_more, turn_ref, d_ref)
    d_h = nn(d_ref[...], w_ref[...])
    gains = first_norm_back(d_h, x_ref, gain_ref, d_mixed_ref, gi_ref)
    factor_weight_grads(d_ref, h_ref, gains, g_two_ref, g_ref)

    first = [go(g_ref.at[r, (1 - x) * 2 + 1 - mine], near_ref.at[0, k], col=core) for k, r in enumerate(order)]
    second = [go(g_ref.at[r, x * 2 + 1 - mine], near_ref.at[1, k], col=core) for k, r in enumerate(order)]
    sides = []
    for k, r in enumerate(order):
        first[k].wait_recv()
        pair_ref[k] = (g_ref[r, (1 - x) * 2 + mine].astype(F32) + near_ref[0, k].astype(F32)).astype(BF)
        sides.append(go(pair_ref.at[k], side_ref.at[k], col=across))

    total = part_ref[row].astype(F32)
    for k, c in enumerate(mixes):
        c.wait_recv()
        total = total + mix_got_ref[k].astype(F32)
    mix_ref[...] = total.astype(BF)
    rest.append(go(mix_ref, mix_other_ref, dp=y))
    for c in (across, cross, core):
        rest.append(go(gi_ref.at[c], gi_all_ref.at[col], col=c))
    own = pltpu.make_async_copy(gi_ref.at[col], gi_all_ref.at[col], local_sem.at[0])
    own.start()

    downs = []
    for k, r in enumerate(order):
        second[k].wait_recv()
        sides[k].wait_recv()
        far_ref[k] = (
            g_ref[r, x * 2 + mine].astype(F32) + near_ref[1, k].astype(F32) + side_ref[k].astype(F32)
        ).astype(BF)
        if k < 3:
            downs.append(go(far_ref.at[k], down_ref.at[k], row=r))
    total = far_ref[3].astype(F32)
    for k in range(3):
        downs[k].wait_recv()
        total = total + down_ref[k].astype(F32)
    last_ref[...] = total.astype(BF)
    end = go(last_ref, end_ref, dp=y)
    end.wait_recv()
    grad_ref[...] = last_ref[...].astype(F32) + end_ref[...].astype(F32)
    for c in rest:
        c.wait_recv()
    for c in started:
        c.wait_send()
    pl.when(row >= 1)(one.wait_send)
    pl.when(row >= 2)(two.wait_send)
    own.wait()


def tail(win, dq, hf, bq, turn, w_rh, h, x_parts, gains, d_mixed, g_two, g_rows, ends, part):
    rows = dq.shape[0]
    parts, _, feat = x_parts.shape
    units = g_rows.shape[2]
    block = (RANK_COLS // 4 + GROUP_COLS, feat)
    cols = (parts, 3, units, feat)
    mix = part.shape[1:]
    wide = g_rows.shape[1:]
    slot = win.shape[1:]
    count = 2 + 2 + 3 + 8 + 4 + 3 + 1 + 1 + 3 + 3 + 3 + 1
    return pl.pallas_call(
        tail_body,
        out_shape=(
            jax.ShapeDtypeStruct(block, F32),
            jax.ShapeDtypeStruct(x_parts.shape, BF),
            jax.ShapeDtypeStruct(cols, BF),
            jax.ShapeDtypeStruct(cols, BF),
            jax.ShapeDtypeStruct(mix, BF),
            jax.ShapeDtypeStruct(mix, BF),
        ),
        in_specs=[VMEM] * 11 + [ANY, VMEM, VMEM],
        out_specs=(VMEM, ANY, VMEM, ANY, VMEM, ANY),
        scratch_shapes=[
            pltpu.VMEM((rows, ALL_COLS), BF),
            pltpu.VMEM(x_parts.shape, BF),
            pltpu.VMEM((2,) + slot, BF),
            pltpu.VMEM((2,) + slot, BF),
            pltpu.VMEM((2,) + slot, BF),
            pltpu.VMEM(wide, BF),
            pltpu.VMEM(cols, BF),
            pltpu.VMEM((3,) + mix, BF),
            pltpu.VMEM((4, parts) + block, BF),
            pltpu.VMEM((2, 4) + block, BF),
            pltpu.VMEM((4,) + block, BF),
            pltpu.VMEM((4,) + block, BF),
            pltpu.VMEM((4,) + block, BF),
            pltpu.VMEM((3,) + block, BF),
            pltpu.VMEM(block, BF),
            pltpu.VMEM(block, BF),
            pltpu.SemaphoreType.DMA((count,)),
            pltpu.SemaphoreType.DMA((count,)),
            pltpu.SemaphoreType.DMA((2,)),
        ],
        compiler_params=comm_params(7),
        cost_estimate=cost_of(2 * rows * D * 800 * 6, 24 << 20),
    )(win, dq, hf, bq, turn, w_rh, h, x_parts, gains, d_mixed, g_two, g_rows, ends, part)


def local(
    tokens_in, segments, gain_attn, gain_ffn, w_heads, w_ranks, w_out, w_gate, w_up, w_down, cotangent
):
    n_row = lax.axis_size("row")
    n_col = lax.axis_size("col")
    row = lax.axis_index("row")
    col = lax.axis_index("col")
    micro, row_tokens, feat = tokens_in.shape
    subs = n_col // micro
    rows = row_tokens // subs
    length = row_tokens * n_row
    head_local = w_heads.shape[1] // FAC
    rank_local = w_ranks.shape[1]
    ffn_local = w_gate.shape[1]
    out_local = w_out.shape[0]
    block = row * subs + col % subs
    past = min(-(-(MAX_DOC - 1) // rows), n_row * subs - 1)
    keys = (past + 1) * rows

    dp_count = lax.axis_size("dp")
    fast = n_col == 4 and n_row == 4 and dp_count == 2 and micro == 2 and past == 4

    heads_t = jnp.transpose(w_heads.reshape(feat, head_local, FAC), (2, 1, 0))
    heads_t = heads_t[jnp.array(FAC_ORDER)].reshape(FAC * head_local, feat)
    pad = jnp.zeros((GROUP_COLS - FAC * head_local, feat), BF)
    w_own = jnp.concatenate([w_ranks.T, heads_t, pad], axis=0)
    gains_own = jnp.concatenate([gain_attn[None], gain_ffn[None], jnp.zeros((6, feat), F32)], axis=0)
    tokens = tokens_in.reshape(n_col, rows, feat)
    if fast:
        dp = lax.axis_index("dp")
        part = ffn_local // (2 * n_col)
        units = -(-part // 16) * 16
        ffn_own = jnp.stack([w_gate.T, w_up.T, w_down]).reshape(3, 2, n_col, part, feat)
        ffn_own = jnp.transpose(lax.dynamic_index_in_dim(ffn_own, dp, 1, False), (1, 0, 2, 3))
        ffn_own = jnp.pad(ffn_own, ((0, 0), (0, 0), (0, units - part), (0, 0)))
    else:
        part = ffn_local // n_col
        units = part * n_row
        w_ffn = jnp.stack([w_gate.T, w_up.T, w_down]).reshape(3, n_col, part, feat)
        w_ffn = lax.all_to_all(jnp.transpose(w_ffn, (1, 0, 2, 3)), "col", 0, 0, tiled=True)
        w_ffn = jnp.transpose(w_ffn, (1, 2, 0, 3)).reshape(3, part, D)
        w_ffn = jnp.transpose(lax.all_gather(w_ffn, "row", axis=0), (1, 0, 2, 3)).reshape(3, units, D)
        w_blocks = lax.all_gather(w_own, ("row", "col"), axis=0).reshape((n_row, n_col) + w_own.shape)
        gains = lax.all_gather(gains_own, "col", axis=0)
        x_parts = lax.all_to_all(tokens, "col", 0, 0, tiled=True)
        w_out_all = lax.all_gather(w_out, ("row", "col"), axis=0).reshape((n_row, n_col) + w_out.shape)

    seg_row = lax.dynamic_index_in_dim(segments, col // subs, 0, keepdims=False)
    padded = jnp.concatenate([jnp.full((1, past * rows), -1, jnp.int32), seg_row], axis=1)
    seg_window = lax.dynamic_slice_in_dim(padded, block * rows, keys, 1)
    own_seg = seg_window[0, past * rows :]
    key_idx = jnp.arange(keys, dtype=jnp.int32)
    query_idx = jnp.arange(rows, dtype=jnp.int32) + past * rows
    before = (own_seg[:, None] == seg_window) & (key_idx[None, :] < query_idx[:, None])
    places = jnp.sum(before.astype(jnp.int32), axis=1)
    inverse = ROPE ** (-(jnp.arange(HD // 2, dtype=F32) * 2.0 / HD))
    angles = places.astype(F32)[:, None] * inverse[None, :]
    cosine = jnp.cos(angles)
    sine = jnp.sin(angles)
    turn = jnp.concatenate([cosine] * 4 + [-sine, sine, -sine, sine], axis=1)

    groups = [[m * subs + s for s in range(subs)] for m in range(micro)]
    if fast:
        x_parts, gains, ffn_parts, mixes, h_one, head_fac, bq_rot, queries, w_rh, kf_window = head(
            tokens, w_own, gains_own, ffn_own, w_out, turn
        )
        kf_window = kf_window.reshape(keys, -1)
        cot_rows = cotangent.reshape(micro * row_tokens, feat)
        heads_out, lse, key_all, value_all, w_rows, cot_near, mixes = attend(
            queries, kf_window, seg_window, ffn_parts, cot_rows, mixes
        )
        mixed, d_mixed, d_heads, g_out, g_gain_two, g_rows, out_pair = middle(
            x_parts, heads_out, mixes, gains, cot_rows, cot_near, ffn_parts, w_rows
        )
        d_q, d_kf, output, g_ends, g_part = attend_back(
            queries, key_all, value_all, d_heads, lse, kf_window, seg_window, out_pair, mixed, g_rows, g_out
        )
        g_rh, grad_input, g_cols, cols_other, g_out, out_other = tail(
            d_kf.reshape(past + 1, rows, -1), d_q, head_fac, bq_rot, turn, w_rh, h_one, x_parts, gains, d_mixed,
            g_gain_two, g_rows, g_ends, g_part,
        )
        grad_input = grad_input.astype(F32)
        g_out = g_out.astype(F32) + out_other.astype(F32)
        g_ffn = jnp.where(dp == 0, jnp.stack([g_cols, cols_other]), jnp.stack([cols_other, g_cols]))
        g_ffn = jnp.transpose(g_ffn[:, :, :, :part], (2, 0, 1, 3, 4)).reshape(3, ffn_local, feat).astype(F32)
    else:
        h_one, head_fac, bq_rot, key_fac, queries, w_rh = front(x_parts, gains, w_blocks, turn)
        gathered = lax.all_gather(key_fac, "row", axis=0)
        gathered = lax.all_gather(gathered, "col", axis=1, axis_index_groups=groups)
        gathered = gathered.reshape(length, key_fac.shape[1])
        padded_kf = jnp.concatenate([jnp.zeros((past * rows, key_fac.shape[1]), BF), gathered], axis=0)
        kf_window = lax.dynamic_slice_in_dim(padded_kf, block * rows, keys, 0)
        heads_out, lse, key_all, value_all = attend(queries, kf_window, seg_window)
        mixed, h_two = mixing(x_parts, heads_out, w_out_all, gains)
        cot_own = lax.all_to_all(cotangent.reshape(n_col, rows, feat), "col", 0, 0, tiled=True)
        cot_own = jnp.transpose(cot_own, (1, 0, 2)).reshape(rows, D)
        cot_all = lax.all_gather(cot_own, "col", axis=0)
        h_all = lax.all_gather(h_two, "col", axis=0)
        out_part, dh_part, g_ffn = ffn(h_all, cot_all, w_ffn)
        dh_sum = lax.psum_scatter(dh_part, "col", scatter_dimension=0, tiled=False).astype(F32)
        out_sum = lax.psum_scatter(out_part, "col", scatter_dimension=0, tiled=False).astype(F32)
        out_parts, d_mixed, d_heads, g_out, g_gain_two = unmix(
            dh_sum, out_sum, mixed, cot_own, heads_out, w_out_all, gains
        )
        d_q, d_kf = attend_back(queries, key_all, value_all, d_heads, lse, kf_window, seg_window)
        spread_kf = jnp.zeros((past * rows + length, d_kf.shape[1]), BF)
        spread_kf = lax.dynamic_update_slice_in_dim(spread_kf, d_kf, block * rows, 0)[past * rows :]
        spread_kf = spread_kf.reshape(n_row, subs, rows, -1)
        own_kf = lax.psum_scatter(spread_kf, "row", scatter_dimension=0, tiled=False)
        own_kf = lax.psum_scatter(own_kf, "col", scatter_dimension=0, tiled=False, axis_index_groups=groups)
        gi_parts, g_rh = back(
            d_q, own_kf, head_fac, bq_rot, turn, w_rh, h_one, x_parts, gains, d_mixed, g_gain_two, n_row
        )
        output = lax.all_to_all(out_parts, "col", 0, 0, tiled=True)
        grad_input = lax.all_to_all(gi_parts, "col", 0, 0, tiled=True)
        g_ffn = lax.psum_scatter(g_ffn.reshape(3, n_row, part, D), "row", scatter_dimension=1, tiled=False)
        g_ffn = jnp.transpose(lax.psum(g_ffn, "dp").reshape(3, part, n_col, feat), (2, 0, 1, 3))
        g_ffn = lax.all_to_all(g_ffn, "col", 0, 0, tiled=True)
        g_ffn = jnp.transpose(g_ffn, (1, 0, 2, 3)).reshape(3, ffn_local, feat).astype(F32)

        def total(values):
            values = values.reshape((n_row * n_col,) + values.shape[2:])
            values = lax.psum_scatter(values, ("row", "col"), scatter_dimension=0, tiled=False)
            return lax.psum(values, "dp").astype(F32)

        g_out = total(g_out)
        g_rh = total(g_rh)

    used = rank_local + FAC * head_local
    own_heads = g_rh[rank_local:used].reshape(FAC, head_local, feat)
    own_heads = jnp.transpose(own_heads[jnp.array(FAC_BACK)], (2, 1, 0)).reshape(w_heads.shape)
    return (
        output.reshape(tokens_in.shape),
        grad_input.reshape(tokens_in.shape),
        g_rh[used],
        g_rh[used + 1],
        own_heads,
        g_rh[:rank_local].T,
        g_out,
        g_ffn[0].T,
        g_ffn[1].T,
        g_ffn[2],
    )


def solution(mesh):
    tokens = P(None, ("dp", "row"), "col")
    both = P("col", "row")
    turned = P("row", "col")
    gain = P("col")
    return jax.shard_map(
        local,
        mesh=mesh,
        in_specs=(tokens, P(None, "dp", None), gain, gain, both, both, turned, both, both, turned, tokens),
        out_specs=(tokens, tokens, gain, gain, both, both, turned, both, both, turned),
        check_vma=False,
    )
```

```python
import functools

import jax
import jax.numpy as jnp
from jax import lax
from jax.experimental import pallas as pl
from jax.experimental.pallas import tpu as pltpu
from jax.sharding import PartitionSpec as P

D = 1024
H = 16
HD = 64
RQ = 6
RK = 2
FAC = 10
MAX_DOC = 1024

EPS = 1e-06
ROPE = 10000.0
NEG = -1e30
BF = jnp.bfloat16
F32 = jnp.float32
LANES = 128
PAIRS = H // 2
FAC_ORDER = (6, 7, 8, 9, 0, 1, 2, 3, 4, 5)
FAC_BACK = (4, 5, 6, 7, 8, 9, 0, 1, 2, 3)
VMEM = pl.BlockSpec(memory_space=pltpu.VMEM)


def nn(a, b):
    return jnp.dot(a, b, preferred_element_type=F32)


def nt(a, b):
    return lax.dot_general(a, b, (((1,), (1,)), ((), ())), preferred_element_type=F32)


def tn(a, b):
    return lax.dot_general(a, b, (((0,), (0,)), ((), ())), preferred_element_type=F32)


def two_pass(a, b):
    high = a.astype(BF)
    low = (a - high.astype(F32)).astype(BF)
    return nn(high, b) + nn(low, b)


def lane_iota(shape):
    return lax.broadcasted_iota(jnp.int32, shape, len(shape) - 1)


def spread(rows, first, width):
    row = lax.broadcasted_iota(jnp.int32, (rows, width), 0)
    head = lax.broadcasted_iota(jnp.int32, (rows, width), 1) // HD
    return (row == head + first).astype(F32).astype(BF)


def collect(rows, width, first):
    head = lax.broadcasted_iota(jnp.int32, (rows, width), 0) // HD
    lane = lax.broadcasted_iota(jnp.int32, (rows, width), 1)
    return (lane == head + first).astype(F32).astype(BF)


GROUP = 4
GROUP_COLS = 48
RANK_COLS = FAC * HD
HEAD_COLS = H // GROUP * GROUP_COLS
ALL_COLS = RANK_COLS + HEAD_COLS


def factor_place(head, j):
    return head // GROUP * GROUP_COLS + j * GROUP + head % GROUP


def head_spread(j, first_head, width):
    row = lax.broadcasted_iota(jnp.int32, (HEAD_COLS, width), 0)
    head = lax.broadcasted_iota(jnp.int32, (HEAD_COLS, width), 1) // HD + first_head
    return (row == factor_place(head, j)).astype(F32).astype(BF)


def head_collect(j):
    head = lax.broadcasted_iota(jnp.int32, (D, HEAD_COLS), 0) // HD
    lane = lax.broadcasted_iota(jnp.int32, (D, HEAD_COLS), 1)
    return (lane == factor_place(head, j)).astype(F32).astype(BF)


def key_columns():
    row = lax.broadcasted_iota(jnp.int32, (HEAD_COLS, LANES), 0)
    lane = lax.broadcasted_iota(jnp.int32, (HEAD_COLS, LANES), 1)
    taken = (row == factor_place(lane % H, lane // H)) & (lane < 2 * RK * H)
    return taken.astype(F32).astype(BF)


def swap_halves(tile):
    lane = lane_iota(tile.shape)
    ahead = pltpu.roll(tile, LANES - HD // 2, 1)
    behind = pltpu.roll(tile, HD // 2, 1)
    return jnp.where(lane % HD < HD // 2, ahead, behind)


def double_left(tile):
    return jnp.where(lane_iota(tile.shape) < HD, tile, pltpu.roll(tile, HD, 1))


def double_right(tile):
    return jnp.where(lane_iota(tile.shape) < HD, pltpu.roll(tile, HD, 1), tile)


def params(**more):
    return pltpu.CompilerParams(vmem_limit_bytes=60 << 20, **more)


def call(body, outs, scratch=(), cost=None):
    return pl.pallas_call(
        body,
        out_shape=outs,
        scratch_shapes=scratch,
        compiler_params=params(),
        cost_estimate=cost,
    )


def cost_of(flops, moved):
    return pl.CostEstimate(flops=int(flops), bytes_accessed=int(moved), transcendentals=0)


MESH = pl.DeviceIdType.MESH
ANY = pl.BlockSpec(memory_space=pl.ANY)


class Mover:
    def __init__(self, send_sem, recv_sem):
        self.send_sem = send_sem
        self.recv_sem = recv_sem
        self.used = 0

    def copy(self, source, target, **place):
        index = self.used
        self.used += 1
        return pltpu.make_async_remote_copy(
            src_ref=source,
            dst_ref=target,
            send_sem=self.send_sem.at[index],
            recv_sem=self.recv_sem.at[index],
            device_id=place,
            device_id_type=MESH,
        )


def greet(partners):
    barrier = pltpu.get_barrier_semaphore()
    count = 0
    for present, place in partners:
        if present is None:
            pl.semaphore_signal(barrier, inc=1, device_id=place, device_id_type=MESH)
            count = count + 1
        else:

            @pl.when(present)
            def _():
                pl.semaphore_signal(barrier, inc=1, device_id=place, device_id_type=MESH)

            count = count + present.astype(jnp.int32)
    pl.semaphore_wait(barrier, count)


def neighbours():
    col = lax.axis_index("col")
    core = col + 1 - 2 * lax.rem(col, 2)
    across = lax.rem(col + 2, 4)
    return col, core, across


def square():
    dp = lax.axis_index("dp")
    x = lax.axis_index("col") // 2
    return dp, (dp * 2 + x, dp * 2 + 1 - x, (1 - dp) * 2 + x, (1 - dp) * 2 + 1 - x)


def comm_params(ident):
    return params(collective_id=ident, has_side_effects=True)


class AttendCopies:
    def __init__(self, cot_ref, rows_ref, near_ref, mixes_ref, send_sem, recv_sem):
        row = lax.axis_index("row")
        col, core, across = neighbours()
        dp, (me, on_x, on_y, _) = square()
        mover = Mover(send_sem, recv_sem)
        self.left = row >= 1
        self.right = row <= 2
        self.both = jnp.logical_and(self.left, self.right)
        self.from_left = row >= 2
        self.from_right = row <= 1
        self.partners = [
            (self.right, {"row": row + 1}),
            (self.left, {"row": row - 1}),
            (None, {"col": across}),
            (None, {"col": core}),
            (None, {"dp": 1 - dp}),
        ]
        self.row = row
        cuts = [pl.ds(0, 2), pl.ds(2, 2)]
        lower, upper = rows_ref.at[row - 1], rows_ref.at[row + 1]
        self.pass_right = [mover.copy(lower.at[c], lower.at[c], row=row + 1) for c in cuts]
        self.pass_left = [mover.copy(upper.at[c], upper.at[c], row=row - 1) for c in cuts]
        self.last_right = [mover.copy(rows_ref.at[0, c], rows_ref.at[0, c], row=row + 1) for c in cuts]
        self.last_left = [mover.copy(rows_ref.at[3, c], rows_ref.at[3, c], row=row - 1) for c in cuts]
        half = cot_ref.shape[0] // 2
        top, low = pl.ds(0, half), pl.ds(half, half)
        self.cots = [
            mover.copy(cot_ref.at[low], near_ref.at[me, low], col=across),
            mover.copy(cot_ref.at[top], near_ref.at[me, top], dp=1 - dp),
            mover.copy(cot_ref.at[top], near_ref.at[me, top], col=across),
            mover.copy(cot_ref.at[low], near_ref.at[me, low], dp=1 - dp),
        ]
        self.relays = [
            mover.copy(near_ref.at[on_x, low], near_ref.at[on_x, low], dp=1 - dp),
            mover.copy(near_ref.at[on_y, top], near_ref.at[on_y, top], col=across),
        ]
        self.mixes = []
        for r in range(4):
            for c in (col, across):
                self.mixes.append(mover.copy(mixes_ref.at[r, c], mixes_ref.at[r, c], col=core))

    def first(self):
        greet(self.partners)
        for k in range(2):
            pl.when(self.both)(self.pass_right[k].start)
            pl.when(self.both)(self.pass_left[k].start)
        for c in self.cots + self.mixes:
            c.start()

    def hand_on(self, k):
        pl.when(self.from_left)(self.pass_right[k].wait_recv)
        pl.when(self.from_right)(self.pass_left[k].wait_recv)
        pl.when(self.row == 2)(self.last_right[k].start)
        pl.when(self.row == 1)(self.last_left[k].start)

    def second(self):
        for c in self.cots[:2]:
            c.wait_recv()
        for c in self.relays:
            c.start()
        self.hand_on(1)

    def last(self):
        for k in range(2):
            pl.when(self.both)(self.pass_right[k].wait_send)
            pl.when(self.both)(self.pass_left[k].wait_send)
            pl.when(self.row == 2)(self.last_right[k].wait_send)
            pl.when(self.row == 1)(self.last_left[k].wait_send)
            pl.when(self.row == 3)(self.last_right[k].wait_recv)
            pl.when(self.row == 0)(self.last_left[k].wait_recv)
        for c in self.cots[:2]:
            c.wait_send()
        for c in self.cots[2:] + self.relays + self.mixes:
            c.wait()


class BackCopies:
    def __init__(self, refs, sems):
        (
            self.pair_ref, self.mixed_ref, self.rows_ref, self.g_out_ref, self.hop_ref,
            self.out_ref, self.ends_ref, self.part_ref,
            self.relay_ref, self.diag_ref, self.far_ref, self.send_ref,
            self.right_ref, self.left_ref, self.got_ref,
            self.near_ref, self.side_ref, self.across_ref,
            self.pieces_ref, self.mine_ref, self.rows_in_ref, self.g_in_ref,
        ) = refs
        send_sem, recv_sem, local_sem = sems
        self.row = row = lax.axis_index("row")
        self.col, core, across = col, _, _ = neighbours()
        cross = lax.rem(core + 2, 4)
        self.dp, self.spots = dp, (me, on_x, on_y, on_both) = square()
        mover = Mover(send_sem, recv_sem)
        self.x, self.mine = x, mine = col // 2, lax.rem(col, 2)
        self.partners = [(None, {"col": c}) for c in (core, across, cross)]
        self.partners += [(None, {"dp": 1 - dp}), (row <= 2, {"row": row + 1}), (row >= 1, {"row": row - 1})]
        half = self.pair_ref.shape[1] // 2
        top, low = pl.ds(0, half), pl.ds(half, half)
        y = 1 - dp
        self.diag = [
            mover.copy(self.pair_ref.at[on_both, top], self.diag_ref.at[0], col=across),
            mover.copy(self.pair_ref.at[on_both, low], self.diag_ref.at[1], dp=y),
        ]
        self.far = [
            mover.copy(self.pair_ref.at[on_x, top], self.far_ref.at[0, top], col=across),
            mover.copy(self.pair_ref.at[on_y, low], self.far_ref.at[1, low], dp=y),
            mover.copy(self.relay_ref.at[0], self.far_ref.at[1, top], dp=y),
            mover.copy(self.relay_ref.at[1], self.far_ref.at[0, low], col=across),
        ]
        self.out = [mover.copy(self.send_ref.at[c], self.out_ref.at[col], col=c) for c in (across, cross, core)]
        self.own = pltpu.make_async_copy(self.send_ref.at[col], self.out_ref.at[col], local_sem.at[0])
        self.hop_right = [
            mover.copy(self.right_ref.at[0], self.got_ref.at[0], row=row + 1),
            mover.copy(self.right_ref.at[1], self.ends_ref.at[0], row=row + 1),
        ]
        self.hop_left = [
            mover.copy(self.left_ref.at[0], self.got_ref.at[1], row=row - 1),
            mover.copy(self.left_ref.at[1], self.ends_ref.at[1], row=row - 1),
        ]
        self.cores = [
            mover.copy(self.g_out_ref.at[r, k * 2 + 1 - mine], self.near_ref.at[k, r], col=core)
            for k in range(2)
            for r in range(4)
        ]
        self.sides = [mover.copy(self.side_ref.at[r], self.across_ref.at[r], col=across) for r in range(4)]
        self.loads = [
            pltpu.make_async_copy(self.pair_ref.at[on_y, top], self.pieces_ref.at[0], local_sem.at[1]),
            pltpu.make_async_copy(self.pair_ref.at[on_x, low], self.pieces_ref.at[1], local_sem.at[2]),
            pltpu.make_async_copy(self.pair_ref.at[me], self.mine_ref, local_sem.at[3]),
        ]
        self.rows_load = pltpu.make_async_copy(self.rows_ref, self.rows_in_ref, local_sem.at[4])
        self.g_loads = [
            pltpu.make_async_copy(
                self.g_out_ref.at[r, lax.rem(x + k, 2) * 2 + mine], self.g_in_ref.at[k, r], local_sem.at[5 + 4 * k + r]
            )
            for k in range(2)
            for r in range(4)
        ]

    def first(self):
        row = self.row
        self.rows_load.start()
        for c in self.loads + self.g_loads:
            c.start()
        greet(self.partners)
        for c in self.diag + self.far[:2] + self.cores:
            c.start()
        self.rows_load.wait()
        hop = self.hop_ref[...].astype(F32)
        ahead = self.rows_in_ref[jnp.minimum(row + 2, 3)].astype(F32)
        self.right_ref[0] = jnp.where(row == 1, ahead + hop, ahead).astype(BF)
        behind = self.rows_in_ref[jnp.maximum(row - 2, 0)].astype(F32)
        self.left_ref[0] = jnp.where(row == 2, behind + hop, behind).astype(BF)
        pl.when(row <= 1)(self.hop_right[0].start)
        pl.when(row >= 2)(self.hop_left[0].start)

    def cross_x(self):
        for c in self.g_loads:
            c.wait()
        for c in self.cores:
            c.wait_recv()
        for r in range(4):
            self.side_ref[r] = (
                self.g_in_ref[1, r].astype(F32) + self.near_ref[1 - self.x, r].astype(F32)
            ).astype(BF)
            self.sides[r].start()

    def second(self):
        row = self.row
        for c in self.loads:
            c.wait()
        for k in range(2):
            self.diag[k].wait_recv()
            self.relay_ref[k] = (self.pieces_ref[k].astype(F32) + self.diag_ref[k].astype(F32)).astype(BF)
            self.far[2 + k].start()

    def last_hop(self):
        row = self.row
        middle = jnp.logical_and(row >= 1, row <= 2)
        pl.when(middle)(self.hop_right[0].wait_recv)
        pl.when(middle)(self.hop_left[0].wait_recv)
        ahead = self.rows_in_ref[jnp.minimum(row + 1, 3)].astype(F32)
        behind = self.rows_in_ref[jnp.maximum(row - 1, 0)].astype(F32)
        self.right_ref[1] = jnp.where(row >= 1, ahead + self.got_ref[0].astype(F32), ahead).astype(BF)
        self.left_ref[1] = jnp.where(row <= 2, behind + self.got_ref[1].astype(F32), behind).astype(BF)
        pl.when(row <= 2)(self.hop_right[1].start)
        pl.when(row >= 1)(self.hop_left[1].start)

    def third(self):
        row = self.row
        for c in self.far:
            c.wait_recv()
        feat = self.send_ref.shape[2]
        for c in range(4):
            lanes = slice(c * feat, (c + 1) * feat)
            self.send_ref[c] = (
                self.mixed_ref[:, lanes]
                + self.mine_ref[:, lanes].astype(F32)
                + self.far_ref[0, :, lanes].astype(F32)
                + self.far_ref[1, :, lanes].astype(F32)
            ).astype(BF)
        for c in self.out:
            c.start()
        self.own.start()

    def last(self):
        row = self.row
        for r in range(4):
            self.sides[r].wait_recv()
            self.part_ref[r] = (
                self.g_in_ref[0, r].astype(F32)
                + self.near_ref[self.x, r].astype(F32)
                + self.across_ref[r].astype(F32)
            ).astype(BF)
        for c in self.out:
            c.wait()
        self.own.wait()
        for c in self.diag + self.far + self.cores + self.sides:
            c.wait_send()
        pl.when(row <= 1)(self.hop_right[0].wait_send)
        pl.when(row >= 2)(self.hop_left[0].wait_send)
        pl.when(row <= 2)(self.hop_right[1].wait_send)
        pl.when(row >= 1)(self.hop_left[1].wait_send)
        pl.when(row >= 1)(self.hop_right[1].wait_recv)
        pl.when(row <= 2)(self.hop_left[1].wait_recv)


def first_norm(x_ref, gain_ref, h_ref):
    parts = x_ref.shape[0]
    feat = x_ref.shape[2]
    xs = [x_ref[c].astype(F32) for c in range(parts)]
    total = sum(jnp.sum(v * v, axis=1, keepdims=True) for v in xs)
    scale = lax.rsqrt(total / D + EPS)
    for c in range(parts):
        lanes = slice(c * feat, (c + 1) * feat)
        h_ref[:, lanes] = (xs[c] * scale * gain_ref[c, :1]).astype(BF)


def place_factor_weights(blocks_ref, w_ref):
    n_row, parts, _, feat = blocks_ref.shape
    ranks_each = RANK_COLS // n_row
    for c in range(parts):
        lanes = slice(c * feat, (c + 1) * feat)
        for r in range(n_row):
            w_ref[r * ranks_each : (r + 1) * ranks_each, lanes] = blocks_ref[r, c, :ranks_each]
            w_ref[RANK_COLS + r * GROUP_COLS : RANK_COLS + (r + 1) * GROUP_COLS, lanes] = blocks_ref[
                r, c, ranks_each:
            ]


def make_factors(h_ref, w_ref, turn_ref, hf_ref, bq_ref, kf_ref):
    both = nt(h_ref[...], w_ref[...])
    heads = both[:, RANK_COLS:]
    hf_ref[...] = heads
    cosine = turn_ref[:, :LANES]
    sine = turn_ref[:, LANES:]
    for tile in range(RANK_COLS // LANES):
        lanes = slice(tile * LANES, (tile + 1) * LANES)
        part = both[:, lanes]
        if tile < 4:
            part = part * cosine + swap_halves(part) * sine
        if tile < 3:
            bq_ref[:, lanes] = part
        else:
            kf_ref[:, (tile - 3) * LANES : (tile - 2) * LANES] = part.astype(BF)
    kf_ref[:, 2 * LANES :] = nn(heads.astype(BF), key_columns()).astype(BF)


def make_queries(hf_ref, bq_ref, q_ref):
    heads = hf_ref[...]
    high = heads.astype(BF)
    low = (heads - high.astype(F32)).astype(BF)
    ranks = []
    for r in range(RQ):
        tile = bq_ref[:, (r // 2) * LANES : (r // 2 + 1) * LANES]
        ranks.append(double_left(tile) if r % 2 == 0 else double_right(tile))
    width = 2 * LANES
    for p in range(D // width):
        lanes = slice(p * width, (p + 1) * width)
        acc = None
        for r in range(RQ):
            pick = head_spread(2 * RK + r, p * (width // HD), width)
            term = (nn(high, pick) + nn(low, pick)) * jnp.concatenate([ranks[r]] * 2, axis=1)
            acc = term if acc is None else acc + term
        q_ref[:, lanes] = (acc / RQ).astype(BF)


def front_body(x_ref, gain_ref, blocks_ref, turn_ref, h_ref, hf_ref, bq_ref, kf_ref, q_ref, w_ref):
    first_norm(x_ref, gain_ref, h_ref)
    place_factor_weights(blocks_ref, w_ref)
    make_factors(h_ref, w_ref, turn_ref, hf_ref, bq_ref, kf_ref)
    make_queries(hf_ref, bq_ref, q_ref)


def front(x_parts, gains, blocks, turn):
    rows = x_parts.shape[1]
    return call(
        front_body,
        (
            jax.ShapeDtypeStruct((rows, D), BF),
            jax.ShapeDtypeStruct((rows, HEAD_COLS), F32),
            jax.ShapeDtypeStruct((rows, RQ * HD), F32),
            jax.ShapeDtypeStruct((rows, 3 * LANES), BF),
            jax.ShapeDtypeStruct((rows, D), BF),
            jax.ShapeDtypeStruct((ALL_COLS, D), BF),
        ),
        cost=cost_of(2 * rows * D * 800 * 3, 6 << 20),
    )(x_parts, gains, blocks, turn)


def head_body(
    tok_ref, ranks_ref, heads_ref, gain_one_ref, gain_two_ref, gate_ref, up_ref, down_ref, mix_ref, seg_all_ref,
    inverse_ref,
    x_ref, gains_ref, parts_ref, mixes_ref, h_ref, hf_ref, bq_ref, q_ref, w_ref, win_ref, seg_ref, turn_ref, rows_ref,
    w_own_ref, gain_ref, ffn_ref, blocks_ref, send_sem, recv_sem,
):
    row = lax.axis_index("row")
    col, core, across = neighbours()
    cross = lax.rem(core + 2, 4)
    side = lax.rem(col, 2)
    rows = [lax.rem(row + k, 4) for k in range(4)]
    back = [lax.rem(row + 4 - k, 4) for k in range(4)]
    dp = lax.axis_index("dp")

    rank_rows = ranks_ref.shape[0]
    place = lax.broadcasted_iota(jnp.int32, (GROUP_COLS, FAC * GROUP), 0)
    lane = lax.broadcasted_iota(jnp.int32, (GROUP_COLS, FAC * GROUP), 1)
    factor = lane % FAC
    spot = jnp.where(factor < RQ, factor + 2 * RK, factor - RQ) * GROUP + lane // FAC
    w_own_ref[:rank_rows] = ranks_ref[...]
    w_own_ref[rank_rows:] = nn((place == spot).astype(F32).astype(BF), heads_ref[...]).astype(BF)
    gain_ref[...] = jnp.zeros_like(gain_ref)
    gain_ref[0:1] = gain_one_ref[...]
    gain_ref[1:2] = gain_two_ref[...]
    greet(
        [(None, {"col": c}) for c in (core, across, cross)]
        + [(None, {"row": r}) for r in rows[1:]]
        + [(None, {"dp": 1 - dp})]
    )
    mover = Mover(send_sem, recv_sem)
    started = []

    def go(source, target, **place):
        c = mover.copy(source, target, **place)
        c.start()
        started.append(c)
        return c

    down = [None] + [go(w_own_ref, blocks_ref.at[row, col], row=rows[k]) for k in range(1, 4)]
    sides = [go(w_own_ref, blocks_ref.at[row, col], col=across)]
    cores = [go(w_own_ref, blocks_ref.at[row, col], col=core)]
    toks = []
    rest = []
    for c in (across, cross, core):
        toks.append(go(gain_ref, gains_ref.at[col], col=c))
        toks.append(go(tok_ref.at[c], x_ref.at[col], col=c))
    units = ffn_ref.shape[2]
    hidden = gate_ref.shape[0]
    unit = hidden // 8
    place = lax.broadcasted_iota(jnp.int32, (4 * units, hidden), 0)
    lane = lax.broadcasted_iota(jnp.int32, (4 * units, hidden), 1)
    inside = place % units
    taken = (inside < unit) & (lane == (dp * 4 + place // units) * unit + inside)
    pick = taken.astype(F32).astype(BF)
    for k, source in enumerate((gate_ref, up_ref, down_ref)):
        chosen = nn(pick, source[...]).astype(BF)
        for c in range(4):
            ffn_ref[c, k] = chosen[c * units : (c + 1) * units]
    ffn = [go(ffn_ref.at[c], parts_ref.at[col], col=c) for c in (across, cross, core)]
    part = mix_ref.shape[0] // 2
    half = pl.ds(pl.multiple_of(dp * part, part), part)
    mix_down = [None] + [go(mix_ref.at[half], mixes_ref.at[row, col, half], row=rows[k]) for k in range(1, 4)]
    blocks_ref[row, col] = w_own_ref[...]
    gains_ref[col] = gain_ref[...]
    x_ref[col] = tok_ref[col]
    parts_ref[col] = ffn_ref[col]
    mixes_ref[row, col] = mix_ref[...]
    zero = jnp.zeros(win_ref.shape[1:], BF)
    has_one = row >= 1
    has_two = row >= 2
    for absent, slot in (
        (jnp.logical_not(has_two), 0),
        (jnp.logical_and(jnp.logical_not(has_two), side == 0), 1),
        (jnp.logical_and(jnp.logical_not(has_one), side == 1), 1),
        (jnp.logical_not(has_one), 2),
        (jnp.logical_and(jnp.logical_not(has_one), side == 0), 3),
    ):

        @pl.when(absent)
        def _():
            win_ref[slot] = zero

    keys = seg_ref.shape[1]
    tokens = tok_ref.shape[1]
    block_no = row * 2 + side
    for slot in range(5):
        index = block_no - 4 + slot
        lanes = pl.ds(pl.multiple_of(jnp.maximum(index, 0) * tokens, tokens), tokens)
        seg_ref[:, slot * tokens : (slot + 1) * tokens] = jnp.where(index >= 0, seg_all_ref[col // 2, :, lanes], -1)
    seg_row = seg_ref[...].astype(F32)
    column = jnp.broadcast_to(seg_row, (LANES, keys)).T
    column = jnp.concatenate([column] * (tokens // LANES), axis=1)
    key_idx = lax.broadcasted_iota(jnp.int32, (keys, tokens), 0)
    query_idx = lax.broadcasted_iota(jnp.int32, (keys, tokens), 1) + (keys - tokens)
    before = (column == seg_row[:, keys - tokens :]) & (key_idx < query_idx)
    places = jnp.sum(jnp.where(before, 1.0, 0.0), axis=0, keepdims=True)
    angles = jnp.broadcast_to(places, (LANES, tokens)).T * inverse_ref[...]
    turn_ref[:, :LANES] = jnp.cos(angles)
    sine = jnp.sin(angles)
    turn_ref[:, LANES:] = jnp.where(lane_iota(sine.shape) % HD < HD // 2, -sine, sine)

    for k in range(1, 4):
        down[k].wait_recv()
        block = blocks_ref.at[back[k], col]
        sides.append(go(block, block, col=across))
        cores.append(go(block, block, col=core))
    for c in toks:
        c.wait_recv()
    first_norm(x_ref, gains_ref, h_ref)
    mix_side = []
    for k in range(1, 4):
        mix_down[k].wait_recv()
        block = mixes_ref.at[back[k], col, half]
        mix_side.append(go(block, block, dp=1 - dp))
    for c in ffn:
        c.wait_recv()
    to_right = mover.copy(parts_ref, rows_ref.at[row], row=row + 1)
    to_left = mover.copy(parts_ref, rows_ref.at[row], row=row - 1)
    pl.when(row <= 2)(to_right.start)
    pl.when(row >= 1)(to_left.start)
    passed = []
    for k in range(4):
        sides[k].wait_recv()
        block = blocks_ref.at[back[k], across]
        passed.append(go(block, block, col=core))
    for c in cores + passed:
        c.wait_recv()
    for k in range(4):
        if k > 0:
            mix_side[k - 1].wait_recv()
        block = mixes_ref.at[back[k], col]
        rest.append(go(block, block, col=across))
    place_factor_weights(blocks_ref, w_ref)
    make_factors(h_ref, w_ref, turn_ref, hf_ref, bq_ref, win_ref.at[4])

    own = win_ref.at[4]
    one = mover.copy(own, win_ref.at[2], row=row + 1)
    two = mover.copy(win_ref.at[2], win_ref.at[0], row=row + 1)
    near = mover.copy(own, win_ref.at[3], col=core)
    pass_one = mover.copy(win_ref.at[2], win_ref.at[1 + 2 * side], col=core)
    pass_two = mover.copy(win_ref.at[0], win_ref.at[1], col=core)
    hands_on = jnp.logical_and(has_one, row <= 2)
    sends_two = jnp.logical_and(has_two, side == 1)
    takes_two = jnp.logical_and(has_two, side == 0)
    pl.when(row <= 2)(one.start)
    pl.when(side == 0)(near.start)

    @pl.when(has_one)
    def _():
        one.wait_recv()
        pass_one.start()

    pl.when(hands_on)(two.start)
    make_queries(hf_ref, bq_ref, q_ref)

    @pl.when(has_two)
    def _():
        two.wait_recv()

    pl.when(sends_two)(pass_two.start)

    @pl.when(has_one)
    def _():
        pass_one.wait_recv()
        pass_one.wait_send()

    pl.when(takes_two)(pass_two.wait_recv)
    pl.when(sends_two)(pass_two.wait_send)
    pl.when(side == 1)(near.wait_recv)
    pl.when(side == 0)(near.wait_send)
    pl.when(row <= 2)(one.wait_send)
    pl.when(hands_on)(two.wait_send)
    pl.when(row <= 2)(to_right.wait_send)
    pl.when(row >= 1)(to_left.wait_send)
    pl.when(row >= 1)(to_right.wait_recv)
    pl.when(row <= 2)(to_left.wait_recv)
    for c in rest:
        c.wait_recv()
    for c in started:
        c.wait_send()


def head(tok, ranks_t, heads_t, gain_one, gain_two, gate_t, up_t, down, w_out, segments, inverse):
    rows, feat = tok.shape[1:]
    units = -(-gate_t.shape[0] // 8 // 16) * 16
    block = (ranks_t.shape[0] + GROUP_COLS, feat)
    ffn = (4, 3, units, feat)
    count = 3 + 4 + 4 + 6 + 3 + 3 + 3 + 4 + 4 + 2 + 5
    return pl.pallas_call(
        head_body,
        out_shape=(
            jax.ShapeDtypeStruct(tok.shape, BF),
            jax.ShapeDtypeStruct((4, 8, feat), F32),
            jax.ShapeDtypeStruct(ffn, BF),
            jax.ShapeDtypeStruct((4, 4) + w_out.shape, BF),
            jax.ShapeDtypeStruct((rows, D), BF),
            jax.ShapeDtypeStruct((rows, HEAD_COLS), F32),
            jax.ShapeDtypeStruct((rows, RQ * HD), F32),
            jax.ShapeDtypeStruct((rows, D), BF),
            jax.ShapeDtypeStruct((ALL_COLS, D), BF),
            jax.ShapeDtypeStruct((5, rows, 3 * LANES), BF),
            jax.ShapeDtypeStruct((1, 5 * rows), jnp.int32),
            jax.ShapeDtypeStruct((rows, 2 * LANES), F32),
            jax.ShapeDtypeStruct((4,) + ffn, BF),
        ),
        in_specs=[VMEM] * 11,
        out_specs=(VMEM,) * 12 + (ANY,),
        scratch_shapes=[
            pltpu.VMEM(block, BF),
            pltpu.VMEM((8, feat), F32),
            pltpu.VMEM(ffn, BF),
            pltpu.VMEM((4, 4) + block, BF),
            pltpu.SemaphoreType.DMA((count,)),
            pltpu.SemaphoreType.DMA((count,)),
        ],
        compiler_params=comm_params(1),
        cost_estimate=cost_of(2 * rows * D * 800 * 3, 14 << 20),
    )(tok, ranks_t, heads_t, gain_one, gain_two, gate_t, up_t, down, w_out, segments, inverse)


def mask_bias(seg_ref, keys, rows):
    seg_row = seg_ref[...].astype(F32)
    wide = jnp.broadcast_to(seg_row, (LANES, keys))
    column = wide.T
    column = jnp.concatenate([column] * (rows // LANES), axis=1)
    key_idx = lax.broadcasted_iota(jnp.int32, (keys, rows), 0)
    query_idx = lax.broadcasted_iota(jnp.int32, (keys, rows), 1) + (keys - rows)
    same = column == seg_row[:, keys - rows :]
    return jnp.where(same & (key_idx <= query_idx), 0.0, NEG)


def attend_body(fast, q_ref, kf_ref, seg_ref, *refs):
    if fast:
        _, cot_ref, _, o_ref, lse_ref, k_ref, v_ref, w_rows_ref, cot_near_ref, mixes_ref = refs[:10]
        bias_ref, dup_ref, send_sem, recv_sem = refs[10:]
        side_work = AttendCopies(cot_ref, w_rows_ref, cot_near_ref, mixes_ref, send_sem, recv_sem)
        side_work.first()
    else:
        o_ref, lse_ref, k_ref, v_ref, bias_ref, dup_ref = refs
    rows = q_ref.shape[0]
    keys = kf_ref.shape[0]
    bias_ref[...] = mask_bias(seg_ref, keys, rows)
    for s in range(2 * RK):
        tile = kf_ref[:, (s // 2) * LANES : (s // 2 + 1) * LANES].astype(F32)
        dup_ref[s] = double_left(tile) if s % 2 == 0 else double_right(tile)

    def pair(p, carried):
        if fast:
            pl.when(p == 2)(lambda: side_work.hand_on(0))
            pl.when(p == 4)(side_work.second)
        lanes = pl.ds(pl.multiple_of(p * LANES, LANES), LANES)
        weights = kf_ref[:, 2 * LANES :]
        made = []
        for kind in range(2):
            acc = None
            for s in range(RK):
                pick = spread(LANES, (kind * RK + s) * H + 2 * p, LANES)
                term = nn(weights, pick) * dup_ref[kind * RK + s]
                acc = term if acc is None else acc + term
            made.append((acc / RK).astype(BF))
        k_tile, v_tile = made
        k_ref[:, lanes] = k_tile
        v_ref[:, lanes] = v_tile
        v_turned = v_tile.astype(F32).T.astype(BF)
        q_turned = (q_ref[:, lanes].astype(F32) * HD**-0.5).T
        half = lax.broadcasted_iota(jnp.int32, q_turned.shape, 0) // HD
        outs = []
        for side in range(2):
            q_side = jnp.where(half == side, q_turned, 0.0).astype(BF)
            scores = nn(k_tile, q_side) + bias_ref[...]
            peak = jnp.max(scores, axis=0, keepdims=True)
            weight = jnp.exp(scores - peak)
            total = jnp.sum(weight, axis=0, keepdims=True)
            probs = (weight * (1.0 / total)).astype(BF)
            outs.append(nn(v_turned[side * HD : (side + 1) * HD], probs))
            lse_ref[2 * p + side] = jnp.broadcast_to(peak + jnp.log(total), (8, rows))
        o_ref[:, lanes] = jnp.concatenate(outs, axis=0).T.astype(BF)
        return carried

    lax.fori_loop(0, PAIRS, pair, 0)
    if fast:
        side_work.last()


def attend(q, kf_window, seg_window, w_rows=None, cot=None, mixes=None):
    rows = q.shape[0]
    keys = kf_window.shape[0]
    fast = w_rows is not None
    outs = [
        jax.ShapeDtypeStruct((rows, D), BF),
        jax.ShapeDtypeStruct((H, 8, rows), F32),
        jax.ShapeDtypeStruct((keys, D), BF),
        jax.ShapeDtypeStruct((keys, D), BF),
    ]
    scratch = [pltpu.VMEM((keys, rows), F32), pltpu.VMEM((2 * RK, keys, LANES), F32)]
    in_specs, out_specs, more = [VMEM] * 3, [VMEM] * 4, []
    if fast:
        outs += [
            jax.ShapeDtypeStruct(w_rows.shape, BF),
            jax.ShapeDtypeStruct((4,) + cot.shape, BF),
            jax.ShapeDtypeStruct(mixes.shape, BF),
        ]
        in_specs += [ANY] * 3
        out_specs += [ANY] * 3
        more = [w_rows, cot, mixes]
        scratch += [
            pltpu.SemaphoreType.DMA((22,)),
            pltpu.SemaphoreType.DMA((22,)),
        ]
    return pl.pallas_call(
        functools.partial(attend_body, fast),
        out_shape=tuple(outs),
        in_specs=in_specs,
        out_specs=tuple(out_specs),
        scratch_shapes=scratch,
        input_output_aliases={3: 4, 5: 6} if fast else {},
        compiler_params=comm_params(3) if fast else params(),
        cost_estimate=cost_of(2 * rows * keys * D * 16, 16 << 20),
    )(q, kf_window, seg_window, *more)


def attend_back_body(fast, q_ref, k_ref, v_ref, do_ref, lse_ref, kf_ref, seg_ref, *refs):
    if fast:
        dq_ref, dkf_ref = refs[5:7]
        bias_ref, dup_ref, sum_ref, fac_ref = refs[10:14]
        side_work = BackCopies(refs[:5] + refs[7:10] + refs[14:28], refs[28:])
        side_work.first()
    else:
        dq_ref, dkf_ref, bias_ref, dup_ref, sum_ref, fac_ref = refs
    rows = q_ref.shape[0]
    keys = kf_ref.shape[0]
    bias_ref[...] = mask_bias(seg_ref, keys, rows)
    for s in range(2 * RK):
        tile = kf_ref[:, (s // 2) * LANES : (s // 2 + 1) * LANES].astype(F32)
        dup_ref[s] = double_left(tile) if s % 2 == 0 else double_right(tile)
    sum_ref[...] = jnp.zeros_like(sum_ref)
    fac_ref[...] = jnp.zeros_like(fac_ref)

    def pair(p, carried):
        if fast:
            pl.when(p == 1)(side_work.cross_x)
            pl.when(p == 3)(side_work.second)
            pl.when(p == 4)(side_work.last_hop)
            pl.when(p == 6)(side_work.third)
        lanes = pl.ds(pl.multiple_of(p * LANES, LANES), LANES)
        k_tile = k_ref[:, lanes]
        v_tile = v_ref[:, lanes]
        k_turned = k_tile.astype(F32).T.astype(BF)
        q_tile = q_ref[:, lanes].astype(F32) * HD**-0.5
        do_tile = do_ref[:, lanes].astype(F32)
        q_turned = q_tile.T
        do_turned = do_tile.T
        half = lax.broadcasted_iota(jnp.int32, q_turned.shape, 0) // HD
        lane_half = lax.broadcasted_iota(jnp.int32, q_tile.shape, 1) // HD
        d_k = None
        d_v = None
        d_q = []
        for side in range(2):
            q_side = jnp.where(half == side, q_turned, 0.0).astype(BF)
            do_side = jnp.where(half == side, do_turned, 0.0).astype(BF)
            scores = nn(k_tile, q_side) + bias_ref[...]
            probs = jnp.exp(scores - lse_ref[2 * p + side][:1])
            d_prob = nn(v_tile, do_side)
            delta = jnp.sum(probs * d_prob, axis=0, keepdims=True)
            d_score = (probs * (d_prob - delta)).astype(BF)
            d_q.append(nn(k_turned[side * HD : (side + 1) * HD], d_score))
            q_back = jnp.where(lane_half == side, q_tile, 0.0).astype(BF)
            do_back = jnp.where(lane_half == side, do_tile, 0.0).astype(BF)
            part_k = nn(d_score, q_back)
            part_v = nn(probs.astype(BF), do_back)
            d_k = part_k if d_k is None else d_k + part_k
            d_v = part_v if d_v is None else d_v + part_v
        dq_ref[:, lanes] = jnp.concatenate(d_q, axis=0).T * HD**-0.5
        weights = kf_ref[:, 2 * LANES :]
        for kind, grad in ((0, d_k), (1, d_v)):
            for s in range(RK):
                slot = kind * RK + s
                pick = spread(LANES, slot * H + 2 * p, LANES)
                sum_ref[slot] += nn(weights, pick) * grad
                fac_ref[...] += two_pass(grad * dup_ref[slot], collect(LANES, LANES, slot * H + 2 * p))
        return carried

    lax.fori_loop(0, PAIRS, pair, 0)
    for tile in range(2):
        first = sum_ref[2 * tile]
        second = sum_ref[2 * tile + 1]
        first = first + pltpu.roll(first, HD, 1)
        second = second + pltpu.roll(second, HD, 1)
        merged = jnp.where(lane_iota(first.shape) < HD, first, second)
        dkf_ref[:, tile * LANES : (tile + 1) * LANES] = (merged / RK).astype(BF)
    dkf_ref[:, 2 * LANES :] = (fac_ref[...] / RK).astype(BF)
    if fast:
        side_work.last()


def attend_back(q, k, v, d_heads, lse, kf_window, seg_window, *more):
    rows = q.shape[0]
    keys = kf_window.shape[0]
    fast = len(more) > 0
    outs = [jax.ShapeDtypeStruct((rows, D), F32), jax.ShapeDtypeStruct(kf_window.shape, BF)]
    scratch = [
        pltpu.VMEM((keys, rows), F32),
        pltpu.VMEM((2 * RK, keys, LANES), F32),
        pltpu.VMEM((2 * RK, keys, LANES), F32),
        pltpu.VMEM((keys, LANES), F32),
    ]
    in_specs, out_specs = [VMEM] * 7, [VMEM] * 2
    if fast:
        in_specs += [ANY, VMEM, ANY, ANY, VMEM]
        grads, g_out = more[2], more[3]
        parts, feat = g_out.shape[1], g_out.shape[3]
        block, hop = g_out.shape[2:], grads.shape[1:]
        outs += [
            jax.ShapeDtypeStruct((parts, rows, feat), BF),
            jax.ShapeDtypeStruct((2,) + hop, BF),
            jax.ShapeDtypeStruct((4,) + block, BF),
        ]
        out_specs += [ANY, ANY, VMEM]
        scratch += [
            pltpu.VMEM((2, rows // 2, D), BF),
            pltpu.VMEM((2, rows // 2, D), BF),
            pltpu.VMEM((2, rows, D), BF),
            pltpu.VMEM((parts, rows, feat), BF),
            pltpu.VMEM((2,) + hop, BF),
            pltpu.VMEM((2,) + hop, BF),
            pltpu.VMEM((2,) + hop, BF),
            pltpu.VMEM((2, 4) + block, BF),
            pltpu.VMEM((4,) + block, BF),
            pltpu.VMEM((4,) + block, BF),
            pltpu.VMEM((2, rows // 2, D), BF),
            pltpu.VMEM((rows, D), BF),
            pltpu.VMEM(grads.shape, BF),
            pltpu.VMEM((2, 4) + block, BF),
            pltpu.SemaphoreType.DMA((25,)),
            pltpu.SemaphoreType.DMA((25,)),
            pltpu.SemaphoreType.DMA((13,)),
        ]
    return pl.pallas_call(
        functools.partial(attend_back_body, fast),
        out_shape=tuple(outs),
        in_specs=in_specs,
        out_specs=tuple(out_specs),
        scratch_shapes=scratch,
        compiler_params=comm_params(6) if fast else params(),
        cost_estimate=cost_of(2 * rows * keys * D * 40, 16 << 20),
    )(q, k, v, d_heads, lse, kf_window, seg_window, *more)


def mixing_body(x_ref, heads_ref, w_out_ref, gain_ref, mixed_ref, h_ref):
    parts, _, feat = x_ref.shape
    rows_of = w_out_ref.shape[0]
    head_rows = w_out_ref.shape[2]
    total = None
    for c in range(parts):
        lanes = slice(c * feat, (c + 1) * feat)
        acc = x_ref[c].astype(F32)
        for r in range(rows_of):
            acc = acc + nn(heads_ref[:, r * head_rows : (r + 1) * head_rows], w_out_ref[r, c])
        mixed_ref[:, lanes] = acc
        part = jnp.sum(acc * acc, axis=1, keepdims=True)
        total = part if total is None else total + part
    scale = lax.rsqrt(total / D + EPS)
    for c in range(parts):
        lanes = slice(c * feat, (c + 1) * feat)
        h_ref[:, lanes] = (mixed_ref[:, lanes] * scale * gain_ref[c, 1:2]).astype(BF)


def mixing(x_parts, heads, w_out, gains):
    rows = heads.shape[0]
    return call(
        mixing_body,
        (jax.ShapeDtypeStruct((rows, D), F32), jax.ShapeDtypeStruct((rows, D), BF)),
        cost=cost_of(2 * rows * D * D, 5 << 20),
    )(x_parts, heads, w_out, gains)


def ffn_steps(blocks, h_at, cot_at, w_ref, hid_ref, dg_ref, du_ref, out_at, back_at):
    def block(t, carried):
        h = h_at(t)[...]
        gate = nt(h, w_ref[0])
        up = nt(h, w_ref[1])
        d_hidden = nt(cot_at(t)[...], w_ref[2])
        sig = 1.0 / (1.0 + jnp.exp(-gate))
        silu = gate * sig
        hidden = (silu * up).astype(BF)
        d_gate = (d_hidden * up * sig * (1.0 + gate * (1.0 - sig))).astype(BF)
        d_up = (d_hidden * silu).astype(BF)
        rows = h.shape[0]
        place = pl.ds(pl.multiple_of(t * rows, rows), rows)
        hid_ref[place] = hidden
        dg_ref[place] = d_gate
        du_ref[place] = d_up
        out_at(t)[...] = nn(hidden, w_ref[2]).astype(BF)
        back_at(t)[...] = (nn(d_gate, w_ref[0]) + nn(d_up, w_ref[1])).astype(BF)
        return carried

    lax.fori_loop(0, blocks, block, 0)


def ffn_body(h_ref, cot_ref, w_ref, out_ref, back_ref, g_ref, hid_ref, dg_ref, du_ref):
    parts, rows, _ = h_ref.shape
    ffn_steps(
        parts, lambda t: h_ref.at[t], lambda t: cot_ref.at[t], w_ref, hid_ref, dg_ref, du_ref,
        lambda t: out_ref.at[t], lambda t: back_ref.at[t],
    )
    h_all = h_ref[...].reshape(parts * rows, D)
    cot_all = cot_ref[...].reshape(parts * rows, D)
    for place, (left, right) in enumerate(((dg_ref, h_all), (du_ref, h_all), (hid_ref, cot_all))):
        g_ref[place] = tn(left[...], right).astype(BF)


def ffn(h_all, cot_all, w):
    parts, rows, _ = h_all.shape
    units = w.shape[1]
    return call(
        ffn_body,
        (
            jax.ShapeDtypeStruct(h_all.shape, BF),
            jax.ShapeDtypeStruct(h_all.shape, BF),
            jax.ShapeDtypeStruct(w.shape, BF),
        ),
        scratch=[pltpu.VMEM((parts * rows, units), BF)] * 3,
        cost=cost_of(2 * parts * rows * 9 * D * units, 20 << 20),
    )(h_all, cot_all, w)


def unmix_math(
    mixed_ref, cot_ref, d_h, heads_ref, w_out_ref, gain_ref, d_mixed_ref, d_heads_ref, g_out_ref, g_gain_ref
):
    rows_of, parts, head_rows, feat = w_out_ref.shape
    mixed = mixed_ref[...]
    scale = lax.rsqrt(jnp.sum(mixed * mixed, axis=1, keepdims=True) / D + EPS)
    normed = mixed * scale
    g_gain_ref[...] = jnp.sum(d_h * normed, axis=0, keepdims=True)
    gain = jnp.concatenate([gain_ref[c, 1:2] for c in range(parts)], axis=1)
    inner = d_h * gain
    dot = jnp.sum(inner * normed, axis=1, keepdims=True) / D
    d_mixed = cot_ref[...].astype(F32) + scale * (inner - normed * dot)
    d_mixed_ref[...] = d_mixed
    low = d_mixed.astype(BF)
    grad = tn(heads_ref[...], low)
    for r in range(rows_of):
        acc = None
        for c in range(parts):
            lanes = slice(c * feat, (c + 1) * feat)
            term = nt(low[:, lanes], w_out_ref[r, c])
            acc = term if acc is None else acc + term
            g_out_ref[r, c] = grad[r * head_rows : (r + 1) * head_rows, lanes].astype(BF)
        d_heads_ref[:, r * head_rows : (r + 1) * head_rows] = acc.astype(BF)


def write_output(mixed_ref, total, out_ref):
    parts, _, feat = out_ref.shape
    for c in range(parts):
        lanes = slice(c * feat, (c + 1) * feat)
        out_ref[c] = (mixed_ref[:, lanes] + total[:, lanes]).astype(BF)


def unmix_body(
    dh_ref, sum_ref, mixed_ref, cot_ref, heads_ref, w_out_ref, gain_ref,
    out_ref, d_mixed_ref, d_heads_ref, g_out_ref, g_gain_ref,
):
    unmix_math(
        mixed_ref, cot_ref, dh_ref[...], heads_ref, w_out_ref, gain_ref,
        d_mixed_ref, d_heads_ref, g_out_ref, g_gain_ref,
    )
    write_output(mixed_ref, sum_ref[...], out_ref)


def middle_body(
    x_ref, heads_ref, w_out_ref, gain_ref, cot_own_ref, cot_in_ref, w_own_ref, rows_ref,
    mixed_ref, d_mixed_ref, d_heads_ref, g_out_ref, g_gain_ref, g_ref, out_pair_ref, hop_ref,
    w_ref, h_ref, cot_ref, hid_ref, dg_ref, du_ref, back_ref, fwd_ref, back_got_ref, fwd_got_ref,
    pair_ref, diag_ref, far_ref, send_sem, recv_sem, w_sem, cot_sem,
):
    row = lax.axis_index("row")
    col, core, across = neighbours()
    dp, (me, on_x, on_y, on_both) = square()
    x, mine = col // 2, lax.rem(col, 2)
    y = 1 - dp
    parts, rows, feat = x_ref.shape
    units = rows_ref.shape[3]
    greet(
        [
            (None, {"col": core}),
            (None, {"col": across}),
            (None, {"dp": y}),
            (row <= 2, {"row": row + 1}),
            (row >= 1, {"row": row - 1}),
        ]
    )
    mover = Mover(send_sem, recv_sem)

    def w_place(r, c):
        return w_ref.at[:, pl.ds(pl.multiple_of(r * units, units), units), pl.ds(c * feat, feat)]

    local = []
    for k in range(4):
        r = lax.rem(row + k, 4)
        for c in range(4):
            source = w_own_ref.at[c] if k == 0 else rows_ref.at[r, c]
            copy = pltpu.make_async_copy(source, w_place(r, c), w_sem.at[k, c])
            copy.start()
            local.append(copy)
    cots = []
    for k in range(4):
        from_x = lax.rem(x + k % 2, 2)
        from_dp = lax.rem(dp + k // 2, 2)
        lanes = pl.ds(pl.multiple_of((from_x * 2 + mine) * feat, feat), feat)
        for c in range(4):
            part = pl.ds(c * rows, rows)
            source = cot_own_ref.at[part] if k == 0 else cot_in_ref.at[from_dp * 2 + from_x, part]
            spot = from_dp * 2 + c // 2
            copy = pltpu.make_async_copy(source, cot_ref.at[lax.rem(mine + c, 2), spot, :, lanes], cot_sem.at[k, c])
            copy.start()
            local.append(copy)
            sent = mover.copy(source, cot_ref.at[lax.rem(mine + c + 1, 2), spot, :, lanes], col=core)
            sent.start()
            cots.append(sent)

    total = None
    for c in range(parts):
        lanes = slice(c * feat, (c + 1) * feat)
        acc = x_ref[c].astype(F32)
        for r in range(4):
            acc = acc + nn(heads_ref[:, r * feat : (r + 1) * feat], w_out_ref[r, c])
        mixed_ref[:, lanes] = acc
        part = jnp.sum(acc * acc, axis=1, keepdims=True)
        total = part if total is None else total + part
    scale = lax.rsqrt(total / D + EPS)
    for c in range(parts):
        lanes = slice(c * feat, (c + 1) * feat)
        h_ref[0, me, :, lanes] = (mixed_ref[:, lanes] * scale * gain_ref[c, 1:2]).astype(BF)

    half = rows // 2
    top, low = pl.ds(0, half), pl.ds(half, half)

    def h_copy(spot, part=None, side=0, **place):
        source = h_ref.at[0, spot] if part is None else h_ref.at[0, spot, part]
        target = h_ref.at[side, spot] if part is None else h_ref.at[side, spot, part]
        return mover.copy(source, target, **place)

    x_low = h_copy(me, low, col=across)
    y_top = h_copy(me, top, dp=y)
    x_top = h_copy(me, top, col=across)
    y_low = h_copy(me, low, dp=y)
    near = h_copy(me, None, 1, col=core)
    both_low = h_copy(on_x, low, dp=y)
    both_top = h_copy(on_y, top, col=across)
    near_first = [h_copy(on_x, low, 1, col=core), h_copy(on_y, top, 1, col=core)]
    near_second = [h_copy(on_x, top, 1, col=core), h_copy(on_y, low, 1, col=core)]
    near_both = h_copy(on_both, None, 1, col=core)
    for c in (x_low, y_top, near, x_top, y_low):
        c.start()
    steps = (
        ((me, top), (me, low)),
        ((on_x, low), (on_y, top)),
        ((on_x, top), (on_y, low)),
        ((on_both, top), (on_both, low)),
    )
    back_near = [[mover.copy(back_ref.at[1, s, p], back_got_ref.at[s, p], col=core) for s, p in two] for two in steps]
    fwd_near = [[mover.copy(fwd_ref.at[1, s, p], fwd_got_ref.at[s, p], col=core) for s, p in two] for two in steps]
    diag = [
        mover.copy(pair_ref.at[on_both, top], diag_ref.at[0], col=across),
        mover.copy(pair_ref.at[on_both, low], diag_ref.at[1], dp=y),
    ]
    far = [
        mover.copy(pair_ref.at[on_x, top], far_ref.at[0, top], col=across),
        mover.copy(pair_ref.at[on_y, low], far_ref.at[1, low], dp=y),
        mover.copy(pair_ref.at[on_y, top], far_ref.at[1, top], dp=y),
        mover.copy(pair_ref.at[on_x, low], far_ref.at[0, low], col=across),
    ]

    def add_pair(k):
        for (s, p), c in zip(steps[k], back_near[k]):
            c.wait_recv()
            pair_ref[s, p] = (back_ref[0, s, p].astype(F32) + back_got_ref[s, p].astype(F32)).astype(BF)

    for copy in local:
        copy.wait()
    for c in cots:
        c.wait_recv()

    def block(t, carried):
        @pl.when(t == 1)
        def _():
            near.wait_recv()

        @pl.when(t == 2)
        def _():
            x_low.wait_recv()
            both_low.start()
            near_first[0].start()
            y_top.wait_recv()
            both_top.start()
            near_first[1].start()

        @pl.when(t == 3)
        def _():
            for c in near_first:
                c.wait_recv()

        @pl.when(t == 4)
        def _():
            x_top.wait_recv()
            near_second[0].start()
            y_low.wait_recv()
            near_second[1].start()

        @pl.when(t == 5)
        def _():
            for c in near_second:
                c.wait_recv()
            add_pair(1)

        @pl.when(t == 6)
        def _():
            both_low.wait_recv()
            both_top.wait_recv()
            near_both.start()

        @pl.when(t == 7)
        def _():
            near_both.wait_recv()
            add_pair(2)
            far[0].start()
            far[1].start()

        name, side = t // 2, lax.rem(t, 2)
        first_dp = lax.rem(dp + jnp.where(name == 3, 1, 0), 2)
        first_x = lax.rem(x + jnp.where(name >= 1, 1, 0), 2)
        first = first_dp * 2 + first_x
        other_dp = lax.rem(dp + jnp.where(name >= 1, 1, 0), 2)
        other_x = lax.rem(x + jnp.where(name == 3, 1, 0), 2)
        other = other_dp * 2 + other_x
        first_rows = pl.ds(pl.multiple_of(jnp.where(name == 1, half, 0), half), half)
        other_rows = pl.ds(pl.multiple_of(jnp.where(name == 1, 0, half), half), half)
        h = jnp.concatenate([h_ref[side, first, first_rows], h_ref[side, other, other_rows]], axis=0)
        cot = jnp.concatenate([cot_ref[side, first, first_rows], cot_ref[side, other, other_rows]], axis=0)
        gate = nt(h, w_ref[0])
        up = nt(h, w_ref[1])
        d_hidden = nt(cot, w_ref[2])
        sig = 1.0 / (1.0 + jnp.exp(-gate))
        silu = gate * sig
        hidden = (silu * up).astype(BF)
        d_gate = (d_hidden * up * sig * (1.0 + gate * (1.0 - sig))).astype(BF)
        d_up = (d_hidden * silu).astype(BF)
        back = (nn(d_gate, w_ref[0]) + nn(d_up, w_ref[1])).astype(BF)
        fwd = nn(hidden, w_ref[2]).astype(BF)
        for spot, part, cut in ((first, first_rows, slice(0, half)), (other, other_rows, slice(half, rows))):
            start = jnp.where(part.start == 0, 0, half)
            place = pl.ds(pl.multiple_of((side * 4 + spot) * rows + start, half), half)
            hid_ref[place] = hidden[cut]
            dg_ref[place] = d_gate[cut]
            du_ref[place] = d_up[cut]
            back_ref[side, spot, part] = back[cut]
            fwd_ref[side, spot, part] = fwd[cut]
        for k in range(4):

            @pl.when(t == 2 * k + 1)
            def _():
                for c in back_near[k] + fwd_near[k]:
                    c.start()

        return carried

    lax.fori_loop(0, 8, block, 0)
    add_pair(3)
    for c in diag:
        c.start()

    hops = []
    for place in range(3):
        to_right = mover.copy(g_ref.at[3, place], hop_ref.at[place], row=row + 1)
        to_left = mover.copy(g_ref.at[0, place], hop_ref.at[place], row=row - 1)
        hops.append((to_right, to_left))

    def gradient(place, left, right):
        grad = tn(left[...], right[...].reshape(8 * rows, D))
        for r in range(4):
            g_ref[r, place] = grad[r * units : (r + 1) * units].astype(BF)
        pl.when(row == 0)(hops[place][0].start)
        pl.when(row == 3)(hops[place][1].start)

    gradient(0, dg_ref, h_ref)
    gradient(1, du_ref, h_ref)
    for k, (s, part) in enumerate(((on_y, top), (on_x, low))):
        if k == 1:
            far[0].wait_send()
        else:
            far[1].wait_send()
        diag[k].wait_recv()
        pair_ref[s, part] = (pair_ref[s, part].astype(F32) + diag_ref[k].astype(F32)).astype(BF)
        far[2 + k].start()
    gradient(2, hid_ref, cot_ref)
    for two, copies in zip(steps, fwd_near):
        for (s, p), c in zip(two, copies):
            c.wait_recv()
            out_pair_ref[s, p] = (fwd_ref[0, s, p].astype(F32) + fwd_got_ref[s, p].astype(F32)).astype(BF)
    add_pair(0)
    for c in far:
        c.wait_recv()
    d_h = pair_ref[me].astype(F32) + far_ref[0].astype(F32) + far_ref[1].astype(F32)
    unmix_math(
        mixed_ref, cot_ref.at[0, me], d_h, heads_ref, w_out_ref, gain_ref,
        d_mixed_ref, d_heads_ref, g_out_ref, g_gain_ref,
    )
    for c in cots + [x_low, y_top, x_top, y_low, near, both_low, both_top, near_both] + near_first + near_second:
        c.wait_send()
    for two in back_near + fwd_near:
        for c in two:
            c.wait_send()
    for c in diag + far[2:]:
        c.wait_send()
    for to_right, to_left in hops:
        pl.when(row == 0)(to_right.wait_send)
        pl.when(row == 3)(to_left.wait_send)
        pl.when(row == 1)(to_right.wait_recv)
        pl.when(row == 2)(to_left.wait_recv)


def middle(x_parts, heads, w_out, gains, cot_own, cot_near, w_own, w_rows):
    parts, rows, feat = x_parts.shape
    units = w_rows.shape[3]
    count = 16 + 12 + 16 + 6 + 6
    square_of = pltpu.VMEM((2, 4, rows, D), BF)
    hidden_of = pltpu.VMEM((8 * rows, 4 * units), BF)
    quarter = pltpu.VMEM((4, rows, D), BF)
    return pl.pallas_call(
        middle_body,
        out_shape=(
            jax.ShapeDtypeStruct((rows, D), F32),
            jax.ShapeDtypeStruct((rows, D), F32),
            jax.ShapeDtypeStruct((rows, D), BF),
            jax.ShapeDtypeStruct(w_out.shape, BF),
            jax.ShapeDtypeStruct((1, D), F32),
            jax.ShapeDtypeStruct((4, 3, units, D), BF),
            jax.ShapeDtypeStruct((4, rows, D), BF),
            jax.ShapeDtypeStruct((3, units, D), BF),
        ),
        in_specs=[VMEM] * 4 + [ANY] * 4,
        out_specs=(VMEM,) * 7 + (ANY,),
        scratch_shapes=[pltpu.VMEM((3, 4 * units, D), BF), square_of, square_of]
        + [hidden_of] * 3
        + [square_of, square_of, quarter, quarter, quarter]
        + [
            pltpu.VMEM((2, rows // 2, D), BF),
            pltpu.VMEM((2, rows, D), BF),
            pltpu.SemaphoreType.DMA((count,)),
            pltpu.SemaphoreType.DMA((count,)),
            pltpu.SemaphoreType.DMA((4, 4)),
            pltpu.SemaphoreType.DMA((4, 4)),
        ],
        compiler_params=comm_params(4),
        cost_estimate=cost_of(2 * 8 * rows * 9 * D * 4 * units, 24 << 20),
    )(x_parts, heads, w_out, gains, cot_own, cot_near, w_own, w_rows)


def unmix(dh, out_sum, mixed, cot_own, heads, w_out, gains):
    rows = heads.shape[0]
    parts, feat = w_out.shape[1], w_out.shape[3]
    outs = (
        jax.ShapeDtypeStruct((parts, rows, feat), BF),
        jax.ShapeDtypeStruct((rows, D), F32),
        jax.ShapeDtypeStruct((rows, D), BF),
        jax.ShapeDtypeStruct(w_out.shape, BF),
        jax.ShapeDtypeStruct((1, D), F32),
    )
    return call(unmix_body, outs, cost=cost_of(4 * rows * D * D, 18 << 20))(
        dh, out_sum, mixed, cot_own, heads, w_out, gains
    )


def query_grads(ranks_taken, dq, high, low, bq_ref):
    fac = None
    folded = []
    for r in ranks_taken:
        tile = bq_ref[:, (r // 2) * LANES : (r // 2 + 1) * LANES]
        rank = double_left(tile) if r % 2 == 0 else double_right(tile)
        product = dq * jnp.concatenate([rank] * PAIRS, axis=1)
        term = two_pass(product, head_collect(2 * RK + r))
        fac = term if fac is None else fac + term
        pick = head_spread(2 * RK + r, 0, D)
        terms = (nn(high, pick) + nn(low, pick)) * dq
        acc = terms[:, :LANES]
        for p in range(1, PAIRS):
            acc = acc + terms[:, p * LANES : (p + 1) * LANES]
        folded.append(acc + pltpu.roll(acc, HD, 1))
    return fac, folded


def turned_back(part, turn_ref):
    return part * turn_ref[:, :LANES] - swap_halves(part) * turn_ref[:, LANES:]


def put_query_grads(folded, first, turn_ref, d_ref):
    lane = lane_iota(folded[0].shape)
    for k in range(len(folded) // 2):
        merged = jnp.where(lane < HD, folded[2 * k], folded[2 * k + 1])
        tile = first // 2 + k
        d_ref[:, tile * LANES : (tile + 1) * LANES] = turned_back(merged, turn_ref).astype(BF)


def put_key_grads(dkf, fac, turn_ref, d_ref):
    d_ref[:, 3 * LANES : 4 * LANES] = turned_back(dkf[:, :LANES], turn_ref).astype(BF)
    d_ref[:, 4 * LANES : 5 * LANES] = dkf[:, LANES : 2 * LANES].astype(BF)
    fac = fac.astype(BF).astype(F32) + nt(dkf[:, 2 * LANES :].astype(BF), key_columns())
    d_ref[:, RANK_COLS:] = fac.astype(BF)


def factor_weight_grads(d_ref, h_ref, gains, g_two_ref, g_ref):
    n_row, parts, _, feat = g_ref.shape
    grad = tn(d_ref[...], h_ref[...])
    ranks_each = RANK_COLS // n_row
    used = FAC * GROUP
    for c in range(parts):
        lanes = slice(c * feat, (c + 1) * feat)
        tail = jnp.concatenate(
            [gains[c], g_two_ref[:, lanes], jnp.zeros((GROUP_COLS - used - 2, feat), F32)], axis=0
        )
        for r in range(n_row):
            first = RANK_COLS + r * GROUP_COLS
            g_ref[r, c, :ranks_each] = grad[r * ranks_each : (r + 1) * ranks_each, lanes].astype(BF)
            g_ref[r, c, ranks_each:] = jnp.concatenate([grad[first : first + used, lanes], tail], axis=0).astype(BF)


def first_norm_back(d_h, x_ref, gain_ref, d_mixed_ref, gi_ref):
    parts, _, feat = x_ref.shape
    xs = [x_ref[c].astype(F32) for c in range(parts)]
    total = sum(jnp.sum(v * v, axis=1, keepdims=True) for v in xs)
    scale = lax.rsqrt(total / D + EPS)
    dot = None
    gains = []
    for c in range(parts):
        normed = xs[c] * scale
        grad = d_h[:, c * feat : (c + 1) * feat]
        gains.append(jnp.sum(grad * normed, axis=0, keepdims=True))
        part = jnp.sum(grad * gain_ref[c, :1] * normed, axis=1, keepdims=True)
        dot = part if dot is None else dot + part
    for c in range(parts):
        lanes = slice(c * feat, (c + 1) * feat)
        normed = xs[c] * scale
        total = d_mixed_ref[:, lanes] + scale * (d_h[:, lanes] * gain_ref[c, :1] - normed * (dot / D))
        gi_ref[c] = total.astype(gi_ref.dtype)
    return gains


def back_body(
    dq_ref, dkf_ref, hf_ref, bq_ref, turn_ref, w_ref, h_ref, x_ref, gain_ref, d_mixed_ref, g_two_ref,
    gi_ref, g_ref, d_ref,
):
    heads = hf_ref[...]
    high = heads.astype(BF)
    low = (heads - high.astype(F32)).astype(BF)
    fac, folded = query_grads(range(RQ), dq_ref[...] * (1.0 / RQ), high, low, bq_ref)
    put_query_grads(folded, 0, turn_ref, d_ref)
    put_key_grads(dkf_ref[...].astype(F32), fac, turn_ref, d_ref)
    gains = first_norm_back(nn(d_ref[...], w_ref[...]), x_ref, gain_ref, d_mixed_ref, gi_ref)
    factor_weight_grads(d_ref, h_ref, gains, g_two_ref, g_ref)


def back(dq, dkf, hf, bq, turn, w_rh, h, x_parts, gains, d_mixed, g_two, n_row):
    rows = dq.shape[0]
    parts, _, feat = x_parts.shape
    each = RANK_COLS // n_row + GROUP_COLS
    return call(
        back_body,
        (jax.ShapeDtypeStruct(x_parts.shape, F32), jax.ShapeDtypeStruct((n_row, parts, each, feat), BF)),
        scratch=[pltpu.VMEM((rows, ALL_COLS), BF)],
        cost=cost_of(2 * rows * D * 800 * 6, 12 << 20),
    )(dq, dkf, hf, bq, turn, w_rh, h, x_parts, gains, d_mixed, g_two)


def tail_body(
    win_ref, dq_ref, hf_ref, bq_ref, turn_ref, w_ref, h_ref, x_ref, gain_ref, d_mixed_ref, g_two_ref,
    rows_ref, ends_ref, part_ref,
    grad_ref, gi_all_ref, cols_ref, cols_other_ref, mix_ref, mix_other_ref,
    d_ref, gi_ref, wnear_ref, wsend_ref, wfar_ref, rows_own_ref, cols_send_ref, mix_got_ref,
    g_ref, near_ref, pair_ref, far_ref, side_ref, down_ref, last_ref, end_ref,
    send_sem, recv_sem, local_sem,
):
    row = lax.axis_index("row")
    col, core, across = neighbours()
    cross = lax.rem(core + 2, 4)
    dp = lax.axis_index("dp")
    x, mine = col // 2, lax.rem(col, 2)
    y = 1 - dp
    order = [lax.rem(row + k, 4) for k in (1, 2, 3, 0)]
    greet(
        [(None, {"col": c}) for c in (core, across, cross)]
        + [(None, {"row": r}) for r in order[:3]]
        + [(None, {"dp": y})]
    )
    mover = Mover(send_sem, recv_sem)
    started = []

    def go(source, target, **place):
        c = mover.copy(source, target, **place)
        c.start()
        started.append(c)
        return c

    rows_own = pltpu.make_async_copy(rows_ref.at[row], rows_own_ref, local_sem.at[1])
    rows_own.start()

    near_one = go(win_ref.at[1], wnear_ref.at[0], col=core)
    near_two = go(win_ref.at[3], wnear_ref.at[1], col=core)
    one = mover.copy(wsend_ref.at[0], wfar_ref.at[0], row=row - 1)
    two = mover.copy(wsend_ref.at[1], wfar_ref.at[1], row=row - 1)
    hands_on = jnp.logical_and(row >= 1, row <= 2)
    left = mine == 0
    heads = hf_ref[...]
    high = heads.astype(BF)
    low = (heads - high.astype(F32)).astype(BF)
    dq = dq_ref[...] * (1.0 / RQ)
    near_one.wait_recv()
    near_two.wait_recv()
    zero = jnp.zeros(wnear_ref.shape[1:], F32)
    from_low = wnear_ref[0].astype(F32)
    from_high = wnear_ref[1].astype(F32)
    wsend_ref[1] = (win_ref[0].astype(F32) + jnp.where(left, zero, from_low)).astype(BF)
    pl.when(row >= 2)(two.start)

    width = x_ref.shape[2]
    rows_own.wait()
    for place in range(3):
        total = rows_own_ref[place].astype(F32)
        total = total + jnp.where(row >= 1, ends_ref[0, place].astype(F32), 0.0)
        total = (total + jnp.where(row <= 2, ends_ref[1, place].astype(F32), 0.0)).astype(BF)
        for c in range(4):
            cols_send_ref[c, place] = total[:, c * width : (c + 1) * width]
    columns = [go(cols_send_ref.at[c], cols_ref.at[col], col=c) for c in (across, cross, core)]
    cols_ref[col] = cols_send_ref[col]
    rest = [go(cols_ref.at[col], cols_other_ref.at[col], dp=y)]

    fac, folded = query_grads(range(0, 4), dq, high, low, bq_ref)
    put_query_grads(folded, 0, turn_ref, d_ref)
    sent_on = win_ref[2].astype(F32) + jnp.where(left, from_low, from_high)
    pl.when(hands_on)(two.wait_recv)
    wsend_ref[0] = jnp.where(hands_on, sent_on + wfar_ref[1].astype(F32), sent_on).astype(BF)
    pl.when(row >= 1)(one.start)

    mixes = [go(part_ref.at[order[k]], mix_got_ref.at[k], row=order[k]) for k in range(3)]

    fac_more, folded = query_grads(range(4, RQ), dq, high, low, bq_ref)
    put_query_grads(folded, 4, turn_ref, d_ref)
    for c, source in zip(columns, (across, cross, core)):
        c.wait_recv()
        rest.append(go(cols_ref.at[source], cols_other_ref.at[source], dp=y))
    d_kf = win_ref[4].astype(F32) + jnp.where(left, from_high, zero)
    pl.when(row <= 2)(one.wait_recv)
    d_kf = jnp.where(row <= 2, d_kf + wfar_ref[0].astype(F32), d_kf)
    put_key_grads(d_kf, fac + fac_more, turn_ref, d_ref)
    d_h = nn(d_ref[...], w_ref[...])
    gains = first_norm_back(d_h, x_ref, gain_ref, d_mixed_ref, gi_ref)
    factor_weight_grads(d_ref, h_ref, gains, g_two_ref, g_ref)

    first = [go(g_ref.at[r, (1 - x) * 2 + 1 - mine], near_ref.at[0, k], col=core) for k, r in enumerate(order)]
    second = [go(g_ref.at[r, x * 2 + 1 - mine], near_ref.at[1, k], col=core) for k, r in enumerate(order)]
    sides = []
    for k, r in enumerate(order):
        first[k].wait_recv()
        pair_ref[k] = (g_ref[r, (1 - x) * 2 + mine].astype(F32) + near_ref[0, k].astype(F32)).astype(BF)
        sides.append(go(pair_ref.at[k], side_ref.at[k], col=across))

    total = part_ref[row].astype(F32)
    for k, c in enumerate(mixes):
        c.wait_recv()
        total = total + mix_got_ref[k].astype(F32)
    mix_ref[...] = total.astype(BF)
    rest.append(go(mix_ref, mix_other_ref, dp=y))
    for c in (across, cross, core):
        rest.append(go(gi_ref.at[c], gi_all_ref.at[col], col=c))
    own = pltpu.make_async_copy(gi_ref.at[col], gi_all_ref.at[col], local_sem.at[0])
    own.start()

    downs = []
    for k, r in enumerate(order):
        second[k].wait_recv()
        sides[k].wait_recv()
        far_ref[k] = (
            g_ref[r, x * 2 + mine].astype(F32) + near_ref[1, k].astype(F32) + side_ref[k].astype(F32)
        ).astype(BF)
        if k < 3:
            downs.append(go(far_ref.at[k], down_ref.at[k], row=r))
    total = far_ref[3].astype(F32)
    for k in range(3):
        downs[k].wait_recv()
        total = total + down_ref[k].astype(F32)
    last_ref[...] = total.astype(BF)
    end = go(last_ref, end_ref, dp=y)
    end.wait_recv()
    grad_ref[...] = last_ref[...].astype(F32) + end_ref[...].astype(F32)
    for c in rest:
        c.wait_recv()
    for c in started:
        c.wait_send()
    pl.when(row >= 1)(one.wait_send)
    pl.when(row >= 2)(two.wait_send)
    own.wait()


def tail(win, dq, hf, bq, turn, w_rh, h, x_parts, gains, d_mixed, g_two, g_rows, ends, part):
    rows = dq.shape[0]
    parts, _, feat = x_parts.shape
    units = g_rows.shape[2]
    block = (RANK_COLS // 4 + GROUP_COLS, feat)
    cols = (parts, 3, units, feat)
    mix = part.shape[1:]
    wide = g_rows.shape[1:]
    slot = win.shape[1:]
    count = 2 + 2 + 3 + 8 + 4 + 3 + 1 + 1 + 3 + 3 + 3 + 1
    return pl.pallas_call(
        tail_body,
        out_shape=(
            jax.ShapeDtypeStruct(block, F32),
            jax.ShapeDtypeStruct(x_parts.shape, BF),
            jax.ShapeDtypeStruct(cols, BF),
            jax.ShapeDtypeStruct(cols, BF),
            jax.ShapeDtypeStruct(mix, BF),
            jax.ShapeDtypeStruct(mix, BF),
        ),
        in_specs=[VMEM] * 11 + [ANY, VMEM, VMEM],
        out_specs=(VMEM, ANY, VMEM, ANY, VMEM, ANY),
        scratch_shapes=[
            pltpu.VMEM((rows, ALL_COLS), BF),
            pltpu.VMEM(x_parts.shape, BF),
            pltpu.VMEM((2,) + slot, BF),
            pltpu.VMEM((2,) + slot, BF),
            pltpu.VMEM((2,) + slot, BF),
            pltpu.VMEM(wide, BF),
            pltpu.VMEM(cols, BF),
            pltpu.VMEM((3,) + mix, BF),
            pltpu.VMEM((4, parts) + block, BF),
            pltpu.VMEM((2, 4) + block, BF),
            pltpu.VMEM((4,) + block, BF),
            pltpu.VMEM((4,) + block, BF),
            pltpu.VMEM((4,) + block, BF),
            pltpu.VMEM((3,) + block, BF),
            pltpu.VMEM(block, BF),
            pltpu.VMEM(block, BF),
            pltpu.SemaphoreType.DMA((count,)),
            pltpu.SemaphoreType.DMA((count,)),
            pltpu.SemaphoreType.DMA((2,)),
        ],
        compiler_params=comm_params(7),
        cost_estimate=cost_of(2 * rows * D * 800 * 6, 24 << 20),
    )(win, dq, hf, bq, turn, w_rh, h, x_parts, gains, d_mixed, g_two, g_rows, ends, part)


def layout_body(
    grad_ref, gi_ref, cols_ref, other_ref, mix_ref, mix_other_ref,
    gi_out_ref, gain_ref, gain_two_ref, heads_ref, ranks_ref, out_ref, gate_ref, up_ref, down_ref,
):
    first = lax.axis_index("dp") == 0
    gi_out_ref[...] = gi_ref[...].astype(F32)
    out_ref[...] = mix_ref[...].astype(F32) + mix_other_ref[...].astype(F32)
    ranks = ranks_ref.shape[0]
    used = heads_ref.shape[0]
    gain_ref[...] = grad_ref[ranks + used : ranks + used + 1]
    gain_two_ref[...] = grad_ref[ranks + used + 1 : ranks + used + 2]
    ranks_ref[...] = grad_ref[:ranks]
    lane = lax.broadcasted_iota(jnp.int32, (used, GROUP_COLS), 1)
    place = lax.broadcasted_iota(jnp.int32, (used, GROUP_COLS), 0)
    factor = place % FAC
    spot = jnp.where(factor < RQ, factor + 2 * RK, factor - RQ) * GROUP + place // FAC
    heads_ref[...] = jnp.dot(
        (lane == spot).astype(F32), grad_ref[ranks:], precision=lax.Precision.HIGHEST, preferred_element_type=F32
    )
    part = down_ref.shape[0] // 8
    for k, target in ((0, gate_ref), (1, up_ref), (2, down_ref)):
        for c in range(4):
            own = cols_ref[c, k].astype(F32)[:part]
            other = other_ref[c, k].astype(F32)[:part]
            target[c * part : (c + 1) * part] = jnp.where(first, own, other)
            target[(4 + c) * part : (5 + c) * part] = jnp.where(first, other, own)


def layout(grad, gi, cols, other, mix, mix_other, heads, ranks, hidden):
    feat = grad.shape[1]
    weight = jax.ShapeDtypeStruct((hidden, feat), F32)
    gain = jax.ShapeDtypeStruct((1, feat), F32)
    return call(
        layout_body,
        (
            jax.ShapeDtypeStruct(gi.shape, F32),
            gain,
            gain,
            jax.ShapeDtypeStruct((heads, feat), F32),
            jax.ShapeDtypeStruct((ranks, feat), F32),
            jax.ShapeDtypeStruct(mix.shape, F32),
            weight,
            weight,
            weight,
        ),
        cost=cost_of(0, 8 << 20),
    )(grad, gi, cols, other, mix, mix_other)


def local(
    tokens_in, segments, gain_attn, gain_ffn, w_heads, w_ranks, w_out, w_gate, w_up, w_down, cotangent
):
    n_row = lax.axis_size("row")
    n_col = lax.axis_size("col")
    row = lax.axis_index("row")
    col = lax.axis_index("col")
    micro, row_tokens, feat = tokens_in.shape
    subs = n_col // micro
    rows = row_tokens // subs
    length = row_tokens * n_row
    head_local = w_heads.shape[1] // FAC
    rank_local = w_ranks.shape[1]
    ffn_local = w_gate.shape[1]
    out_local = w_out.shape[0]
    block = row * subs + col % subs
    past = min(-(-(MAX_DOC - 1) // rows), n_row * subs - 1)
    keys = (past + 1) * rows

    dp_count = lax.axis_size("dp")
    fast = n_col == 4 and n_row == 4 and dp_count == 2 and micro == 2 and past == 4

    tokens = tokens_in.reshape(n_col, rows, feat)
    inverse = ROPE ** (-(jnp.arange(HD // 2, dtype=F32) * 2.0 / HD))
    if not fast:
        heads_t = jnp.transpose(w_heads.reshape(feat, head_local, FAC), (2, 1, 0))
        heads_t = heads_t[jnp.array(FAC_ORDER)].reshape(FAC * head_local, feat)
        pad = jnp.zeros((GROUP_COLS - FAC * head_local, feat), BF)
        w_own = jnp.concatenate([w_ranks.T, heads_t, pad], axis=0)
        gains_own = jnp.concatenate([gain_attn[None], gain_ffn[None], jnp.zeros((6, feat), F32)], axis=0)
        part = ffn_local // n_col
        units = part * n_row
        w_ffn = jnp.stack([w_gate.T, w_up.T, w_down]).reshape(3, n_col, part, feat)
        w_ffn = lax.all_to_all(jnp.transpose(w_ffn, (1, 0, 2, 3)), "col", 0, 0, tiled=True)
        w_ffn = jnp.transpose(w_ffn, (1, 2, 0, 3)).reshape(3, part, D)
        w_ffn = jnp.transpose(lax.all_gather(w_ffn, "row", axis=0), (1, 0, 2, 3)).reshape(3, units, D)
        w_blocks = lax.all_gather(w_own, ("row", "col"), axis=0).reshape((n_row, n_col) + w_own.shape)
        gains = lax.all_gather(gains_own, "col", axis=0)
        x_parts = lax.all_to_all(tokens, "col", 0, 0, tiled=True)
        w_out_all = lax.all_gather(w_out, ("row", "col"), axis=0).reshape((n_row, n_col) + w_out.shape)

        seg_row = lax.dynamic_index_in_dim(segments, col // subs, 0, keepdims=False)
        padded = jnp.concatenate([jnp.full((1, past * rows), -1, jnp.int32), seg_row], axis=1)
        seg_window = lax.dynamic_slice_in_dim(padded, block * rows, keys, 1)
        own_seg = seg_window[0, past * rows :]
        key_idx = jnp.arange(keys, dtype=jnp.int32)
        query_idx = jnp.arange(rows, dtype=jnp.int32) + past * rows
        before = (own_seg[:, None] == seg_window) & (key_idx[None, :] < query_idx[:, None])
        places = jnp.sum(before.astype(jnp.int32), axis=1)
        angles = places.astype(F32)[:, None] * inverse[None, :]
        cosine = jnp.cos(angles)
        sine = jnp.sin(angles)
        turn = jnp.concatenate([cosine] * 4 + [-sine, sine, -sine, sine], axis=1)

    groups = [[m * subs + s for s in range(subs)] for m in range(micro)]
    if fast:
        (
            x_parts, gains, ffn_parts, mixes, h_one, head_fac, bq_rot, queries, w_rh, kf_window, seg_window, turn, w_rows
        ) = head(
            tokens, w_ranks.T, w_heads.T, gain_attn.reshape(1, feat), gain_ffn.reshape(1, feat), w_gate.T, w_up.T,
            w_down, w_out, segments, jnp.concatenate([inverse] * 4).reshape(1, LANES),
        )
        kf_window = kf_window.reshape(keys, -1)
        cot_rows = cotangent.reshape(micro * row_tokens, feat)
        heads_out, lse, key_all, value_all, w_rows, cot_near, mixes = attend(
            queries, kf_window, seg_window, w_rows, cot_rows, mixes
        )
        mixed, d_mixed, d_heads, g_out, g_gain_two, g_rows, out_pair, hop = middle(
            x_parts, heads_out, mixes, gains, cot_rows, cot_near, ffn_parts, w_rows
        )
        d_q, d_kf, output, g_ends, g_part = attend_back(
            queries, key_all, value_all, d_heads, lse, kf_window, seg_window, out_pair, mixed, g_rows, g_out, hop
        )
        g_rh, grad_input, g_cols, cols_other, g_out, out_other = tail(
            d_kf.reshape(past + 1, rows, -1), d_q, head_fac, bq_rot, turn, w_rh, h_one, x_parts, gains, d_mixed,
            g_gain_two, g_rows, g_ends, g_part,
        )
        grad_input, g_one, g_two, own_heads, own_ranks, g_out, own_gate, own_up, own_down = layout(
            g_rh, grad_input, g_cols, cols_other, g_out, out_other, w_heads.shape[1], w_ranks.shape[1], ffn_local
        )
        return (
            output.reshape(tokens_in.shape),
            grad_input.reshape(tokens_in.shape),
            g_one.reshape(feat),
            g_two.reshape(feat),
            own_heads.T,
            own_ranks.T,
            g_out,
            own_gate.T,
            own_up.T,
            own_down,
        )
    else:
        h_one, head_fac, bq_rot, key_fac, queries, w_rh = front(x_parts, gains, w_blocks, turn)
        gathered = lax.all_gather(key_fac, "row", axis=0)
        gathered = lax.all_gather(gathered, "col", axis=1, axis_index_groups=groups)
        gathered = gathered.reshape(length, key_fac.shape[1])
        padded_kf = jnp.concatenate([jnp.zeros((past * rows, key_fac.shape[1]), BF), gathered], axis=0)
        kf_window = lax.dynamic_slice_in_dim(padded_kf, block * rows, keys, 0)
        heads_out, lse, key_all, value_all = attend(queries, kf_window, seg_window)
        mixed, h_two = mixing(x_parts, heads_out, w_out_all, gains)
        cot_own = lax.all_to_all(cotangent.reshape(n_col, rows, feat), "col", 0, 0, tiled=True)
        cot_own = jnp.transpose(cot_own, (1, 0, 2)).reshape(rows, D)
        cot_all = lax.all_gather(cot_own, "col", axis=0)
        h_all = lax.all_gather(h_two, "col", axis=0)
        out_part, dh_part, g_ffn = ffn(h_all, cot_all, w_ffn)
        dh_sum = lax.psum_scatter(dh_part, "col", scatter_dimension=0, tiled=False).astype(F32)
        out_sum = lax.psum_scatter(out_part, "col", scatter_dimension=0, tiled=False).astype(F32)
        out_parts, d_mixed, d_heads, g_out, g_gain_two = unmix(
            dh_sum, out_sum, mixed, cot_own, heads_out, w_out_all, gains
        )
        d_q, d_kf = attend_back(queries, key_all, value_all, d_heads, lse, kf_window, seg_window)
        spread_kf = jnp.zeros((past * rows + length, d_kf.shape[1]), BF)
        spread_kf = lax.dynamic_update_slice_in_dim(spread_kf, d_kf, block * rows, 0)[past * rows :]
        spread_kf = spread_kf.reshape(n_row, subs, rows, -1)
        own_kf = lax.psum_scatter(spread_kf, "row", scatter_dimension=0, tiled=False)
        own_kf = lax.psum_scatter(own_kf, "col", scatter_dimension=0, tiled=False, axis_index_groups=groups)
        gi_parts, g_rh = back(
            d_q, own_kf, head_fac, bq_rot, turn, w_rh, h_one, x_parts, gains, d_mixed, g_gain_two, n_row
        )
        output = lax.all_to_all(out_parts, "col", 0, 0, tiled=True)
        grad_input = lax.all_to_all(gi_parts, "col", 0, 0, tiled=True)
        g_ffn = lax.psum_scatter(g_ffn.reshape(3, n_row, part, D), "row", scatter_dimension=1, tiled=False)
        g_ffn = jnp.transpose(lax.psum(g_ffn, "dp").reshape(3, part, n_col, feat), (2, 0, 1, 3))
        g_ffn = lax.all_to_all(g_ffn, "col", 0, 0, tiled=True)
        g_ffn = jnp.transpose(g_ffn, (1, 0, 2, 3)).reshape(3, ffn_local, feat).astype(F32)

        def total(values):
            values = values.reshape((n_row * n_col,) + values.shape[2:])
            values = lax.psum_scatter(values, ("row", "col"), scatter_dimension=0, tiled=False)
            return lax.psum(values, "dp").astype(F32)

        g_out = total(g_out)
        g_rh = total(g_rh)

    used = rank_local + FAC * head_local
    own_heads = g_rh[rank_local:used].reshape(FAC, head_local, feat)
    own_heads = jnp.transpose(own_heads[jnp.array(FAC_BACK)], (2, 1, 0)).reshape(w_heads.shape)
    return (
        output.reshape(tokens_in.shape),
        grad_input.reshape(tokens_in.shape),
        g_rh[used],
        g_rh[used + 1],
        own_heads,
        g_rh[:rank_local].T,
        g_out,
        g_ffn[0].T,
        g_ffn[1].T,
        g_ffn[2],
    )


def solution(mesh):
    tokens = P(None, ("dp", "row"), "col")
    both = P("col", "row")
    turned = P("row", "col")
    gain = P("col")
    return jax.shard_map(
        local,
        mesh=mesh,
        in_specs=(tokens, P(None, "dp", None), gain, gain, both, both, turned, both, both, turned, tokens),
        out_specs=(tokens, tokens, gain, gain, both, both, turned, both, both, turned),
        check_vma=False,
    )
```

```python
import functools

import jax
import jax.numpy as jnp
from jax import lax
from jax.experimental import pallas as pl
from jax.experimental.pallas import tpu as pltpu
from jax.sharding import PartitionSpec as P

D = 1024
H = 16
HD = 64
RQ = 6
RK = 2
FAC = 10
MAX_DOC = 1024

EPS = 1e-06
ROPE = 10000.0
NEG = -1e30
BF = jnp.bfloat16
F32 = jnp.float32
LANES = 128
PAIRS = H // 2
FAC_ORDER = (6, 7, 8, 9, 0, 1, 2, 3, 4, 5)
FAC_BACK = (4, 5, 6, 7, 8, 9, 0, 1, 2, 3)
VMEM = pl.BlockSpec(memory_space=pltpu.VMEM)


def nn(a, b):
    return jnp.dot(a, b, preferred_element_type=F32)


def nt(a, b):
    return lax.dot_general(a, b, (((1,), (1,)), ((), ())), preferred_element_type=F32)


def tn(a, b):
    return lax.dot_general(a, b, (((0,), (0,)), ((), ())), preferred_element_type=F32)


def two_pass(a, b):
    high = a.astype(BF)
    low = (a - high.astype(F32)).astype(BF)
    return nn(high, b) + nn(low, b)


def lane_iota(shape):
    return lax.broadcasted_iota(jnp.int32, shape, len(shape) - 1)


def spread(rows, first, width):
    row = lax.broadcasted_iota(jnp.int32, (rows, width), 0)
    head = lax.broadcasted_iota(jnp.int32, (rows, width), 1) // HD
    return (row == head + first).astype(F32).astype(BF)


def collect(rows, width, first):
    head = lax.broadcasted_iota(jnp.int32, (rows, width), 0) // HD
    lane = lax.broadcasted_iota(jnp.int32, (rows, width), 1)
    return (lane == head + first).astype(F32).astype(BF)


GROUP = 4
GROUP_COLS = 48
RANK_COLS = FAC * HD
HEAD_COLS = H // GROUP * GROUP_COLS
ALL_COLS = RANK_COLS + HEAD_COLS


def factor_place(head, j):
    return head // GROUP * GROUP_COLS + j * GROUP + head % GROUP


def head_spread(j, first_head, width):
    row = lax.broadcasted_iota(jnp.int32, (HEAD_COLS, width), 0)
    head = lax.broadcasted_iota(jnp.int32, (HEAD_COLS, width), 1) // HD + first_head
    return (row == factor_place(head, j)).astype(F32).astype(BF)


def head_collect(j):
    head = lax.broadcasted_iota(jnp.int32, (D, HEAD_COLS), 0) // HD
    lane = lax.broadcasted_iota(jnp.int32, (D, HEAD_COLS), 1)
    return (lane == factor_place(head, j)).astype(F32).astype(BF)


def key_columns():
    row = lax.broadcasted_iota(jnp.int32, (HEAD_COLS, LANES), 0)
    lane = lax.broadcasted_iota(jnp.int32, (HEAD_COLS, LANES), 1)
    taken = (row == factor_place(lane % H, lane // H)) & (lane < 2 * RK * H)
    return taken.astype(F32).astype(BF)


def swap_halves(tile):
    lane = lane_iota(tile.shape)
    ahead = pltpu.roll(tile, LANES - HD // 2, 1)
    behind = pltpu.roll(tile, HD // 2, 1)
    return jnp.where(lane % HD < HD // 2, ahead, behind)


def double_left(tile):
    return jnp.where(lane_iota(tile.shape) < HD, tile, pltpu.roll(tile, HD, 1))


def double_right(tile):
    return jnp.where(lane_iota(tile.shape) < HD, pltpu.roll(tile, HD, 1), tile)


def params(**more):
    return pltpu.CompilerParams(vmem_limit_bytes=60 << 20, **more)


def call(body, outs, scratch=(), cost=None):
    return pl.pallas_call(
        body,
        out_shape=outs,
        scratch_shapes=scratch,
        compiler_params=params(),
        cost_estimate=cost,
    )


def cost_of(flops, moved):
    return pl.CostEstimate(flops=int(flops), bytes_accessed=int(moved), transcendentals=0)


MESH = pl.DeviceIdType.MESH
ANY = pl.BlockSpec(memory_space=pl.ANY)


class Mover:
    def __init__(self, send_sem, recv_sem):
        self.send_sem = send_sem
        self.recv_sem = recv_sem
        self.used = 0

    def copy(self, source, target, **place):
        index = self.used
        self.used += 1
        return pltpu.make_async_remote_copy(
            src_ref=source,
            dst_ref=target,
            send_sem=self.send_sem.at[index],
            recv_sem=self.recv_sem.at[index],
            device_id=place,
            device_id_type=MESH,
        )


def greet(partners):
    barrier = pltpu.get_barrier_semaphore()
    count = 0
    for present, place in partners:
        if present is None:
            pl.semaphore_signal(barrier, inc=1, device_id=place, device_id_type=MESH)
            count = count + 1
        else:

            @pl.when(present)
            def _():
                pl.semaphore_signal(barrier, inc=1, device_id=place, device_id_type=MESH)

            count = count + present.astype(jnp.int32)
    pl.semaphore_wait(barrier, count)


def neighbours():
    col = lax.axis_index("col")
    core = col + 1 - 2 * lax.rem(col, 2)
    across = lax.rem(col + 2, 4)
    return col, core, across


def square():
    dp = lax.axis_index("dp")
    x = lax.axis_index("col") // 2
    return dp, (dp * 2 + x, dp * 2 + 1 - x, (1 - dp) * 2 + x, (1 - dp) * 2 + 1 - x)


def comm_params(ident):
    return params(collective_id=ident, has_side_effects=True)


class AttendCopies:
    def __init__(self, head_end, cot_ref, rows_ref, near_ref, mixes_ref, send_sem, recv_sem):
        self.head_end = head_end
        row = lax.axis_index("row")
        col, core, across = neighbours()
        dp, (me, on_x, on_y, _) = square()
        mover = Mover(send_sem, recv_sem)
        self.left = row >= 1
        self.right = row <= 2
        self.both = jnp.logical_and(self.left, self.right)
        self.from_left = row >= 2
        self.from_right = row <= 1
        self.row = row
        cuts = [pl.ds(0, 2), pl.ds(2, 2)]
        lower, upper = rows_ref.at[jnp.maximum(row - 1, 0)], rows_ref.at[jnp.minimum(row + 1, 3)]
        self.pass_right = [mover.copy(lower.at[c], lower.at[c], row=row + 1) for c in cuts]
        self.pass_left = [mover.copy(upper.at[c], upper.at[c], row=row - 1) for c in cuts]
        self.last_right = [mover.copy(rows_ref.at[0, c], rows_ref.at[0, c], row=row + 1) for c in cuts]
        self.last_left = [mover.copy(rows_ref.at[3, c], rows_ref.at[3, c], row=row - 1) for c in cuts]
        half = cot_ref.shape[0] // 2
        top, low = pl.ds(0, half), pl.ds(half, half)
        self.cots = [
            mover.copy(cot_ref.at[low], near_ref.at[me, low], col=across),
            mover.copy(cot_ref.at[top], near_ref.at[me, top], dp=1 - dp),
            mover.copy(cot_ref.at[top], near_ref.at[me, top], col=across),
            mover.copy(cot_ref.at[low], near_ref.at[me, low], dp=1 - dp),
        ]
        self.relays = [
            mover.copy(near_ref.at[on_x, low], near_ref.at[on_x, low], dp=1 - dp),
            mover.copy(near_ref.at[on_y, top], near_ref.at[on_y, top], col=across),
        ]
        self.mixes = []
        for r in range(4):
            for c in (col, across):
                self.mixes.append(mover.copy(mixes_ref.at[r, c], mixes_ref.at[r, c], col=core))

    def first(self):
        for k in range(2):
            pl.when(self.both)(self.pass_right[k].start)
            pl.when(self.both)(self.pass_left[k].start)
        for c in self.cots:
            c.start()

    def early(self):
        self.head_end()
        for c in self.mixes:
            c.start()
        self.hand_on(0)

    def hand_on(self, k):
        pl.when(self.from_left)(self.pass_right[k].wait_recv)
        pl.when(self.from_right)(self.pass_left[k].wait_recv)
        pl.when(self.row == 2)(self.last_right[k].start)
        pl.when(self.row == 1)(self.last_left[k].start)

    def second(self):
        for c in self.cots[:2]:
            c.wait_recv()
        for c in self.relays:
            c.start()
        self.hand_on(1)

    def last(self):
        for k in range(2):
            pl.when(self.both)(self.pass_right[k].wait_send)
            pl.when(self.both)(self.pass_left[k].wait_send)
            pl.when(self.row == 2)(self.last_right[k].wait_send)
            pl.when(self.row == 1)(self.last_left[k].wait_send)
            pl.when(self.row == 3)(self.last_right[k].wait_recv)
            pl.when(self.row == 0)(self.last_left[k].wait_recv)
        for c in self.cots[:2]:
            c.wait_send()
        for c in self.cots[2:] + self.relays + self.mixes:
            c.wait()


class BackCopies:
    def __init__(self, refs, sems):
        (
            self.pair_ref, self.mixed_ref, self.rows_ref, self.g_out_ref, self.hop_ref,
            self.out_ref, self.ends_ref, self.part_ref,
            self.relay_ref, self.diag_ref, self.far_ref, self.send_ref,
            self.right_ref, self.left_ref, self.got_ref,
            self.near_ref, self.side_ref, self.across_ref,
            self.pieces_ref, self.mine_ref, self.rows_in_ref, self.g_in_ref,
        ) = refs
        send_sem, recv_sem, local_sem = sems
        self.row = row = lax.axis_index("row")
        self.col, core, across = col, _, _ = neighbours()
        cross = lax.rem(core + 2, 4)
        self.dp, self.spots = dp, (me, on_x, on_y, on_both) = square()
        mover = Mover(send_sem, recv_sem)
        self.x, self.mine = x, mine = col // 2, lax.rem(col, 2)
        self.partners = [(None, {"col": c}) for c in (core, across, cross)]
        self.partners += [(None, {"dp": 1 - dp})] + [(None, {"row": lax.rem(row + k, 4)}) for k in range(1, 4)]
        half = self.pair_ref.shape[1] // 2
        top, low = pl.ds(0, half), pl.ds(half, half)
        y = 1 - dp
        self.diag = [
            mover.copy(self.pair_ref.at[on_both, top], self.diag_ref.at[0], col=across),
            mover.copy(self.pair_ref.at[on_both, low], self.diag_ref.at[1], dp=y),
        ]
        self.far = [
            mover.copy(self.pair_ref.at[on_x, top], self.far_ref.at[0, top], col=across),
            mover.copy(self.pair_ref.at[on_y, low], self.far_ref.at[1, low], dp=y),
            mover.copy(self.relay_ref.at[0], self.far_ref.at[1, top], dp=y),
            mover.copy(self.relay_ref.at[1], self.far_ref.at[0, low], col=across),
        ]
        self.out = [mover.copy(self.send_ref.at[c], self.out_ref.at[col], col=c) for c in (across, cross, core)]
        self.own = pltpu.make_async_copy(self.send_ref.at[col], self.out_ref.at[col], local_sem.at[0])
        self.hop_right = [
            mover.copy(self.right_ref.at[0], self.got_ref.at[0], row=row + 1),
            mover.copy(self.right_ref.at[1], self.ends_ref.at[0], row=row + 1),
        ]
        self.hop_left = [
            mover.copy(self.left_ref.at[0], self.got_ref.at[1], row=row - 1),
            mover.copy(self.left_ref.at[1], self.ends_ref.at[1], row=row - 1),
        ]
        self.cores = [
            mover.copy(self.g_out_ref.at[r, k * 2 + 1 - mine], self.near_ref.at[k, r], col=core)
            for k in range(2)
            for r in range(4)
        ]
        self.sides = [mover.copy(self.side_ref.at[r], self.across_ref.at[r], col=across) for r in range(4)]
        self.loads = [
            pltpu.make_async_copy(self.pair_ref.at[on_y, top], self.pieces_ref.at[0], local_sem.at[1]),
            pltpu.make_async_copy(self.pair_ref.at[on_x, low], self.pieces_ref.at[1], local_sem.at[2]),
            pltpu.make_async_copy(self.pair_ref.at[me], self.mine_ref, local_sem.at[3]),
        ]
        self.rows_load = pltpu.make_async_copy(self.rows_ref, self.rows_in_ref, local_sem.at[4])
        self.g_loads = [
            pltpu.make_async_copy(
                self.g_out_ref.at[r, lax.rem(x + k, 2) * 2 + mine], self.g_in_ref.at[k, r], local_sem.at[5 + 4 * k + r]
            )
            for k in range(2)
            for r in range(4)
        ]

    def first(self):
        row = self.row
        self.rows_load.start()
        for c in self.loads + self.g_loads:
            c.start()
        greet(self.partners)
        for c in self.diag + self.far[:2] + self.cores:
            c.start()
        self.rows_load.wait()
        hop = self.hop_ref[...].astype(F32)
        ahead = self.rows_in_ref[jnp.minimum(row + 2, 3)].astype(F32)
        self.right_ref[0] = jnp.where(row == 1, ahead + hop, ahead).astype(BF)
        behind = self.rows_in_ref[jnp.maximum(row - 2, 0)].astype(F32)
        self.left_ref[0] = jnp.where(row == 2, behind + hop, behind).astype(BF)
        pl.when(row <= 1)(self.hop_right[0].start)
        pl.when(row >= 2)(self.hop_left[0].start)

    def cross_x(self):
        for c in self.g_loads:
            c.wait()
        for c in self.cores:
            c.wait_recv()
        for r in range(4):
            self.side_ref[r] = (
                self.g_in_ref[1, r].astype(F32) + self.near_ref[1 - self.x, r].astype(F32)
            ).astype(BF)
            self.sides[r].start()

    def second(self):
        row = self.row
        for c in self.loads:
            c.wait()
        for k in range(2):
            self.diag[k].wait_recv()
            self.relay_ref[k] = (self.pieces_ref[k].astype(F32) + self.diag_ref[k].astype(F32)).astype(BF)
            self.far[2 + k].start()

    def last_hop(self):
        row = self.row
        middle = jnp.logical_and(row >= 1, row <= 2)
        pl.when(middle)(self.hop_right[0].wait_recv)
        pl.when(middle)(self.hop_left[0].wait_recv)
        ahead = self.rows_in_ref[jnp.minimum(row + 1, 3)].astype(F32)
        behind = self.rows_in_ref[jnp.maximum(row - 1, 0)].astype(F32)
        self.right_ref[1] = jnp.where(row >= 1, ahead + self.got_ref[0].astype(F32), ahead).astype(BF)
        self.left_ref[1] = jnp.where(row <= 2, behind + self.got_ref[1].astype(F32), behind).astype(BF)
        pl.when(row <= 2)(self.hop_right[1].start)
        pl.when(row >= 1)(self.hop_left[1].start)

    def third(self):
        row = self.row
        for c in self.far:
            c.wait_recv()
        feat = self.send_ref.shape[2]
        for c in range(4):
            lanes = slice(c * feat, (c + 1) * feat)
            self.send_ref[c] = (
                self.mixed_ref[:, lanes]
                + self.mine_ref[:, lanes].astype(F32)
                + self.far_ref[0, :, lanes].astype(F32)
                + self.far_ref[1, :, lanes].astype(F32)
            ).astype(BF)
        for c in self.out:
            c.start()
        self.own.start()

    def last(self):
        row = self.row
        for r in range(4):
            self.sides[r].wait_recv()
            self.part_ref[r] = (
                self.g_in_ref[0, r].astype(F32)
                + self.near_ref[self.x, r].astype(F32)
                + self.across_ref[r].astype(F32)
            ).astype(BF)
        for c in self.out:
            c.wait()
        self.own.wait()
        for c in self.diag + self.far + self.cores + self.sides:
            c.wait_send()
        pl.when(row <= 1)(self.hop_right[0].wait_send)
        pl.when(row >= 2)(self.hop_left[0].wait_send)
        pl.when(row <= 2)(self.hop_right[1].wait_send)
        pl.when(row >= 1)(self.hop_left[1].wait_send)
        pl.when(row >= 1)(self.hop_right[1].wait_recv)
        pl.when(row <= 2)(self.hop_left[1].wait_recv)


def first_norm(x_ref, gain_ref, h_ref):
    parts = x_ref.shape[0]
    feat = x_ref.shape[2]
    xs = [x_ref[c].astype(F32) for c in range(parts)]
    total = sum(jnp.sum(v * v, axis=1, keepdims=True) for v in xs)
    scale = lax.rsqrt(total / D + EPS)
    for c in range(parts):
        lanes = slice(c * feat, (c + 1) * feat)
        h_ref[:, lanes] = (xs[c] * scale * gain_ref[c, :1]).astype(BF)


def place_factor_weights(blocks_ref, w_ref):
    n_row, parts, _, feat = blocks_ref.shape
    ranks_each = RANK_COLS // n_row
    for c in range(parts):
        lanes = slice(c * feat, (c + 1) * feat)
        for r in range(n_row):
            w_ref[r * ranks_each : (r + 1) * ranks_each, lanes] = blocks_ref[r, c, :ranks_each]
            w_ref[RANK_COLS + r * GROUP_COLS : RANK_COLS + (r + 1) * GROUP_COLS, lanes] = blocks_ref[
                r, c, ranks_each:
            ]


def make_factors(h_ref, w_ref, turn_ref, hf_ref, bq_ref, kf_ref):
    both = nt(h_ref[...], w_ref[...])
    heads = both[:, RANK_COLS:]
    hf_ref[...] = heads
    cosine = turn_ref[:, :LANES]
    sine = turn_ref[:, LANES:]
    for tile in range(RANK_COLS // LANES):
        lanes = slice(tile * LANES, (tile + 1) * LANES)
        part = both[:, lanes]
        if tile < 4:
            part = part * cosine + swap_halves(part) * sine
        if tile < 3:
            bq_ref[:, lanes] = part
        else:
            kf_ref[:, (tile - 3) * LANES : (tile - 2) * LANES] = part.astype(BF)
    kf_ref[:, 2 * LANES :] = nn(heads.astype(BF), key_columns()).astype(BF)


def make_queries(hf_ref, bq_ref, q_ref):
    heads = hf_ref[...]
    high = heads.astype(BF)
    low = (heads - high.astype(F32)).astype(BF)
    ranks = []
    for r in range(RQ):
        tile = bq_ref[:, (r // 2) * LANES : (r // 2 + 1) * LANES]
        ranks.append(double_left(tile) if r % 2 == 0 else double_right(tile))
    width = 2 * LANES
    for p in range(D // width):
        lanes = slice(p * width, (p + 1) * width)
        acc = None
        for r in range(RQ):
            pick = head_spread(2 * RK + r, p * (width // HD), width)
            term = (nn(high, pick) + nn(low, pick)) * jnp.concatenate([ranks[r]] * 2, axis=1)
            acc = term if acc is None else acc + term
        q_ref[:, lanes] = (acc / RQ).astype(BF)


def front_body(x_ref, gain_ref, blocks_ref, turn_ref, h_ref, hf_ref, bq_ref, kf_ref, q_ref, w_ref):
    first_norm(x_ref, gain_ref, h_ref)
    place_factor_weights(blocks_ref, w_ref)
    make_factors(h_ref, w_ref, turn_ref, hf_ref, bq_ref, kf_ref)
    make_queries(hf_ref, bq_ref, q_ref)


def front(x_parts, gains, blocks, turn):
    rows = x_parts.shape[1]
    return call(
        front_body,
        (
            jax.ShapeDtypeStruct((rows, D), BF),
            jax.ShapeDtypeStruct((rows, HEAD_COLS), F32),
            jax.ShapeDtypeStruct((rows, RQ * HD), F32),
            jax.ShapeDtypeStruct((rows, 3 * LANES), BF),
            jax.ShapeDtypeStruct((rows, D), BF),
            jax.ShapeDtypeStruct((ALL_COLS, D), BF),
        ),
        cost=cost_of(2 * rows * D * 800 * 3, 6 << 20),
    )(x_parts, gains, blocks, turn)


def head_body(
    tok_ref, ranks_ref, heads_ref, gain_one_ref, gain_two_ref, gate_ref, up_ref, down_ref, mix_ref, seg_all_ref,
    inverse_ref,
    x_ref, gains_ref, parts_ref, mixes_ref, h_ref, hf_ref, bq_ref, q_ref, w_ref, win_ref, seg_ref, turn_ref, rows_ref,
    w_own_ref, gain_ref, ffn_ref, blocks_ref, send_sem, recv_sem,
):
    row = lax.axis_index("row")
    col, core, across = neighbours()
    cross = lax.rem(core + 2, 4)
    side = lax.rem(col, 2)
    rows = [lax.rem(row + k, 4) for k in range(4)]
    back = [lax.rem(row + 4 - k, 4) for k in range(4)]
    dp = lax.axis_index("dp")

    rank_rows = ranks_ref.shape[0]
    place = lax.broadcasted_iota(jnp.int32, (GROUP_COLS, FAC * GROUP), 0)
    lane = lax.broadcasted_iota(jnp.int32, (GROUP_COLS, FAC * GROUP), 1)
    factor = lane % FAC
    spot = jnp.where(factor < RQ, factor + 2 * RK, factor - RQ) * GROUP + lane // FAC
    w_own_ref[:rank_rows] = ranks_ref[...]
    w_own_ref[rank_rows:] = nn((place == spot).astype(F32).astype(BF), heads_ref[...]).astype(BF)
    gain_ref[...] = jnp.zeros_like(gain_ref)
    gain_ref[0:1] = gain_one_ref[...]
    gain_ref[1:2] = gain_two_ref[...]
    greet(
        [(None, {"col": c}) for c in (core, across, cross)]
        + [(None, {"row": r}) for r in rows[1:]]
        + [(None, {"dp": 1 - dp})]
    )
    mover = Mover(send_sem, recv_sem)
    started = []

    def go(source, target, **place):
        c = mover.copy(source, target, **place)
        c.start()
        started.append(c)
        return c

    down = [None] + [go(w_own_ref, blocks_ref.at[row, col], row=rows[k]) for k in range(1, 4)]
    sides = [go(w_own_ref, blocks_ref.at[row, col], col=across)]
    cores = [go(w_own_ref, blocks_ref.at[row, col], col=core)]
    toks = []
    rest = []
    for c in (across, cross, core):
        toks.append(go(gain_ref, gains_ref.at[col], col=c))
        toks.append(go(tok_ref.at[c], x_ref.at[col], col=c))
    units = ffn_ref.shape[2]
    hidden = gate_ref.shape[0]
    unit = hidden // 8
    place = lax.broadcasted_iota(jnp.int32, (4 * units, hidden), 0)
    lane = lax.broadcasted_iota(jnp.int32, (4 * units, hidden), 1)
    inside = place % units
    taken = (inside < unit) & (lane == (dp * 4 + place // units) * unit + inside)
    pick = taken.astype(F32).astype(BF)
    for k, source in enumerate((gate_ref, up_ref, down_ref)):
        chosen = nn(pick, source[...]).astype(BF)
        for c in range(4):
            ffn_ref[c, k] = chosen[c * units : (c + 1) * units]
    ffn = [go(ffn_ref.at[c], parts_ref.at[col], col=c) for c in (across, cross, core)]
    part = mix_ref.shape[0] // 2
    half = pl.ds(pl.multiple_of(dp * part, part), part)
    mix_down = [None] + [go(mix_ref.at[half], mixes_ref.at[row, col, half], row=rows[k]) for k in range(1, 4)]
    blocks_ref[row, col] = w_own_ref[...]
    gains_ref[col] = gain_ref[...]
    x_ref[col] = tok_ref[col]
    parts_ref[col] = ffn_ref[col]
    mixes_ref[row, col] = mix_ref[...]
    zero = jnp.zeros(win_ref.shape[1:], BF)
    has_one = row >= 1
    has_two = row >= 2
    for absent, slot in (
        (jnp.logical_not(has_two), 0),
        (jnp.logical_and(jnp.logical_not(has_two), side == 0), 1),
        (jnp.logical_and(jnp.logical_not(has_one), side == 1), 1),
        (jnp.logical_not(has_one), 2),
        (jnp.logical_and(jnp.logical_not(has_one), side == 0), 3),
    ):

        @pl.when(absent)
        def _():
            win_ref[slot] = zero

    keys = seg_ref.shape[1]
    tokens = tok_ref.shape[1]
    block_no = row * 2 + side
    for slot in range(5):
        index = block_no - 4 + slot
        lanes = pl.ds(pl.multiple_of(jnp.maximum(index, 0) * tokens, tokens), tokens)
        seg_ref[:, slot * tokens : (slot + 1) * tokens] = jnp.where(index >= 0, seg_all_ref[col // 2, :, lanes], -1)
    seg_row = seg_ref[...].astype(F32)
    column = jnp.broadcast_to(seg_row, (LANES, keys)).T
    column = jnp.concatenate([column] * (tokens // LANES), axis=1)
    key_idx = lax.broadcasted_iota(jnp.int32, (keys, tokens), 0)
    query_idx = lax.broadcasted_iota(jnp.int32, (keys, tokens), 1) + (keys - tokens)
    before = (column == seg_row[:, keys - tokens :]) & (key_idx < query_idx)
    places = jnp.sum(jnp.where(before, 1.0, 0.0), axis=0, keepdims=True)
    angles = jnp.broadcast_to(places, (LANES, tokens)).T * inverse_ref[...]
    turn_ref[:, :LANES] = jnp.cos(angles)
    sine = jnp.sin(angles)
    turn_ref[:, LANES:] = jnp.where(lane_iota(sine.shape) % HD < HD // 2, -sine, sine)

    for k in range(1, 4):
        down[k].wait_recv()
        block = blocks_ref.at[back[k], col]
        sides.append(go(block, block, col=across))
        cores.append(go(block, block, col=core))
    for c in toks:
        c.wait_recv()
    first_norm(x_ref, gains_ref, h_ref)
    mix_side = []
    for k in range(1, 4):
        mix_down[k].wait_recv()
        block = mixes_ref.at[back[k], col, half]
        mix_side.append(go(block, block, dp=1 - dp))
    for c in ffn:
        c.wait_recv()
    to_right = mover.copy(parts_ref, rows_ref.at[row], row=row + 1)
    to_left = mover.copy(parts_ref, rows_ref.at[row], row=row - 1)
    pl.when(row <= 2)(to_right.start)
    pl.when(row >= 1)(to_left.start)
    passed = []
    for k in range(4):
        sides[k].wait_recv()
        block = blocks_ref.at[back[k], across]
        passed.append(go(block, block, col=core))
    for c in cores + passed:
        c.wait_recv()
    for k in range(4):
        if k > 0:
            mix_side[k - 1].wait_recv()
        block = mixes_ref.at[back[k], col]
        rest.append(go(block, block, col=across))
    place_factor_weights(blocks_ref, w_ref)
    make_factors(h_ref, w_ref, turn_ref, hf_ref, bq_ref, win_ref.at[4])

    own = win_ref.at[4]
    one = mover.copy(own, win_ref.at[2], row=row + 1)
    two = mover.copy(win_ref.at[2], win_ref.at[0], row=row + 1)
    near = mover.copy(own, win_ref.at[3], col=core)
    pass_one = mover.copy(win_ref.at[2], win_ref.at[1 + 2 * side], col=core)
    pass_two = mover.copy(win_ref.at[0], win_ref.at[1], col=core)
    hands_on = jnp.logical_and(has_one, row <= 2)
    sends_two = jnp.logical_and(has_two, side == 1)
    takes_two = jnp.logical_and(has_two, side == 0)
    pl.when(row <= 2)(one.start)
    pl.when(side == 0)(near.start)

    @pl.when(has_one)
    def _():
        one.wait_recv()
        pass_one.start()

    pl.when(hands_on)(two.start)
    make_queries(hf_ref, bq_ref, q_ref)

    @pl.when(has_two)
    def _():
        two.wait_recv()

    pl.when(sends_two)(pass_two.start)

    @pl.when(has_one)
    def _():
        pass_one.wait_recv()
        pass_one.wait_send()

    pl.when(takes_two)(pass_two.wait_recv)
    pl.when(sends_two)(pass_two.wait_send)
    pl.when(side == 1)(near.wait_recv)
    pl.when(side == 0)(near.wait_send)
    pl.when(row <= 2)(one.wait_send)
    pl.when(hands_on)(two.wait_send)
    pl.when(row <= 2)(to_right.wait_send)
    pl.when(row >= 1)(to_left.wait_send)
    pl.when(row >= 1)(to_right.wait_recv)
    pl.when(row <= 2)(to_left.wait_recv)

    def end():
        for c in rest:
            c.wait_recv()
        for c in started:
            c.wait_send()

    return end


def head_attend_body(*refs):
    head_in, cot_ref = refs[:11], refs[11]
    outs, scratch = refs[12:30], refs[30:]
    head_out = outs[:13]
    o_ref, lse_ref, k_ref, v_ref, near_ref = outs[13:]
    mixes_ref, q_ref, win_ref, seg_ref, rows_ref = (head_out[k] for k in (3, 7, 9, 10, 12))
    end = head_body(*head_in, *head_out, *scratch[:6])
    attend_body(
        True, q_ref, win_ref, seg_ref, end, cot_ref, o_ref, lse_ref, k_ref, v_ref, rows_ref, near_ref, mixes_ref,
        *scratch[6:],
    )


def head_attend(tok, ranks_t, heads_t, gain_one, gain_two, gate_t, up_t, down, w_out, segments, inverse, cot):
    rows, feat = tok.shape[1:]
    units = -(-gate_t.shape[0] // 8 // 16) * 16
    block = (ranks_t.shape[0] + GROUP_COLS, feat)
    ffn = (4, 3, units, feat)
    count = 3 + 4 + 4 + 6 + 3 + 3 + 3 + 4 + 4 + 2 + 5
    return pl.pallas_call(
        head_attend_body,
        out_shape=(
            jax.ShapeDtypeStruct(tok.shape, BF),
            jax.ShapeDtypeStruct((4, 8, feat), F32),
            jax.ShapeDtypeStruct(ffn, BF),
            jax.ShapeDtypeStruct((4, 4) + w_out.shape, BF),
            jax.ShapeDtypeStruct((rows, D), BF),
            jax.ShapeDtypeStruct((rows, HEAD_COLS), F32),
            jax.ShapeDtypeStruct((rows, RQ * HD), F32),
            jax.ShapeDtypeStruct((rows, D), BF),
            jax.ShapeDtypeStruct((ALL_COLS, D), BF),
            jax.ShapeDtypeStruct((5, rows, 3 * LANES), BF),
            jax.ShapeDtypeStruct((1, 5 * rows), jnp.int32),
            jax.ShapeDtypeStruct((rows, 2 * LANES), F32),
            jax.ShapeDtypeStruct((4,) + ffn, BF),
            *attend_shapes(rows, 5 * rows),
            jax.ShapeDtypeStruct((4,) + cot.shape, BF),
        ),
        in_specs=[VMEM] * 11 + [ANY],
        out_specs=(VMEM,) * 12 + (ANY,) + (VMEM,) * 4 + (ANY,),
        scratch_shapes=[
            pltpu.VMEM(block, BF),
            pltpu.VMEM((8, feat), F32),
            pltpu.VMEM(ffn, BF),
            pltpu.VMEM((4, 4) + block, BF),
            pltpu.SemaphoreType.DMA((count,)),
            pltpu.SemaphoreType.DMA((count,)),
            pltpu.VMEM((5 * rows, rows), F32),
            pltpu.VMEM((2 * RK, 5 * rows, LANES), F32),
            pltpu.SemaphoreType.DMA((22,)),
            pltpu.SemaphoreType.DMA((22,)),
        ],
        compiler_params=comm_params(1),
        cost_estimate=cost_of(2 * rows * D * (800 * 3 + 5 * rows * 16), 30 << 20),
    )(tok, ranks_t, heads_t, gain_one, gain_two, gate_t, up_t, down, w_out, segments, inverse, cot)


def window_lanes(ref, lanes):
    value = ref[..., lanes]
    return value.reshape(-1, value.shape[-1])


def mask_bias(seg_ref, keys, rows):
    seg_row = seg_ref[...].astype(F32)
    wide = jnp.broadcast_to(seg_row, (LANES, keys))
    column = wide.T
    column = jnp.concatenate([column] * (rows // LANES), axis=1)
    key_idx = lax.broadcasted_iota(jnp.int32, (keys, rows), 0)
    query_idx = lax.broadcasted_iota(jnp.int32, (keys, rows), 1) + (keys - rows)
    same = column == seg_row[:, keys - rows :]
    return jnp.where(same & (key_idx <= query_idx), 0.0, NEG)


def attend_body(fast, q_ref, kf_ref, seg_ref, *refs):
    if fast:
        head_end, cot_ref, o_ref, lse_ref, k_ref, v_ref, w_rows_ref, cot_near_ref, mixes_ref = refs[:9]
        bias_ref, dup_ref, send_sem, recv_sem = refs[9:]
        side_work = AttendCopies(head_end, cot_ref, w_rows_ref, cot_near_ref, mixes_ref, send_sem, recv_sem)
        side_work.first()
    else:
        o_ref, lse_ref, k_ref, v_ref, bias_ref, dup_ref = refs
    rows = q_ref.shape[0]
    keys = seg_ref.shape[1]
    bias_ref[...] = mask_bias(seg_ref, keys, rows)
    for s in range(2 * RK):
        tile = window_lanes(kf_ref, slice((s // 2) * LANES, (s // 2 + 1) * LANES)).astype(F32)
        dup_ref[s] = double_left(tile) if s % 2 == 0 else double_right(tile)

    def pair(p, carried):
        if fast:
            pl.when(p == 2)(side_work.early)
            pl.when(p == 4)(side_work.second)
        lanes = pl.ds(pl.multiple_of(p * LANES, LANES), LANES)
        weights = window_lanes(kf_ref, slice(2 * LANES, 3 * LANES))
        made = []
        for kind in range(2):
            acc = None
            for s in range(RK):
                pick = spread(LANES, (kind * RK + s) * H + 2 * p, LANES)
                term = nn(weights, pick) * dup_ref[kind * RK + s]
                acc = term if acc is None else acc + term
            made.append((acc / RK).astype(BF))
        k_tile, v_tile = made
        k_ref[:, lanes] = k_tile
        v_ref[:, lanes] = v_tile
        v_turned = v_tile.astype(F32).T.astype(BF)
        q_turned = (q_ref[:, lanes].astype(F32) * HD**-0.5).T
        half = lax.broadcasted_iota(jnp.int32, q_turned.shape, 0) // HD
        outs = []
        for side in range(2):
            q_side = jnp.where(half == side, q_turned, 0.0).astype(BF)
            scores = nn(k_tile, q_side) + bias_ref[...]
            peak = jnp.max(scores, axis=0, keepdims=True)
            weight = jnp.exp(scores - peak)
            total = jnp.sum(weight, axis=0, keepdims=True)
            probs = (weight * (1.0 / total)).astype(BF)
            outs.append(nn(v_turned[side * HD : (side + 1) * HD], probs))
            lse_ref[2 * p + side] = jnp.broadcast_to(peak + jnp.log(total), (8, rows))
        o_ref[:, lanes] = jnp.concatenate(outs, axis=0).T.astype(BF)
        return carried

    lax.fori_loop(0, PAIRS, pair, 0)
    if fast:
        side_work.last()


def attend_shapes(rows, keys):
    return [
        jax.ShapeDtypeStruct((rows, D), BF),
        jax.ShapeDtypeStruct((H, 8, rows), F32),
        jax.ShapeDtypeStruct((keys, D), BF),
        jax.ShapeDtypeStruct((keys, D), BF),
    ]


def attend(q, kf_window, seg_window):
    rows = q.shape[0]
    keys = kf_window.shape[0]
    return call(
        functools.partial(attend_body, False),
        tuple(attend_shapes(rows, keys)),
        scratch=(pltpu.VMEM((keys, rows), F32), pltpu.VMEM((2 * RK, keys, LANES), F32)),
        cost=cost_of(2 * rows * keys * D * 16, 16 << 20),
    )(q, kf_window, seg_window)


def attend_back_body(fast, q_ref, k_ref, v_ref, do_ref, lse_ref, kf_ref, seg_ref, *refs):
    if fast:
        dq_ref, dkf_ref = refs[5:7]
        bias_ref, dup_ref, sum_ref, fac_ref = refs[10:14]
        side_work = BackCopies(refs[:5] + refs[7:10] + refs[14:28], refs[28:])
        side_work.first()
    else:
        dq_ref, dkf_ref, bias_ref, dup_ref, sum_ref, fac_ref = refs
    rows = q_ref.shape[0]
    keys = seg_ref.shape[1]
    bias_ref[...] = mask_bias(seg_ref, keys, rows)
    for s in range(2 * RK):
        tile = window_lanes(kf_ref, slice((s // 2) * LANES, (s // 2 + 1) * LANES)).astype(F32)
        dup_ref[s] = double_left(tile) if s % 2 == 0 else double_right(tile)
    sum_ref[...] = jnp.zeros_like(sum_ref)
    fac_ref[...] = jnp.zeros_like(fac_ref)

    def pair(p, carried):
        if fast:
            pl.when(p == 1)(side_work.cross_x)
            pl.when(p == 3)(side_work.second)
            pl.when(p == 4)(side_work.last_hop)
            pl.when(p == 6)(side_work.third)
        lanes = pl.ds(pl.multiple_of(p * LANES, LANES), LANES)
        k_tile = k_ref[:, lanes]
        v_tile = v_ref[:, lanes]
        k_turned = k_tile.astype(F32).T.astype(BF)
        q_tile = q_ref[:, lanes].astype(F32) * HD**-0.5
        do_tile = do_ref[:, lanes].astype(F32)
        q_turned = q_tile.T
        do_turned = do_tile.T
        half = lax.broadcasted_iota(jnp.int32, q_turned.shape, 0) // HD
        lane_half = lax.broadcasted_iota(jnp.int32, q_tile.shape, 1) // HD
        d_k = None
        d_v = None
        d_q = []
        for side in range(2):
            q_side = jnp.where(half == side, q_turned, 0.0).astype(BF)
            do_side = jnp.where(half == side, do_turned, 0.0).astype(BF)
            scores = nn(k_tile, q_side) + bias_ref[...]
            probs = jnp.exp(scores - lse_ref[2 * p + side][:1])
            d_prob = nn(v_tile, do_side)
            delta = jnp.sum(probs * d_prob, axis=0, keepdims=True)
            d_score = (probs * (d_prob - delta)).astype(BF)
            d_q.append(nn(k_turned[side * HD : (side + 1) * HD], d_score))
            q_back = jnp.where(lane_half == side, q_tile, 0.0).astype(BF)
            do_back = jnp.where(lane_half == side, do_tile, 0.0).astype(BF)
            part_k = nn(d_score, q_back)
            part_v = nn(probs.astype(BF), do_back)
            d_k = part_k if d_k is None else d_k + part_k
            d_v = part_v if d_v is None else d_v + part_v
        dq_ref[:, lanes] = jnp.concatenate(d_q, axis=0).T * HD**-0.5
        weights = window_lanes(kf_ref, slice(2 * LANES, 3 * LANES))
        for kind, grad in ((0, d_k), (1, d_v)):
            for s in range(RK):
                slot = kind * RK + s
                pick = spread(LANES, slot * H + 2 * p, LANES)
                sum_ref[slot] += nn(weights, pick) * grad
                fac_ref[...] += two_pass(grad * dup_ref[slot], collect(LANES, LANES, slot * H + 2 * p))
        return carried

    lax.fori_loop(0, PAIRS, pair, 0)
    for tile in range(2):
        first = sum_ref[2 * tile]
        second = sum_ref[2 * tile + 1]
        first = first + pltpu.roll(first, HD, 1)
        second = second + pltpu.roll(second, HD, 1)
        merged = jnp.where(lane_iota(first.shape) < HD, first, second)
        blocks = dkf_ref.shape[:-1] + (LANES,)
        dkf_ref[..., tile * LANES : (tile + 1) * LANES] = (merged / RK).astype(BF).reshape(blocks)
    dkf_ref[..., 2 * LANES :] = (fac_ref[...] / RK).astype(BF).reshape(blocks)
    if fast:
        side_work.last()


def back_scratch(rows, keys):
    return [
        pltpu.VMEM((keys, rows), F32),
        pltpu.VMEM((2 * RK, keys, LANES), F32),
        pltpu.VMEM((2 * RK, keys, LANES), F32),
        pltpu.VMEM((keys, LANES), F32),
    ]


def attend_back(q, k, v, d_heads, lse, kf_window, seg_window):
    rows = q.shape[0]
    keys = kf_window.shape[0]
    return call(
        functools.partial(attend_back_body, False),
        (jax.ShapeDtypeStruct((rows, D), F32), jax.ShapeDtypeStruct(kf_window.shape, BF)),
        scratch=back_scratch(rows, keys),
        cost=cost_of(2 * rows * keys * D * 40, 16 << 20),
    )(q, k, v, d_heads, lse, kf_window, seg_window)


def mixing_body(x_ref, heads_ref, w_out_ref, gain_ref, mixed_ref, h_ref):
    parts, _, feat = x_ref.shape
    rows_of = w_out_ref.shape[0]
    head_rows = w_out_ref.shape[2]
    total = None
    for c in range(parts):
        lanes = slice(c * feat, (c + 1) * feat)
        acc = x_ref[c].astype(F32)
        for r in range(rows_of):
            acc = acc + nn(heads_ref[:, r * head_rows : (r + 1) * head_rows], w_out_ref[r, c])
        mixed_ref[:, lanes] = acc
        part = jnp.sum(acc * acc, axis=1, keepdims=True)
        total = part if total is None else total + part
    scale = lax.rsqrt(total / D + EPS)
    for c in range(parts):
        lanes = slice(c * feat, (c + 1) * feat)
        h_ref[:, lanes] = (mixed_ref[:, lanes] * scale * gain_ref[c, 1:2]).astype(BF)


def mixing(x_parts, heads, w_out, gains):
    rows = heads.shape[0]
    return call(
        mixing_body,
        (jax.ShapeDtypeStruct((rows, D), F32), jax.ShapeDtypeStruct((rows, D), BF)),
        cost=cost_of(2 * rows * D * D, 5 << 20),
    )(x_parts, heads, w_out, gains)


def ffn_steps(blocks, h_at, cot_at, w_ref, hid_ref, dg_ref, du_ref, out_at, back_at):
    def block(t, carried):
        h = h_at(t)[...]
        gate = nt(h, w_ref[0])
        up = nt(h, w_ref[1])
        d_hidden = nt(cot_at(t)[...], w_ref[2])
        sig = 1.0 / (1.0 + jnp.exp(-gate))
        silu = gate * sig
        hidden = (silu * up).astype(BF)
        d_gate = (d_hidden * up * sig * (1.0 + gate * (1.0 - sig))).astype(BF)
        d_up = (d_hidden * silu).astype(BF)
        rows = h.shape[0]
        place = pl.ds(pl.multiple_of(t * rows, rows), rows)
        hid_ref[place] = hidden
        dg_ref[place] = d_gate
        du_ref[place] = d_up
        out_at(t)[...] = nn(hidden, w_ref[2]).astype(BF)
        back_at(t)[...] = (nn(d_gate, w_ref[0]) + nn(d_up, w_ref[1])).astype(BF)
        return carried

    lax.fori_loop(0, blocks, block, 0)


def ffn_body(h_ref, cot_ref, w_ref, out_ref, back_ref, g_ref, hid_ref, dg_ref, du_ref):
    parts, rows, _ = h_ref.shape
    ffn_steps(
        parts, lambda t: h_ref.at[t], lambda t: cot_ref.at[t], w_ref, hid_ref, dg_ref, du_ref,
        lambda t: out_ref.at[t], lambda t: back_ref.at[t],
    )
    h_all = h_ref[...].reshape(parts * rows, D)
    cot_all = cot_ref[...].reshape(parts * rows, D)
    for place, (left, right) in enumerate(((dg_ref, h_all), (du_ref, h_all), (hid_ref, cot_all))):
        g_ref[place] = tn(left[...], right).astype(BF)


def ffn(h_all, cot_all, w):
    parts, rows, _ = h_all.shape
    units = w.shape[1]
    return call(
        ffn_body,
        (
            jax.ShapeDtypeStruct(h_all.shape, BF),
            jax.ShapeDtypeStruct(h_all.shape, BF),
            jax.ShapeDtypeStruct(w.shape, BF),
        ),
        scratch=[pltpu.VMEM((parts * rows, units), BF)] * 3,
        cost=cost_of(2 * parts * rows * 9 * D * units, 20 << 20),
    )(h_all, cot_all, w)


def unmix_math(
    mixed_ref, cot_ref, d_h, heads_ref, w_out_ref, gain_ref, d_mixed_ref, d_heads_ref, g_out_ref, g_gain_ref
):
    rows_of, parts, head_rows, feat = w_out_ref.shape
    mixed = mixed_ref[...]
    scale = lax.rsqrt(jnp.sum(mixed * mixed, axis=1, keepdims=True) / D + EPS)
    normed = mixed * scale
    g_gain_ref[...] = jnp.sum(d_h * normed, axis=0, keepdims=True)
    gain = jnp.concatenate([gain_ref[c, 1:2] for c in range(parts)], axis=1)
    inner = d_h * gain
    dot = jnp.sum(inner * normed, axis=1, keepdims=True) / D
    d_mixed = cot_ref[...].astype(F32) + scale * (inner - normed * dot)
    d_mixed_ref[...] = d_mixed
    low = d_mixed.astype(BF)
    grad = tn(heads_ref[...], low)
    for r in range(rows_of):
        acc = None
        for c in range(parts):
            lanes = slice(c * feat, (c + 1) * feat)
            term = nt(low[:, lanes], w_out_ref[r, c])
            acc = term if acc is None else acc + term
            g_out_ref[r, c] = grad[r * head_rows : (r + 1) * head_rows, lanes].astype(BF)
        d_heads_ref[:, r * head_rows : (r + 1) * head_rows] = acc.astype(BF)


def write_output(mixed_ref, total, out_ref):
    parts, _, feat = out_ref.shape
    for c in range(parts):
        lanes = slice(c * feat, (c + 1) * feat)
        out_ref[c] = (mixed_ref[:, lanes] + total[:, lanes]).astype(BF)


def unmix_body(
    dh_ref, sum_ref, mixed_ref, cot_ref, heads_ref, w_out_ref, gain_ref,
    out_ref, d_mixed_ref, d_heads_ref, g_out_ref, g_gain_ref,
):
    unmix_math(
        mixed_ref, cot_ref, dh_ref[...], heads_ref, w_out_ref, gain_ref,
        d_mixed_ref, d_heads_ref, g_out_ref, g_gain_ref,
    )
    write_output(mixed_ref, sum_ref[...], out_ref)


def middle_body(
    x_ref, heads_ref, w_out_ref, gain_ref, cot_own_ref, cot_in_ref, w_own_ref, rows_ref,
    mixed_ref, d_mixed_ref, d_heads_ref, g_out_ref, g_gain_ref, g_ref, out_pair_ref, hop_ref,
    w_ref, h_ref, cot_ref, hid_ref, dg_ref, du_ref, back_ref, fwd_ref, back_got_ref, fwd_got_ref,
    pair_ref, diag_ref, far_ref, send_sem, recv_sem, w_sem, cot_sem,
):
    row = lax.axis_index("row")
    col, core, across = neighbours()
    dp, (me, on_x, on_y, on_both) = square()
    x, mine = col // 2, lax.rem(col, 2)
    y = 1 - dp
    parts, rows, feat = x_ref.shape
    units = rows_ref.shape[3]
    greet(
        [
            (None, {"col": core}),
            (None, {"col": across}),
            (None, {"dp": y}),
            (row <= 2, {"row": row + 1}),
            (row >= 1, {"row": row - 1}),
        ]
    )
    mover = Mover(send_sem, recv_sem)

    def w_place(r, c):
        return w_ref.at[:, pl.ds(pl.multiple_of(r * units, units), units), pl.ds(c * feat, feat)]

    local = []
    for k in range(4):
        r = lax.rem(row + k, 4)
        for c in range(4):
            source = w_own_ref.at[c] if k == 0 else rows_ref.at[r, c]
            copy = pltpu.make_async_copy(source, w_place(r, c), w_sem.at[k, c])
            copy.start()
            local.append(copy)
    cots = []
    for k in range(4):
        from_x = lax.rem(x + k % 2, 2)
        from_dp = lax.rem(dp + k // 2, 2)
        lanes = pl.ds(pl.multiple_of((from_x * 2 + mine) * feat, feat), feat)
        for c in range(4):
            part = pl.ds(c * rows, rows)
            source = cot_own_ref.at[part] if k == 0 else cot_in_ref.at[from_dp * 2 + from_x, part]
            spot = from_dp * 2 + c // 2
            copy = pltpu.make_async_copy(source, cot_ref.at[lax.rem(mine + c, 2), spot, :, lanes], cot_sem.at[k, c])
            copy.start()
            local.append(copy)
            sent = mover.copy(source, cot_ref.at[lax.rem(mine + c + 1, 2), spot, :, lanes], col=core)
            sent.start()
            cots.append(sent)

    total = None
    for c in range(parts):
        lanes = slice(c * feat, (c + 1) * feat)
        acc = x_ref[c].astype(F32)
        for r in range(4):
            acc = acc + nn(heads_ref[:, r * feat : (r + 1) * feat], w_out_ref[r, c])
        mixed_ref[:, lanes] = acc
        part = jnp.sum(acc * acc, axis=1, keepdims=True)
        total = part if total is None else total + part
    scale = lax.rsqrt(total / D + EPS)
    for c in range(parts):
        lanes = slice(c * feat, (c + 1) * feat)
        h_ref[0, me, :, lanes] = (mixed_ref[:, lanes] * scale * gain_ref[c, 1:2]).astype(BF)

    half = rows // 2
    top, low = pl.ds(0, half), pl.ds(half, half)

    def h_copy(spot, part=None, side=0, **place):
        source = h_ref.at[0, spot] if part is None else h_ref.at[0, spot, part]
        target = h_ref.at[side, spot] if part is None else h_ref.at[side, spot, part]
        return mover.copy(source, target, **place)

    x_low = h_copy(me, low, col=across)
    y_top = h_copy(me, top, dp=y)
    x_top = h_copy(me, top, col=across)
    y_low = h_copy(me, low, dp=y)
    near = h_copy(me, None, 1, col=core)
    both_low = h_copy(on_x, low, dp=y)
    both_top = h_copy(on_y, top, col=across)
    near_first = [h_copy(on_x, low, 1, col=core), h_copy(on_y, top, 1, col=core)]
    near_second = [h_copy(on_x, top, 1, col=core), h_copy(on_y, low, 1, col=core)]
    near_both = h_copy(on_both, None, 1, col=core)
    for c in (x_low, y_top, near, x_top, y_low):
        c.start()
    steps = (
        ((me, top), (me, low)),
        ((on_x, low), (on_y, top)),
        ((on_x, top), (on_y, low)),
        ((on_both, top), (on_both, low)),
    )
    back_near = [[mover.copy(back_ref.at[1, s, p], back_got_ref.at[s, p], col=core) for s, p in two] for two in steps]
    fwd_near = [[mover.copy(fwd_ref.at[1, s, p], fwd_got_ref.at[s, p], col=core) for s, p in two] for two in steps]
    diag = [
        mover.copy(pair_ref.at[on_both, top], diag_ref.at[0], col=across),
        mover.copy(pair_ref.at[on_both, low], diag_ref.at[1], dp=y),
    ]
    far = [
        mover.copy(pair_ref.at[on_x, top], far_ref.at[0, top], col=across),
        mover.copy(pair_ref.at[on_y, low], far_ref.at[1, low], dp=y),
        mover.copy(pair_ref.at[on_y, top], far_ref.at[1, top], dp=y),
        mover.copy(pair_ref.at[on_x, low], far_ref.at[0, low], col=across),
    ]

    def add_pair(k):
        for (s, p), c in zip(steps[k], back_near[k]):
            c.wait_recv()
            pair_ref[s, p] = (back_ref[0, s, p].astype(F32) + back_got_ref[s, p].astype(F32)).astype(BF)

    for copy in local:
        copy.wait()
    for c in cots:
        c.wait_recv()

    def block(t, carried):
        @pl.when(t == 1)
        def _():
            near.wait_recv()

        @pl.when(t == 2)
        def _():
            x_low.wait_recv()
            both_low.start()
            near_first[0].start()
            y_top.wait_recv()
            both_top.start()
            near_first[1].start()

        @pl.when(t == 3)
        def _():
            for c in near_first:
                c.wait_recv()

        @pl.when(t == 4)
        def _():
            x_top.wait_recv()
            near_second[0].start()
            y_low.wait_recv()
            near_second[1].start()

        @pl.when(t == 5)
        def _():
            for c in near_second:
                c.wait_recv()
            add_pair(1)

        @pl.when(t == 6)
        def _():
            both_low.wait_recv()
            both_top.wait_recv()
            near_both.start()

        @pl.when(t == 7)
        def _():
            near_both.wait_recv()
            add_pair(2)
            far[0].start()
            far[1].start()

        name, side = t // 2, lax.rem(t, 2)
        first_dp = lax.rem(dp + jnp.where(name == 3, 1, 0), 2)
        first_x = lax.rem(x + jnp.where(name >= 1, 1, 0), 2)
        first = first_dp * 2 + first_x
        other_dp = lax.rem(dp + jnp.where(name >= 1, 1, 0), 2)
        other_x = lax.rem(x + jnp.where(name == 3, 1, 0), 2)
        other = other_dp * 2 + other_x
        first_rows = pl.ds(pl.multiple_of(jnp.where(name == 1, half, 0), half), half)
        other_rows = pl.ds(pl.multiple_of(jnp.where(name == 1, 0, half), half), half)
        h = jnp.concatenate([h_ref[side, first, first_rows], h_ref[side, other, other_rows]], axis=0)
        cot = jnp.concatenate([cot_ref[side, first, first_rows], cot_ref[side, other, other_rows]], axis=0)
        gate = nt(h, w_ref[0])
        up = nt(h, w_ref[1])
        d_hidden = nt(cot, w_ref[2])
        sig = 1.0 / (1.0 + jnp.exp(-gate))
        silu = gate * sig
        hidden = (silu * up).astype(BF)
        d_gate = (d_hidden * up * sig * (1.0 + gate * (1.0 - sig))).astype(BF)
        d_up = (d_hidden * silu).astype(BF)
        back = (nn(d_gate, w_ref[0]) + nn(d_up, w_ref[1])).astype(BF)
        fwd = nn(hidden, w_ref[2]).astype(BF)
        for spot, part, cut in ((first, first_rows, slice(0, half)), (other, other_rows, slice(half, rows))):
            start = jnp.where(part.start == 0, 0, half)
            place = pl.ds(pl.multiple_of((side * 4 + spot) * rows + start, half), half)
            hid_ref[place] = hidden[cut]
            dg_ref[place] = d_gate[cut]
            du_ref[place] = d_up[cut]
            back_ref[side, spot, part] = back[cut]
            fwd_ref[side, spot, part] = fwd[cut]
        for k in range(4):

            @pl.when(t == 2 * k + 1)
            def _():
                for c in back_near[k] + fwd_near[k]:
                    c.start()

        return carried

    lax.fori_loop(0, 8, block, 0)
    add_pair(3)
    for c in diag:
        c.start()

    hops = []
    for place in range(3):
        to_right = mover.copy(g_ref.at[3, place], hop_ref.at[place], row=row + 1)
        to_left = mover.copy(g_ref.at[0, place], hop_ref.at[place], row=row - 1)
        hops.append((to_right, to_left))

    def gradient(place, left, right):
        grad = tn(left[...], right[...].reshape(8 * rows, D))
        for r in range(4):
            g_ref[r, place] = grad[r * units : (r + 1) * units].astype(BF)
        pl.when(row == 0)(hops[place][0].start)
        pl.when(row == 3)(hops[place][1].start)

    gradient(0, dg_ref, h_ref)
    gradient(1, du_ref, h_ref)
    for k, (s, part) in enumerate(((on_y, top), (on_x, low))):
        if k == 1:
            far[0].wait_send()
        else:
            far[1].wait_send()
        diag[k].wait_recv()
        pair_ref[s, part] = (pair_ref[s, part].astype(F32) + diag_ref[k].astype(F32)).astype(BF)
        far[2 + k].start()
    gradient(2, hid_ref, cot_ref)
    for two, copies in zip(steps, fwd_near):
        for (s, p), c in zip(two, copies):
            c.wait_recv()
            out_pair_ref[s, p] = (fwd_ref[0, s, p].astype(F32) + fwd_got_ref[s, p].astype(F32)).astype(BF)
    add_pair(0)
    for c in far:
        c.wait_recv()
    d_h = pair_ref[me].astype(F32) + far_ref[0].astype(F32) + far_ref[1].astype(F32)
    unmix_math(
        mixed_ref, cot_ref.at[0, me], d_h, heads_ref, w_out_ref, gain_ref,
        d_mixed_ref, d_heads_ref, g_out_ref, g_gain_ref,
    )
    for c in cots + [x_low, y_top, x_top, y_low, near, both_low, both_top, near_both] + near_first + near_second:
        c.wait_send()
    for two in back_near + fwd_near:
        for c in two:
            c.wait_send()
    for c in diag + far[2:]:
        c.wait_send()
    for to_right, to_left in hops:
        pl.when(row == 0)(to_right.wait_send)
        pl.when(row == 3)(to_left.wait_send)
        pl.when(row == 1)(to_right.wait_recv)
        pl.when(row == 2)(to_left.wait_recv)


def middle(x_parts, heads, w_out, gains, cot_own, cot_near, w_own, w_rows):
    parts, rows, feat = x_parts.shape
    units = w_rows.shape[3]
    count = 16 + 12 + 16 + 6 + 6
    square_of = pltpu.VMEM((2, 4, rows, D), BF)
    hidden_of = pltpu.VMEM((8 * rows, 4 * units), BF)
    quarter = pltpu.VMEM((4, rows, D), BF)
    return pl.pallas_call(
        middle_body,
        out_shape=(
            jax.ShapeDtypeStruct((rows, D), F32),
            jax.ShapeDtypeStruct((rows, D), F32),
            jax.ShapeDtypeStruct((rows, D), BF),
            jax.ShapeDtypeStruct(w_out.shape, BF),
            jax.ShapeDtypeStruct((1, D), F32),
            jax.ShapeDtypeStruct((4, 3, units, D), BF),
            jax.ShapeDtypeStruct((4, rows, D), BF),
            jax.ShapeDtypeStruct((3, units, D), BF),
        ),
        in_specs=[VMEM] * 4 + [ANY] * 4,
        out_specs=(VMEM,) * 7 + (ANY,),
        scratch_shapes=[pltpu.VMEM((3, 4 * units, D), BF), square_of, square_of]
        + [hidden_of] * 3
        + [square_of, square_of, quarter, quarter, quarter]
        + [
            pltpu.VMEM((2, rows // 2, D), BF),
            pltpu.VMEM((2, rows, D), BF),
            pltpu.SemaphoreType.DMA((count,)),
            pltpu.SemaphoreType.DMA((count,)),
            pltpu.SemaphoreType.DMA((4, 4)),
            pltpu.SemaphoreType.DMA((4, 4)),
        ],
        compiler_params=comm_params(4),
        cost_estimate=cost_of(2 * 8 * rows * 9 * D * 4 * units, 24 << 20),
    )(x_parts, heads, w_out, gains, cot_own, cot_near, w_own, w_rows)


def unmix(dh, out_sum, mixed, cot_own, heads, w_out, gains):
    rows = heads.shape[0]
    parts, feat = w_out.shape[1], w_out.shape[3]
    outs = (
        jax.ShapeDtypeStruct((parts, rows, feat), BF),
        jax.ShapeDtypeStruct((rows, D), F32),
        jax.ShapeDtypeStruct((rows, D), BF),
        jax.ShapeDtypeStruct(w_out.shape, BF),
        jax.ShapeDtypeStruct((1, D), F32),
    )
    return call(unmix_body, outs, cost=cost_of(4 * rows * D * D, 18 << 20))(
        dh, out_sum, mixed, cot_own, heads, w_out, gains
    )


def query_grads(ranks_taken, dq, high, low, bq_ref):
    fac = None
    folded = []
    for r in ranks_taken:
        tile = bq_ref[:, (r // 2) * LANES : (r // 2 + 1) * LANES]
        rank = double_left(tile) if r % 2 == 0 else double_right(tile)
        product = dq * jnp.concatenate([rank] * PAIRS, axis=1)
        term = two_pass(product, head_collect(2 * RK + r))
        fac = term if fac is None else fac + term
        pick = head_spread(2 * RK + r, 0, D)
        terms = (nn(high, pick) + nn(low, pick)) * dq
        acc = terms[:, :LANES]
        for p in range(1, PAIRS):
            acc = acc + terms[:, p * LANES : (p + 1) * LANES]
        folded.append(acc + pltpu.roll(acc, HD, 1))
    return fac, folded


def turned_back(part, turn_ref):
    return part * turn_ref[:, :LANES] - swap_halves(part) * turn_ref[:, LANES:]


def put_query_grads(folded, first, turn_ref, d_ref):
    lane = lane_iota(folded[0].shape)
    for k in range(len(folded) // 2):
        merged = jnp.where(lane < HD, folded[2 * k], folded[2 * k + 1])
        tile = first // 2 + k
        d_ref[:, tile * LANES : (tile + 1) * LANES] = turned_back(merged, turn_ref).astype(BF)


def put_key_grads(dkf, fac, turn_ref, d_ref):
    d_ref[:, 3 * LANES : 4 * LANES] = turned_back(dkf[:, :LANES], turn_ref).astype(BF)
    d_ref[:, 4 * LANES : 5 * LANES] = dkf[:, LANES : 2 * LANES].astype(BF)
    fac = fac.astype(BF).astype(F32) + nt(dkf[:, 2 * LANES :].astype(BF), key_columns())
    d_ref[:, RANK_COLS:] = fac.astype(BF)


def factor_weight_grads(d_ref, h_ref, gains, g_two_ref, g_ref):
    n_row, parts, _, feat = g_ref.shape
    grad = tn(d_ref[...], h_ref[...])
    ranks_each = RANK_COLS // n_row
    used = FAC * GROUP
    for c in range(parts):
        lanes = slice(c * feat, (c + 1) * feat)
        tail = jnp.concatenate(
            [gains[c], g_two_ref[:, lanes], jnp.zeros((GROUP_COLS - used - 2, feat), F32)], axis=0
        )
        for r in range(n_row):
            first = RANK_COLS + r * GROUP_COLS
            g_ref[r, c, :ranks_each] = grad[r * ranks_each : (r + 1) * ranks_each, lanes].astype(BF)
            g_ref[r, c, ranks_each:] = jnp.concatenate([grad[first : first + used, lanes], tail], axis=0).astype(BF)


def first_norm_back(d_h, x_ref, gain_ref, d_mixed_ref, gi_ref):
    parts, _, feat = x_ref.shape
    xs = [x_ref[c].astype(F32) for c in range(parts)]
    total = sum(jnp.sum(v * v, axis=1, keepdims=True) for v in xs)
    scale = lax.rsqrt(total / D + EPS)
    dot = None
    gains = []
    for c in range(parts):
        normed = xs[c] * scale
        grad = d_h[:, c * feat : (c + 1) * feat]
        gains.append(jnp.sum(grad * normed, axis=0, keepdims=True))
        part = jnp.sum(grad * gain_ref[c, :1] * normed, axis=1, keepdims=True)
        dot = part if dot is None else dot + part
    for c in range(parts):
        lanes = slice(c * feat, (c + 1) * feat)
        normed = xs[c] * scale
        total = d_mixed_ref[:, lanes] + scale * (d_h[:, lanes] * gain_ref[c, :1] - normed * (dot / D))
        gi_ref[c] = total.astype(gi_ref.dtype)
    return gains


def back_body(
    dq_ref, dkf_ref, hf_ref, bq_ref, turn_ref, w_ref, h_ref, x_ref, gain_ref, d_mixed_ref, g_two_ref,
    gi_ref, g_ref, d_ref,
):
    heads = hf_ref[...]
    high = heads.astype(BF)
    low = (heads - high.astype(F32)).astype(BF)
    fac, folded = query_grads(range(RQ), dq_ref[...] * (1.0 / RQ), high, low, bq_ref)
    put_query_grads(folded, 0, turn_ref, d_ref)
    put_key_grads(dkf_ref[...].astype(F32), fac, turn_ref, d_ref)
    gains = first_norm_back(nn(d_ref[...], w_ref[...]), x_ref, gain_ref, d_mixed_ref, gi_ref)
    factor_weight_grads(d_ref, h_ref, gains, g_two_ref, g_ref)


def back(dq, dkf, hf, bq, turn, w_rh, h, x_parts, gains, d_mixed, g_two, n_row):
    rows = dq.shape[0]
    parts, _, feat = x_parts.shape
    each = RANK_COLS // n_row + GROUP_COLS
    return call(
        back_body,
        (jax.ShapeDtypeStruct(x_parts.shape, F32), jax.ShapeDtypeStruct((n_row, parts, each, feat), BF)),
        scratch=[pltpu.VMEM((rows, ALL_COLS), BF)],
        cost=cost_of(2 * rows * D * 800 * 6, 12 << 20),
    )(dq, dkf, hf, bq, turn, w_rh, h, x_parts, gains, d_mixed, g_two)


def tail_body(
    win_ref, dq_ref, hf_ref, bq_ref, turn_ref, w_ref, h_ref, x_ref, gain_ref, d_mixed_ref, g_two_ref,
    rows_ref, ends_ref, part_ref,
    grad_ref, gi_all_ref, cols_ref, cols_other_ref, mix_ref, mix_other_ref,
    d_ref, gi_ref, wnear_ref, wsend_ref, wfar_ref, rows_own_ref, cols_send_ref, mix_got_ref,
    g_ref, near_ref, pair_ref, far_ref, side_ref, down_ref, last_ref, end_ref,
    send_sem, recv_sem, local_sem,
):
    row = lax.axis_index("row")
    col, core, across = neighbours()
    cross = lax.rem(core + 2, 4)
    dp = lax.axis_index("dp")
    x, mine = col // 2, lax.rem(col, 2)
    y = 1 - dp
    order = [lax.rem(row + k, 4) for k in (1, 2, 3, 0)]
    mover = Mover(send_sem, recv_sem)
    started = []

    def go(source, target, **place):
        c = mover.copy(source, target, **place)
        c.start()
        started.append(c)
        return c

    rows_own = pltpu.make_async_copy(rows_ref.at[row], rows_own_ref, local_sem.at[1])
    rows_own.start()

    near_one = go(win_ref.at[1], wnear_ref.at[0], col=core)
    near_two = go(win_ref.at[3], wnear_ref.at[1], col=core)
    one = mover.copy(wsend_ref.at[0], wfar_ref.at[0], row=row - 1)
    two = mover.copy(wsend_ref.at[1], wfar_ref.at[1], row=row - 1)
    hands_on = jnp.logical_and(row >= 1, row <= 2)
    left = mine == 0
    heads = hf_ref[...]
    high = heads.astype(BF)
    low = (heads - high.astype(F32)).astype(BF)
    dq = dq_ref[...] * (1.0 / RQ)
    near_one.wait_recv()
    near_two.wait_recv()
    zero = jnp.zeros(wnear_ref.shape[1:], F32)
    from_low = wnear_ref[0].astype(F32)
    from_high = wnear_ref[1].astype(F32)
    wsend_ref[1] = (win_ref[0].astype(F32) + jnp.where(left, zero, from_low)).astype(BF)
    pl.when(row >= 2)(two.start)

    width = x_ref.shape[2]
    rows_own.wait()
    for place in range(3):
        total = rows_own_ref[place].astype(F32)
        total = total + jnp.where(row >= 1, ends_ref[0, place].astype(F32), 0.0)
        total = (total + jnp.where(row <= 2, ends_ref[1, place].astype(F32), 0.0)).astype(BF)
        for c in range(4):
            cols_send_ref[c, place] = total[:, c * width : (c + 1) * width]
    columns = [go(cols_send_ref.at[c], cols_ref.at[col], col=c) for c in (across, cross, core)]
    cols_ref[col] = cols_send_ref[col]
    rest = [go(cols_ref.at[col], cols_other_ref.at[col], dp=y)]

    fac, folded = query_grads(range(0, 4), dq, high, low, bq_ref)
    put_query_grads(folded, 0, turn_ref, d_ref)
    sent_on = win_ref[2].astype(F32) + jnp.where(left, from_low, from_high)
    pl.when(hands_on)(two.wait_recv)
    wsend_ref[0] = jnp.where(hands_on, sent_on + wfar_ref[1].astype(F32), sent_on).astype(BF)
    pl.when(row >= 1)(one.start)

    mixes = [go(part_ref.at[order[k]], mix_got_ref.at[k], row=order[k]) for k in range(3)]

    fac_more, folded = query_grads(range(4, RQ), dq, high, low, bq_ref)
    put_query_grads(folded, 4, turn_ref, d_ref)
    for c, source in zip(columns, (across, cross, core)):
        c.wait_recv()
        rest.append(go(cols_ref.at[source], cols_other_ref.at[source], dp=y))
    d_kf = win_ref[4].astype(F32) + jnp.where(left, from_high, zero)
    pl.when(row <= 2)(one.wait_recv)
    d_kf = jnp.where(row <= 2, d_kf + wfar_ref[0].astype(F32), d_kf)
    put_key_grads(d_kf, fac + fac_more, turn_ref, d_ref)
    d_h = nn(d_ref[...], w_ref[...])
    gains = first_norm_back(d_h, x_ref, gain_ref, d_mixed_ref, gi_ref)
    factor_weight_grads(d_ref, h_ref, gains, g_two_ref, g_ref)

    first = [go(g_ref.at[r, (1 - x) * 2 + 1 - mine], near_ref.at[0, k], col=core) for k, r in enumerate(order)]
    second = [go(g_ref.at[r, x * 2 + 1 - mine], near_ref.at[1, k], col=core) for k, r in enumerate(order)]
    sides = []
    for k, r in enumerate(order):
        first[k].wait_recv()
        pair_ref[k] = (g_ref[r, (1 - x) * 2 + mine].astype(F32) + near_ref[0, k].astype(F32)).astype(BF)
        sides.append(go(pair_ref.at[k], side_ref.at[k], col=across))

    total = part_ref[row].astype(F32)
    for k, c in enumerate(mixes):
        c.wait_recv()
        total = total + mix_got_ref[k].astype(F32)
    mix_ref[...] = total.astype(BF)
    rest.append(go(mix_ref, mix_other_ref, dp=y))
    for c in (across, cross, core):
        rest.append(go(gi_ref.at[c], gi_all_ref.at[col], col=c))
    own = pltpu.make_async_copy(gi_ref.at[col], gi_all_ref.at[col], local_sem.at[0])
    own.start()

    downs = []
    for k, r in enumerate(order):
        second[k].wait_recv()
        sides[k].wait_recv()
        far_ref[k] = (
            g_ref[r, x * 2 + mine].astype(F32) + near_ref[1, k].astype(F32) + side_ref[k].astype(F32)
        ).astype(BF)
        if k < 3:
            downs.append(go(far_ref.at[k], down_ref.at[k], row=r))
    total = far_ref[3].astype(F32)
    for k in range(3):
        downs[k].wait_recv()
        total = total + down_ref[k].astype(F32)
    last_ref[...] = total.astype(BF)
    end = go(last_ref, end_ref, dp=y)
    end.wait_recv()
    grad_ref[...] = last_ref[...].astype(F32) + end_ref[...].astype(F32)
    for c in rest:
        c.wait_recv()
    for c in started:
        c.wait_send()
    pl.when(row >= 1)(one.wait_send)
    pl.when(row >= 2)(two.wait_send)
    own.wait()


def back_tail_body(*refs):
    attend_in, side_in, tail_in = refs[:7], refs[7:12], refs[12:21]
    out_ref, *tail_out = refs[21:28]
    scratch = refs[28:]
    dq_ref, dkf_ref, ends_ref, part_ref = scratch[:4]
    hf_ref, bq_ref, turn_ref, w_ref, h_ref, x_ref, gain_ref, d_mixed_ref, g_two_ref = tail_in
    attend_back_body(
        True, *attend_in, *side_in, dq_ref, dkf_ref, out_ref, ends_ref, part_ref, *scratch[4:25]
    )
    tail_body(
        dkf_ref, dq_ref, hf_ref, bq_ref, turn_ref, w_ref, h_ref, x_ref, gain_ref, d_mixed_ref, g_two_ref,
        side_in[2], ends_ref, part_ref, *tail_out, *scratch[25:],
    )


def back_tail(attend_in, side_in, tail_in):
    kf_window, g_rows, g_out = attend_in[5], side_in[2], side_in[3]
    x_parts = tail_in[5]
    parts, rows, feat = x_parts.shape
    units = g_rows.shape[2]
    block = (RANK_COLS // 4 + GROUP_COLS, feat)
    cols = (parts, 3, units, feat)
    mix = g_out.shape[2:]
    wide = g_rows.shape[1:]
    slot = kf_window.shape[1:]
    count = 2 + 2 + 3 + 8 + 4 + 3 + 1 + 1 + 3 + 3 + 3 + 1
    return pl.pallas_call(
        back_tail_body,
        out_shape=(
            jax.ShapeDtypeStruct(x_parts.shape, BF),
            jax.ShapeDtypeStruct(block, F32),
            jax.ShapeDtypeStruct(x_parts.shape, BF),
            jax.ShapeDtypeStruct(cols, BF),
            jax.ShapeDtypeStruct(cols, BF),
            jax.ShapeDtypeStruct(mix, BF),
            jax.ShapeDtypeStruct(mix, BF),
        ),
        in_specs=[VMEM] * 7 + [ANY, VMEM, ANY, ANY, VMEM] + [VMEM] * 9,
        out_specs=(ANY, VMEM, ANY, VMEM, ANY, VMEM, ANY),
        scratch_shapes=[
            pltpu.VMEM((rows, D), F32),
            pltpu.VMEM(kf_window.shape, BF),
            pltpu.VMEM((2,) + wide, BF),
            pltpu.VMEM((4,) + mix, BF),
        ]
        + back_scratch(rows, 5 * rows)
        + [
            pltpu.VMEM((2, rows // 2, D), BF),
            pltpu.VMEM((2, rows // 2, D), BF),
            pltpu.VMEM((2, rows, D), BF),
            pltpu.VMEM((parts, rows, feat), BF),
            pltpu.VMEM((2,) + wide, BF),
            pltpu.VMEM((2,) + wide, BF),
            pltpu.VMEM((2,) + wide, BF),
            pltpu.VMEM((2, 4) + mix, BF),
            pltpu.VMEM((4,) + mix, BF),
            pltpu.VMEM((4,) + mix, BF),
            pltpu.VMEM((2, rows // 2, D), BF),
            pltpu.VMEM((rows, D), BF),
            pltpu.VMEM(g_rows.shape, BF),
            pltpu.VMEM((2, 4) + mix, BF),
            pltpu.SemaphoreType.DMA((25,)),
            pltpu.SemaphoreType.DMA((25,)),
            pltpu.SemaphoreType.DMA((13,)),
        ]
        + [
            pltpu.VMEM((rows, ALL_COLS), BF),
            pltpu.VMEM(x_parts.shape, BF),
            pltpu.VMEM((2,) + slot, BF),
            pltpu.VMEM((2,) + slot, BF),
            pltpu.VMEM((2,) + slot, BF),
            pltpu.VMEM(wide, BF),
            pltpu.VMEM(cols, BF),
            pltpu.VMEM((3,) + mix, BF),
            pltpu.VMEM((4, parts) + block, BF),
            pltpu.VMEM((2, 4) + block, BF),
            pltpu.VMEM((4,) + block, BF),
            pltpu.VMEM((4,) + block, BF),
            pltpu.VMEM((4,) + block, BF),
            pltpu.VMEM((3,) + block, BF),
            pltpu.VMEM(block, BF),
            pltpu.VMEM(block, BF),
            pltpu.SemaphoreType.DMA((count,)),
            pltpu.SemaphoreType.DMA((count,)),
            pltpu.SemaphoreType.DMA((2,)),
        ],
        compiler_params=comm_params(7),
        cost_estimate=cost_of(2 * rows * 5 * rows * D * 40, 40 << 20),
    )(*attend_in, *side_in, *tail_in)


def layout_body(
    grad_ref, gi_ref, cols_ref, other_ref, mix_ref, mix_other_ref,
    gi_out_ref, gain_ref, gain_two_ref, heads_ref, ranks_ref, out_ref, gate_ref, up_ref, down_ref,
):
    first = lax.axis_index("dp") == 0
    gi_out_ref[...] = gi_ref[...].astype(F32)
    out_ref[...] = mix_ref[...].astype(F32) + mix_other_ref[...].astype(F32)
    ranks = ranks_ref.shape[0]
    used = heads_ref.shape[0]
    gain_ref[...] = grad_ref[ranks + used : ranks + used + 1]
    gain_two_ref[...] = grad_ref[ranks + used + 1 : ranks + used + 2]
    ranks_ref[...] = grad_ref[:ranks]
    lane = lax.broadcasted_iota(jnp.int32, (used, GROUP_COLS), 1)
    place = lax.broadcasted_iota(jnp.int32, (used, GROUP_COLS), 0)
    factor = place % FAC
    spot = jnp.where(factor < RQ, factor + 2 * RK, factor - RQ) * GROUP + place // FAC
    heads_ref[...] = jnp.dot(
        (lane == spot).astype(F32), grad_ref[ranks:], precision=lax.Precision.HIGHEST, preferred_element_type=F32
    )
    part = down_ref.shape[0] // 8
    for k, target in ((0, gate_ref), (1, up_ref), (2, down_ref)):
        for c in range(4):
            own = cols_ref[c, k].astype(F32)[:part]
            other = other_ref[c, k].astype(F32)[:part]
            target[c * part : (c + 1) * part] = jnp.where(first, own, other)
            target[(4 + c) * part : (5 + c) * part] = jnp.where(first, other, own)


def layout(grad, gi, cols, other, mix, mix_other, heads, ranks, hidden):
    feat = grad.shape[1]
    weight = jax.ShapeDtypeStruct((hidden, feat), F32)
    gain = jax.ShapeDtypeStruct((1, feat), F32)
    return call(
        layout_body,
        (
            jax.ShapeDtypeStruct(gi.shape, F32),
            gain,
            gain,
            jax.ShapeDtypeStruct((heads, feat), F32),
            jax.ShapeDtypeStruct((ranks, feat), F32),
            jax.ShapeDtypeStruct(mix.shape, F32),
            weight,
            weight,
            weight,
        ),
        cost=cost_of(0, 8 << 20),
    )(grad, gi, cols, other, mix, mix_other)


def local(
    tokens_in, segments, gain_attn, gain_ffn, w_heads, w_ranks, w_out, w_gate, w_up, w_down, cotangent
):
    n_row = lax.axis_size("row")
    n_col = lax.axis_size("col")
    row = lax.axis_index("row")
    col = lax.axis_index("col")
    micro, row_tokens, feat = tokens_in.shape
    subs = n_col // micro
    rows = row_tokens // subs
    length = row_tokens * n_row
    head_local = w_heads.shape[1] // FAC
    rank_local = w_ranks.shape[1]
    ffn_local = w_gate.shape[1]
    out_local = w_out.shape[0]
    block = row * subs + col % subs
    past = min(-(-(MAX_DOC - 1) // rows), n_row * subs - 1)
    keys = (past + 1) * rows

    dp_count = lax.axis_size("dp")
    fast = n_col == 4 and n_row == 4 and dp_count == 2 and micro == 2 and past == 4

    tokens = tokens_in.reshape(n_col, rows, feat)
    inverse = ROPE ** (-(jnp.arange(HD // 2, dtype=F32) * 2.0 / HD))
    if not fast:
        heads_t = jnp.transpose(w_heads.reshape(feat, head_local, FAC), (2, 1, 0))
        heads_t = heads_t[jnp.array(FAC_ORDER)].reshape(FAC * head_local, feat)
        pad = jnp.zeros((GROUP_COLS - FAC * head_local, feat), BF)
        w_own = jnp.concatenate([w_ranks.T, heads_t, pad], axis=0)
        gains_own = jnp.concatenate([gain_attn[None], gain_ffn[None], jnp.zeros((6, feat), F32)], axis=0)
        part = ffn_local // n_col
        units = part * n_row
        w_ffn = jnp.stack([w_gate.T, w_up.T, w_down]).reshape(3, n_col, part, feat)
        w_ffn = lax.all_to_all(jnp.transpose(w_ffn, (1, 0, 2, 3)), "col", 0, 0, tiled=True)
        w_ffn = jnp.transpose(w_ffn, (1, 2, 0, 3)).reshape(3, part, D)
        w_ffn = jnp.transpose(lax.all_gather(w_ffn, "row", axis=0), (1, 0, 2, 3)).reshape(3, units, D)
        w_blocks = lax.all_gather(w_own, ("row", "col"), axis=0).reshape((n_row, n_col) + w_own.shape)
        gains = lax.all_gather(gains_own, "col", axis=0)
        x_parts = lax.all_to_all(tokens, "col", 0, 0, tiled=True)
        w_out_all = lax.all_gather(w_out, ("row", "col"), axis=0).reshape((n_row, n_col) + w_out.shape)

        seg_row = lax.dynamic_index_in_dim(segments, col // subs, 0, keepdims=False)
        padded = jnp.concatenate([jnp.full((1, past * rows), -1, jnp.int32), seg_row], axis=1)
        seg_window = lax.dynamic_slice_in_dim(padded, block * rows, keys, 1)
        own_seg = seg_window[0, past * rows :]
        key_idx = jnp.arange(keys, dtype=jnp.int32)
        query_idx = jnp.arange(rows, dtype=jnp.int32) + past * rows
        before = (own_seg[:, None] == seg_window) & (key_idx[None, :] < query_idx[:, None])
        places = jnp.sum(before.astype(jnp.int32), axis=1)
        angles = places.astype(F32)[:, None] * inverse[None, :]
        cosine = jnp.cos(angles)
        sine = jnp.sin(angles)
        turn = jnp.concatenate([cosine] * 4 + [-sine, sine, -sine, sine], axis=1)

    groups = [[m * subs + s for s in range(subs)] for m in range(micro)]
    if fast:
        cot_rows = cotangent.reshape(micro * row_tokens, feat)
        (
            x_parts, gains, ffn_parts, mixes, h_one, head_fac, bq_rot, queries, w_rh, kf_window, seg_window, turn, w_rows,
            heads_out, lse, key_all, value_all, cot_near,
        ) = head_attend(
            tokens, w_ranks.T, w_heads.T, gain_attn.reshape(1, feat), gain_ffn.reshape(1, feat), w_gate.T, w_up.T,
            w_down, w_out, segments, jnp.concatenate([inverse] * 4).reshape(1, LANES), cot_rows,
        )
        mixed, d_mixed, d_heads, g_out, g_gain_two, g_rows, out_pair, hop = middle(
            x_parts, heads_out, mixes, gains, cot_rows, cot_near, ffn_parts, w_rows
        )
        output, g_rh, grad_input, g_cols, cols_other, g_out, out_other = back_tail(
            (queries, key_all, value_all, d_heads, lse, kf_window, seg_window),
            (out_pair, mixed, g_rows, g_out, hop),
            (head_fac, bq_rot, turn, w_rh, h_one, x_parts, gains, d_mixed, g_gain_two),
        )
        grad_input, g_one, g_two, own_heads, own_ranks, g_out, own_gate, own_up, own_down = layout(
            g_rh, grad_input, g_cols, cols_other, g_out, out_other, w_heads.shape[1], w_ranks.shape[1], ffn_local
        )
        return (
            output.reshape(tokens_in.shape),
            grad_input.reshape(tokens_in.shape),
            g_one.reshape(feat),
            g_two.reshape(feat),
            own_heads.T,
            own_ranks.T,
            g_out,
            own_gate.T,
            own_up.T,
            own_down,
        )
    else:
        h_one, head_fac, bq_rot, key_fac, queries, w_rh = front(x_parts, gains, w_blocks, turn)
        gathered = lax.all_gather(key_fac, "row", axis=0)
        gathered = lax.all_gather(gathered, "col", axis=1, axis_index_groups=groups)
        gathered = gathered.reshape(length, key_fac.shape[1])
        padded_kf = jnp.concatenate([jnp.zeros((past * rows, key_fac.shape[1]), BF), gathered], axis=0)
        kf_window = lax.dynamic_slice_in_dim(padded_kf, block * rows, keys, 0)
        heads_out, lse, key_all, value_all = attend(queries, kf_window, seg_window)
        mixed, h_two = mixing(x_parts, heads_out, w_out_all, gains)
        cot_own = lax.all_to_all(cotangent.reshape(n_col, rows, feat), "col", 0, 0, tiled=True)
        cot_own = jnp.transpose(cot_own, (1, 0, 2)).reshape(rows, D)
        cot_all = lax.all_gather(cot_own, "col", axis=0)
        h_all = lax.all_gather(h_two, "col", axis=0)
        out_part, dh_part, g_ffn = ffn(h_all, cot_all, w_ffn)
        dh_sum = lax.psum_scatter(dh_part, "col", scatter_dimension=0, tiled=False).astype(F32)
        out_sum = lax.psum_scatter(out_part, "col", scatter_dimension=0, tiled=False).astype(F32)
        out_parts, d_mixed, d_heads, g_out, g_gain_two = unmix(
            dh_sum, out_sum, mixed, cot_own, heads_out, w_out_all, gains
        )
        d_q, d_kf = attend_back(queries, key_all, value_all, d_heads, lse, kf_window, seg_window)
        spread_kf = jnp.zeros((past * rows + length, d_kf.shape[1]), BF)
        spread_kf = lax.dynamic_update_slice_in_dim(spread_kf, d_kf, block * rows, 0)[past * rows :]
        spread_kf = spread_kf.reshape(n_row, subs, rows, -1)
        own_kf = lax.psum_scatter(spread_kf, "row", scatter_dimension=0, tiled=False)
        own_kf = lax.psum_scatter(own_kf, "col", scatter_dimension=0, tiled=False, axis_index_groups=groups)
        gi_parts, g_rh = back(
            d_q, own_kf, head_fac, bq_rot, turn, w_rh, h_one, x_parts, gains, d_mixed, g_gain_two, n_row
        )
        output = lax.all_to_all(out_parts, "col", 0, 0, tiled=True)
        grad_input = lax.all_to_all(gi_parts, "col", 0, 0, tiled=True)
        g_ffn = lax.psum_scatter(g_ffn.reshape(3, n_row, part, D), "row", scatter_dimension=1, tiled=False)
        g_ffn = jnp.transpose(lax.psum(g_ffn, "dp").reshape(3, part, n_col, feat), (2, 0, 1, 3))
        g_ffn = lax.all_to_all(g_ffn, "col", 0, 0, tiled=True)
        g_ffn = jnp.transpose(g_ffn, (1, 0, 2, 3)).reshape(3, ffn_local, feat).astype(F32)

        def total(values):
            values = values.reshape((n_row * n_col,) + values.shape[2:])
            values = lax.psum_scatter(values, ("row", "col"), scatter_dimension=0, tiled=False)
            return lax.psum(values, "dp").astype(F32)

        g_out = total(g_out)
        g_rh = total(g_rh)

    used = rank_local + FAC * head_local
    own_heads = g_rh[rank_local:used].reshape(FAC, head_local, feat)
    own_heads = jnp.transpose(own_heads[jnp.array(FAC_BACK)], (2, 1, 0)).reshape(w_heads.shape)
    return (
        output.reshape(tokens_in.shape),
        grad_input.reshape(tokens_in.shape),
        g_rh[used],
        g_rh[used + 1],
        own_heads,
        g_rh[:rank_local].T,
        g_out,
        g_ffn[0].T,
        g_ffn[1].T,
        g_ffn[2],
    )


def solution(mesh):
    tokens = P(None, ("dp", "row"), "col")
    both = P("col", "row")
    turned = P("row", "col")
    gain = P("col")
    return jax.shard_map(
        local,
        mesh=mesh,
        in_specs=(tokens, P(None, "dp", None), gain, gain, both, both, turned, both, both, turned, tokens),
        out_specs=(tokens, tokens, gain, gain, both, both, turned, both, both, turned),
        check_vma=False,
    )
```

```python
import functools

import jax
import jax.numpy as jnp
import numpy as np
from jax import lax
from jax.experimental import pallas as pl
from jax.experimental.pallas import tpu as pltpu
from jax.sharding import PartitionSpec as P

D = 1024
H = 16
HD = 64
RQ = 6
RK = 2
FAC = 10
MAX_DOC = 1024

EPS = 1e-06
ROPE = 10000.0
NEG = -1e30
BF = jnp.bfloat16
F32 = jnp.float32
LANES = 128
PAIRS = H // 2
FAC_ORDER = (6, 7, 8, 9, 0, 1, 2, 3, 4, 5)
FAC_BACK = (4, 5, 6, 7, 8, 9, 0, 1, 2, 3)
VMEM = pl.BlockSpec(memory_space=pltpu.VMEM)


def nn(a, b):
    return jnp.dot(a, b, preferred_element_type=F32)


def nt(a, b):
    return lax.dot_general(a, b, (((1,), (1,)), ((), ())), preferred_element_type=F32)


def tn(a, b):
    return lax.dot_general(a, b, (((0,), (0,)), ((), ())), preferred_element_type=F32)


def two_pass(a, b):
    high = a.astype(BF)
    low = (a - high.astype(F32)).astype(BF)
    return nn(high, b) + nn(low, b)


def lane_iota(shape):
    return lax.broadcasted_iota(jnp.int32, shape, len(shape) - 1)


def spread(rows, first, width):
    row = lax.broadcasted_iota(jnp.int32, (rows, width), 0)
    head = lax.broadcasted_iota(jnp.int32, (rows, width), 1) // HD
    return (row == head + first).astype(F32).astype(BF)


def collect(rows, width, first):
    head = lax.broadcasted_iota(jnp.int32, (rows, width), 0) // HD
    lane = lax.broadcasted_iota(jnp.int32, (rows, width), 1)
    return (lane == head + first).astype(F32).astype(BF)


GROUP = 4
GROUP_COLS = 48
RANK_COLS = FAC * HD
HEAD_COLS = H // GROUP * GROUP_COLS
ALL_COLS = RANK_COLS + HEAD_COLS


def factor_place(head, j):
    return head // GROUP * GROUP_COLS + j * GROUP + head % GROUP


def head_spread(j, first_head, width):
    row = lax.broadcasted_iota(jnp.int32, (HEAD_COLS, width), 0)
    head = lax.broadcasted_iota(jnp.int32, (HEAD_COLS, width), 1) // HD + first_head
    return (row == factor_place(head, j)).astype(F32).astype(BF)


def head_collect(j):
    head = lax.broadcasted_iota(jnp.int32, (D, HEAD_COLS), 0) // HD
    lane = lax.broadcasted_iota(jnp.int32, (D, HEAD_COLS), 1)
    return (lane == factor_place(head, j)).astype(F32).astype(BF)


def key_columns():
    row = lax.broadcasted_iota(jnp.int32, (HEAD_COLS, LANES), 0)
    lane = lax.broadcasted_iota(jnp.int32, (HEAD_COLS, LANES), 1)
    taken = (row == factor_place(lane % H, lane // H)) & (lane < 2 * RK * H)
    return taken.astype(F32).astype(BF)


def swap_halves(tile):
    lane = lane_iota(tile.shape)
    ahead = pltpu.roll(tile, LANES - HD // 2, 1)
    behind = pltpu.roll(tile, HD // 2, 1)
    return jnp.where(lane % HD < HD // 2, ahead, behind)


def double_left(tile):
    return jnp.where(lane_iota(tile.shape) < HD, tile, pltpu.roll(tile, HD, 1))


def double_right(tile):
    return jnp.where(lane_iota(tile.shape) < HD, pltpu.roll(tile, HD, 1), tile)


def params(**more):
    return pltpu.CompilerParams(vmem_limit_bytes=60 << 20, **more)


def call(body, outs, scratch=(), cost=None):
    return pl.pallas_call(
        body,
        out_shape=outs,
        scratch_shapes=scratch,
        compiler_params=params(),
        cost_estimate=cost,
    )


def cost_of(flops, moved):
    return pl.CostEstimate(flops=int(flops), bytes_accessed=int(moved), transcendentals=0)


MESH = pl.DeviceIdType.MESH
ANY = pl.BlockSpec(memory_space=pl.ANY)


class Mover:
    def __init__(self, send_sem, recv_sem):
        self.send_sem = send_sem
        self.recv_sem = recv_sem
        self.used = 0

    def copy(self, source, target, **place):
        index = self.used
        self.used += 1
        return pltpu.make_async_remote_copy(
            src_ref=source,
            dst_ref=target,
            send_sem=self.send_sem.at[index],
            recv_sem=self.recv_sem.at[index],
            device_id=place,
            device_id_type=MESH,
        )


def greet(partners):
    barrier = pltpu.get_barrier_semaphore()
    count = 0
    for present, place in partners:
        if present is None:
            pl.semaphore_signal(barrier, inc=1, device_id=place, device_id_type=MESH)
            count = count + 1
        else:

            @pl.when(present)
            def _():
                pl.semaphore_signal(barrier, inc=1, device_id=place, device_id_type=MESH)

            count = count + present.astype(jnp.int32)
    pl.semaphore_wait(barrier, count)


def neighbours():
    col = lax.axis_index("col")
    core = col + 1 - 2 * lax.rem(col, 2)
    across = lax.rem(col + 2, 4)
    return col, core, across


def square():
    dp = lax.axis_index("dp")
    x = lax.axis_index("col") // 2
    return dp, (dp * 2 + x, dp * 2 + 1 - x, (1 - dp) * 2 + x, (1 - dp) * 2 + 1 - x)


def comm_params(ident):
    return params(collective_id=ident, has_side_effects=True)


class AttendCopies:
    def __init__(self, head_end, cot_ref, rows_ref, near_ref, mixes_ref, send_sem, recv_sem):
        self.head_end = head_end
        row = lax.axis_index("row")
        col, core, across = neighbours()
        dp, (me, on_x, on_y, _) = square()
        mover = Mover(send_sem, recv_sem)
        self.left = row >= 1
        self.right = row <= 2
        self.both = jnp.logical_and(self.left, self.right)
        self.from_left = row >= 2
        self.from_right = row <= 1
        self.row = row
        cuts = [pl.ds(0, 2), pl.ds(2, 2)]
        lower, upper = rows_ref.at[jnp.maximum(row - 1, 0)], rows_ref.at[jnp.minimum(row + 1, 3)]
        self.pass_right = [mover.copy(lower.at[c], lower.at[c], row=row + 1) for c in cuts]
        self.pass_left = [mover.copy(upper.at[c], upper.at[c], row=row - 1) for c in cuts]
        self.last_right = [mover.copy(rows_ref.at[0, c], rows_ref.at[0, c], row=row + 1) for c in cuts]
        self.last_left = [mover.copy(rows_ref.at[3, c], rows_ref.at[3, c], row=row - 1) for c in cuts]
        half = cot_ref.shape[0] // 2
        top, low = pl.ds(0, half), pl.ds(half, half)
        self.cots = [
            mover.copy(cot_ref.at[low], near_ref.at[me, low], col=across),
            mover.copy(cot_ref.at[top], near_ref.at[me, top], dp=1 - dp),
            mover.copy(cot_ref.at[top], near_ref.at[me, top], col=across),
            mover.copy(cot_ref.at[low], near_ref.at[me, low], dp=1 - dp),
        ]
        self.relays = [
            mover.copy(near_ref.at[on_x, low], near_ref.at[on_x, low], dp=1 - dp),
            mover.copy(near_ref.at[on_y, top], near_ref.at[on_y, top], col=across),
        ]
        self.mixes = []
        for r in range(4):
            for c in (col, across):
                self.mixes.append(mover.copy(mixes_ref.at[r, c], mixes_ref.at[r, c], col=core))

    def first(self):
        for k in range(2):
            pl.when(self.both)(self.pass_right[k].start)
            pl.when(self.both)(self.pass_left[k].start)
        for c in self.cots:
            c.start()

    def early(self):
        self.head_end()
        for c in self.mixes:
            c.start()
        self.hand_on(0)

    def hand_on(self, k):
        pl.when(self.from_left)(self.pass_right[k].wait_recv)
        pl.when(self.from_right)(self.pass_left[k].wait_recv)
        pl.when(self.row == 2)(self.last_right[k].start)
        pl.when(self.row == 1)(self.last_left[k].start)

    def second(self):
        for c in self.cots[:2]:
            c.wait_recv()
        for c in self.relays:
            c.start()
        self.hand_on(1)

    def last(self):
        for k in range(2):
            pl.when(self.both)(self.pass_right[k].wait_send)
            pl.when(self.both)(self.pass_left[k].wait_send)
            pl.when(self.row == 2)(self.last_right[k].wait_send)
            pl.when(self.row == 1)(self.last_left[k].wait_send)
            pl.when(self.row == 3)(self.last_right[k].wait_recv)
            pl.when(self.row == 0)(self.last_left[k].wait_recv)
        for c in self.cots[:2]:
            c.wait_send()
        for c in self.cots[2:] + self.relays + self.mixes:
            c.wait()


class BackCopies:
    def __init__(self, refs, sems):
        (
            self.pair_ref, self.mixed_ref, self.rows_ref, self.g_out_ref, self.hop_ref,
            self.out_ref, self.ends_ref, self.part_ref,
            self.relay_ref, self.diag_ref, self.far_ref, self.send_ref,
            self.right_ref, self.left_ref, self.got_ref,
            self.near_ref, self.side_ref, self.across_ref,
            self.pieces_ref, self.mine_ref, self.rows_in_ref, self.g_in_ref,
        ) = refs
        send_sem, recv_sem, local_sem = sems
        self.row = row = lax.axis_index("row")
        self.col, core, across = col, _, _ = neighbours()
        cross = lax.rem(core + 2, 4)
        self.dp, self.spots = dp, (me, on_x, on_y, on_both) = square()
        mover = Mover(send_sem, recv_sem)
        self.x, self.mine = x, mine = col // 2, lax.rem(col, 2)
        self.partners = [(None, {"col": c}) for c in (core, across, cross)]
        self.partners += [(None, {"dp": 1 - dp})] + [(None, {"row": lax.rem(row + k, 4)}) for k in range(1, 4)]
        half = self.pair_ref.shape[1] // 2
        top, low = pl.ds(0, half), pl.ds(half, half)
        y = 1 - dp
        self.diag = [
            mover.copy(self.pair_ref.at[on_both, top], self.diag_ref.at[0], col=across),
            mover.copy(self.pair_ref.at[on_both, low], self.diag_ref.at[1], dp=y),
        ]
        self.far = [
            mover.copy(self.pair_ref.at[on_x, top], self.far_ref.at[0, top], col=across),
            mover.copy(self.pair_ref.at[on_y, low], self.far_ref.at[1, low], dp=y),
            mover.copy(self.relay_ref.at[0], self.far_ref.at[1, top], dp=y),
            mover.copy(self.relay_ref.at[1], self.far_ref.at[0, low], col=across),
        ]
        self.out = [mover.copy(self.send_ref.at[c], self.out_ref.at[col], col=c) for c in (across, cross, core)]
        self.own = pltpu.make_async_copy(self.send_ref.at[col], self.out_ref.at[col], local_sem.at[0])
        self.hop_right = [
            mover.copy(self.right_ref.at[0], self.got_ref.at[0], row=row + 1),
            mover.copy(self.right_ref.at[1], self.ends_ref.at[0], row=row + 1),
        ]
        self.hop_left = [
            mover.copy(self.left_ref.at[0], self.got_ref.at[1], row=row - 1),
            mover.copy(self.left_ref.at[1], self.ends_ref.at[1], row=row - 1),
        ]
        self.cores = [
            mover.copy(self.g_out_ref.at[r, k * 2 + 1 - mine], self.near_ref.at[k, r], col=core)
            for k in range(2)
            for r in range(4)
        ]
        self.sides = [mover.copy(self.side_ref.at[r], self.across_ref.at[r], col=across) for r in range(4)]
        self.loads = [
            pltpu.make_async_copy(self.pair_ref.at[on_y, top], self.pieces_ref.at[0], local_sem.at[1]),
            pltpu.make_async_copy(self.pair_ref.at[on_x, low], self.pieces_ref.at[1], local_sem.at[2]),
            pltpu.make_async_copy(self.pair_ref.at[me], self.mine_ref, local_sem.at[3]),
        ]
        self.rows_load = pltpu.make_async_copy(self.rows_ref, self.rows_in_ref, local_sem.at[4])
        self.g_loads = [
            pltpu.make_async_copy(
                self.g_out_ref.at[r, lax.rem(x + k, 2) * 2 + mine], self.g_in_ref.at[k, r], local_sem.at[5 + 4 * k + r]
            )
            for k in range(2)
            for r in range(4)
        ]

    def first(self):
        row = self.row
        self.rows_load.start()
        for c in self.loads + self.g_loads:
            c.start()
        greet(self.partners)
        for c in self.diag + self.far[:2] + self.cores:
            c.start()
        self.rows_load.wait()
        hop = self.hop_ref[...].astype(F32)
        ahead = self.rows_in_ref[jnp.minimum(row + 2, 3)].astype(F32)
        self.right_ref[0] = jnp.where(row == 1, ahead + hop, ahead).astype(BF)
        behind = self.rows_in_ref[jnp.maximum(row - 2, 0)].astype(F32)
        self.left_ref[0] = jnp.where(row == 2, behind + hop, behind).astype(BF)
        pl.when(row <= 1)(self.hop_right[0].start)
        pl.when(row >= 2)(self.hop_left[0].start)

    def cross_x(self):
        for c in self.g_loads:
            c.wait()
        for c in self.cores:
            c.wait_recv()
        for r in range(4):
            self.side_ref[r] = (
                self.g_in_ref[1, r].astype(F32) + self.near_ref[1 - self.x, r].astype(F32)
            ).astype(BF)
            self.sides[r].start()

    def second(self):
        row = self.row
        for c in self.loads:
            c.wait()
        for k in range(2):
            self.diag[k].wait_recv()
            self.relay_ref[k] = (self.pieces_ref[k].astype(F32) + self.diag_ref[k].astype(F32)).astype(BF)
            self.far[2 + k].start()

    def last_hop(self):
        row = self.row
        middle = jnp.logical_and(row >= 1, row <= 2)
        pl.when(middle)(self.hop_right[0].wait_recv)
        pl.when(middle)(self.hop_left[0].wait_recv)
        ahead = self.rows_in_ref[jnp.minimum(row + 1, 3)].astype(F32)
        behind = self.rows_in_ref[jnp.maximum(row - 1, 0)].astype(F32)
        self.right_ref[1] = jnp.where(row >= 1, ahead + self.got_ref[0].astype(F32), ahead).astype(BF)
        self.left_ref[1] = jnp.where(row <= 2, behind + self.got_ref[1].astype(F32), behind).astype(BF)
        pl.when(row <= 2)(self.hop_right[1].start)
        pl.when(row >= 1)(self.hop_left[1].start)

    def third(self):
        row = self.row
        for c in self.far:
            c.wait_recv()
        feat = self.send_ref.shape[2]
        for c in range(4):
            lanes = slice(c * feat, (c + 1) * feat)
            self.send_ref[c] = (
                self.mixed_ref[:, lanes]
                + self.mine_ref[:, lanes].astype(F32)
                + self.far_ref[0, :, lanes].astype(F32)
                + self.far_ref[1, :, lanes].astype(F32)
            ).astype(BF)
        for c in self.out:
            c.start()
        self.own.start()

    def last(self):
        row = self.row
        for r in range(4):
            self.sides[r].wait_recv()
            self.part_ref[r] = (
                self.g_in_ref[0, r].astype(F32)
                + self.near_ref[self.x, r].astype(F32)
                + self.across_ref[r].astype(F32)
            ).astype(BF)
        for c in self.out:
            c.wait()
        self.own.wait()
        for c in self.diag + self.far + self.cores + self.sides:
            c.wait_send()
        pl.when(row <= 1)(self.hop_right[0].wait_send)
        pl.when(row >= 2)(self.hop_left[0].wait_send)
        pl.when(row <= 2)(self.hop_right[1].wait_send)
        pl.when(row >= 1)(self.hop_left[1].wait_send)
        pl.when(row >= 1)(self.hop_right[1].wait_recv)
        pl.when(row <= 2)(self.hop_left[1].wait_recv)


def first_norm(x_ref, gain_ref, h_ref):
    parts = x_ref.shape[0]
    feat = x_ref.shape[2]
    xs = [x_ref[c].astype(F32) for c in range(parts)]
    total = sum(jnp.sum(v * v, axis=1, keepdims=True) for v in xs)
    scale = lax.rsqrt(total / D + EPS)
    for c in range(parts):
        lanes = slice(c * feat, (c + 1) * feat)
        h_ref[:, lanes] = (xs[c] * scale * gain_ref[c, :1]).astype(BF)


def place_factor_weights(blocks_ref, w_ref):
    n_row, parts, _, feat = blocks_ref.shape
    ranks_each = RANK_COLS // n_row
    for c in range(parts):
        lanes = slice(c * feat, (c + 1) * feat)
        for r in range(n_row):
            w_ref[r * ranks_each : (r + 1) * ranks_each, lanes] = blocks_ref[r, c, :ranks_each]
            w_ref[RANK_COLS + r * GROUP_COLS : RANK_COLS + (r + 1) * GROUP_COLS, lanes] = blocks_ref[
                r, c, ranks_each:
            ]


def make_factors(h_ref, w_ref, turn_ref, hf_ref, bq_ref, kf_ref):
    both = nt(h_ref[...], w_ref[...])
    heads = both[:, RANK_COLS:]
    hf_ref[...] = heads
    cosine = turn_ref[:, :LANES]
    sine = turn_ref[:, LANES:]
    for tile in range(RANK_COLS // LANES):
        lanes = slice(tile * LANES, (tile + 1) * LANES)
        part = both[:, lanes]
        if tile < 4:
            part = part * cosine + swap_halves(part) * sine
        if tile < 3:
            bq_ref[:, lanes] = part
        else:
            kf_ref[:, (tile - 3) * LANES : (tile - 2) * LANES] = part.astype(BF)
    kf_ref[:, 2 * LANES :] = nn(heads.astype(BF), key_columns()).astype(BF)


def make_queries(hf_ref, bq_ref, q_ref):
    heads = hf_ref[...]
    high = heads.astype(BF)
    low = (heads - high.astype(F32)).astype(BF)
    ranks = []
    for r in range(RQ):
        tile = bq_ref[:, (r // 2) * LANES : (r // 2 + 1) * LANES]
        ranks.append(double_left(tile) if r % 2 == 0 else double_right(tile))
    width = 2 * LANES
    for p in range(D // width):
        lanes = slice(p * width, (p + 1) * width)
        acc = None
        for r in range(RQ):
            pick = head_spread(2 * RK + r, p * (width // HD), width)
            term = (nn(high, pick) + nn(low, pick)) * jnp.concatenate([ranks[r]] * 2, axis=1)
            acc = term if acc is None else acc + term
        q_ref[:, lanes] = (acc / RQ).astype(BF)


def front_body(x_ref, gain_ref, blocks_ref, turn_ref, h_ref, hf_ref, bq_ref, kf_ref, q_ref, w_ref):
    first_norm(x_ref, gain_ref, h_ref)
    place_factor_weights(blocks_ref, w_ref)
    make_factors(h_ref, w_ref, turn_ref, hf_ref, bq_ref, kf_ref)
    make_queries(hf_ref, bq_ref, q_ref)


def front(x_parts, gains, blocks, turn):
    rows = x_parts.shape[1]
    return call(
        front_body,
        (
            jax.ShapeDtypeStruct((rows, D), BF),
            jax.ShapeDtypeStruct((rows, HEAD_COLS), F32),
            jax.ShapeDtypeStruct((rows, RQ * HD), F32),
            jax.ShapeDtypeStruct((rows, 3 * LANES), BF),
            jax.ShapeDtypeStruct((rows, D), BF),
            jax.ShapeDtypeStruct((ALL_COLS, D), BF),
        ),
        cost=cost_of(2 * rows * D * 800 * 3, 6 << 20),
    )(x_parts, gains, blocks, turn)


def head_body(
    tok_ref, ranks_ref, heads_ref, gain_one_ref, gain_two_ref, gate_ref, up_ref, down_ref, mix_ref, seg_all_ref,
    inverse_ref,
    x_ref, gains_ref, parts_ref, mixes_ref, h_ref, hf_ref, bq_ref, q_ref, w_ref, win_ref, seg_ref, turn_ref, rows_ref,
    w_own_ref, gain_ref, ffn_ref, blocks_ref, send_sem, recv_sem,
):
    row = lax.axis_index("row")
    col, core, across = neighbours()
    cross = lax.rem(core + 2, 4)
    side = lax.rem(col, 2)
    rows = [lax.rem(row + k, 4) for k in range(4)]
    back = [lax.rem(row + 4 - k, 4) for k in range(4)]
    dp = lax.axis_index("dp")

    rank_rows = ranks_ref.shape[0]
    place = lax.broadcasted_iota(jnp.int32, (GROUP_COLS, FAC * GROUP), 0)
    lane = lax.broadcasted_iota(jnp.int32, (GROUP_COLS, FAC * GROUP), 1)
    factor = lane % FAC
    spot = jnp.where(factor < RQ, factor + 2 * RK, factor - RQ) * GROUP + lane // FAC
    w_own_ref[:rank_rows] = ranks_ref[...]
    w_own_ref[rank_rows:] = nn((place == spot).astype(F32).astype(BF), heads_ref[...]).astype(BF)
    gain_ref[...] = jnp.zeros_like(gain_ref)
    gain_ref[0:1] = gain_one_ref[...]
    gain_ref[1:2] = gain_two_ref[...]
    greet(
        [(None, {"col": c}) for c in (core, across, cross)]
        + [(None, {"row": r}) for r in rows[1:]]
        + [(None, {"dp": 1 - dp})]
    )
    mover = Mover(send_sem, recv_sem)
    started = []

    def go(source, target, **place):
        c = mover.copy(source, target, **place)
        c.start()
        started.append(c)
        return c

    down = [None] + [go(w_own_ref, blocks_ref.at[row, col], row=rows[k]) for k in range(1, 4)]
    sides = [go(w_own_ref, blocks_ref.at[row, col], col=across)]
    cores = [go(w_own_ref, blocks_ref.at[row, col], col=core)]
    toks = []
    rest = []
    for c in (across, cross, core):
        toks.append(go(gain_ref, gains_ref.at[col], col=c))
        toks.append(go(tok_ref.at[c], x_ref.at[col], col=c))
    units = ffn_ref.shape[2]
    hidden = gate_ref.shape[0]
    unit = hidden // 8
    place = lax.broadcasted_iota(jnp.int32, (4 * units, hidden), 0)
    lane = lax.broadcasted_iota(jnp.int32, (4 * units, hidden), 1)
    inside = place % units
    taken = (inside < unit) & (lane == (dp * 4 + place // units) * unit + inside)
    pick = taken.astype(F32).astype(BF)
    for k, source in enumerate((gate_ref, up_ref, down_ref)):
        chosen = nn(pick, source[...]).astype(BF)
        for c in range(4):
            ffn_ref[c, k] = chosen[c * units : (c + 1) * units]
    ffn = [go(ffn_ref.at[c], parts_ref.at[col], col=c) for c in (across, cross, core)]
    part = mix_ref.shape[0] // 2
    half = pl.ds(pl.multiple_of(dp * part, part), part)
    mix_down = [None] + [go(mix_ref.at[half], mixes_ref.at[row, col, half], row=rows[k]) for k in range(1, 4)]
    blocks_ref[row, col] = w_own_ref[...]
    gains_ref[col] = gain_ref[...]
    x_ref[col] = tok_ref[col]
    parts_ref[col] = ffn_ref[col]
    mixes_ref[row, col] = mix_ref[...]
    zero = jnp.zeros(win_ref.shape[1:], BF)
    has_one = row >= 1
    has_two = row >= 2
    for absent, slot in (
        (jnp.logical_not(has_two), 0),
        (jnp.logical_and(jnp.logical_not(has_two), side == 0), 1),
        (jnp.logical_and(jnp.logical_not(has_one), side == 1), 1),
        (jnp.logical_not(has_one), 2),
        (jnp.logical_and(jnp.logical_not(has_one), side == 0), 3),
    ):

        @pl.when(absent)
        def _():
            win_ref[slot] = zero

    keys = seg_ref.shape[1]
    tokens = tok_ref.shape[1]
    block_no = row * 2 + side
    for slot in range(5):
        index = block_no - 4 + slot
        lanes = pl.ds(pl.multiple_of(jnp.maximum(index, 0) * tokens, tokens), tokens)
        seg_ref[:, slot * tokens : (slot + 1) * tokens] = jnp.where(index >= 0, seg_all_ref[col // 2, :, lanes], -1)
    seg_row = seg_ref[...].astype(F32)
    column = jnp.broadcast_to(seg_row, (LANES, keys)).T
    column = jnp.concatenate([column] * (tokens // LANES), axis=1)
    key_idx = lax.broadcasted_iota(jnp.int32, (keys, tokens), 0)
    query_idx = lax.broadcasted_iota(jnp.int32, (keys, tokens), 1) + (keys - tokens)
    before = (column == seg_row[:, keys - tokens :]) & (key_idx < query_idx)
    places = jnp.sum(jnp.where(before, 1.0, 0.0), axis=0, keepdims=True)
    angles = jnp.broadcast_to(places, (LANES, tokens)).T * inverse_ref[...]
    turn_ref[:, :LANES] = jnp.cos(angles)
    sine = jnp.sin(angles)
    turn_ref[:, LANES:] = jnp.where(lane_iota(sine.shape) % HD < HD // 2, -sine, sine)

    for k in range(1, 4):
        down[k].wait_recv()
        block = blocks_ref.at[back[k], col]
        sides.append(go(block, block, col=across))
        cores.append(go(block, block, col=core))
    for c in toks:
        c.wait_recv()
    first_norm(x_ref, gains_ref, h_ref)
    mix_side = []
    for k in range(1, 4):
        mix_down[k].wait_recv()
        block = mixes_ref.at[back[k], col, half]
        mix_side.append(go(block, block, dp=1 - dp))
    for c in ffn:
        c.wait_recv()
    to_right = mover.copy(parts_ref, rows_ref.at[row], row=row + 1)
    to_left = mover.copy(parts_ref, rows_ref.at[row], row=row - 1)
    pl.when(row <= 2)(to_right.start)
    pl.when(row >= 1)(to_left.start)
    passed = []
    for k in range(4):
        sides[k].wait_recv()
        block = blocks_ref.at[back[k], across]
        passed.append(go(block, block, col=core))
    for c in cores + passed:
        c.wait_recv()
    for k in range(4):
        if k > 0:
            mix_side[k - 1].wait_recv()
        block = mixes_ref.at[back[k], col]
        rest.append(go(block, block, col=across))
    place_factor_weights(blocks_ref, w_ref)
    make_factors(h_ref, w_ref, turn_ref, hf_ref, bq_ref, win_ref.at[4])

    own = win_ref.at[4]
    one = mover.copy(own, win_ref.at[2], row=row + 1)
    two = mover.copy(win_ref.at[2], win_ref.at[0], row=row + 1)
    near = mover.copy(own, win_ref.at[3], col=core)
    pass_one = mover.copy(win_ref.at[2], win_ref.at[1 + 2 * side], col=core)
    pass_two = mover.copy(win_ref.at[0], win_ref.at[1], col=core)
    hands_on = jnp.logical_and(has_one, row <= 2)
    sends_two = jnp.logical_and(has_two, side == 1)
    takes_two = jnp.logical_and(has_two, side == 0)
    pl.when(row <= 2)(one.start)
    pl.when(side == 0)(near.start)

    @pl.when(has_one)
    def _():
        one.wait_recv()
        pass_one.start()

    pl.when(hands_on)(two.start)
    make_queries(hf_ref, bq_ref, q_ref)

    @pl.when(has_two)
    def _():
        two.wait_recv()

    pl.when(sends_two)(pass_two.start)

    @pl.when(has_one)
    def _():
        pass_one.wait_recv()
        pass_one.wait_send()

    pl.when(takes_two)(pass_two.wait_recv)
    pl.when(sends_two)(pass_two.wait_send)
    pl.when(side == 1)(near.wait_recv)
    pl.when(side == 0)(near.wait_send)
    pl.when(row <= 2)(one.wait_send)
    pl.when(hands_on)(two.wait_send)
    pl.when(row <= 2)(to_right.wait_send)
    pl.when(row >= 1)(to_left.wait_send)
    pl.when(row >= 1)(to_right.wait_recv)
    pl.when(row <= 2)(to_left.wait_recv)

    def end():
        for c in rest:
            c.wait_recv()
        for c in started:
            c.wait_send()

    return end


KEPT = (0, 2, 3, 4, 5, 6, 7, 8, 9, 11)


def head_attend_body(*refs):
    head_in, cot_ref = refs[:11], refs[11]
    outs, scratch = refs[12:30], refs[30:]
    kept = dict(zip(KEPT, scratch[10:20]))
    tiles = scratch[20:23]
    keep_sem, tile_sem = scratch[23:]
    head_out = [kept.get(k, outs[k]) for k in range(13)]
    o_out, lse_ref, k_out, v_out, near_ref = outs[13:]
    mixes_ref, q_ref, win_ref, seg_ref, rows_ref = (head_out[k] for k in (3, 7, 9, 10, 12))
    end = head_body(*head_in, *head_out, *scratch[:6])
    copies = [pltpu.make_async_copy(kept[k], outs[k], keep_sem.at[n]) for n, k in enumerate(KEPT)]
    for k, c in zip(KEPT, copies):
        if k != 3:
            c.start()

    def tile_copies(p):
        lanes = pl.ds(pl.multiple_of(p * LANES, LANES), LANES)
        return [
            pltpu.make_async_copy(source.at[:, lanes], target.at[:, lanes], tile_sem.at[n, p])
            for n, (source, target) in enumerate(zip(tiles, (o_out, k_out, v_out)))
        ]

    def store(p):
        for c in tile_copies(p):
            c.start()

    attend_body(
        True, q_ref, win_ref, seg_ref, end, cot_ref, tiles[0], lse_ref, tiles[1], tiles[2], rows_ref, near_ref,
        mixes_ref, *scratch[6:10], store=store,
    )
    copies[KEPT.index(3)].start()
    for p in range(PAIRS):
        for c in tile_copies(p):
            c.wait()
    for c in copies:
        c.wait()


def head_attend(tok, ranks_t, heads_t, gain_one, gain_two, gate_t, up_t, down, w_out, segments, inverse, cot):
    rows, feat = tok.shape[1:]
    units = -(-gate_t.shape[0] // 8 // 16) * 16
    block = (ranks_t.shape[0] + GROUP_COLS, feat)
    ffn = (4, 3, units, feat)
    count = 3 + 4 + 4 + 6 + 3 + 3 + 3 + 4 + 4 + 2 + 5
    outs = (
        jax.ShapeDtypeStruct(tok.shape, BF),
        jax.ShapeDtypeStruct((4, 8, feat), F32),
        jax.ShapeDtypeStruct(ffn, BF),
        jax.ShapeDtypeStruct((4, 4) + w_out.shape, BF),
        jax.ShapeDtypeStruct((rows, D), BF),
        jax.ShapeDtypeStruct((rows, HEAD_COLS), F32),
        jax.ShapeDtypeStruct((rows, RQ * HD), F32),
        jax.ShapeDtypeStruct((rows, D), BF),
        jax.ShapeDtypeStruct((ALL_COLS, D), BF),
        jax.ShapeDtypeStruct((5, rows, 3 * LANES), BF),
        jax.ShapeDtypeStruct((1, 5 * rows), jnp.int32),
        jax.ShapeDtypeStruct((rows, 2 * LANES), F32),
        jax.ShapeDtypeStruct((4,) + ffn, BF),
        *attend_shapes(rows, 5 * rows),
        jax.ShapeDtypeStruct((4,) + cot.shape, BF),
    )
    out_specs = [VMEM] * 12 + [ANY] + [ANY, VMEM, ANY, ANY] + [ANY]
    for k in KEPT:
        out_specs[k] = ANY
    return pl.pallas_call(
        head_attend_body,
        out_shape=outs,
        in_specs=[VMEM] * 11 + [ANY],
        out_specs=tuple(out_specs),
        scratch_shapes=[
            pltpu.VMEM(block, BF),
            pltpu.VMEM((8, feat), F32),
            pltpu.VMEM(ffn, BF),
            pltpu.VMEM((4, 4) + block, BF),
            pltpu.SemaphoreType.DMA((count,)),
            pltpu.SemaphoreType.DMA((count,)),
            pltpu.VMEM((5 * rows, rows), F32),
            pltpu.VMEM((2 * RK, 5 * rows, LANES), F32),
            pltpu.SemaphoreType.DMA((22,)),
            pltpu.SemaphoreType.DMA((22,)),
        ]
        + [pltpu.VMEM(outs[k].shape, outs[k].dtype) for k in KEPT + (13, 15, 16)]
        + [pltpu.SemaphoreType.DMA((len(KEPT),)), pltpu.SemaphoreType.DMA((3, PAIRS))],
        compiler_params=comm_params(1),
        cost_estimate=cost_of(2 * rows * D * (800 * 3 + 5 * rows * 16), 30 << 20),
    )(tok, ranks_t, heads_t, gain_one, gain_two, gate_t, up_t, down, w_out, segments, inverse, cot)


def window_lanes(ref, lanes):
    value = ref[..., lanes]
    return value.reshape(-1, value.shape[-1])


def mask_bias(seg_ref, keys, rows):
    seg_row = seg_ref[...].astype(F32)
    wide = jnp.broadcast_to(seg_row, (LANES, keys))
    column = wide.T
    column = jnp.concatenate([column] * (rows // LANES), axis=1)
    key_idx = lax.broadcasted_iota(jnp.int32, (keys, rows), 0)
    query_idx = lax.broadcasted_iota(jnp.int32, (keys, rows), 1) + (keys - rows)
    same = column == seg_row[:, keys - rows :]
    return jnp.where(same & (key_idx <= query_idx), 0.0, NEG)


def attend_body(fast, q_ref, kf_ref, seg_ref, *refs, store=None):
    if fast:
        head_end, cot_ref, o_ref, lse_ref, k_ref, v_ref, w_rows_ref, cot_near_ref, mixes_ref = refs[:9]
        bias_ref, dup_ref, send_sem, recv_sem = refs[9:]
        side_work = AttendCopies(head_end, cot_ref, w_rows_ref, cot_near_ref, mixes_ref, send_sem, recv_sem)
        side_work.first()
    else:
        o_ref, lse_ref, k_ref, v_ref, bias_ref, dup_ref = refs
    rows = q_ref.shape[0]
    keys = seg_ref.shape[1]
    bias_ref[...] = mask_bias(seg_ref, keys, rows)
    for s in range(2 * RK):
        tile = window_lanes(kf_ref, slice((s // 2) * LANES, (s // 2 + 1) * LANES)).astype(F32)
        dup_ref[s] = double_left(tile) if s % 2 == 0 else double_right(tile)

    def pair(p, carried):
        if fast:
            pl.when(p == 2)(side_work.early)
            pl.when(p == 4)(side_work.second)
        lanes = pl.ds(pl.multiple_of(p * LANES, LANES), LANES)
        weights = window_lanes(kf_ref, slice(2 * LANES, 3 * LANES))
        made = []
        for kind in range(2):
            acc = None
            for s in range(RK):
                pick = spread(LANES, (kind * RK + s) * H + 2 * p, LANES)
                term = nn(weights, pick) * dup_ref[kind * RK + s]
                acc = term if acc is None else acc + term
            made.append((acc / RK).astype(BF))
        k_tile, v_tile = made
        k_ref[:, lanes] = k_tile
        v_ref[:, lanes] = v_tile
        v_turned = v_tile.astype(F32).T.astype(BF)
        q_turned = (q_ref[:, lanes].astype(F32) * HD**-0.5).T
        half = lax.broadcasted_iota(jnp.int32, q_turned.shape, 0) // HD
        outs = []
        for side in range(2):
            q_side = jnp.where(half == side, q_turned, 0.0).astype(BF)
            scores = nn(k_tile, q_side) + bias_ref[...]
            peak = jnp.max(scores, axis=0, keepdims=True)
            weight = jnp.exp(scores - peak)
            total = jnp.sum(weight, axis=0, keepdims=True)
            probs = (weight * (1.0 / total)).astype(BF)
            outs.append(nn(v_turned[side * HD : (side + 1) * HD], probs))
            lse_ref[2 * p + side] = jnp.broadcast_to(peak + jnp.log(total), (8, rows))
        o_ref[:, lanes] = jnp.concatenate(outs, axis=0).T.astype(BF)
        if fast:
            store(p)
        return carried

    lax.fori_loop(0, PAIRS, pair, 0)
    if fast:
        side_work.last()


def attend_shapes(rows, keys):
    return [
        jax.ShapeDtypeStruct((rows, D), BF),
        jax.ShapeDtypeStruct((H, 8, rows), F32),
        jax.ShapeDtypeStruct((keys, D), BF),
        jax.ShapeDtypeStruct((keys, D), BF),
    ]


def attend(q, kf_window, seg_window):
    rows = q.shape[0]
    keys = kf_window.shape[0]
    return call(
        functools.partial(attend_body, False),
        tuple(attend_shapes(rows, keys)),
        scratch=(pltpu.VMEM((keys, rows), F32), pltpu.VMEM((2 * RK, keys, LANES), F32)),
        cost=cost_of(2 * rows * keys * D * 16, 16 << 20),
    )(q, kf_window, seg_window)


def attend_back_body(fast, q_ref, k_ref, v_ref, do_ref, lse_ref, kf_ref, seg_ref, *refs, load=None):
    if fast:
        dq_ref, dkf_ref = refs[5:7]
        bias_ref, dup_ref, sum_ref, fac_ref = refs[10:14]
        side_work = BackCopies(refs[:5] + refs[7:10] + refs[14:28], refs[28:])
        side_work.first()
    else:
        dq_ref, dkf_ref, bias_ref, dup_ref, sum_ref, fac_ref = refs
    rows = q_ref.shape[0]
    keys = seg_ref.shape[1]
    bias_ref[...] = mask_bias(seg_ref, keys, rows)
    for s in range(2 * RK):
        tile = window_lanes(kf_ref, slice((s // 2) * LANES, (s // 2 + 1) * LANES)).astype(F32)
        dup_ref[s] = double_left(tile) if s % 2 == 0 else double_right(tile)
    sum_ref[...] = jnp.zeros_like(sum_ref)
    fac_ref[...] = jnp.zeros_like(fac_ref)

    def pair(p, carried):
        if fast:
            pl.when(p == 1)(side_work.cross_x)
            pl.when(p == 3)(side_work.second)
            pl.when(p == 4)(side_work.last_hop)
            pl.when(p == 6)(side_work.third)
            load(p)
        lanes = pl.ds(pl.multiple_of(p * LANES, LANES), LANES)
        k_tile = k_ref[:, lanes]
        v_tile = v_ref[:, lanes]
        k_turned = k_tile.astype(F32).T.astype(BF)
        q_tile = q_ref[:, lanes].astype(F32) * HD**-0.5
        do_tile = do_ref[:, lanes].astype(F32)
        q_turned = q_tile.T
        do_turned = do_tile.T
        half = lax.broadcasted_iota(jnp.int32, q_turned.shape, 0) // HD
        lane_half = lax.broadcasted_iota(jnp.int32, q_tile.shape, 1) // HD
        d_k = None
        d_v = None
        d_q = []
        for side in range(2):
            q_side = jnp.where(half == side, q_turned, 0.0).astype(BF)
            do_side = jnp.where(half == side, do_turned, 0.0).astype(BF)
            scores = nn(k_tile, q_side) + bias_ref[...]
            probs = jnp.exp(scores - lse_ref[2 * p + side][:1])
            d_prob = nn(v_tile, do_side)
            delta = jnp.sum(probs * d_prob, axis=0, keepdims=True)
            d_score = (probs * (d_prob - delta)).astype(BF)
            d_q.append(nn(k_turned[side * HD : (side + 1) * HD], d_score))
            q_back = jnp.where(lane_half == side, q_tile, 0.0).astype(BF)
            do_back = jnp.where(lane_half == side, do_tile, 0.0).astype(BF)
            part_k = nn(d_score, q_back)
            part_v = nn(probs.astype(BF), do_back)
            d_k = part_k if d_k is None else d_k + part_k
            d_v = part_v if d_v is None else d_v + part_v
        dq_ref[:, lanes] = jnp.concatenate(d_q, axis=0).T * HD**-0.5
        weights = window_lanes(kf_ref, slice(2 * LANES, 3 * LANES))
        for kind, grad in ((0, d_k), (1, d_v)):
            for s in range(RK):
                slot = kind * RK + s
                pick = spread(LANES, slot * H + 2 * p, LANES)
                sum_ref[slot] += nn(weights, pick) * grad
                product = (grad * dup_ref[slot]).astype(BF)
                fac_ref[...] += nn(product, collect(LANES, LANES, slot * H + 2 * p))
        return carried

    lax.fori_loop(0, PAIRS, pair, 0)
    for tile in range(2):
        first = sum_ref[2 * tile]
        second = sum_ref[2 * tile + 1]
        first = first + pltpu.roll(first, HD, 1)
        second = second + pltpu.roll(second, HD, 1)
        merged = jnp.where(lane_iota(first.shape) < HD, first, second)
        blocks = dkf_ref.shape[:-1] + (LANES,)
        dkf_ref[..., tile * LANES : (tile + 1) * LANES] = (merged / RK).astype(BF).reshape(blocks)
    dkf_ref[..., 2 * LANES :] = (fac_ref[...] / RK).astype(BF).reshape(blocks)
    if fast:
        side_work.last()


def back_scratch(rows, keys):
    return [
        pltpu.VMEM((keys, rows), F32),
        pltpu.VMEM((2 * RK, keys, LANES), F32),
        pltpu.VMEM((2 * RK, keys, LANES), F32),
        pltpu.VMEM((keys, LANES), F32),
    ]


def attend_back(q, k, v, d_heads, lse, kf_window, seg_window):
    rows = q.shape[0]
    keys = kf_window.shape[0]
    return call(
        functools.partial(attend_back_body, False),
        (jax.ShapeDtypeStruct((rows, D), F32), jax.ShapeDtypeStruct(kf_window.shape, BF)),
        scratch=back_scratch(rows, keys),
        cost=cost_of(2 * rows * keys * D * 40, 16 << 20),
    )(q, k, v, d_heads, lse, kf_window, seg_window)


def mixing_body(x_ref, heads_ref, w_out_ref, gain_ref, mixed_ref, h_ref):
    parts, _, feat = x_ref.shape
    rows_of = w_out_ref.shape[0]
    head_rows = w_out_ref.shape[2]
    total = None
    for c in range(parts):
        lanes = slice(c * feat, (c + 1) * feat)
        acc = x_ref[c].astype(F32)
        for r in range(rows_of):
            acc = acc + nn(heads_ref[:, r * head_rows : (r + 1) * head_rows], w_out_ref[r, c])
        mixed_ref[:, lanes] = acc
        part = jnp.sum(acc * acc, axis=1, keepdims=True)
        total = part if total is None else total + part
    scale = lax.rsqrt(total / D + EPS)
    for c in range(parts):
        lanes = slice(c * feat, (c + 1) * feat)
        h_ref[:, lanes] = (mixed_ref[:, lanes] * scale * gain_ref[c, 1:2]).astype(BF)


def mixing(x_parts, heads, w_out, gains):
    rows = heads.shape[0]
    return call(
        mixing_body,
        (jax.ShapeDtypeStruct((rows, D), F32), jax.ShapeDtypeStruct((rows, D), BF)),
        cost=cost_of(2 * rows * D * D, 5 << 20),
    )(x_parts, heads, w_out, gains)


def ffn_steps(blocks, h_at, cot_at, w_ref, hid_ref, dg_ref, du_ref, out_at, back_at):
    def block(t, carried):
        h = h_at(t)[...]
        gate = nt(h, w_ref[0])
        up = nt(h, w_ref[1])
        d_hidden = nt(cot_at(t)[...], w_ref[2])
        sig = 1.0 / (1.0 + jnp.exp(-gate))
        silu = gate * sig
        hidden = (silu * up).astype(BF)
        d_gate = (d_hidden * up * sig * (1.0 + gate * (1.0 - sig))).astype(BF)
        d_up = (d_hidden * silu).astype(BF)
        rows = h.shape[0]
        place = pl.ds(pl.multiple_of(t * rows, rows), rows)
        hid_ref[place] = hidden
        dg_ref[place] = d_gate
        du_ref[place] = d_up
        out_at(t)[...] = nn(hidden, w_ref[2]).astype(BF)
        back_at(t)[...] = (nn(d_gate, w_ref[0]) + nn(d_up, w_ref[1])).astype(BF)
        return carried

    lax.fori_loop(0, blocks, block, 0)


def ffn_body(h_ref, cot_ref, w_ref, out_ref, back_ref, g_ref, hid_ref, dg_ref, du_ref):
    parts, rows, _ = h_ref.shape
    ffn_steps(
        parts, lambda t: h_ref.at[t], lambda t: cot_ref.at[t], w_ref, hid_ref, dg_ref, du_ref,
        lambda t: out_ref.at[t], lambda t: back_ref.at[t],
    )
    h_all = h_ref[...].reshape(parts * rows, D)
    cot_all = cot_ref[...].reshape(parts * rows, D)
    for place, (left, right) in enumerate(((dg_ref, h_all), (du_ref, h_all), (hid_ref, cot_all))):
        g_ref[place] = tn(left[...], right).astype(BF)


def ffn(h_all, cot_all, w):
    parts, rows, _ = h_all.shape
    units = w.shape[1]
    return call(
        ffn_body,
        (
            jax.ShapeDtypeStruct(h_all.shape, BF),
            jax.ShapeDtypeStruct(h_all.shape, BF),
            jax.ShapeDtypeStruct(w.shape, BF),
        ),
        scratch=[pltpu.VMEM((parts * rows, units), BF)] * 3,
        cost=cost_of(2 * parts * rows * 9 * D * units, 20 << 20),
    )(h_all, cot_all, w)


def unmix_math(
    mixed_ref, cot_ref, d_h, heads_ref, w_out_ref, gain_ref, d_mixed_ref, d_heads_ref, g_out_ref, g_gain_ref
):
    rows_of, parts, head_rows, feat = w_out_ref.shape
    mixed = mixed_ref[...]
    scale = lax.rsqrt(jnp.sum(mixed * mixed, axis=1, keepdims=True) / D + EPS)
    normed = mixed * scale
    g_gain_ref[...] = jnp.sum(d_h * normed, axis=0, keepdims=True)
    gain = jnp.concatenate([gain_ref[c, 1:2] for c in range(parts)], axis=1)
    inner = d_h * gain
    dot = jnp.sum(inner * normed, axis=1, keepdims=True) / D
    d_mixed = cot_ref[...].astype(F32) + scale * (inner - normed * dot)
    d_mixed_ref[...] = d_mixed
    low = d_mixed.astype(BF)
    grad = tn(heads_ref[...], low)
    for r in range(rows_of):
        acc = None
        for c in range(parts):
            lanes = slice(c * feat, (c + 1) * feat)
            term = nt(low[:, lanes], w_out_ref[r, c])
            acc = term if acc is None else acc + term
            g_out_ref[r, c] = grad[r * head_rows : (r + 1) * head_rows, lanes].astype(BF)
        d_heads_ref[:, r * head_rows : (r + 1) * head_rows] = acc.astype(BF)


def write_output(mixed_ref, total, out_ref):
    parts, _, feat = out_ref.shape
    for c in range(parts):
        lanes = slice(c * feat, (c + 1) * feat)
        out_ref[c] = (mixed_ref[:, lanes] + total[:, lanes]).astype(BF)


def unmix_body(
    dh_ref, sum_ref, mixed_ref, cot_ref, heads_ref, w_out_ref, gain_ref,
    out_ref, d_mixed_ref, d_heads_ref, g_out_ref, g_gain_ref,
):
    unmix_math(
        mixed_ref, cot_ref, dh_ref[...], heads_ref, w_out_ref, gain_ref,
        d_mixed_ref, d_heads_ref, g_out_ref, g_gain_ref,
    )
    write_output(mixed_ref, sum_ref[...], out_ref)


def middle_body(
    x_ref, heads_ref, w_out_ref, gain_ref, cot_own_ref, cot_in_ref, w_own_ref, rows_ref,
    mixed_out, d_mixed_ref, d_heads_ref, g_out_ref, g_gain_ref, g_hbm, out_pair_hbm, hop_ref,
    w_ref, h_ref, cot_ref, hid_ref, dg_ref, du_ref, back_ref, fwd_ref, back_got_ref, fwd_got_ref,
    pair_ref, diag_ref, far_ref, send_sem, recv_sem, w_sem, cot_sem,
    mixed_ref, g_ref, out_pair_ref, leave_sem,
):
    row = lax.axis_index("row")
    col, core, across = neighbours()
    dp, (me, on_x, on_y, on_both) = square()
    x, mine = col // 2, lax.rem(col, 2)
    y = 1 - dp
    parts, rows, feat = x_ref.shape
    units = rows_ref.shape[3]
    greet(
        [
            (None, {"col": core}),
            (None, {"col": across}),
            (None, {"dp": y}),
            (row <= 2, {"row": row + 1}),
            (row >= 1, {"row": row - 1}),
        ]
    )
    mover = Mover(send_sem, recv_sem)

    def w_place(r, c):
        return w_ref.at[:, pl.ds(pl.multiple_of(r * units, units), units), pl.ds(c * feat, feat)]

    local = []
    for k in range(4):
        r = lax.rem(row + k, 4)
        for c in range(4):
            source = w_own_ref.at[c] if k == 0 else rows_ref.at[r, c]
            copy = pltpu.make_async_copy(source, w_place(r, c), w_sem.at[k, c])
            copy.start()
            local.append(copy)
    cots = []
    for k in range(4):
        from_x = lax.rem(x + k % 2, 2)
        from_dp = lax.rem(dp + k // 2, 2)
        lanes = pl.ds(pl.multiple_of((from_x * 2 + mine) * feat, feat), feat)
        for c in range(4):
            part = pl.ds(c * rows, rows)
            source = cot_own_ref.at[part] if k == 0 else cot_in_ref.at[from_dp * 2 + from_x, part]
            spot = from_dp * 2 + c // 2
            copy = pltpu.make_async_copy(source, cot_ref.at[lax.rem(mine + c, 2), spot, :, lanes], cot_sem.at[k, c])
            copy.start()
            local.append(copy)
            sent = mover.copy(source, cot_ref.at[lax.rem(mine + c + 1, 2), spot, :, lanes], col=core)
            sent.start()
            cots.append(sent)

    total = None
    for c in range(parts):
        lanes = slice(c * feat, (c + 1) * feat)
        acc = x_ref[c].astype(F32)
        for r in range(4):
            acc = acc + nn(heads_ref[:, r * feat : (r + 1) * feat], w_out_ref[r, c])
        mixed_ref[:, lanes] = acc
        part = jnp.sum(acc * acc, axis=1, keepdims=True)
        total = part if total is None else total + part
    scale = lax.rsqrt(total / D + EPS)
    for c in range(parts):
        lanes = slice(c * feat, (c + 1) * feat)
        h_ref[0, me, :, lanes] = (mixed_ref[:, lanes] * scale * gain_ref[c, 1:2]).astype(BF)

    leave = [
        pltpu.make_async_copy(source, target, leave_sem.at[n])
        for n, (source, target) in enumerate(
            ((mixed_ref, mixed_out), (g_ref, g_hbm), (out_pair_ref, out_pair_hbm))
        )
    ]
    leave[0].start()

    half = rows // 2
    top, low = pl.ds(0, half), pl.ds(half, half)

    def h_copy(spot, part=None, side=0, **place):
        source = h_ref.at[0, spot] if part is None else h_ref.at[0, spot, part]
        target = h_ref.at[side, spot] if part is None else h_ref.at[side, spot, part]
        return mover.copy(source, target, **place)

    x_low = h_copy(me, low, col=across)
    y_top = h_copy(me, top, dp=y)
    x_top = h_copy(me, top, col=across)
    y_low = h_copy(me, low, dp=y)
    near = h_copy(me, None, 1, col=core)
    both_low = h_copy(on_x, low, dp=y)
    both_top = h_copy(on_y, top, col=across)
    near_first = [h_copy(on_x, low, 1, col=core), h_copy(on_y, top, 1, col=core)]
    near_second = [h_copy(on_x, top, 1, col=core), h_copy(on_y, low, 1, col=core)]
    near_both = h_copy(on_both, None, 1, col=core)
    for c in (x_low, y_top, near, x_top, y_low):
        c.start()
    steps = (
        ((me, top), (me, low)),
        ((on_x, low), (on_y, top)),
        ((on_x, top), (on_y, low)),
        ((on_both, top), (on_both, low)),
    )
    back_near = [[mover.copy(back_ref.at[1, s, p], back_got_ref.at[s, p], col=core) for s, p in two] for two in steps]
    fwd_near = [[mover.copy(fwd_ref.at[1, s, p], fwd_got_ref.at[s, p], col=core) for s, p in two] for two in steps]
    diag = [
        mover.copy(pair_ref.at[on_both, low], diag_ref.at[0], col=across),
        mover.copy(pair_ref.at[on_both, top], diag_ref.at[1], dp=y),
    ]
    far = [
        mover.copy(pair_ref.at[on_x, low], far_ref.at[0, low], col=across),
        mover.copy(pair_ref.at[on_y, top], far_ref.at[1, top], dp=y),
        mover.copy(pair_ref.at[on_y, low], far_ref.at[1, low], dp=y),
        mover.copy(pair_ref.at[on_x, top], far_ref.at[0, top], col=across),
    ]

    def add_pair(k):
        for (s, p), c in zip(steps[k], back_near[k]):
            c.wait_recv()
            pair_ref[s, p] = (back_ref[0, s, p].astype(F32) + back_got_ref[s, p].astype(F32)).astype(BF)

    for copy in local:
        copy.wait()
    for c in cots:
        c.wait_recv()

    def block(t, carried):
        @pl.when(t == 1)
        def _():
            near.wait_recv()

        @pl.when(t == 2)
        def _():
            x_low.wait_recv()
            both_low.start()
            near_first[0].start()
            y_top.wait_recv()
            both_top.start()
            near_first[1].start()

        @pl.when(t == 3)
        def _():
            for c in near_first:
                c.wait_recv()

        @pl.when(t == 4)
        def _():
            x_top.wait_recv()
            near_second[0].start()
            y_low.wait_recv()
            near_second[1].start()

        @pl.when(t == 5)
        def _():
            for c in near_second:
                c.wait_recv()
            add_pair(1)
            far[0].start()
            far[1].start()

        @pl.when(t == 6)
        def _():
            both_low.wait_recv()
            both_top.wait_recv()
            near_both.start()

        @pl.when(t == 7)
        def _():
            near_both.wait_recv()
            add_pair(2)

        name, side = t // 2, lax.rem(t, 2)
        first_dp = lax.rem(dp + jnp.where(name == 3, 1, 0), 2)
        first_x = lax.rem(x + jnp.where(name >= 1, 1, 0), 2)
        first = first_dp * 2 + first_x
        other_dp = lax.rem(dp + jnp.where(name >= 1, 1, 0), 2)
        other_x = lax.rem(x + jnp.where(name == 3, 1, 0), 2)
        other = other_dp * 2 + other_x
        first_rows = pl.ds(pl.multiple_of(jnp.where(name == 1, half, 0), half), half)
        other_rows = pl.ds(pl.multiple_of(jnp.where(name == 1, 0, half), half), half)
        h = jnp.concatenate([h_ref[side, first, first_rows], h_ref[side, other, other_rows]], axis=0)
        cot = jnp.concatenate([cot_ref[side, first, first_rows], cot_ref[side, other, other_rows]], axis=0)
        gate = nt(h, w_ref[0])
        up = nt(h, w_ref[1])
        d_hidden = nt(cot, w_ref[2])
        sig = 1.0 / (1.0 + jnp.exp(-gate))
        silu = gate * sig
        hidden = (silu * up).astype(BF)
        d_gate = (d_hidden * up * sig * (1.0 + gate * (1.0 - sig))).astype(BF)
        d_up = (d_hidden * silu).astype(BF)
        back = (nn(d_gate, w_ref[0]) + nn(d_up, w_ref[1])).astype(BF)
        fwd = nn(hidden, w_ref[2]).astype(BF)
        for spot, part, cut in ((first, first_rows, slice(0, half)), (other, other_rows, slice(half, rows))):
            start = jnp.where(part.start == 0, 0, half)
            place = pl.ds(pl.multiple_of((side * 4 + spot) * rows + start, half), half)
            hid_ref[place] = hidden[cut]
            dg_ref[place] = d_gate[cut]
            du_ref[place] = d_up[cut]
            back_ref[side, spot, part] = back[cut]
            fwd_ref[side, spot, part] = fwd[cut]
        for k in range(4):

            @pl.when(t == 2 * k + 1)
            def _():
                for c in back_near[k] + fwd_near[k]:
                    c.start()

        return carried

    lax.fori_loop(0, 8, block, 0)
    add_pair(3)
    for c in diag:
        c.start()

    hops = []
    for place in range(3):
        to_right = mover.copy(g_ref.at[3, place], hop_ref.at[place], row=row + 1)
        to_left = mover.copy(g_ref.at[0, place], hop_ref.at[place], row=row - 1)
        hops.append((to_right, to_left))

    def gradient(place, left, right):
        grad = tn(left[...], right[...].reshape(8 * rows, D))
        for r in range(4):
            g_ref[r, place] = grad[r * units : (r + 1) * units].astype(BF)
        pl.when(row == 0)(hops[place][0].start)
        pl.when(row == 3)(hops[place][1].start)

    gradient(0, dg_ref, h_ref)
    gradient(1, du_ref, h_ref)
    for k, (s, part) in enumerate(((on_y, low), (on_x, top))):
        diag[k].wait_recv()
        pair_ref[s, part] = (pair_ref[s, part].astype(F32) + diag_ref[k].astype(F32)).astype(BF)
        far[2 + k].start()
    gradient(2, hid_ref, cot_ref)
    leave[1].start()
    for two, copies in zip(steps, fwd_near):
        for (s, p), c in zip(two, copies):
            c.wait_recv()
            out_pair_ref[s, p] = (fwd_ref[0, s, p].astype(F32) + fwd_got_ref[s, p].astype(F32)).astype(BF)
    leave[2].start()
    add_pair(0)
    for c in far:
        c.wait_recv()
    d_h = pair_ref[me].astype(F32) + far_ref[0].astype(F32) + far_ref[1].astype(F32)
    unmix_math(
        mixed_ref, cot_ref.at[0, me], d_h, heads_ref, w_out_ref, gain_ref,
        d_mixed_ref, d_heads_ref, g_out_ref, g_gain_ref,
    )
    for c in cots + [x_low, y_top, x_top, y_low, near, both_low, both_top, near_both] + near_first + near_second:
        c.wait_send()
    for two in back_near + fwd_near:
        for c in two:
            c.wait_send()
    for c in diag + far:
        c.wait_send()
    for c in leave:
        c.wait()
    for to_right, to_left in hops:
        pl.when(row == 0)(to_right.wait_send)
        pl.when(row == 3)(to_left.wait_send)
        pl.when(row == 1)(to_right.wait_recv)
        pl.when(row == 2)(to_left.wait_recv)


def middle(x_parts, heads, w_out, gains, cot_own, cot_near, w_own, w_rows):
    parts, rows, feat = x_parts.shape
    units = w_rows.shape[3]
    count = 16 + 12 + 16 + 6 + 6
    square_of = pltpu.VMEM((2, 4, rows, D), BF)
    hidden_of = pltpu.VMEM((8 * rows, 4 * units), BF)
    quarter = pltpu.VMEM((4, rows, D), BF)
    return pl.pallas_call(
        middle_body,
        out_shape=(
            jax.ShapeDtypeStruct((rows, D), F32),
            jax.ShapeDtypeStruct((rows, D), F32),
            jax.ShapeDtypeStruct((rows, D), BF),
            jax.ShapeDtypeStruct(w_out.shape, BF),
            jax.ShapeDtypeStruct((1, D), F32),
            jax.ShapeDtypeStruct((4, 3, units, D), BF),
            jax.ShapeDtypeStruct((4, rows, D), BF),
            jax.ShapeDtypeStruct((3, units, D), BF),
        ),
        in_specs=[VMEM] * 4 + [ANY] * 4,
        out_specs=(ANY,) + (VMEM,) * 4 + (ANY,) * 3,
        scratch_shapes=[pltpu.VMEM((3, 4 * units, D), BF), square_of, square_of]
        + [hidden_of] * 3
        + [square_of, square_of, quarter, quarter, quarter]
        + [
            pltpu.VMEM((2, rows // 2, D), BF),
            pltpu.VMEM((2, rows, D), BF),
            pltpu.SemaphoreType.DMA((count,)),
            pltpu.SemaphoreType.DMA((count,)),
            pltpu.SemaphoreType.DMA((4, 4)),
            pltpu.SemaphoreType.DMA((4, 4)),
            pltpu.VMEM((rows, D), F32),
            pltpu.VMEM((4, 3, units, D), BF),
            quarter,
            pltpu.SemaphoreType.DMA((3,)),
        ],
        compiler_params=comm_params(4),
        cost_estimate=cost_of(2 * 8 * rows * 9 * D * 4 * units, 24 << 20),
    )(x_parts, heads, w_out, gains, cot_own, cot_near, w_own, w_rows)


def unmix(dh, out_sum, mixed, cot_own, heads, w_out, gains):
    rows = heads.shape[0]
    parts, feat = w_out.shape[1], w_out.shape[3]
    outs = (
        jax.ShapeDtypeStruct((parts, rows, feat), BF),
        jax.ShapeDtypeStruct((rows, D), F32),
        jax.ShapeDtypeStruct((rows, D), BF),
        jax.ShapeDtypeStruct(w_out.shape, BF),
        jax.ShapeDtypeStruct((1, D), F32),
    )
    return call(unmix_body, outs, cost=cost_of(4 * rows * D * D, 18 << 20))(
        dh, out_sum, mixed, cot_own, heads, w_out, gains
    )


def query_grads(ranks_taken, dq, high, low, bq_ref):
    fac = None
    folded = []
    for r in ranks_taken:
        tile = bq_ref[:, (r // 2) * LANES : (r // 2 + 1) * LANES]
        rank = double_left(tile) if r % 2 == 0 else double_right(tile)
        product = dq * jnp.concatenate([rank] * PAIRS, axis=1)
        term = two_pass(product, head_collect(2 * RK + r))
        fac = term if fac is None else fac + term
        pick = head_spread(2 * RK + r, 0, D)
        terms = (nn(high, pick) + nn(low, pick)) * dq
        acc = terms[:, :LANES]
        for p in range(1, PAIRS):
            acc = acc + terms[:, p * LANES : (p + 1) * LANES]
        folded.append(acc + pltpu.roll(acc, HD, 1))
    return fac, folded


def turned_back(part, turn_ref):
    return part * turn_ref[:, :LANES] - swap_halves(part) * turn_ref[:, LANES:]


def put_query_grads(folded, first, turn_ref, d_ref):
    lane = lane_iota(folded[0].shape)
    for k in range(len(folded) // 2):
        merged = jnp.where(lane < HD, folded[2 * k], folded[2 * k + 1])
        tile = first // 2 + k
        d_ref[:, tile * LANES : (tile + 1) * LANES] = turned_back(merged, turn_ref).astype(BF)


def put_key_grads(dkf, fac, turn_ref, d_ref):
    d_ref[:, 3 * LANES : 4 * LANES] = turned_back(dkf[:, :LANES], turn_ref).astype(BF)
    d_ref[:, 4 * LANES : 5 * LANES] = dkf[:, LANES : 2 * LANES].astype(BF)
    fac = fac.astype(BF).astype(F32) + nt(dkf[:, 2 * LANES :].astype(BF), key_columns())
    d_ref[:, RANK_COLS:] = fac.astype(BF)


def factor_weight_grads(d_ref, h_ref, gains, g_two_ref, g_ref):
    n_row, parts, _, feat = g_ref.shape
    grad = tn(d_ref[...], h_ref[...])
    ranks_each = RANK_COLS // n_row
    used = FAC * GROUP
    for c in range(parts):
        lanes = slice(c * feat, (c + 1) * feat)
        tail = jnp.concatenate(
            [gains[c], g_two_ref[:, lanes], jnp.zeros((GROUP_COLS - used - 2, feat), F32)], axis=0
        )
        for r in range(n_row):
            first = RANK_COLS + r * GROUP_COLS
            g_ref[r, c, :ranks_each] = grad[r * ranks_each : (r + 1) * ranks_each, lanes].astype(BF)
            g_ref[r, c, ranks_each:] = jnp.concatenate([grad[first : first + used, lanes], tail], axis=0).astype(BF)


def first_norm_back(d_h, x_ref, gain_ref, d_mixed_ref, gi_ref):
    parts, _, feat = x_ref.shape
    xs = [x_ref[c].astype(F32) for c in range(parts)]
    total = sum(jnp.sum(v * v, axis=1, keepdims=True) for v in xs)
    scale = lax.rsqrt(total / D + EPS)
    dot = None
    gains = []
    for c in range(parts):
        normed = xs[c] * scale
        grad = d_h[:, c * feat : (c + 1) * feat]
        gains.append(jnp.sum(grad * normed, axis=0, keepdims=True))
        part = jnp.sum(grad * gain_ref[c, :1] * normed, axis=1, keepdims=True)
        dot = part if dot is None else dot + part
    for c in range(parts):
        lanes = slice(c * feat, (c + 1) * feat)
        normed = xs[c] * scale
        total = d_mixed_ref[:, lanes] + scale * (d_h[:, lanes] * gain_ref[c, :1] - normed * (dot / D))
        gi_ref[c] = total.astype(gi_ref.dtype)
    return gains


def back_body(
    dq_ref, dkf_ref, hf_ref, bq_ref, turn_ref, w_ref, h_ref, x_ref, gain_ref, d_mixed_ref, g_two_ref,
    gi_ref, g_ref, d_ref,
):
    heads = hf_ref[...]
    high = heads.astype(BF)
    low = (heads - high.astype(F32)).astype(BF)
    fac, folded = query_grads(range(RQ), dq_ref[...] * (1.0 / RQ), high, low, bq_ref)
    put_query_grads(folded, 0, turn_ref, d_ref)
    put_key_grads(dkf_ref[...].astype(F32), fac, turn_ref, d_ref)
    gains = first_norm_back(nn(d_ref[...], w_ref[...]), x_ref, gain_ref, d_mixed_ref, gi_ref)
    factor_weight_grads(d_ref, h_ref, gains, g_two_ref, g_ref)


def back(dq, dkf, hf, bq, turn, w_rh, h, x_parts, gains, d_mixed, g_two, n_row):
    rows = dq.shape[0]
    parts, _, feat = x_parts.shape
    each = RANK_COLS // n_row + GROUP_COLS
    return call(
        back_body,
        (jax.ShapeDtypeStruct(x_parts.shape, F32), jax.ShapeDtypeStruct((n_row, parts, each, feat), BF)),
        scratch=[pltpu.VMEM((rows, ALL_COLS), BF)],
        cost=cost_of(2 * rows * D * 800 * 6, 12 << 20),
    )(dq, dkf, hf, bq, turn, w_rh, h, x_parts, gains, d_mixed, g_two)


def tail_body(
    win_ref, dq_ref, hf_ref, bq_ref, turn_ref, w_ref, h_ref, x_ref, gain_ref, d_mixed_ref, g_two_ref,
    rows_ref, ends_ref, part_ref,
    grad_ref, gi_all_ref, cols_ref, cols_other_ref, mix_ref, mix_other_ref,
    d_ref, gi_ref, wnear_ref, wsend_ref, wfar_ref, rows_own_ref, cols_send_ref, mix_got_ref,
    g_ref, near_ref, pair_ref, far_ref, side_ref, down_ref, last_ref, end_ref,
    send_sem, recv_sem, local_sem,
):
    row = lax.axis_index("row")
    col, core, across = neighbours()
    cross = lax.rem(core + 2, 4)
    dp = lax.axis_index("dp")
    x, mine = col // 2, lax.rem(col, 2)
    y = 1 - dp
    order = [lax.rem(row + k, 4) for k in (1, 2, 3, 0)]
    mover = Mover(send_sem, recv_sem)
    started = []

    def go(source, target, **place):
        c = mover.copy(source, target, **place)
        c.start()
        started.append(c)
        return c

    rows_own = pltpu.make_async_copy(rows_ref.at[row], rows_own_ref, local_sem.at[1])
    rows_own.start()

    near_one = go(win_ref.at[1], wnear_ref.at[0], col=core)
    near_two = go(win_ref.at[3], wnear_ref.at[1], col=core)
    one = mover.copy(wsend_ref.at[0], wfar_ref.at[0], row=row - 1)
    two = mover.copy(wsend_ref.at[1], wfar_ref.at[1], row=row - 1)
    hands_on = jnp.logical_and(row >= 1, row <= 2)
    left = mine == 0
    heads = hf_ref[...]
    high = heads.astype(BF)
    low = (heads - high.astype(F32)).astype(BF)
    dq = dq_ref[...] * (1.0 / RQ)
    near_one.wait_recv()
    near_two.wait_recv()
    zero = jnp.zeros(wnear_ref.shape[1:], F32)
    from_low = wnear_ref[0].astype(F32)
    from_high = wnear_ref[1].astype(F32)
    wsend_ref[1] = (win_ref[0].astype(F32) + jnp.where(left, zero, from_low)).astype(BF)
    pl.when(row >= 2)(two.start)

    width = x_ref.shape[2]
    rows_own.wait()
    for place in range(3):
        total = rows_own_ref[place].astype(F32)
        total = total + jnp.where(row >= 1, ends_ref[0, place].astype(F32), 0.0)
        total = (total + jnp.where(row <= 2, ends_ref[1, place].astype(F32), 0.0)).astype(BF)
        for c in range(4):
            cols_send_ref[c, place] = total[:, c * width : (c + 1) * width]
    columns = [go(cols_send_ref.at[c], cols_ref.at[col], col=c) for c in (across, cross, core)]
    cols_ref[col] = cols_send_ref[col]
    rest = [go(cols_ref.at[col], cols_other_ref.at[col], dp=y)]

    fac, folded = query_grads(range(0, 4), dq, high, low, bq_ref)
    put_query_grads(folded, 0, turn_ref, d_ref)
    sent_on = win_ref[2].astype(F32) + jnp.where(left, from_low, from_high)
    pl.when(hands_on)(two.wait_recv)
    wsend_ref[0] = jnp.where(hands_on, sent_on + wfar_ref[1].astype(F32), sent_on).astype(BF)
    pl.when(row >= 1)(one.start)

    mixes = [go(part_ref.at[order[k]], mix_got_ref.at[k], row=order[k]) for k in range(3)]

    fac_more, folded = query_grads(range(4, RQ), dq, high, low, bq_ref)
    put_query_grads(folded, 4, turn_ref, d_ref)
    for c, source in zip(columns, (across, cross, core)):
        c.wait_recv()
        rest.append(go(cols_ref.at[source], cols_other_ref.at[source], dp=y))
    d_kf = win_ref[4].astype(F32) + jnp.where(left, from_high, zero)
    pl.when(row <= 2)(one.wait_recv)
    d_kf = jnp.where(row <= 2, d_kf + wfar_ref[0].astype(F32), d_kf)
    put_key_grads(d_kf, fac + fac_more, turn_ref, d_ref)
    d_h = nn(d_ref[...], w_ref[...])
    gains = first_norm_back(d_h, x_ref, gain_ref, d_mixed_ref, gi_ref)
    factor_weight_grads(d_ref, h_ref, gains, g_two_ref, g_ref)

    first = [go(g_ref.at[r, (1 - x) * 2 + 1 - mine], near_ref.at[0, k], col=core) for k, r in enumerate(order)]
    second = [go(g_ref.at[r, x * 2 + 1 - mine], near_ref.at[1, k], col=core) for k, r in enumerate(order)]
    sides = []
    for k, r in enumerate(order):
        first[k].wait_recv()
        pair_ref[k] = (g_ref[r, (1 - x) * 2 + mine].astype(F32) + near_ref[0, k].astype(F32)).astype(BF)
        sides.append(go(pair_ref.at[k], side_ref.at[k], col=across))

    total = part_ref[row].astype(F32)
    for k, c in enumerate(mixes):
        c.wait_recv()
        total = total + mix_got_ref[k].astype(F32)
    mix_ref[...] = total.astype(BF)
    rest.append(go(mix_ref, mix_other_ref, dp=y))
    for c in (across, cross, core):
        rest.append(go(gi_ref.at[c], gi_all_ref.at[col], col=c))
    own = pltpu.make_async_copy(gi_ref.at[col], gi_all_ref.at[col], local_sem.at[0])
    own.start()

    downs = []
    for k, r in enumerate(order):
        second[k].wait_recv()
        sides[k].wait_recv()
        far_ref[k] = (
            g_ref[r, x * 2 + mine].astype(F32) + near_ref[1, k].astype(F32) + side_ref[k].astype(F32)
        ).astype(BF)
        if k < 3:
            downs.append(go(far_ref.at[k], down_ref.at[k], row=r))
    total = far_ref[3].astype(F32)
    for k in range(3):
        downs[k].wait_recv()
        total = total + down_ref[k].astype(F32)
    last_ref[...] = total.astype(BF)
    end = go(last_ref, end_ref, dp=y)
    end.wait_recv()
    grad_ref[...] = last_ref[...].astype(F32) + end_ref[...].astype(F32)
    for c in rest:
        c.wait_recv()
    for c in started:
        c.wait_send()
    pl.when(row >= 1)(one.wait_send)
    pl.when(row >= 2)(two.wait_send)
    own.wait()


def back_tail_body(*refs):
    attend_in, side_in, tail_in = refs[:7], refs[7:12], refs[12:21]
    out_ref, *tail_out = refs[21:28]
    scratch = refs[28:]
    dq_ref, dkf_ref, ends_ref, part_ref = scratch[:4]
    gain_ref, g_two_ref = tail_in[6], tail_in[8]
    q_ref, k_hbm, v_hbm, *attend_rest = attend_in
    pair_in, mixed_hbm, *side_rest = side_in
    *scratch, k_ref, v_ref, mixed_ref, hf_ref, bq_ref, turn_ref, w_ref, h_ref, x_ref, d_mixed_ref = scratch[:-2]
    tile_sem, load_sem = refs[-2:]

    def tile_copies(p):
        lanes = pl.ds(pl.multiple_of(p * LANES, LANES), LANES)
        return [
            pltpu.make_async_copy(source.at[:, lanes], target.at[:, lanes], tile_sem.at[n, p])
            for n, (source, target) in enumerate(((k_hbm, k_ref), (v_hbm, v_ref)))
        ]

    for p in range(PAIRS):
        for c in tile_copies(p):
            c.start()
    sources = (mixed_hbm, *(tail_in[k] for k in (0, 1, 2, 3, 4, 5, 7)))
    targets = (mixed_ref, hf_ref, bq_ref, turn_ref, w_ref, h_ref, x_ref, d_mixed_ref)
    loads = [pltpu.make_async_copy(a, b, load_sem.at[n]) for n, (a, b) in enumerate(zip(sources, targets))]
    for c in loads:
        c.start()

    def load(p):
        for c in tile_copies(p):
            c.wait()
        pl.when(p == 5)(loads[0].wait)

    attend_back_body(
        True, q_ref, k_ref, v_ref, *attend_rest, pair_in, mixed_ref, *side_rest, dq_ref, dkf_ref, out_ref, ends_ref,
        part_ref, *scratch[4:25], load=load,
    )
    for c in loads[1:]:
        c.wait()
    tail_body(
        dkf_ref, dq_ref, hf_ref, bq_ref, turn_ref, w_ref, h_ref, x_ref, gain_ref, d_mixed_ref, g_two_ref,
        side_in[2], ends_ref, part_ref, *tail_out, *scratch[25:],
    )


def back_tail(attend_in, side_in, tail_in):
    kf_window, g_rows, g_out = attend_in[5], side_in[2], side_in[3]
    x_parts = tail_in[5]
    parts, rows, feat = x_parts.shape
    units = g_rows.shape[2]
    block = (RANK_COLS // 4 + GROUP_COLS, feat)
    cols = (parts, 3, units, feat)
    mix = g_out.shape[2:]
    wide = g_rows.shape[1:]
    slot = kf_window.shape[1:]
    count = 2 + 2 + 3 + 8 + 4 + 3 + 1 + 1 + 3 + 3 + 3 + 1
    return pl.pallas_call(
        back_tail_body,
        out_shape=(
            jax.ShapeDtypeStruct(x_parts.shape, BF),
            jax.ShapeDtypeStruct(block, F32),
            jax.ShapeDtypeStruct(x_parts.shape, BF),
            jax.ShapeDtypeStruct(cols, BF),
            jax.ShapeDtypeStruct(cols, BF),
            jax.ShapeDtypeStruct(mix, BF),
            jax.ShapeDtypeStruct(mix, BF),
        ),
        in_specs=[VMEM, ANY, ANY] + [VMEM] * 4 + [ANY] * 4 + [VMEM] + [ANY] * 6 + [VMEM, ANY, VMEM],
        out_specs=(ANY, VMEM, ANY, VMEM, ANY, VMEM, ANY),
        scratch_shapes=[
            pltpu.VMEM((rows, D), F32),
            pltpu.VMEM(kf_window.shape, BF),
            pltpu.VMEM((2,) + wide, BF),
            pltpu.VMEM((4,) + mix, BF),
        ]
        + back_scratch(rows, 5 * rows)
        + [
            pltpu.VMEM((2, rows // 2, D), BF),
            pltpu.VMEM((2, rows // 2, D), BF),
            pltpu.VMEM((2, rows, D), BF),
            pltpu.VMEM((parts, rows, feat), BF),
            pltpu.VMEM((2,) + wide, BF),
            pltpu.VMEM((2,) + wide, BF),
            pltpu.VMEM((2,) + wide, BF),
            pltpu.VMEM((2, 4) + mix, BF),
            pltpu.VMEM((4,) + mix, BF),
            pltpu.VMEM((4,) + mix, BF),
            pltpu.VMEM((2, rows // 2, D), BF),
            pltpu.VMEM((rows, D), BF),
            pltpu.VMEM(g_rows.shape, BF),
            pltpu.VMEM((2, 4) + mix, BF),
            pltpu.SemaphoreType.DMA((25,)),
            pltpu.SemaphoreType.DMA((25,)),
            pltpu.SemaphoreType.DMA((13,)),
        ]
        + [
            pltpu.VMEM((rows, ALL_COLS), BF),
            pltpu.VMEM(x_parts.shape, BF),
            pltpu.VMEM((2,) + slot, BF),
            pltpu.VMEM((2,) + slot, BF),
            pltpu.VMEM((2,) + slot, BF),
            pltpu.VMEM(wide, BF),
            pltpu.VMEM(cols, BF),
            pltpu.VMEM((3,) + mix, BF),
            pltpu.VMEM((4, parts) + block, BF),
            pltpu.VMEM((2, 4) + block, BF),
            pltpu.VMEM((4,) + block, BF),
            pltpu.VMEM((4,) + block, BF),
            pltpu.VMEM((4,) + block, BF),
            pltpu.VMEM((3,) + block, BF),
            pltpu.VMEM(block, BF),
            pltpu.VMEM(block, BF),
            pltpu.SemaphoreType.DMA((count,)),
            pltpu.SemaphoreType.DMA((count,)),
            pltpu.SemaphoreType.DMA((2,)),
        ]
        + [
            pltpu.VMEM(a.shape, a.dtype)
            for a in (attend_in[1], attend_in[2], side_in[1], *(tail_in[k] for k in (0, 1, 2, 3, 4, 5, 7)))
        ]
        + [pltpu.SemaphoreType.DMA((2, PAIRS)), pltpu.SemaphoreType.DMA((8,))],
        compiler_params=comm_params(7),
        cost_estimate=cost_of(2 * rows * 5 * rows * D * 40, 40 << 20),
    )(*attend_in, *side_in, *tail_in)


def layout_body(
    grad_ref, gi_ref, cols_ref, other_ref, mix_ref, mix_other_ref, y_ref,
    y_out_ref, gi_out_ref, gain_ref, gain_two_ref, heads_ref, ranks_ref, out_ref, gate_ref, up_ref, down_ref,
):
    first = lax.axis_index("dp") == 0
    y_out_ref[...] = y_ref[...]
    gi_out_ref[...] = gi_ref[...].astype(F32)
    out_ref[...] = mix_ref[...].astype(F32) + mix_other_ref[...].astype(F32)
    ranks = ranks_ref.shape[0]
    used = heads_ref.shape[0]
    gain_ref[...] = grad_ref[ranks + used : ranks + used + 1]
    gain_two_ref[...] = grad_ref[ranks + used + 1 : ranks + used + 2]
    ranks_ref[...] = grad_ref[:ranks]
    lane = lax.broadcasted_iota(jnp.int32, (used, GROUP_COLS), 1)
    place = lax.broadcasted_iota(jnp.int32, (used, GROUP_COLS), 0)
    factor = place % FAC
    spot = jnp.where(factor < RQ, factor + 2 * RK, factor - RQ) * GROUP + place // FAC
    heads_ref[...] = jnp.dot(
        (lane == spot).astype(F32), grad_ref[ranks:], precision=lax.Precision.HIGHEST, preferred_element_type=F32
    )
    part = down_ref.shape[0] // 8
    for k, target in ((0, gate_ref), (1, up_ref), (2, down_ref)):
        for c in range(4):
            own = cols_ref[c, k].astype(F32)[:part]
            other = other_ref[c, k].astype(F32)[:part]
            target[c * part : (c + 1) * part] = jnp.where(first, own, other)
            target[(4 + c) * part : (5 + c) * part] = jnp.where(first, other, own)


def layout(grad, gi, cols, other, mix, mix_other, y, heads, ranks, hidden):
    feat = grad.shape[1]
    weight = jax.ShapeDtypeStruct((hidden, feat), F32)
    gain = jax.ShapeDtypeStruct((1, feat), F32)
    return call(
        layout_body,
        (
            jax.ShapeDtypeStruct(y.shape, y.dtype),
            jax.ShapeDtypeStruct(gi.shape, F32),
            gain,
            gain,
            jax.ShapeDtypeStruct((heads, feat), F32),
            jax.ShapeDtypeStruct((ranks, feat), F32),
            jax.ShapeDtypeStruct(mix.shape, F32),
            weight,
            weight,
            weight,
        ),
        cost=cost_of(0, 8 << 20),
    )(grad, gi, cols, other, mix, mix_other, y)


def local(
    tokens_in, segments, gain_attn, gain_ffn, w_heads, w_ranks, w_out, w_gate, w_up, w_down, cotangent
):
    n_row = lax.axis_size("row")
    n_col = lax.axis_size("col")
    row = lax.axis_index("row")
    col = lax.axis_index("col")
    micro, row_tokens, feat = tokens_in.shape
    subs = n_col // micro
    rows = row_tokens // subs
    length = row_tokens * n_row
    head_local = w_heads.shape[1] // FAC
    rank_local = w_ranks.shape[1]
    ffn_local = w_gate.shape[1]
    out_local = w_out.shape[0]
    block = row * subs + col % subs
    past = min(-(-(MAX_DOC - 1) // rows), n_row * subs - 1)
    keys = (past + 1) * rows

    dp_count = lax.axis_size("dp")
    fast = n_col == 4 and n_row == 4 and dp_count == 2 and micro == 2 and past == 4

    tokens = tokens_in.reshape(n_col, rows, feat)
    turns = (ROPE ** (-(np.arange(HD // 2) * 2.0 / HD))).astype(np.float32)
    if not fast:
        inverse = ROPE ** (-(jnp.arange(HD // 2, dtype=F32) * 2.0 / HD))
        heads_t = jnp.transpose(w_heads.reshape(feat, head_local, FAC), (2, 1, 0))
        heads_t = heads_t[jnp.array(FAC_ORDER)].reshape(FAC * head_local, feat)
        pad = jnp.zeros((GROUP_COLS - FAC * head_local, feat), BF)
        w_own = jnp.concatenate([w_ranks.T, heads_t, pad], axis=0)
        gains_own = jnp.concatenate([gain_attn[None], gain_ffn[None], jnp.zeros((6, feat), F32)], axis=0)
        part = ffn_local // n_col
        units = part * n_row
        w_ffn = jnp.stack([w_gate.T, w_up.T, w_down]).reshape(3, n_col, part, feat)
        w_ffn = lax.all_to_all(jnp.transpose(w_ffn, (1, 0, 2, 3)), "col", 0, 0, tiled=True)
        w_ffn = jnp.transpose(w_ffn, (1, 2, 0, 3)).reshape(3, part, D)
        w_ffn = jnp.transpose(lax.all_gather(w_ffn, "row", axis=0), (1, 0, 2, 3)).reshape(3, units, D)
        w_blocks = lax.all_gather(w_own, ("row", "col"), axis=0).reshape((n_row, n_col) + w_own.shape)
        gains = lax.all_gather(gains_own, "col", axis=0)
        x_parts = lax.all_to_all(tokens, "col", 0, 0, tiled=True)
        w_out_all = lax.all_gather(w_out, ("row", "col"), axis=0).reshape((n_row, n_col) + w_out.shape)

        seg_row = lax.dynamic_index_in_dim(segments, col // subs, 0, keepdims=False)
        padded = jnp.concatenate([jnp.full((1, past * rows), -1, jnp.int32), seg_row], axis=1)
        seg_window = lax.dynamic_slice_in_dim(padded, block * rows, keys, 1)
        own_seg = seg_window[0, past * rows :]
        key_idx = jnp.arange(keys, dtype=jnp.int32)
        query_idx = jnp.arange(rows, dtype=jnp.int32) + past * rows
        before = (own_seg[:, None] == seg_window) & (key_idx[None, :] < query_idx[:, None])
        places = jnp.sum(before.astype(jnp.int32), axis=1)
        angles = places.astype(F32)[:, None] * inverse[None, :]
        cosine = jnp.cos(angles)
        sine = jnp.sin(angles)
        turn = jnp.concatenate([cosine] * 4 + [-sine, sine, -sine, sine], axis=1)

    groups = [[m * subs + s for s in range(subs)] for m in range(micro)]
    if fast:
        cot_rows = cotangent.reshape(micro * row_tokens, feat)
        (
            x_parts, gains, ffn_parts, mixes, h_one, head_fac, bq_rot, queries, w_rh, kf_window, seg_window, turn, w_rows,
            heads_out, lse, key_all, value_all, cot_near,
        ) = head_attend(
            tokens, w_ranks.T, w_heads.T, gain_attn.reshape(1, feat), gain_ffn.reshape(1, feat), w_gate.T, w_up.T,
            w_down, w_out, segments, np.tile(turns, 4).reshape(1, LANES), cot_rows,
        )
        mixed, d_mixed, d_heads, g_out, g_gain_two, g_rows, out_pair, hop = middle(
            x_parts, heads_out, mixes, gains, cot_rows, cot_near, ffn_parts, w_rows
        )
        output, g_rh, grad_input, g_cols, cols_other, g_out, out_other = back_tail(
            (queries, key_all, value_all, d_heads, lse, kf_window, seg_window),
            (out_pair, mixed, g_rows, g_out, hop),
            (head_fac, bq_rot, turn, w_rh, h_one, x_parts, gains, d_mixed, g_gain_two),
        )
        output, grad_input, g_one, g_two, own_heads, own_ranks, g_out, own_gate, own_up, own_down = layout(
            g_rh, grad_input, g_cols, cols_other, g_out, out_other, output, w_heads.shape[1], w_ranks.shape[1], ffn_local
        )
        return (
            output.reshape(tokens_in.shape),
            grad_input.reshape(tokens_in.shape),
            g_one.reshape(feat),
            g_two.reshape(feat),
            own_heads.T,
            own_ranks.T,
            g_out,
            own_gate.T,
            own_up.T,
            own_down,
        )
    else:
        h_one, head_fac, bq_rot, key_fac, queries, w_rh = front(x_parts, gains, w_blocks, turn)
        gathered = lax.all_gather(key_fac, "row", axis=0)
        gathered = lax.all_gather(gathered, "col", axis=1, axis_index_groups=groups)
        gathered = gathered.reshape(length, key_fac.shape[1])
        padded_kf = jnp.concatenate([jnp.zeros((past * rows, key_fac.shape[1]), BF), gathered], axis=0)
        kf_window = lax.dynamic_slice_in_dim(padded_kf, block * rows, keys, 0)
        heads_out, lse, key_all, value_all = attend(queries, kf_window, seg_window)
        mixed, h_two = mixing(x_parts, heads_out, w_out_all, gains)
        cot_own = lax.all_to_all(cotangent.reshape(n_col, rows, feat), "col", 0, 0, tiled=True)
        cot_own = jnp.transpose(cot_own, (1, 0, 2)).reshape(rows, D)
        cot_all = lax.all_gather(cot_own, "col", axis=0)
        h_all = lax.all_gather(h_two, "col", axis=0)
        out_part, dh_part, g_ffn = ffn(h_all, cot_all, w_ffn)
        dh_sum = lax.psum_scatter(dh_part, "col", scatter_dimension=0, tiled=False).astype(F32)
        out_sum = lax.psum_scatter(out_part, "col", scatter_dimension=0, tiled=False).astype(F32)
        out_parts, d_mixed, d_heads, g_out, g_gain_two = unmix(
            dh_sum, out_sum, mixed, cot_own, heads_out, w_out_all, gains
        )
        d_q, d_kf = attend_back(queries, key_all, value_all, d_heads, lse, kf_window, seg_window)
        spread_kf = jnp.zeros((past * rows + length, d_kf.shape[1]), BF)
        spread_kf = lax.dynamic_update_slice_in_dim(spread_kf, d_kf, block * rows, 0)[past * rows :]
        spread_kf = spread_kf.reshape(n_row, subs, rows, -1)
        own_kf = lax.psum_scatter(spread_kf, "row", scatter_dimension=0, tiled=False)
        own_kf = lax.psum_scatter(own_kf, "col", scatter_dimension=0, tiled=False, axis_index_groups=groups)
        gi_parts, g_rh = back(
            d_q, own_kf, head_fac, bq_rot, turn, w_rh, h_one, x_parts, gains, d_mixed, g_gain_two, n_row
        )
        output = lax.all_to_all(out_parts, "col", 0, 0, tiled=True)
        grad_input = lax.all_to_all(gi_parts, "col", 0, 0, tiled=True)
        g_ffn = lax.psum_scatter(g_ffn.reshape(3, n_row, part, D), "row", scatter_dimension=1, tiled=False)
        g_ffn = jnp.transpose(lax.psum(g_ffn, "dp").reshape(3, part, n_col, feat), (2, 0, 1, 3))
        g_ffn = lax.all_to_all(g_ffn, "col", 0, 0, tiled=True)
        g_ffn = jnp.transpose(g_ffn, (1, 0, 2, 3)).reshape(3, ffn_local, feat).astype(F32)

        def total(values):
            values = values.reshape((n_row * n_col,) + values.shape[2:])
            values = lax.psum_scatter(values, ("row", "col"), scatter_dimension=0, tiled=False)
            return lax.psum(values, "dp").astype(F32)

        g_out = total(g_out)
        g_rh = total(g_rh)

    used = rank_local + FAC * head_local
    own_heads = g_rh[rank_local:used].reshape(FAC, head_local, feat)
    own_heads = jnp.transpose(own_heads[jnp.array(FAC_BACK)], (2, 1, 0)).reshape(w_heads.shape)
    return (
        output.reshape(tokens_in.shape),
        grad_input.reshape(tokens_in.shape),
        g_rh[used],
        g_rh[used + 1],
        own_heads,
        g_rh[:rank_local].T,
        g_out,
        g_ffn[0].T,
        g_ffn[1].T,
        g_ffn[2],
    )


def solution(mesh):
    tokens = P(None, ("dp", "row"), "col")
    both = P("col", "row")
    turned = P("row", "col")
    gain = P("col")
    return jax.shard_map(
        local,
        mesh=mesh,
        in_specs=(tokens, P(None, "dp", None), gain, gain, both, both, turned, both, both, turned, tokens),
        out_specs=(tokens, tokens, gain, gain, both, both, turned, both, both, turned),
        check_vma=False,
    )
```

```python
import functools

import jax
import jax.numpy as jnp
import numpy as np
from jax import lax
from jax.experimental import pallas as pl
from jax.experimental.pallas import tpu as pltpu
from jax.sharding import PartitionSpec as P

D = 1024
H = 16
HD = 64
RQ = 6
RK = 2
FAC = 10
MAX_DOC = 1024

EPS = 1e-06
ROPE = 10000.0
NEG = -1e30
BF = jnp.bfloat16
F32 = jnp.float32
LANES = 128
PAIRS = H // 2
FAC_ORDER = (6, 7, 8, 9, 0, 1, 2, 3, 4, 5)
FAC_BACK = (4, 5, 6, 7, 8, 9, 0, 1, 2, 3)
VMEM = pl.BlockSpec(memory_space=pltpu.VMEM)


def nn(a, b):
    return jnp.dot(a, b, preferred_element_type=F32)


def nt(a, b):
    return lax.dot_general(a, b, (((1,), (1,)), ((), ())), preferred_element_type=F32)


def tn(a, b):
    return lax.dot_general(a, b, (((0,), (0,)), ((), ())), preferred_element_type=F32)


def two_pass(a, b):
    high = a.astype(BF)
    low = (a - high.astype(F32)).astype(BF)
    return nn(high, b) + nn(low, b)


def lane_iota(shape):
    return lax.broadcasted_iota(jnp.int32, shape, len(shape) - 1)


def spread(rows, first, width):
    row = lax.broadcasted_iota(jnp.int32, (rows, width), 0)
    head = lax.broadcasted_iota(jnp.int32, (rows, width), 1) // HD
    return (row == head + first).astype(F32).astype(BF)


def collect(rows, width, first):
    head = lax.broadcasted_iota(jnp.int32, (rows, width), 0) // HD
    lane = lax.broadcasted_iota(jnp.int32, (rows, width), 1)
    return (lane == head + first).astype(F32).astype(BF)


GROUP = 4
GROUP_COLS = 48
RANK_COLS = FAC * HD
HEAD_COLS = H // GROUP * GROUP_COLS
ALL_COLS = RANK_COLS + HEAD_COLS


def factor_place(head, j):
    return head // GROUP * GROUP_COLS + j * GROUP + head % GROUP


def head_spread(j, first_head, width):
    row = lax.broadcasted_iota(jnp.int32, (HEAD_COLS, width), 0)
    head = lax.broadcasted_iota(jnp.int32, (HEAD_COLS, width), 1) // HD + first_head
    return (row == factor_place(head, j)).astype(F32).astype(BF)


def head_collect(j):
    head = lax.broadcasted_iota(jnp.int32, (D, HEAD_COLS), 0) // HD
    lane = lax.broadcasted_iota(jnp.int32, (D, HEAD_COLS), 1)
    return (lane == factor_place(head, j)).astype(F32).astype(BF)


def key_columns():
    row = lax.broadcasted_iota(jnp.int32, (HEAD_COLS, LANES), 0)
    lane = lax.broadcasted_iota(jnp.int32, (HEAD_COLS, LANES), 1)
    taken = (row == factor_place(lane % H, lane // H)) & (lane < 2 * RK * H)
    return taken.astype(F32).astype(BF)


def swap_halves(tile):
    lane = lane_iota(tile.shape)
    ahead = pltpu.roll(tile, LANES - HD // 2, 1)
    behind = pltpu.roll(tile, HD // 2, 1)
    return jnp.where(lane % HD < HD // 2, ahead, behind)


def double_left(tile):
    return jnp.where(lane_iota(tile.shape) < HD, tile, pltpu.roll(tile, HD, 1))


def double_right(tile):
    return jnp.where(lane_iota(tile.shape) < HD, pltpu.roll(tile, HD, 1), tile)


def params(**more):
    return pltpu.CompilerParams(vmem_limit_bytes=60 << 20, **more)


def call(body, outs, scratch=(), cost=None):
    return pl.pallas_call(
        body,
        out_shape=outs,
        scratch_shapes=scratch,
        compiler_params=params(),
        cost_estimate=cost,
    )


def cost_of(flops, moved):
    return pl.CostEstimate(flops=int(flops), bytes_accessed=int(moved), transcendentals=0)


MESH = pl.DeviceIdType.MESH
ANY = pl.BlockSpec(memory_space=pl.ANY)


class Mover:
    def __init__(self, send_sem, recv_sem):
        self.send_sem = send_sem
        self.recv_sem = recv_sem
        self.used = 0

    def copy(self, source, target, **place):
        index = self.used
        self.used += 1
        return pltpu.make_async_remote_copy(
            src_ref=source,
            dst_ref=target,
            send_sem=self.send_sem.at[index],
            recv_sem=self.recv_sem.at[index],
            device_id=place,
            device_id_type=MESH,
        )


def greet(partners):
    barrier = pltpu.get_barrier_semaphore()
    count = 0
    for present, place in partners:
        if present is None:
            pl.semaphore_signal(barrier, inc=1, device_id=place, device_id_type=MESH)
            count = count + 1
        else:

            @pl.when(present)
            def _():
                pl.semaphore_signal(barrier, inc=1, device_id=place, device_id_type=MESH)

            count = count + present.astype(jnp.int32)
    pl.semaphore_wait(barrier, count)


def neighbours():
    col = lax.axis_index("col")
    core = col + 1 - 2 * lax.rem(col, 2)
    across = lax.rem(col + 2, 4)
    return col, core, across


def square():
    dp = lax.axis_index("dp")
    x = lax.axis_index("col") // 2
    return dp, (dp * 2 + x, dp * 2 + 1 - x, (1 - dp) * 2 + x, (1 - dp) * 2 + 1 - x)


def comm_params(ident):
    return params(collective_id=ident, has_side_effects=True)


class AttendCopies:
    def __init__(self, cot_ref, rows_ref, near_ref, mixes_ref, send_sem, recv_sem):
        row = lax.axis_index("row")
        col, core, across = neighbours()
        dp, (me, on_x, on_y, _) = square()
        mover = Mover(send_sem, recv_sem)
        self.left = row >= 1
        self.right = row <= 2
        self.both = jnp.logical_and(self.left, self.right)
        self.from_left = row >= 2
        self.from_right = row <= 1
        self.row = row
        cuts = [pl.ds(0, 2), pl.ds(2, 2)]
        lower, upper = rows_ref.at[jnp.maximum(row - 1, 0)], rows_ref.at[jnp.minimum(row + 1, 3)]
        self.pass_right = [mover.copy(lower.at[c], lower.at[c], row=row + 1) for c in cuts]
        self.pass_left = [mover.copy(upper.at[c], upper.at[c], row=row - 1) for c in cuts]
        self.last_right = [mover.copy(rows_ref.at[0, c], rows_ref.at[0, c], row=row + 1) for c in cuts]
        self.last_left = [mover.copy(rows_ref.at[3, c], rows_ref.at[3, c], row=row - 1) for c in cuts]
        half = cot_ref.shape[0] // 2
        top, low = pl.ds(0, half), pl.ds(half, half)
        self.cots = [
            mover.copy(cot_ref.at[low], near_ref.at[me, low], col=across),
            mover.copy(cot_ref.at[top], near_ref.at[me, top], dp=1 - dp),
            mover.copy(cot_ref.at[top], near_ref.at[me, top], col=across),
            mover.copy(cot_ref.at[low], near_ref.at[me, low], dp=1 - dp),
        ]
        self.relays = [
            mover.copy(near_ref.at[on_x, low], near_ref.at[on_x, low], dp=1 - dp),
            mover.copy(near_ref.at[on_y, top], near_ref.at[on_y, top], col=across),
        ]
        self.mixes = []
        for r in range(4):
            for c in (col, across):
                self.mixes.append(mover.copy(mixes_ref.at[r, c], mixes_ref.at[r, c], col=core))

    def first(self):
        for k in range(2):
            pl.when(self.both)(self.pass_right[k].start)
            pl.when(self.both)(self.pass_left[k].start)
        for c in self.cots:
            c.start()

    def early(self):
        self.head_end()
        for c in self.mixes:
            c.start()
        self.hand_on(0)

    def hand_on(self, k):
        pl.when(self.from_left)(self.pass_right[k].wait_recv)
        pl.when(self.from_right)(self.pass_left[k].wait_recv)
        pl.when(self.row == 2)(self.last_right[k].start)
        pl.when(self.row == 1)(self.last_left[k].start)

    def second(self):
        for c in self.cots[:2]:
            c.wait_recv()
        for c in self.relays:
            c.start()
        self.hand_on(1)

    def last(self):
        for k in range(2):
            pl.when(self.both)(self.pass_right[k].wait_send)
            pl.when(self.both)(self.pass_left[k].wait_send)
            pl.when(self.row == 2)(self.last_right[k].wait_send)
            pl.when(self.row == 1)(self.last_left[k].wait_send)
            pl.when(self.row == 3)(self.last_right[k].wait_recv)
            pl.when(self.row == 0)(self.last_left[k].wait_recv)
        for c in self.cots[:2]:
            c.wait_send()
        for c in self.cots[2:] + self.relays + self.mixes:
            c.wait()


class BackCopies:
    def __init__(self, refs, sems):
        (
            self.pair_ref, self.mixed_ref, self.rows_ref, self.g_out_ref, self.hop_ref,
            self.out_ref, self.ends_ref, self.part_ref,
            self.relay_ref, self.diag_ref, self.far_ref, self.send_ref,
            self.right_ref, self.left_ref, self.got_ref,
            self.near_ref, self.side_ref, self.across_ref,
            self.pieces_ref, self.mine_ref, self.rows_in_ref, self.g_in_ref,
        ) = refs
        send_sem, recv_sem, local_sem = sems
        self.row = row = lax.axis_index("row")
        self.col, core, across = col, _, _ = neighbours()
        cross = lax.rem(core + 2, 4)
        self.dp, self.spots = dp, (me, on_x, on_y, on_both) = square()
        mover = Mover(send_sem, recv_sem)
        self.x, self.mine = x, mine = col // 2, lax.rem(col, 2)
        self.partners = [(None, {"col": c}) for c in (core, across, cross)]
        self.partners += [(None, {"dp": 1 - dp})] + [(None, {"row": lax.rem(row + k, 4)}) for k in range(1, 4)]
        half = self.pair_ref.shape[1] // 2
        top, low = pl.ds(0, half), pl.ds(half, half)
        y = 1 - dp
        self.diag = [
            mover.copy(self.pair_ref.at[on_both, top], self.diag_ref.at[0], col=across),
            mover.copy(self.pair_ref.at[on_both, low], self.diag_ref.at[1], dp=y),
        ]
        self.far = [
            mover.copy(self.pair_ref.at[on_x, top], self.far_ref.at[0, top], col=across),
            mover.copy(self.pair_ref.at[on_y, low], self.far_ref.at[1, low], dp=y),
            mover.copy(self.relay_ref.at[0], self.far_ref.at[1, top], dp=y),
            mover.copy(self.relay_ref.at[1], self.far_ref.at[0, low], col=across),
        ]
        self.out = [mover.copy(self.send_ref.at[c], self.out_ref.at[col], col=c) for c in (across, cross, core)]
        self.own = pltpu.make_async_copy(self.send_ref.at[col], self.out_ref.at[col], local_sem.at[0])
        self.hop_right = [
            mover.copy(self.right_ref.at[0], self.got_ref.at[0], row=row + 1),
            mover.copy(self.right_ref.at[1], self.ends_ref.at[0], row=row + 1),
        ]
        self.hop_left = [
            mover.copy(self.left_ref.at[0], self.got_ref.at[1], row=row - 1),
            mover.copy(self.left_ref.at[1], self.ends_ref.at[1], row=row - 1),
        ]
        self.cores = [
            mover.copy(self.g_out_ref.at[r, k * 2 + 1 - mine], self.near_ref.at[k, r], col=core)
            for k in range(2)
            for r in range(4)
        ]
        self.sides = [mover.copy(self.side_ref.at[r], self.across_ref.at[r], col=across) for r in range(4)]
        self.loads = [
            pltpu.make_async_copy(self.pair_ref.at[on_y, top], self.pieces_ref.at[0], local_sem.at[1]),
            pltpu.make_async_copy(self.pair_ref.at[on_x, low], self.pieces_ref.at[1], local_sem.at[2]),
            pltpu.make_async_copy(self.pair_ref.at[me], self.mine_ref, local_sem.at[3]),
        ]
        self.rows_load = pltpu.make_async_copy(self.rows_ref, self.rows_in_ref, local_sem.at[4])
        self.g_loads = [
            pltpu.make_async_copy(
                self.g_out_ref.at[r, lax.rem(x + k, 2) * 2 + mine], self.g_in_ref.at[k, r], local_sem.at[5 + 4 * k + r]
            )
            for k in range(2)
            for r in range(4)
        ]

    def first(self):
        row = self.row
        self.rows_load.start()
        for c in self.loads + self.g_loads:
            c.start()
        greet(self.partners)
        for c in self.diag + self.far[:2] + self.cores:
            c.start()
        self.rows_load.wait()
        hop = self.hop_ref[...].astype(F32)
        ahead = self.rows_in_ref[jnp.minimum(row + 2, 3)].astype(F32)
        self.right_ref[0] = jnp.where(row == 1, ahead + hop, ahead).astype(BF)
        behind = self.rows_in_ref[jnp.maximum(row - 2, 0)].astype(F32)
        self.left_ref[0] = jnp.where(row == 2, behind + hop, behind).astype(BF)
        pl.when(row <= 1)(self.hop_right[0].start)
        pl.when(row >= 2)(self.hop_left[0].start)

    def cross_x(self):
        for c in self.g_loads:
            c.wait()
        for c in self.cores:
            c.wait_recv()
        for r in range(4):
            self.side_ref[r] = (
                self.g_in_ref[1, r].astype(F32) + self.near_ref[1 - self.x, r].astype(F32)
            ).astype(BF)
            self.sides[r].start()

    def second(self):
        row = self.row
        for c in self.loads:
            c.wait()
        for k in range(2):
            self.diag[k].wait_recv()
            self.relay_ref[k] = (self.pieces_ref[k].astype(F32) + self.diag_ref[k].astype(F32)).astype(BF)
            self.far[2 + k].start()

    def last_hop(self):
        row = self.row
        middle = jnp.logical_and(row >= 1, row <= 2)
        pl.when(middle)(self.hop_right[0].wait_recv)
        pl.when(middle)(self.hop_left[0].wait_recv)
        ahead = self.rows_in_ref[jnp.minimum(row + 1, 3)].astype(F32)
        behind = self.rows_in_ref[jnp.maximum(row - 1, 0)].astype(F32)
        self.right_ref[1] = jnp.where(row >= 1, ahead + self.got_ref[0].astype(F32), ahead).astype(BF)
        self.left_ref[1] = jnp.where(row <= 2, behind + self.got_ref[1].astype(F32), behind).astype(BF)
        pl.when(row <= 2)(self.hop_right[1].start)
        pl.when(row >= 1)(self.hop_left[1].start)

    def third(self):
        row = self.row
        for c in self.far:
            c.wait_recv()
        feat = self.send_ref.shape[2]
        for c in range(4):
            lanes = slice(c * feat, (c + 1) * feat)
            self.send_ref[c] = (
                self.mixed_ref[:, lanes]
                + self.mine_ref[:, lanes].astype(F32)
                + self.far_ref[0, :, lanes].astype(F32)
                + self.far_ref[1, :, lanes].astype(F32)
            ).astype(BF)
        for c in self.out:
            c.start()
        self.own.start()

    def last(self):
        row = self.row
        for r in range(4):
            self.sides[r].wait_recv()
            self.part_ref[r] = (
                self.g_in_ref[0, r].astype(F32)
                + self.near_ref[self.x, r].astype(F32)
                + self.across_ref[r].astype(F32)
            ).astype(BF)
        for c in self.out:
            c.wait()
        self.own.wait()
        for c in self.diag + self.far + self.cores + self.sides:
            c.wait_send()
        pl.when(row <= 1)(self.hop_right[0].wait_send)
        pl.when(row >= 2)(self.hop_left[0].wait_send)
        pl.when(row <= 2)(self.hop_right[1].wait_send)
        pl.when(row >= 1)(self.hop_left[1].wait_send)
        pl.when(row >= 1)(self.hop_right[1].wait_recv)
        pl.when(row <= 2)(self.hop_left[1].wait_recv)


def first_norm(x_ref, gain_ref, h_ref):
    parts = x_ref.shape[0]
    feat = x_ref.shape[2]
    xs = [x_ref[c].astype(F32) for c in range(parts)]
    total = sum(jnp.sum(v * v, axis=1, keepdims=True) for v in xs)
    scale = lax.rsqrt(total / D + EPS)
    for c in range(parts):
        lanes = slice(c * feat, (c + 1) * feat)
        h_ref[:, lanes] = (xs[c] * scale * gain_ref[c, :1]).astype(BF)


def place_factor_weights(blocks_ref, w_ref):
    n_row, parts, _, feat = blocks_ref.shape
    ranks_each = RANK_COLS // n_row
    for c in range(parts):
        lanes = slice(c * feat, (c + 1) * feat)
        for r in range(n_row):
            w_ref[r * ranks_each : (r + 1) * ranks_each, lanes] = blocks_ref[r, c, :ranks_each]
            w_ref[RANK_COLS + r * GROUP_COLS : RANK_COLS + (r + 1) * GROUP_COLS, lanes] = blocks_ref[
                r, c, ranks_each:
            ]


def make_factors(h_ref, w_ref, turn_ref, hf_ref, bq_ref, kf_ref):
    both = nt(h_ref[...], w_ref[...])
    heads = both[:, RANK_COLS:]
    hf_ref[...] = heads
    cosine = turn_ref[:, :LANES]
    sine = turn_ref[:, LANES:]
    for tile in range(RANK_COLS // LANES):
        lanes = slice(tile * LANES, (tile + 1) * LANES)
        part = both[:, lanes]
        if tile < 4:
            part = part * cosine + swap_halves(part) * sine
        if tile < 3:
            bq_ref[:, lanes] = part
        else:
            kf_ref[:, (tile - 3) * LANES : (tile - 2) * LANES] = part.astype(BF)
    kf_ref[:, 2 * LANES :] = nn(heads.astype(BF), key_columns()).astype(BF)


def make_queries(hf_ref, bq_ref, q_ref):
    heads = hf_ref[...]
    high = heads.astype(BF)
    low = (heads - high.astype(F32)).astype(BF)
    ranks = []
    for r in range(RQ):
        tile = bq_ref[:, (r // 2) * LANES : (r // 2 + 1) * LANES]
        ranks.append(double_left(tile) if r % 2 == 0 else double_right(tile))
    width = 2 * LANES
    for p in range(D // width):
        lanes = slice(p * width, (p + 1) * width)
        acc = None
        for r in range(RQ):
            pick = head_spread(2 * RK + r, p * (width // HD), width)
            term = (nn(high, pick) + nn(low, pick)) * jnp.concatenate([ranks[r]] * 2, axis=1)
            acc = term if acc is None else acc + term
        q_ref[:, lanes] = (acc / RQ).astype(BF)


def front_body(x_ref, gain_ref, blocks_ref, turn_ref, h_ref, hf_ref, bq_ref, kf_ref, q_ref, w_ref):
    first_norm(x_ref, gain_ref, h_ref)
    place_factor_weights(blocks_ref, w_ref)
    make_factors(h_ref, w_ref, turn_ref, hf_ref, bq_ref, kf_ref)
    make_queries(hf_ref, bq_ref, q_ref)


def front(x_parts, gains, blocks, turn):
    rows = x_parts.shape[1]
    return call(
        front_body,
        (
            jax.ShapeDtypeStruct((rows, D), BF),
            jax.ShapeDtypeStruct((rows, HEAD_COLS), F32),
            jax.ShapeDtypeStruct((rows, RQ * HD), F32),
            jax.ShapeDtypeStruct((rows, 3 * LANES), BF),
            jax.ShapeDtypeStruct((rows, D), BF),
            jax.ShapeDtypeStruct((ALL_COLS, D), BF),
        ),
        cost=cost_of(2 * rows * D * 800 * 3, 6 << 20),
    )(x_parts, gains, blocks, turn)


def head_body(
    tok_ref, ranks_ref, heads_ref, gain_one_ref, gain_two_ref, gate_ref, up_ref, down_ref, mix_ref, seg_all_ref,
    inverse_ref,
    x_ref, gains_ref, parts_ref, mixes_ref, h_ref, hf_ref, bq_ref, q_ref, w_ref, win_ref, seg_ref, turn_ref, rows_ref,
    w_own_ref, gain_ref, ffn_ref, blocks_ref, send_sem, recv_sem, next_copies,
):
    row = lax.axis_index("row")
    col, core, across = neighbours()
    cross = lax.rem(core + 2, 4)
    side = lax.rem(col, 2)
    rows = [lax.rem(row + k, 4) for k in range(4)]
    back = [lax.rem(row + 4 - k, 4) for k in range(4)]
    dp = lax.axis_index("dp")

    rank_rows = ranks_ref.shape[0]
    place = lax.broadcasted_iota(jnp.int32, (GROUP_COLS, FAC * GROUP), 0)
    lane = lax.broadcasted_iota(jnp.int32, (GROUP_COLS, FAC * GROUP), 1)
    factor = lane % FAC
    spot = jnp.where(factor < RQ, factor + 2 * RK, factor - RQ) * GROUP + lane // FAC
    w_own_ref[:rank_rows] = ranks_ref[...]
    w_own_ref[rank_rows:] = nn((place == spot).astype(F32).astype(BF), heads_ref[...]).astype(BF)
    gain_ref[...] = jnp.zeros_like(gain_ref)
    gain_ref[0:1] = gain_one_ref[...]
    gain_ref[1:2] = gain_two_ref[...]
    greet(
        [(None, {"col": c}) for c in (core, across, cross)]
        + [(None, {"row": r}) for r in rows[1:]]
        + [(None, {"dp": 1 - dp})]
    )
    mover = Mover(send_sem, recv_sem)
    started = []

    def go(source, target, **place):
        c = mover.copy(source, target, **place)
        c.start()
        started.append(c)
        return c

    down = [None] + [go(w_own_ref, blocks_ref.at[row, col], row=rows[k]) for k in range(1, 4)]
    sides = [go(w_own_ref, blocks_ref.at[row, col], col=across)]
    cores = [go(w_own_ref, blocks_ref.at[row, col], col=core)]
    toks = []
    rest = []
    for c in (across, cross, core):
        toks.append(go(gain_ref, gains_ref.at[col], col=c))
        toks.append(go(tok_ref.at[c], x_ref.at[col], col=c))
    units = ffn_ref.shape[2]
    hidden = gate_ref.shape[0]
    unit = hidden // 8
    place = lax.broadcasted_iota(jnp.int32, (4 * units, hidden), 0)
    lane = lax.broadcasted_iota(jnp.int32, (4 * units, hidden), 1)
    inside = place % units
    taken = (inside < unit) & (lane == (dp * 4 + place // units) * unit + inside)
    pick = taken.astype(F32).astype(BF)
    for k, source in enumerate((gate_ref, up_ref, down_ref)):
        chosen = nn(pick, source[...]).astype(BF)
        for c in range(4):
            ffn_ref[c, k] = chosen[c * units : (c + 1) * units]
    ffn = [go(ffn_ref.at[c], parts_ref.at[col], col=c) for c in (across, cross, core)]
    part = mix_ref.shape[0] // 2
    half = pl.ds(pl.multiple_of(dp * part, part), part)
    mix_down = [None] + [go(mix_ref.at[half], mixes_ref.at[row, col, half], row=rows[k]) for k in range(1, 4)]
    blocks_ref[row, col] = w_own_ref[...]
    gains_ref[col] = gain_ref[...]
    x_ref[col] = tok_ref[col]
    parts_ref[col] = ffn_ref[col]
    mixes_ref[row, col] = mix_ref[...]
    zero = jnp.zeros(win_ref.shape[1:], BF)
    has_one = row >= 1
    has_two = row >= 2
    for absent, slot in (
        (jnp.logical_not(has_two), 0),
        (jnp.logical_and(jnp.logical_not(has_two), side == 0), 1),
        (jnp.logical_and(jnp.logical_not(has_one), side == 1), 1),
        (jnp.logical_not(has_one), 2),
        (jnp.logical_and(jnp.logical_not(has_one), side == 0), 3),
    ):

        @pl.when(absent)
        def _():
            win_ref[slot] = zero

    keys = seg_ref.shape[1]
    tokens = tok_ref.shape[1]
    block_no = row * 2 + side
    for slot in range(5):
        index = block_no - 4 + slot
        lanes = pl.ds(pl.multiple_of(jnp.maximum(index, 0) * tokens, tokens), tokens)
        seg_ref[:, slot * tokens : (slot + 1) * tokens] = jnp.where(index >= 0, seg_all_ref[col // 2, :, lanes], -1)
    seg_row = seg_ref[...].astype(F32)
    column = jnp.broadcast_to(seg_row, (LANES, keys)).T
    column = jnp.concatenate([column] * (tokens // LANES), axis=1)
    key_idx = lax.broadcasted_iota(jnp.int32, (keys, tokens), 0)
    query_idx = lax.broadcasted_iota(jnp.int32, (keys, tokens), 1) + (keys - tokens)
    before = (column == seg_row[:, keys - tokens :]) & (key_idx < query_idx)
    places = jnp.sum(jnp.where(before, 1.0, 0.0), axis=0, keepdims=True)
    angles = jnp.broadcast_to(places, (LANES, tokens)).T * inverse_ref[...]
    turn_ref[:, :LANES] = jnp.cos(angles)
    sine = jnp.sin(angles)
    turn_ref[:, LANES:] = jnp.where(lane_iota(sine.shape) % HD < HD // 2, -sine, sine)

    for k in range(1, 4):
        down[k].wait_recv()
        block = blocks_ref.at[back[k], col]
        sides.append(go(block, block, col=across))
        cores.append(go(block, block, col=core))
    for c in toks:
        c.wait_recv()
    first_norm(x_ref, gains_ref, h_ref)
    mix_side = []
    for k in range(1, 4):
        mix_down[k].wait_recv()
        block = mixes_ref.at[back[k], col, half]
        mix_side.append(go(block, block, dp=1 - dp))
    for c in ffn:
        c.wait_recv()
    to_right = mover.copy(parts_ref, rows_ref.at[row], row=row + 1)
    to_left = mover.copy(parts_ref, rows_ref.at[row], row=row - 1)
    pl.when(row <= 2)(to_right.start)
    pl.when(row >= 1)(to_left.start)
    passed = []
    for k in range(4):
        sides[k].wait_recv()
        block = blocks_ref.at[back[k], across]
        passed.append(go(block, block, col=core))
    for c in cores + passed:
        c.wait_recv()
    for k in range(4):
        if k > 0:
            mix_side[k - 1].wait_recv()
        block = mixes_ref.at[back[k], col]
        rest.append(go(block, block, col=across))
    place_factor_weights(blocks_ref, w_ref)
    make_factors(h_ref, w_ref, turn_ref, hf_ref, bq_ref, win_ref.at[4])

    own = win_ref.at[4]
    one = mover.copy(own, win_ref.at[2], row=row + 1)
    two = mover.copy(win_ref.at[2], win_ref.at[0], row=row + 1)
    near = mover.copy(own, win_ref.at[3], col=core)
    pass_one = mover.copy(win_ref.at[2], win_ref.at[1 + 2 * side], col=core)
    pass_two = mover.copy(win_ref.at[0], win_ref.at[1], col=core)
    hands_on = jnp.logical_and(has_one, row <= 2)
    sends_two = jnp.logical_and(has_two, side == 1)
    takes_two = jnp.logical_and(has_two, side == 0)
    pl.when(row <= 2)(one.start)
    pl.when(side == 0)(near.start)

    @pl.when(has_one)
    def _():
        one.wait_recv()
        pass_one.start()

    pl.when(hands_on)(two.start)
    pl.when(row >= 1)(to_right.wait_recv)
    pl.when(row <= 2)(to_left.wait_recv)
    next_copies()
    make_queries(hf_ref, bq_ref, q_ref)

    @pl.when(has_two)
    def _():
        two.wait_recv()

    pl.when(sends_two)(pass_two.start)

    @pl.when(has_one)
    def _():
        pass_one.wait_recv()
        pass_one.wait_send()

    pl.when(takes_two)(pass_two.wait_recv)
    pl.when(sends_two)(pass_two.wait_send)
    pl.when(side == 1)(near.wait_recv)
    pl.when(side == 0)(near.wait_send)
    pl.when(row <= 2)(one.wait_send)
    pl.when(hands_on)(two.wait_send)
    pl.when(row <= 2)(to_right.wait_send)
    pl.when(row >= 1)(to_left.wait_send)

    def end():
        for c in rest:
            c.wait_recv()
        for c in started:
            c.wait_send()

    return end


KEPT = (0, 2, 3, 4, 5, 6, 7, 8, 9, 11)


def head_attend_body(*refs):
    head_in, cot_ref = refs[:11], refs[11]
    outs, scratch = refs[12:30], refs[30:]
    kept = dict(zip(KEPT, scratch[10:20]))
    tiles = scratch[20:23]
    keep_sem, tile_sem = scratch[23:]
    head_out = [kept.get(k, outs[k]) for k in range(13)]
    o_out, lse_ref, k_out, v_out, near_ref = outs[13:]
    mixes_ref, q_ref, win_ref, seg_ref, rows_ref = (head_out[k] for k in (3, 7, 9, 10, 12))
    side_work = AttendCopies(cot_ref, rows_ref, near_ref, mixes_ref, *scratch[8:10])
    side_work.head_end = head_body(*head_in, *head_out, *scratch[:6], side_work.first)
    copies = [pltpu.make_async_copy(kept[k], outs[k], keep_sem.at[n]) for n, k in enumerate(KEPT)]
    for k, c in zip(KEPT, copies):
        if k != 3:
            c.start()

    def tile_copies(p):
        lanes = pl.ds(pl.multiple_of(p * LANES, LANES), LANES)
        return [
            pltpu.make_async_copy(source.at[:, lanes], target.at[:, lanes], tile_sem.at[n, p])
            for n, (source, target) in enumerate(zip(tiles, (o_out, k_out, v_out)))
        ]

    def store(p):
        for c in tile_copies(p):
            c.start()

    attend_body(
        True, q_ref, win_ref, seg_ref, tiles[0], lse_ref, tiles[1], tiles[2], *scratch[6:8],
        store=store, side_work=side_work,
    )
    copies[KEPT.index(3)].start()
    for p in range(PAIRS):
        for c in tile_copies(p):
            c.wait()
    for c in copies:
        c.wait()


def head_attend(tok, ranks_t, heads_t, gain_one, gain_two, gate_t, up_t, down, w_out, segments, inverse, cot):
    rows, feat = tok.shape[1:]
    units = -(-gate_t.shape[0] // 8 // 16) * 16
    block = (ranks_t.shape[0] + GROUP_COLS, feat)
    ffn = (4, 3, units, feat)
    count = 3 + 4 + 4 + 6 + 3 + 3 + 3 + 4 + 4 + 2 + 5
    outs = (
        jax.ShapeDtypeStruct(tok.shape, BF),
        jax.ShapeDtypeStruct((4, 8, feat), F32),
        jax.ShapeDtypeStruct(ffn, BF),
        jax.ShapeDtypeStruct((4, 4) + w_out.shape, BF),
        jax.ShapeDtypeStruct((rows, D), BF),
        jax.ShapeDtypeStruct((rows, HEAD_COLS), F32),
        jax.ShapeDtypeStruct((rows, RQ * HD), F32),
        jax.ShapeDtypeStruct((rows, D), BF),
        jax.ShapeDtypeStruct((ALL_COLS, D), BF),
        jax.ShapeDtypeStruct((5, rows, 3 * LANES), BF),
        jax.ShapeDtypeStruct((1, 5 * rows), jnp.int32),
        jax.ShapeDtypeStruct((rows, 2 * LANES), F32),
        jax.ShapeDtypeStruct((4,) + ffn, BF),
        *attend_shapes(rows, 5 * rows),
        jax.ShapeDtypeStruct((4,) + cot.shape, BF),
    )
    out_specs = [VMEM] * 12 + [ANY] + [ANY, VMEM, ANY, ANY] + [ANY]
    for k in KEPT:
        out_specs[k] = ANY
    return pl.pallas_call(
        head_attend_body,
        out_shape=outs,
        in_specs=[VMEM] * 11 + [ANY],
        out_specs=tuple(out_specs),
        scratch_shapes=[
            pltpu.VMEM(block, BF),
            pltpu.VMEM((8, feat), F32),
            pltpu.VMEM(ffn, BF),
            pltpu.VMEM((4, 4) + block, BF),
            pltpu.SemaphoreType.DMA((count,)),
            pltpu.SemaphoreType.DMA((count,)),
            pltpu.VMEM((5 * rows, rows), F32),
            pltpu.VMEM((2 * RK, 5 * rows, LANES), F32),
            pltpu.SemaphoreType.DMA((22,)),
            pltpu.SemaphoreType.DMA((22,)),
        ]
        + [pltpu.VMEM(outs[k].shape, outs[k].dtype) for k in KEPT + (13, 15, 16)]
        + [pltpu.SemaphoreType.DMA((len(KEPT),)), pltpu.SemaphoreType.DMA((3, PAIRS))],
        compiler_params=comm_params(1),
        cost_estimate=cost_of(2 * rows * D * (800 * 3 + 5 * rows * 16), 30 << 20),
    )(tok, ranks_t, heads_t, gain_one, gain_two, gate_t, up_t, down, w_out, segments, inverse, cot)


def window_lanes(ref, lanes):
    value = ref[..., lanes]
    return value.reshape(-1, value.shape[-1])


def mask_bias(seg_ref, keys, rows):
    seg_row = seg_ref[...].astype(F32)
    wide = jnp.broadcast_to(seg_row, (LANES, keys))
    column = wide.T
    column = jnp.concatenate([column] * (rows // LANES), axis=1)
    key_idx = lax.broadcasted_iota(jnp.int32, (keys, rows), 0)
    query_idx = lax.broadcasted_iota(jnp.int32, (keys, rows), 1) + (keys - rows)
    same = column == seg_row[:, keys - rows :]
    return jnp.where(same & (key_idx <= query_idx), 0.0, NEG)


def attend_body(fast, q_ref, kf_ref, seg_ref, *refs, store=None, side_work=None):
    o_ref, lse_ref, k_ref, v_ref, bias_ref, dup_ref = refs
    rows = q_ref.shape[0]
    keys = seg_ref.shape[1]
    bias_ref[...] = mask_bias(seg_ref, keys, rows)
    for s in range(2 * RK):
        tile = window_lanes(kf_ref, slice((s // 2) * LANES, (s // 2 + 1) * LANES)).astype(F32)
        dup_ref[s] = double_left(tile) if s % 2 == 0 else double_right(tile)

    def pair(p, carried):
        if fast:
            pl.when(p == 1)(side_work.early)
            pl.when(p == 3)(side_work.second)
        lanes = pl.ds(pl.multiple_of(p * LANES, LANES), LANES)
        weights = window_lanes(kf_ref, slice(2 * LANES, 3 * LANES))
        made = []
        for kind in range(2):
            acc = None
            for s in range(RK):
                pick = spread(LANES, (kind * RK + s) * H + 2 * p, LANES)
                term = nn(weights, pick) * dup_ref[kind * RK + s]
                acc = term if acc is None else acc + term
            made.append((acc / RK).astype(BF))
        k_tile, v_tile = made
        k_ref[:, lanes] = k_tile
        v_ref[:, lanes] = v_tile
        v_turned = v_tile.astype(F32).T.astype(BF)
        q_turned = (q_ref[:, lanes].astype(F32) * HD**-0.5).T
        half = lax.broadcasted_iota(jnp.int32, q_turned.shape, 0) // HD
        outs = []
        for side in range(2):
            q_side = jnp.where(half == side, q_turned, 0.0).astype(BF)
            scores = nn(k_tile, q_side) + bias_ref[...]
            peak = jnp.max(scores, axis=0, keepdims=True)
            weight = jnp.exp(scores - peak)
            total = jnp.sum(weight, axis=0, keepdims=True)
            probs = (weight * (1.0 / total)).astype(BF)
            outs.append(nn(v_turned[side * HD : (side + 1) * HD], probs))
            lse_ref[2 * p + side] = jnp.broadcast_to(peak + jnp.log(total), (8, rows))
        o_ref[:, lanes] = jnp.concatenate(outs, axis=0).T.astype(BF)
        if fast:
            store(p)
        return carried

    lax.fori_loop(0, PAIRS, pair, 0)
    if fast:
        side_work.last()


def attend_shapes(rows, keys):
    return [
        jax.ShapeDtypeStruct((rows, D), BF),
        jax.ShapeDtypeStruct((H, 8, rows), F32),
        jax.ShapeDtypeStruct((keys, D), BF),
        jax.ShapeDtypeStruct((keys, D), BF),
    ]


def attend(q, kf_window, seg_window):
    rows = q.shape[0]
    keys = kf_window.shape[0]
    return call(
        functools.partial(attend_body, False),
        tuple(attend_shapes(rows, keys)),
        scratch=(pltpu.VMEM((keys, rows), F32), pltpu.VMEM((2 * RK, keys, LANES), F32)),
        cost=cost_of(2 * rows * keys * D * 16, 16 << 20),
    )(q, kf_window, seg_window)


def attend_back_body(fast, q_ref, k_ref, v_ref, do_ref, lse_ref, kf_ref, seg_ref, *refs, load=None):
    if fast:
        dq_ref, dkf_ref = refs[5:7]
        bias_ref, dup_ref, sum_ref, fac_ref = refs[10:14]
        side_work = BackCopies(refs[:5] + refs[7:10] + refs[14:28], refs[28:])
        side_work.first()
    else:
        dq_ref, dkf_ref, bias_ref, dup_ref, sum_ref, fac_ref = refs
    rows = q_ref.shape[0]
    keys = seg_ref.shape[1]
    bias_ref[...] = mask_bias(seg_ref, keys, rows)
    for s in range(2 * RK):
        tile = window_lanes(kf_ref, slice((s // 2) * LANES, (s // 2 + 1) * LANES)).astype(F32)
        dup_ref[s] = double_left(tile) if s % 2 == 0 else double_right(tile)
    sum_ref[...] = jnp.zeros_like(sum_ref)
    fac_ref[...] = jnp.zeros_like(fac_ref)

    def pair(p, carried):
        if fast:
            pl.when(p == 3)(side_work.second)
            pl.when(p == 3)(side_work.cross_x)
            pl.when(p == 4)(side_work.last_hop)
            pl.when(p == 6)(side_work.third)
            load(p)
        lanes = pl.ds(pl.multiple_of(p * LANES, LANES), LANES)
        k_tile = k_ref[:, lanes]
        v_tile = v_ref[:, lanes]
        k_turned = k_tile.astype(F32).T.astype(BF)
        q_tile = q_ref[:, lanes].astype(F32) * HD**-0.5
        do_tile = do_ref[:, lanes].astype(F32)
        q_turned = q_tile.T
        do_turned = do_tile.T
        half = lax.broadcasted_iota(jnp.int32, q_turned.shape, 0) // HD
        lane_half = lax.broadcasted_iota(jnp.int32, q_tile.shape, 1) // HD
        d_k = None
        d_v = None
        d_q = []
        for side in range(2):
            q_side = jnp.where(half == side, q_turned, 0.0).astype(BF)
            do_side = jnp.where(half == side, do_turned, 0.0).astype(BF)
            scores = nn(k_tile, q_side) + bias_ref[...]
            probs = jnp.exp(scores - lse_ref[2 * p + side][:1])
            d_prob = nn(v_tile, do_side)
            delta = jnp.sum(probs * d_prob, axis=0, keepdims=True)
            d_score = (probs * (d_prob - delta)).astype(BF)
            d_q.append(nn(k_turned[side * HD : (side + 1) * HD], d_score))
            q_back = jnp.where(lane_half == side, q_tile, 0.0).astype(BF)
            do_back = jnp.where(lane_half == side, do_tile, 0.0).astype(BF)
            part_k = nn(d_score, q_back)
            part_v = nn(probs.astype(BF), do_back)
            d_k = part_k if d_k is None else d_k + part_k
            d_v = part_v if d_v is None else d_v + part_v
        dq_ref[:, lanes] = jnp.concatenate(d_q, axis=0).T * HD**-0.5
        weights = window_lanes(kf_ref, slice(2 * LANES, 3 * LANES))
        for kind, grad in ((0, d_k), (1, d_v)):
            for s in range(RK):
                slot = kind * RK + s
                pick = spread(LANES, slot * H + 2 * p, LANES)
                sum_ref[slot] += nn(weights, pick) * grad
                product = (grad * dup_ref[slot]).astype(BF)
                fac_ref[...] += nn(product, collect(LANES, LANES, slot * H + 2 * p))
        return carried

    lax.fori_loop(0, PAIRS, pair, 0)
    for tile in range(2):
        first = sum_ref[2 * tile]
        second = sum_ref[2 * tile + 1]
        first = first + pltpu.roll(first, HD, 1)
        second = second + pltpu.roll(second, HD, 1)
        merged = jnp.where(lane_iota(first.shape) < HD, first, second)
        blocks = dkf_ref.shape[:-1] + (LANES,)
        dkf_ref[..., tile * LANES : (tile + 1) * LANES] = (merged / RK).astype(BF).reshape(blocks)
    dkf_ref[..., 2 * LANES :] = (fac_ref[...] / RK).astype(BF).reshape(blocks)
    if fast:
        side_work.last()


def back_scratch(rows, keys):
    return [
        pltpu.VMEM((keys, rows), F32),
        pltpu.VMEM((2 * RK, keys, LANES), F32),
        pltpu.VMEM((2 * RK, keys, LANES), F32),
        pltpu.VMEM((keys, LANES), F32),
    ]


def attend_back(q, k, v, d_heads, lse, kf_window, seg_window):
    rows = q.shape[0]
    keys = kf_window.shape[0]
    return call(
        functools.partial(attend_back_body, False),
        (jax.ShapeDtypeStruct((rows, D), F32), jax.ShapeDtypeStruct(kf_window.shape, BF)),
        scratch=back_scratch(rows, keys),
        cost=cost_of(2 * rows * keys * D * 40, 16 << 20),
    )(q, k, v, d_heads, lse, kf_window, seg_window)


def mixing_body(x_ref, heads_ref, w_out_ref, gain_ref, mixed_ref, h_ref):
    parts, _, feat = x_ref.shape
    rows_of = w_out_ref.shape[0]
    head_rows = w_out_ref.shape[2]
    total = None
    for c in range(parts):
        lanes = slice(c * feat, (c + 1) * feat)
        acc = x_ref[c].astype(F32)
        for r in range(rows_of):
            acc = acc + nn(heads_ref[:, r * head_rows : (r + 1) * head_rows], w_out_ref[r, c])
        mixed_ref[:, lanes] = acc
        part = jnp.sum(acc * acc, axis=1, keepdims=True)
        total = part if total is None else total + part
    scale = lax.rsqrt(total / D + EPS)
    for c in range(parts):
        lanes = slice(c * feat, (c + 1) * feat)
        h_ref[:, lanes] = (mixed_ref[:, lanes] * scale * gain_ref[c, 1:2]).astype(BF)


def mixing(x_parts, heads, w_out, gains):
    rows = heads.shape[0]
    return call(
        mixing_body,
        (jax.ShapeDtypeStruct((rows, D), F32), jax.ShapeDtypeStruct((rows, D), BF)),
        cost=cost_of(2 * rows * D * D, 5 << 20),
    )(x_parts, heads, w_out, gains)


def ffn_steps(blocks, h_at, cot_at, w_ref, hid_ref, dg_ref, du_ref, out_at, back_at):
    def block(t, carried):
        h = h_at(t)[...]
        gate = nt(h, w_ref[0])
        up = nt(h, w_ref[1])
        d_hidden = nt(cot_at(t)[...], w_ref[2])
        sig = 1.0 / (1.0 + jnp.exp(-gate))
        silu = gate * sig
        hidden = (silu * up).astype(BF)
        d_gate = (d_hidden * up * sig * (1.0 + gate * (1.0 - sig))).astype(BF)
        d_up = (d_hidden * silu).astype(BF)
        rows = h.shape[0]
        place = pl.ds(pl.multiple_of(t * rows, rows), rows)
        hid_ref[place] = hidden
        dg_ref[place] = d_gate
        du_ref[place] = d_up
        out_at(t)[...] = nn(hidden, w_ref[2]).astype(BF)
        back_at(t)[...] = (nn(d_gate, w_ref[0]) + nn(d_up, w_ref[1])).astype(BF)
        return carried

    lax.fori_loop(0, blocks, block, 0)


def ffn_body(h_ref, cot_ref, w_ref, out_ref, back_ref, g_ref, hid_ref, dg_ref, du_ref):
    parts, rows, _ = h_ref.shape
    ffn_steps(
        parts, lambda t: h_ref.at[t], lambda t: cot_ref.at[t], w_ref, hid_ref, dg_ref, du_ref,
        lambda t: out_ref.at[t], lambda t: back_ref.at[t],
    )
    h_all = h_ref[...].reshape(parts * rows, D)
    cot_all = cot_ref[...].reshape(parts * rows, D)
    for place, (left, right) in enumerate(((dg_ref, h_all), (du_ref, h_all), (hid_ref, cot_all))):
        g_ref[place] = tn(left[...], right).astype(BF)


def ffn(h_all, cot_all, w):
    parts, rows, _ = h_all.shape
    units = w.shape[1]
    return call(
        ffn_body,
        (
            jax.ShapeDtypeStruct(h_all.shape, BF),
            jax.ShapeDtypeStruct(h_all.shape, BF),
            jax.ShapeDtypeStruct(w.shape, BF),
        ),
        scratch=[pltpu.VMEM((parts * rows, units), BF)] * 3,
        cost=cost_of(2 * parts * rows * 9 * D * units, 20 << 20),
    )(h_all, cot_all, w)


def unmix_math(
    mixed_ref, cot_ref, d_h, heads_ref, w_out_ref, gain_ref, d_mixed_ref, d_heads_ref, g_out_ref, g_gain_ref
):
    rows_of, parts, head_rows, feat = w_out_ref.shape
    mixed = mixed_ref[...]
    scale = lax.rsqrt(jnp.sum(mixed * mixed, axis=1, keepdims=True) / D + EPS)
    normed = mixed * scale
    g_gain_ref[...] = jnp.sum(d_h * normed, axis=0, keepdims=True)
    gain = jnp.concatenate([gain_ref[c, 1:2] for c in range(parts)], axis=1)
    inner = d_h * gain
    dot = jnp.sum(inner * normed, axis=1, keepdims=True) / D
    d_mixed = cot_ref[...].astype(F32) + scale * (inner - normed * dot)
    d_mixed_ref[...] = d_mixed
    low = d_mixed.astype(BF)
    grad = tn(heads_ref[...], low)
    for r in range(rows_of):
        acc = None
        for c in range(parts):
            lanes = slice(c * feat, (c + 1) * feat)
            term = nt(low[:, lanes], w_out_ref[r, c])
            acc = term if acc is None else acc + term
            g_out_ref[r, c] = grad[r * head_rows : (r + 1) * head_rows, lanes].astype(BF)
        d_heads_ref[:, r * head_rows : (r + 1) * head_rows] = acc.astype(BF)


def write_output(mixed_ref, total, out_ref):
    parts, _, feat = out_ref.shape
    for c in range(parts):
        lanes = slice(c * feat, (c + 1) * feat)
        out_ref[c] = (mixed_ref[:, lanes] + total[:, lanes]).astype(BF)


def unmix_body(
    dh_ref, sum_ref, mixed_ref, cot_ref, heads_ref, w_out_ref, gain_ref,
    out_ref, d_mixed_ref, d_heads_ref, g_out_ref, g_gain_ref,
):
    unmix_math(
        mixed_ref, cot_ref, dh_ref[...], heads_ref, w_out_ref, gain_ref,
        d_mixed_ref, d_heads_ref, g_out_ref, g_gain_ref,
    )
    write_output(mixed_ref, sum_ref[...], out_ref)


def middle_body(
    x_ref, heads_ref, w_out_ref, gain_ref, cot_own_ref, cot_in_ref, w_own_ref, rows_ref,
    mixed_out, d_mixed_ref, d_heads_ref, g_out_ref, g_gain_ref, g_hbm, out_pair_hbm, hop_ref,
    w_ref, h_ref, cot_ref, hid_ref, dg_ref, du_ref, back_ref, fwd_ref, back_got_ref, fwd_got_ref,
    pair_ref, diag_ref, far_ref, send_sem, recv_sem, w_sem, cot_sem,
    mixed_ref, g_ref, out_pair_ref, leave_sem,
):
    row = lax.axis_index("row")
    col, core, across = neighbours()
    dp, (me, on_x, on_y, on_both) = square()
    x, mine = col // 2, lax.rem(col, 2)
    y = 1 - dp
    parts, rows, feat = x_ref.shape
    units = rows_ref.shape[3]
    greet(
        [
            (None, {"col": core}),
            (None, {"col": across}),
            (None, {"dp": y}),
            (row <= 2, {"row": row + 1}),
            (row >= 1, {"row": row - 1}),
        ]
    )
    mover = Mover(send_sem, recv_sem)

    def w_place(r, c):
        return w_ref.at[:, pl.ds(pl.multiple_of(r * units, units), units), pl.ds(c * feat, feat)]

    local = []
    for k in range(4):
        r = lax.rem(row + k, 4)
        for c in range(4):
            source = w_own_ref.at[c] if k == 0 else rows_ref.at[r, c]
            copy = pltpu.make_async_copy(source, w_place(r, c), w_sem.at[k, c])
            copy.start()
            local.append(copy)
    cots = []
    for k in range(4):
        from_x = lax.rem(x + k % 2, 2)
        from_dp = lax.rem(dp + k // 2, 2)
        lanes = pl.ds(pl.multiple_of((from_x * 2 + mine) * feat, feat), feat)
        for c in range(4):
            part = pl.ds(c * rows, rows)
            source = cot_own_ref.at[part] if k == 0 else cot_in_ref.at[from_dp * 2 + from_x, part]
            spot = from_dp * 2 + c // 2
            copy = pltpu.make_async_copy(source, cot_ref.at[lax.rem(mine + c, 2), spot, :, lanes], cot_sem.at[k, c])
            copy.start()
            local.append(copy)
            sent = mover.copy(source, cot_ref.at[lax.rem(mine + c + 1, 2), spot, :, lanes], col=core)
            sent.start()
            cots.append(sent)

    total = None
    for c in range(parts):
        lanes = slice(c * feat, (c + 1) * feat)
        acc = x_ref[c].astype(F32)
        for r in range(4):
            acc = acc + nn(heads_ref[:, r * feat : (r + 1) * feat], w_out_ref[r, c])
        mixed_ref[:, lanes] = acc
        part = jnp.sum(acc * acc, axis=1, keepdims=True)
        total = part if total is None else total + part
    scale = lax.rsqrt(total / D + EPS)
    for c in range(parts):
        lanes = slice(c * feat, (c + 1) * feat)
        h_ref[0, me, :, lanes] = (mixed_ref[:, lanes] * scale * gain_ref[c, 1:2]).astype(BF)

    leave = [
        pltpu.make_async_copy(source, target, leave_sem.at[n])
        for n, (source, target) in enumerate(
            ((mixed_ref, mixed_out), (g_ref, g_hbm), (out_pair_ref, out_pair_hbm))
        )
    ]
    leave[0].start()

    half = rows // 2
    top, low = pl.ds(0, half), pl.ds(half, half)

    def h_copy(spot, part=None, side=0, **place):
        source = h_ref.at[0, spot] if part is None else h_ref.at[0, spot, part]
        target = h_ref.at[side, spot] if part is None else h_ref.at[side, spot, part]
        return mover.copy(source, target, **place)

    x_low = h_copy(me, low, col=across)
    y_top = h_copy(me, top, dp=y)
    x_top = h_copy(me, top, col=across)
    y_low = h_copy(me, low, dp=y)
    near = h_copy(me, None, 1, col=core)
    both_low = h_copy(on_x, low, dp=y)
    both_top = h_copy(on_y, top, col=across)
    near_first = [h_copy(on_x, low, 1, col=core), h_copy(on_y, top, 1, col=core)]
    near_second = [h_copy(on_x, top, 1, col=core), h_copy(on_y, low, 1, col=core)]
    near_both = h_copy(on_both, None, 1, col=core)
    for c in (x_low, y_top, near, x_top, y_low):
        c.start()
    steps = (
        ((me, top), (me, low)),
        ((on_x, low), (on_y, top)),
        ((on_x, top), (on_y, low)),
        ((on_both, top), (on_both, low)),
    )
    back_near = [[mover.copy(back_ref.at[1, s, p], back_got_ref.at[s, p], col=core) for s, p in two] for two in steps]
    fwd_near = [[mover.copy(fwd_ref.at[1, s, p], fwd_got_ref.at[s, p], col=core) for s, p in two] for two in steps]
    diag = [
        mover.copy(pair_ref.at[on_both, low], diag_ref.at[0], col=across),
        mover.copy(pair_ref.at[on_both, top], diag_ref.at[1], dp=y),
    ]
    far = [
        mover.copy(pair_ref.at[on_x, low], far_ref.at[0, low], col=across),
        mover.copy(pair_ref.at[on_y, top], far_ref.at[1, top], dp=y),
        mover.copy(pair_ref.at[on_y, low], far_ref.at[1, low], dp=y),
        mover.copy(pair_ref.at[on_x, top], far_ref.at[0, top], col=across),
    ]

    def add_pair(k):
        for (s, p), c in zip(steps[k], back_near[k]):
            c.wait_recv()
            pair_ref[s, p] = (back_ref[0, s, p].astype(F32) + back_got_ref[s, p].astype(F32)).astype(BF)

    for copy in local:
        copy.wait()
    for c in cots:
        c.wait_recv()

    def block(t, carried):
        @pl.when(t == 1)
        def _():
            near.wait_recv()

        @pl.when(t == 2)
        def _():
            x_low.wait_recv()
            both_low.start()
            near_first[0].start()
            y_top.wait_recv()
            both_top.start()
            near_first[1].start()

        @pl.when(t == 3)
        def _():
            for c in near_first:
                c.wait_recv()

        @pl.when(t == 4)
        def _():
            x_top.wait_recv()
            near_second[0].start()
            y_low.wait_recv()
            near_second[1].start()

        @pl.when(t == 5)
        def _():
            for c in near_second:
                c.wait_recv()
            add_pair(1)
            far[0].start()
            far[1].start()

        @pl.when(t == 6)
        def _():
            both_low.wait_recv()
            both_top.wait_recv()
            near_both.start()

        @pl.when(t == 7)
        def _():
            near_both.wait_recv()
            add_pair(2)

        name, side = t // 2, lax.rem(t, 2)
        first_dp = lax.rem(dp + jnp.where(name == 3, 1, 0), 2)
        first_x = lax.rem(x + jnp.where(name >= 1, 1, 0), 2)
        first = first_dp * 2 + first_x
        other_dp = lax.rem(dp + jnp.where(name >= 1, 1, 0), 2)
        other_x = lax.rem(x + jnp.where(name == 3, 1, 0), 2)
        other = other_dp * 2 + other_x
        first_rows = pl.ds(pl.multiple_of(jnp.where(name == 1, half, 0), half), half)
        other_rows = pl.ds(pl.multiple_of(jnp.where(name == 1, 0, half), half), half)
        h = jnp.concatenate([h_ref[side, first, first_rows], h_ref[side, other, other_rows]], axis=0)
        cot = jnp.concatenate([cot_ref[side, first, first_rows], cot_ref[side, other, other_rows]], axis=0)
        gate = nt(h, w_ref[0])
        up = nt(h, w_ref[1])
        d_hidden = nt(cot, w_ref[2])
        sig = 1.0 / (1.0 + jnp.exp(-gate))
        silu = gate * sig
        hidden = (silu * up).astype(BF)
        d_gate = (d_hidden * up * sig * (1.0 + gate * (1.0 - sig))).astype(BF)
        d_up = (d_hidden * silu).astype(BF)
        back = (nn(d_gate, w_ref[0]) + nn(d_up, w_ref[1])).astype(BF)
        fwd = nn(hidden, w_ref[2]).astype(BF)
        for spot, part, cut in ((first, first_rows, slice(0, half)), (other, other_rows, slice(half, rows))):
            start = jnp.where(part.start == 0, 0, half)
            place = pl.ds(pl.multiple_of((side * 4 + spot) * rows + start, half), half)
            hid_ref[place] = hidden[cut]
            dg_ref[place] = d_gate[cut]
            du_ref[place] = d_up[cut]
            back_ref[side, spot, part] = back[cut]
            fwd_ref[side, spot, part] = fwd[cut]
        for k in range(4):

            @pl.when(t == 2 * k + 1)
            def _():
                for c in back_near[k] + fwd_near[k]:
                    c.start()

        return carried

    lax.fori_loop(0, 8, block, 0)
    add_pair(3)
    for c in diag:
        c.start()

    hops = []
    for place in range(3):
        to_right = mover.copy(g_ref.at[3, place], hop_ref.at[place], row=row + 1)
        to_left = mover.copy(g_ref.at[0, place], hop_ref.at[place], row=row - 1)
        hops.append((to_right, to_left))

    def gradient(place, left, right):
        grad = tn(left[...], right[...].reshape(8 * rows, D))
        for r in range(4):
            g_ref[r, place] = grad[r * units : (r + 1) * units].astype(BF)
        pl.when(row == 0)(hops[place][0].start)
        pl.when(row == 3)(hops[place][1].start)

    gradient(0, dg_ref, h_ref)
    gradient(1, du_ref, h_ref)
    for k, (s, part) in enumerate(((on_y, low), (on_x, top))):
        diag[k].wait_recv()
        pair_ref[s, part] = (pair_ref[s, part].astype(F32) + diag_ref[k].astype(F32)).astype(BF)
        far[2 + k].start()
    gradient(2, hid_ref, cot_ref)
    leave[1].start()
    for two, copies in zip(steps, fwd_near):
        for (s, p), c in zip(two, copies):
            c.wait_recv()
            out_pair_ref[s, p] = (fwd_ref[0, s, p].astype(F32) + fwd_got_ref[s, p].astype(F32)).astype(BF)
    leave[2].start()
    add_pair(0)
    for c in far:
        c.wait_recv()
    d_h = pair_ref[me].astype(F32) + far_ref[0].astype(F32) + far_ref[1].astype(F32)
    unmix_math(
        mixed_ref, cot_ref.at[0, me], d_h, heads_ref, w_out_ref, gain_ref,
        d_mixed_ref, d_heads_ref, g_out_ref, g_gain_ref,
    )
    for c in cots + [x_low, y_top, x_top, y_low, near, both_low, both_top, near_both] + near_first + near_second:
        c.wait_send()
    for two in back_near + fwd_near:
        for c in two:
            c.wait_send()
    for c in diag + far:
        c.wait_send()
    for c in leave:
        c.wait()
    for to_right, to_left in hops:
        pl.when(row == 0)(to_right.wait_send)
        pl.when(row == 3)(to_left.wait_send)
        pl.when(row == 1)(to_right.wait_recv)
        pl.when(row == 2)(to_left.wait_recv)


def middle(x_parts, heads, w_out, gains, cot_own, cot_near, w_own, w_rows):
    parts, rows, feat = x_parts.shape
    units = w_rows.shape[3]
    count = 16 + 12 + 16 + 6 + 6
    square_of = pltpu.VMEM((2, 4, rows, D), BF)
    hidden_of = pltpu.VMEM((8 * rows, 4 * units), BF)
    quarter = pltpu.VMEM((4, rows, D), BF)
    return pl.pallas_call(
        middle_body,
        out_shape=(
            jax.ShapeDtypeStruct((rows, D), F32),
            jax.ShapeDtypeStruct((rows, D), F32),
            jax.ShapeDtypeStruct((rows, D), BF),
            jax.ShapeDtypeStruct(w_out.shape, BF),
            jax.ShapeDtypeStruct((1, D), F32),
            jax.ShapeDtypeStruct((4, 3, units, D), BF),
            jax.ShapeDtypeStruct((4, rows, D), BF),
            jax.ShapeDtypeStruct((3, units, D), BF),
        ),
        in_specs=[VMEM] * 4 + [ANY] * 4,
        out_specs=(ANY,) + (VMEM,) * 4 + (ANY,) * 3,
        scratch_shapes=[pltpu.VMEM((3, 4 * units, D), BF), square_of, square_of]
        + [hidden_of] * 3
        + [square_of, square_of, quarter, quarter, quarter]
        + [
            pltpu.VMEM((2, rows // 2, D), BF),
            pltpu.VMEM((2, rows, D), BF),
            pltpu.SemaphoreType.DMA((count,)),
            pltpu.SemaphoreType.DMA((count,)),
            pltpu.SemaphoreType.DMA((4, 4)),
            pltpu.SemaphoreType.DMA((4, 4)),
            pltpu.VMEM((rows, D), F32),
            pltpu.VMEM((4, 3, units, D), BF),
            quarter,
            pltpu.SemaphoreType.DMA((3,)),
        ],
        compiler_params=comm_params(4),
        cost_estimate=cost_of(2 * 8 * rows * 9 * D * 4 * units, 24 << 20),
    )(x_parts, heads, w_out, gains, cot_own, cot_near, w_own, w_rows)


def unmix(dh, out_sum, mixed, cot_own, heads, w_out, gains):
    rows = heads.shape[0]
    parts, feat = w_out.shape[1], w_out.shape[3]
    outs = (
        jax.ShapeDtypeStruct((parts, rows, feat), BF),
        jax.ShapeDtypeStruct((rows, D), F32),
        jax.ShapeDtypeStruct((rows, D), BF),
        jax.ShapeDtypeStruct(w_out.shape, BF),
        jax.ShapeDtypeStruct((1, D), F32),
    )
    return call(unmix_body, outs, cost=cost_of(4 * rows * D * D, 18 << 20))(
        dh, out_sum, mixed, cot_own, heads, w_out, gains
    )


def query_grads(ranks_taken, dq, high, low, bq_ref):
    fac = None
    folded = []
    for r in ranks_taken:
        tile = bq_ref[:, (r // 2) * LANES : (r // 2 + 1) * LANES]
        rank = double_left(tile) if r % 2 == 0 else double_right(tile)
        product = dq * jnp.concatenate([rank] * PAIRS, axis=1)
        term = two_pass(product, head_collect(2 * RK + r))
        fac = term if fac is None else fac + term
        pick = head_spread(2 * RK + r, 0, D)
        terms = (nn(high, pick) + nn(low, pick)) * dq
        acc = terms[:, :LANES]
        for p in range(1, PAIRS):
            acc = acc + terms[:, p * LANES : (p + 1) * LANES]
        folded.append(acc + pltpu.roll(acc, HD, 1))
    return fac, folded


def turned_back(part, turn_ref):
    return part * turn_ref[:, :LANES] - swap_halves(part) * turn_ref[:, LANES:]


def put_query_grads(folded, first, turn_ref, d_ref):
    lane = lane_iota(folded[0].shape)
    for k in range(len(folded) // 2):
        merged = jnp.where(lane < HD, folded[2 * k], folded[2 * k + 1])
        tile = first // 2 + k
        d_ref[:, tile * LANES : (tile + 1) * LANES] = turned_back(merged, turn_ref).astype(BF)


def put_key_grads(dkf, fac, turn_ref, d_ref):
    d_ref[:, 3 * LANES : 4 * LANES] = turned_back(dkf[:, :LANES], turn_ref).astype(BF)
    d_ref[:, 4 * LANES : 5 * LANES] = dkf[:, LANES : 2 * LANES].astype(BF)
    fac = fac.astype(BF).astype(F32) + nt(dkf[:, 2 * LANES :].astype(BF), key_columns())
    d_ref[:, RANK_COLS:] = fac.astype(BF)


def factor_weight_grads(d_ref, h_ref, gains, g_two_ref, g_ref):
    n_row, parts, _, feat = g_ref.shape
    grad = tn(d_ref[...], h_ref[...])
    ranks_each = RANK_COLS // n_row
    used = FAC * GROUP
    for c in range(parts):
        lanes = slice(c * feat, (c + 1) * feat)
        tail = jnp.concatenate(
            [gains[c], g_two_ref[:, lanes], jnp.zeros((GROUP_COLS - used - 2, feat), F32)], axis=0
        )
        for r in range(n_row):
            first = RANK_COLS + r * GROUP_COLS
            g_ref[r, c, :ranks_each] = grad[r * ranks_each : (r + 1) * ranks_each, lanes].astype(BF)
            g_ref[r, c, ranks_each:] = jnp.concatenate([grad[first : first + used, lanes], tail], axis=0).astype(BF)


def first_norm_back(d_h, x_ref, gain_ref, d_mixed_ref, gi_ref):
    parts, _, feat = x_ref.shape
    xs = [x_ref[c].astype(F32) for c in range(parts)]
    total = sum(jnp.sum(v * v, axis=1, keepdims=True) for v in xs)
    scale = lax.rsqrt(total / D + EPS)
    dot = None
    gains = []
    for c in range(parts):
        normed = xs[c] * scale
        grad = d_h[:, c * feat : (c + 1) * feat]
        gains.append(jnp.sum(grad * normed, axis=0, keepdims=True))
        part = jnp.sum(grad * gain_ref[c, :1] * normed, axis=1, keepdims=True)
        dot = part if dot is None else dot + part
    for c in range(parts):
        lanes = slice(c * feat, (c + 1) * feat)
        normed = xs[c] * scale
        total = d_mixed_ref[:, lanes] + scale * (d_h[:, lanes] * gain_ref[c, :1] - normed * (dot / D))
        gi_ref[c] = total.astype(gi_ref.dtype)
    return gains


def back_body(
    dq_ref, dkf_ref, hf_ref, bq_ref, turn_ref, w_ref, h_ref, x_ref, gain_ref, d_mixed_ref, g_two_ref,
    gi_ref, g_ref, d_ref,
):
    heads = hf_ref[...]
    high = heads.astype(BF)
    low = (heads - high.astype(F32)).astype(BF)
    fac, folded = query_grads(range(RQ), dq_ref[...] * (1.0 / RQ), high, low, bq_ref)
    put_query_grads(folded, 0, turn_ref, d_ref)
    put_key_grads(dkf_ref[...].astype(F32), fac, turn_ref, d_ref)
    gains = first_norm_back(nn(d_ref[...], w_ref[...]), x_ref, gain_ref, d_mixed_ref, gi_ref)
    factor_weight_grads(d_ref, h_ref, gains, g_two_ref, g_ref)


def back(dq, dkf, hf, bq, turn, w_rh, h, x_parts, gains, d_mixed, g_two, n_row):
    rows = dq.shape[0]
    parts, _, feat = x_parts.shape
    each = RANK_COLS // n_row + GROUP_COLS
    return call(
        back_body,
        (jax.ShapeDtypeStruct(x_parts.shape, F32), jax.ShapeDtypeStruct((n_row, parts, each, feat), BF)),
        scratch=[pltpu.VMEM((rows, ALL_COLS), BF)],
        cost=cost_of(2 * rows * D * 800 * 6, 12 << 20),
    )(dq, dkf, hf, bq, turn, w_rh, h, x_parts, gains, d_mixed, g_two)


def tail_body(
    win_ref, dq_ref, hf_ref, bq_ref, turn_ref, w_ref, h_ref, x_ref, gain_ref, d_mixed_ref, g_two_ref,
    rows_ref, ends_ref, part_ref,
    grad_ref, gi_all_ref, cols_ref, cols_other_ref, mix_ref, mix_other_ref,
    d_ref, gi_ref, wnear_ref, wsend_ref, wfar_ref, rows_own_ref, cols_send_ref, mix_got_ref,
    g_ref, near_ref, pair_ref, far_ref, side_ref, down_ref, last_ref, end_ref,
    send_sem, recv_sem, local_sem,
):
    row = lax.axis_index("row")
    col, core, across = neighbours()
    cross = lax.rem(core + 2, 4)
    dp = lax.axis_index("dp")
    x, mine = col // 2, lax.rem(col, 2)
    y = 1 - dp
    order = [lax.rem(row + k, 4) for k in (1, 2, 3, 0)]
    mover = Mover(send_sem, recv_sem)
    started = []

    def go(source, target, **place):
        c = mover.copy(source, target, **place)
        c.start()
        started.append(c)
        return c

    rows_own = pltpu.make_async_copy(rows_ref.at[row], rows_own_ref, local_sem.at[1])
    rows_own.start()

    near_one = go(win_ref.at[1], wnear_ref.at[0], col=core)
    near_two = go(win_ref.at[3], wnear_ref.at[1], col=core)
    one = mover.copy(wsend_ref.at[0], wfar_ref.at[0], row=row - 1)
    two = mover.copy(wsend_ref.at[1], wfar_ref.at[1], row=row - 1)
    hands_on = jnp.logical_and(row >= 1, row <= 2)
    left = mine == 0
    heads = hf_ref[...]
    high = heads.astype(BF)
    low = (heads - high.astype(F32)).astype(BF)
    dq = dq_ref[...] * (1.0 / RQ)
    near_one.wait_recv()
    near_two.wait_recv()
    zero = jnp.zeros(wnear_ref.shape[1:], F32)
    from_low = wnear_ref[0].astype(F32)
    from_high = wnear_ref[1].astype(F32)
    wsend_ref[1] = (win_ref[0].astype(F32) + jnp.where(left, zero, from_low)).astype(BF)
    pl.when(row >= 2)(two.start)

    width = x_ref.shape[2]
    rows_own.wait()
    for place in range(3):
        total = rows_own_ref[place].astype(F32)
        total = total + jnp.where(row >= 1, ends_ref[0, place].astype(F32), 0.0)
        total = (total + jnp.where(row <= 2, ends_ref[1, place].astype(F32), 0.0)).astype(BF)
        for c in range(4):
            cols_send_ref[c, place] = total[:, c * width : (c + 1) * width]
    columns = [go(cols_send_ref.at[c], cols_ref.at[col], col=c) for c in (across, cross, core)]
    cols_ref[col] = cols_send_ref[col]
    rest = [go(cols_ref.at[col], cols_other_ref.at[col], dp=y)]

    fac, folded = query_grads(range(0, 4), dq, high, low, bq_ref)
    put_query_grads(folded, 0, turn_ref, d_ref)
    sent_on = win_ref[2].astype(F32) + jnp.where(left, from_low, from_high)
    pl.when(hands_on)(two.wait_recv)
    wsend_ref[0] = jnp.where(hands_on, sent_on + wfar_ref[1].astype(F32), sent_on).astype(BF)
    pl.when(row >= 1)(one.start)

    mixes = [go(part_ref.at[order[k]], mix_got_ref.at[k], row=order[k]) for k in range(3)]

    fac_more, folded = query_grads(range(4, RQ), dq, high, low, bq_ref)
    put_query_grads(folded, 4, turn_ref, d_ref)
    for c, source in zip(columns, (across, cross, core)):
        c.wait_recv()
        rest.append(go(cols_ref.at[source], cols_other_ref.at[source], dp=y))
    d_kf = win_ref[4].astype(F32) + jnp.where(left, from_high, zero)
    pl.when(row <= 2)(one.wait_recv)
    d_kf = jnp.where(row <= 2, d_kf + wfar_ref[0].astype(F32), d_kf)
    put_key_grads(d_kf, fac + fac_more, turn_ref, d_ref)
    d_h = nn(d_ref[...], w_ref[...])
    gains = first_norm_back(d_h, x_ref, gain_ref, d_mixed_ref, gi_ref)
    factor_weight_grads(d_ref, h_ref, gains, g_two_ref, g_ref)

    first = [go(g_ref.at[r, (1 - x) * 2 + 1 - mine], near_ref.at[0, k], col=core) for k, r in enumerate(order)]
    second = [go(g_ref.at[r, x * 2 + 1 - mine], near_ref.at[1, k], col=core) for k, r in enumerate(order)]
    sides = []
    for k, r in enumerate(order):
        first[k].wait_recv()
        pair_ref[k] = (g_ref[r, (1 - x) * 2 + mine].astype(F32) + near_ref[0, k].astype(F32)).astype(BF)
        sides.append(go(pair_ref.at[k], side_ref.at[k], col=across))

    total = part_ref[row].astype(F32)
    for k, c in enumerate(mixes):
        c.wait_recv()
        total = total + mix_got_ref[k].astype(F32)
    mix_ref[...] = total.astype(BF)
    rest.append(go(mix_ref, mix_other_ref, dp=y))
    for c in (across, cross, core):
        rest.append(go(gi_ref.at[c], gi_all_ref.at[col], col=c))
    own = pltpu.make_async_copy(gi_ref.at[col], gi_all_ref.at[col], local_sem.at[0])
    own.start()

    downs = []
    for k, r in enumerate(order):
        second[k].wait_recv()
        sides[k].wait_recv()
        far_ref[k] = (
            g_ref[r, x * 2 + mine].astype(F32) + near_ref[1, k].astype(F32) + side_ref[k].astype(F32)
        ).astype(BF)
        if k < 3:
            downs.append(go(far_ref.at[k], down_ref.at[k], row=r))
    total = far_ref[3].astype(F32)
    for k in range(3):
        downs[k].wait_recv()
        total = total + down_ref[k].astype(F32)
    last_ref[...] = total.astype(BF)
    end = go(last_ref, end_ref, dp=y)
    end.wait_recv()
    grad_ref[...] = last_ref[...].astype(F32) + end_ref[...].astype(F32)
    for c in rest:
        c.wait_recv()
    for c in started:
        c.wait_send()
    pl.when(row >= 1)(one.wait_send)
    pl.when(row >= 2)(two.wait_send)
    own.wait()


def back_tail_body(*refs):
    attend_in, side_in, tail_in = refs[:7], refs[7:12], refs[12:21]
    out_ref, *tail_out = refs[21:28]
    scratch = refs[28:]
    dq_ref, dkf_ref, ends_ref, part_ref = scratch[:4]
    gain_ref, g_two_ref = tail_in[6], tail_in[8]
    q_ref, k_hbm, v_hbm, *attend_rest = attend_in
    pair_in, mixed_hbm, *side_rest = side_in
    *scratch, k_ref, v_ref, mixed_ref, hf_ref, bq_ref, turn_ref, w_ref, h_ref, x_ref, d_mixed_ref = scratch[:-2]
    tile_sem, load_sem = refs[-2:]

    def tile_copies(p):
        lanes = pl.ds(pl.multiple_of(p * LANES, LANES), LANES)
        return [
            pltpu.make_async_copy(source.at[:, lanes], target.at[:, lanes], tile_sem.at[n, p])
            for n, (source, target) in enumerate(((k_hbm, k_ref), (v_hbm, v_ref)))
        ]

    for p in range(PAIRS):
        for c in tile_copies(p):
            c.start()
    sources = (mixed_hbm, *(tail_in[k] for k in (0, 1, 2, 3, 4, 5, 7)))
    targets = (mixed_ref, hf_ref, bq_ref, turn_ref, w_ref, h_ref, x_ref, d_mixed_ref)
    loads = [pltpu.make_async_copy(a, b, load_sem.at[n]) for n, (a, b) in enumerate(zip(sources, targets))]
    for c in loads:
        c.start()

    def load(p):
        for c in tile_copies(p):
            c.wait()
        pl.when(p == 5)(loads[0].wait)

    attend_back_body(
        True, q_ref, k_ref, v_ref, *attend_rest, pair_in, mixed_ref, *side_rest, dq_ref, dkf_ref, out_ref, ends_ref,
        part_ref, *scratch[4:25], load=load,
    )
    for c in loads[1:]:
        c.wait()
    tail_body(
        dkf_ref, dq_ref, hf_ref, bq_ref, turn_ref, w_ref, h_ref, x_ref, gain_ref, d_mixed_ref, g_two_ref,
        side_in[2], ends_ref, part_ref, *tail_out, *scratch[25:],
    )


def back_tail(attend_in, side_in, tail_in):
    kf_window, g_rows, g_out = attend_in[5], side_in[2], side_in[3]
    x_parts = tail_in[5]
    parts, rows, feat = x_parts.shape
    units = g_rows.shape[2]
    block = (RANK_COLS // 4 + GROUP_COLS, feat)
    cols = (parts, 3, units, feat)
    mix = g_out.shape[2:]
    wide = g_rows.shape[1:]
    slot = kf_window.shape[1:]
    count = 2 + 2 + 3 + 8 + 4 + 3 + 1 + 1 + 3 + 3 + 3 + 1
    return pl.pallas_call(
        back_tail_body,
        out_shape=(
            jax.ShapeDtypeStruct(x_parts.shape, BF),
            jax.ShapeDtypeStruct(block, F32),
            jax.ShapeDtypeStruct(x_parts.shape, BF),
            jax.ShapeDtypeStruct(cols, BF),
            jax.ShapeDtypeStruct(cols, BF),
            jax.ShapeDtypeStruct(mix, BF),
            jax.ShapeDtypeStruct(mix, BF),
        ),
        in_specs=[VMEM, ANY, ANY] + [VMEM] * 4 + [ANY] * 4 + [VMEM] + [ANY] * 6 + [VMEM, ANY, VMEM],
        out_specs=(ANY, VMEM, ANY, VMEM, ANY, VMEM, ANY),
        scratch_shapes=[
            pltpu.VMEM((rows, D), F32),
            pltpu.VMEM(kf_window.shape, BF),
            pltpu.VMEM((2,) + wide, BF),
            pltpu.VMEM((4,) + mix, BF),
        ]
        + back_scratch(rows, 5 * rows)
        + [
            pltpu.VMEM((2, rows // 2, D), BF),
            pltpu.VMEM((2, rows // 2, D), BF),
            pltpu.VMEM((2, rows, D), BF),
            pltpu.VMEM((parts, rows, feat), BF),
            pltpu.VMEM((2,) + wide, BF),
            pltpu.VMEM((2,) + wide, BF),
            pltpu.VMEM((2,) + wide, BF),
            pltpu.VMEM((2, 4) + mix, BF),
            pltpu.VMEM((4,) + mix, BF),
            pltpu.VMEM((4,) + mix, BF),
            pltpu.VMEM((2, rows // 2, D), BF),
            pltpu.VMEM((rows, D), BF),
            pltpu.VMEM(g_rows.shape, BF),
            pltpu.VMEM((2, 4) + mix, BF),
            pltpu.SemaphoreType.DMA((25,)),
            pltpu.SemaphoreType.DMA((25,)),
            pltpu.SemaphoreType.DMA((13,)),
        ]
        + [
            pltpu.VMEM((rows, ALL_COLS), BF),
            pltpu.VMEM(x_parts.shape, BF),
            pltpu.VMEM((2,) + slot, BF),
            pltpu.VMEM((2,) + slot, BF),
            pltpu.VMEM((2,) + slot, BF),
            pltpu.VMEM(wide, BF),
            pltpu.VMEM(cols, BF),
            pltpu.VMEM((3,) + mix, BF),
            pltpu.VMEM((4, parts) + block, BF),
            pltpu.VMEM((2, 4) + block, BF),
            pltpu.VMEM((4,) + block, BF),
            pltpu.VMEM((4,) + block, BF),
            pltpu.VMEM((4,) + block, BF),
            pltpu.VMEM((3,) + block, BF),
            pltpu.VMEM(block, BF),
            pltpu.VMEM(block, BF),
            pltpu.SemaphoreType.DMA((count,)),
            pltpu.SemaphoreType.DMA((count,)),
            pltpu.SemaphoreType.DMA((2,)),
        ]
        + [
            pltpu.VMEM(a.shape, a.dtype)
            for a in (attend_in[1], attend_in[2], side_in[1], *(tail_in[k] for k in (0, 1, 2, 3, 4, 5, 7)))
        ]
        + [pltpu.SemaphoreType.DMA((2, PAIRS)), pltpu.SemaphoreType.DMA((8,))],
        compiler_params=comm_params(7),
        cost_estimate=cost_of(2 * rows * 5 * rows * D * 40, 40 << 20),
    )(*attend_in, *side_in, *tail_in)


def layout_body(
    grad_ref, gi_ref, cols_ref, other_ref, mix_ref, mix_other_ref, y_ref,
    y_out_ref, gi_out_ref, gain_ref, gain_two_ref, heads_ref, ranks_ref, out_ref, gate_ref, up_ref, down_ref,
):
    first = lax.axis_index("dp") == 0
    y_out_ref[...] = y_ref[...]
    gi_out_ref[...] = gi_ref[...].astype(F32)
    out_ref[...] = mix_ref[...].astype(F32) + mix_other_ref[...].astype(F32)
    ranks = ranks_ref.shape[0]
    used = heads_ref.shape[0]
    gain_ref[...] = grad_ref[ranks + used : ranks + used + 1]
    gain_two_ref[...] = grad_ref[ranks + used + 1 : ranks + used + 2]
    ranks_ref[...] = grad_ref[:ranks]
    lane = lax.broadcasted_iota(jnp.int32, (used, GROUP_COLS), 1)
    place = lax.broadcasted_iota(jnp.int32, (used, GROUP_COLS), 0)
    factor = place % FAC
    spot = jnp.where(factor < RQ, factor + 2 * RK, factor - RQ) * GROUP + place // FAC
    heads_ref[...] = jnp.dot(
        (lane == spot).astype(F32), grad_ref[ranks:], precision=lax.Precision.HIGHEST, preferred_element_type=F32
    )
    part = down_ref.shape[0] // 8
    for k, target in ((0, gate_ref), (1, up_ref), (2, down_ref)):
        for c in range(4):
            own = cols_ref[c, k].astype(F32)[:part]
            other = other_ref[c, k].astype(F32)[:part]
            target[c * part : (c + 1) * part] = jnp.where(first, own, other)
            target[(4 + c) * part : (5 + c) * part] = jnp.where(first, other, own)


def layout(grad, gi, cols, other, mix, mix_other, y, heads, ranks, hidden):
    feat = grad.shape[1]
    weight = jax.ShapeDtypeStruct((hidden, feat), F32)
    gain = jax.ShapeDtypeStruct((1, feat), F32)
    return call(
        layout_body,
        (
            jax.ShapeDtypeStruct(y.shape, y.dtype),
            jax.ShapeDtypeStruct(gi.shape, F32),
            gain,
            gain,
            jax.ShapeDtypeStruct((heads, feat), F32),
            jax.ShapeDtypeStruct((ranks, feat), F32),
            jax.ShapeDtypeStruct(mix.shape, F32),
            weight,
            weight,
            weight,
        ),
        cost=cost_of(0, 8 << 20),
    )(grad, gi, cols, other, mix, mix_other, y)


def local(
    tokens_in, segments, gain_attn, gain_ffn, w_heads, w_ranks, w_out, w_gate, w_up, w_down, cotangent
):
    n_row = lax.axis_size("row")
    n_col = lax.axis_size("col")
    row = lax.axis_index("row")
    col = lax.axis_index("col")
    micro, row_tokens, feat = tokens_in.shape
    subs = n_col // micro
    rows = row_tokens // subs
    length = row_tokens * n_row
    head_local = w_heads.shape[1] // FAC
    rank_local = w_ranks.shape[1]
    ffn_local = w_gate.shape[1]
    out_local = w_out.shape[0]
    block = row * subs + col % subs
    past = min(-(-(MAX_DOC - 1) // rows), n_row * subs - 1)
    keys = (past + 1) * rows

    dp_count = lax.axis_size("dp")
    fast = n_col == 4 and n_row == 4 and dp_count == 2 and micro == 2 and past == 4

    tokens = tokens_in.reshape(n_col, rows, feat)
    turns = (ROPE ** (-(np.arange(HD // 2) * 2.0 / HD))).astype(np.float32)
    if not fast:
        inverse = ROPE ** (-(jnp.arange(HD // 2, dtype=F32) * 2.0 / HD))
        heads_t = jnp.transpose(w_heads.reshape(feat, head_local, FAC), (2, 1, 0))
        heads_t = heads_t[jnp.array(FAC_ORDER)].reshape(FAC * head_local, feat)
        pad = jnp.zeros((GROUP_COLS - FAC * head_local, feat), BF)
        w_own = jnp.concatenate([w_ranks.T, heads_t, pad], axis=0)
        gains_own = jnp.concatenate([gain_attn[None], gain_ffn[None], jnp.zeros((6, feat), F32)], axis=0)
        part = ffn_local // n_col
        units = part * n_row
        w_ffn = jnp.stack([w_gate.T, w_up.T, w_down]).reshape(3, n_col, part, feat)
        w_ffn = lax.all_to_all(jnp.transpose(w_ffn, (1, 0, 2, 3)), "col", 0, 0, tiled=True)
        w_ffn = jnp.transpose(w_ffn, (1, 2, 0, 3)).reshape(3, part, D)
        w_ffn = jnp.transpose(lax.all_gather(w_ffn, "row", axis=0), (1, 0, 2, 3)).reshape(3, units, D)
        w_blocks = lax.all_gather(w_own, ("row", "col"), axis=0).reshape((n_row, n_col) + w_own.shape)
        gains = lax.all_gather(gains_own, "col", axis=0)
        x_parts = lax.all_to_all(tokens, "col", 0, 0, tiled=True)
        w_out_all = lax.all_gather(w_out, ("row", "col"), axis=0).reshape((n_row, n_col) + w_out.shape)

        seg_row = lax.dynamic_index_in_dim(segments, col // subs, 0, keepdims=False)
        padded = jnp.concatenate([jnp.full((1, past * rows), -1, jnp.int32), seg_row], axis=1)
        seg_window = lax.dynamic_slice_in_dim(padded, block * rows, keys, 1)
        own_seg = seg_window[0, past * rows :]
        key_idx = jnp.arange(keys, dtype=jnp.int32)
        query_idx = jnp.arange(rows, dtype=jnp.int32) + past * rows
        before = (own_seg[:, None] == seg_window) & (key_idx[None, :] < query_idx[:, None])
        places = jnp.sum(before.astype(jnp.int32), axis=1)
        angles = places.astype(F32)[:, None] * inverse[None, :]
        cosine = jnp.cos(angles)
        sine = jnp.sin(angles)
        turn = jnp.concatenate([cosine] * 4 + [-sine, sine, -sine, sine], axis=1)

    groups = [[m * subs + s for s in range(subs)] for m in range(micro)]
    if fast:
        cot_rows = cotangent.reshape(micro * row_tokens, feat)
        (
            x_parts, gains, ffn_parts, mixes, h_one, head_fac, bq_rot, queries, w_rh, kf_window, seg_window, turn, w_rows,
            heads_out, lse, key_all, value_all, cot_near,
        ) = head_attend(
            tokens, w_ranks.T, w_heads.T, gain_attn.reshape(1, feat), gain_ffn.reshape(1, feat), w_gate.T, w_up.T,
            w_down, w_out, segments, np.tile(turns, 4).reshape(1, LANES), cot_rows,
        )
        mixed, d_mixed, d_heads, g_out, g_gain_two, g_rows, out_pair, hop = middle(
            x_parts, heads_out, mixes, gains, cot_rows, cot_near, ffn_parts, w_rows
        )
        output, g_rh, grad_input, g_cols, cols_other, g_out, out_other = back_tail(
            (queries, key_all, value_all, d_heads, lse, kf_window, seg_window),
            (out_pair, mixed, g_rows, g_out, hop),
            (head_fac, bq_rot, turn, w_rh, h_one, x_parts, gains, d_mixed, g_gain_two),
        )
        output, grad_input, g_one, g_two, own_heads, own_ranks, g_out, own_gate, own_up, own_down = layout(
            g_rh, grad_input, g_cols, cols_other, g_out, out_other, output, w_heads.shape[1], w_ranks.shape[1], ffn_local
        )
        return (
            output.reshape(tokens_in.shape),
            grad_input.reshape(tokens_in.shape),
            g_one.reshape(feat),
            g_two.reshape(feat),
            own_heads.T,
            own_ranks.T,
            g_out,
            own_gate.T,
            own_up.T,
            own_down,
        )
    else:
        h_one, head_fac, bq_rot, key_fac, queries, w_rh = front(x_parts, gains, w_blocks, turn)
        gathered = lax.all_gather(key_fac, "row", axis=0)
        gathered = lax.all_gather(gathered, "col", axis=1, axis_index_groups=groups)
        gathered = gathered.reshape(length, key_fac.shape[1])
        padded_kf = jnp.concatenate([jnp.zeros((past * rows, key_fac.shape[1]), BF), gathered], axis=0)
        kf_window = lax.dynamic_slice_in_dim(padded_kf, block * rows, keys, 0)
        heads_out, lse, key_all, value_all = attend(queries, kf_window, seg_window)
        mixed, h_two = mixing(x_parts, heads_out, w_out_all, gains)
        cot_own = lax.all_to_all(cotangent.reshape(n_col, rows, feat), "col", 0, 0, tiled=True)
        cot_own = jnp.transpose(cot_own, (1, 0, 2)).reshape(rows, D)
        cot_all = lax.all_gather(cot_own, "col", axis=0)
        h_all = lax.all_gather(h_two, "col", axis=0)
        out_part, dh_part, g_ffn = ffn(h_all, cot_all, w_ffn)
        dh_sum = lax.psum_scatter(dh_part, "col", scatter_dimension=0, tiled=False).astype(F32)
        out_sum = lax.psum_scatter(out_part, "col", scatter_dimension=0, tiled=False).astype(F32)
        out_parts, d_mixed, d_heads, g_out, g_gain_two = unmix(
            dh_sum, out_sum, mixed, cot_own, heads_out, w_out_all, gains
        )
        d_q, d_kf = attend_back(queries, key_all, value_all, d_heads, lse, kf_window, seg_window)
        spread_kf = jnp.zeros((past * rows + length, d_kf.shape[1]), BF)
        spread_kf = lax.dynamic_update_slice_in_dim(spread_kf, d_kf, block * rows, 0)[past * rows :]
        spread_kf = spread_kf.reshape(n_row, subs, rows, -1)
        own_kf = lax.psum_scatter(spread_kf, "row", scatter_dimension=0, tiled=False)
        own_kf = lax.psum_scatter(own_kf, "col", scatter_dimension=0, tiled=False, axis_index_groups=groups)
        gi_parts, g_rh = back(
            d_q, own_kf, head_fac, bq_rot, turn, w_rh, h_one, x_parts, gains, d_mixed, g_gain_two, n_row
        )
        output = lax.all_to_all(out_parts, "col", 0, 0, tiled=True)
        grad_input = lax.all_to_all(gi_parts, "col", 0, 0, tiled=True)
        g_ffn = lax.psum_scatter(g_ffn.reshape(3, n_row, part, D), "row", scatter_dimension=1, tiled=False)
        g_ffn = jnp.transpose(lax.psum(g_ffn, "dp").reshape(3, part, n_col, feat), (2, 0, 1, 3))
        g_ffn = lax.all_to_all(g_ffn, "col", 0, 0, tiled=True)
        g_ffn = jnp.transpose(g_ffn, (1, 0, 2, 3)).reshape(3, ffn_local, feat).astype(F32)

        def total(values):
            values = values.reshape((n_row * n_col,) + values.shape[2:])
            values = lax.psum_scatter(values, ("row", "col"), scatter_dimension=0, tiled=False)
            return lax.psum(values, "dp").astype(F32)

        g_out = total(g_out)
        g_rh = total(g_rh)

    used = rank_local + FAC * head_local
    own_heads = g_rh[rank_local:used].reshape(FAC, head_local, feat)
    own_heads = jnp.transpose(own_heads[jnp.array(FAC_BACK)], (2, 1, 0)).reshape(w_heads.shape)
    return (
        output.reshape(tokens_in.shape),
        grad_input.reshape(tokens_in.shape),
        g_rh[used],
        g_rh[used + 1],
        own_heads,
        g_rh[:rank_local].T,
        g_out,
        g_ffn[0].T,
        g_ffn[1].T,
        g_ffn[2],
    )


def solution(mesh):
    tokens = P(None, ("dp", "row"), "col")
    both = P("col", "row")
    turned = P("row", "col")
    gain = P("col")
    return jax.shard_map(
        local,
        mesh=mesh,
        in_specs=(tokens, P(None, "dp", None), gain, gain, both, both, turned, both, both, turned, tokens),
        out_specs=(tokens, tokens, gain, gain, both, both, turned, both, both, turned),
        check_vma=False,
    )
```

```python
import functools

import jax
import jax.numpy as jnp
import numpy as np
from jax import lax
from jax.experimental import pallas as pl
from jax.experimental.pallas import tpu as pltpu
from jax.sharding import PartitionSpec as P

D = 1024
H = 16
HD = 64
RQ = 6
RK = 2
FAC = 10
MAX_DOC = 1024

EPS = 1e-06
ROPE = 10000.0
NEG = -1e30
BF = jnp.bfloat16
F32 = jnp.float32
LANES = 128
PAIRS = H // 2
FAC_ORDER = (6, 7, 8, 9, 0, 1, 2, 3, 4, 5)
FAC_BACK = (4, 5, 6, 7, 8, 9, 0, 1, 2, 3)
VMEM = pl.BlockSpec(memory_space=pltpu.VMEM)


def nn(a, b):
    return jnp.dot(a, b, preferred_element_type=F32)


def nt(a, b):
    return lax.dot_general(a, b, (((1,), (1,)), ((), ())), preferred_element_type=F32)


def tn(a, b):
    return lax.dot_general(a, b, (((0,), (0,)), ((), ())), preferred_element_type=F32)


def two_pass(a, b):
    high = a.astype(BF)
    low = (a - high.astype(F32)).astype(BF)
    return nn(high, b) + nn(low, b)


def lane_iota(shape):
    return lax.broadcasted_iota(jnp.int32, shape, len(shape) - 1)


def spread(rows, first, width):
    row = lax.broadcasted_iota(jnp.int32, (rows, width), 0)
    head = lax.broadcasted_iota(jnp.int32, (rows, width), 1) // HD
    return (row == head + first).astype(F32).astype(BF)


def collect(rows, width, first):
    head = lax.broadcasted_iota(jnp.int32, (rows, width), 0) // HD
    lane = lax.broadcasted_iota(jnp.int32, (rows, width), 1)
    return (lane == head + first).astype(F32).astype(BF)


GROUP = 4
GROUP_COLS = 48
RANK_COLS = FAC * HD
HEAD_COLS = H // GROUP * GROUP_COLS
ALL_COLS = RANK_COLS + HEAD_COLS


def factor_place(head, j):
    return head // GROUP * GROUP_COLS + j * GROUP + head % GROUP


def head_spread(j, first_head, width):
    row = lax.broadcasted_iota(jnp.int32, (HEAD_COLS, width), 0)
    head = lax.broadcasted_iota(jnp.int32, (HEAD_COLS, width), 1) // HD + first_head
    return (row == factor_place(head, j)).astype(F32).astype(BF)


def head_collect(j):
    head = lax.broadcasted_iota(jnp.int32, (D, HEAD_COLS), 0) // HD
    lane = lax.broadcasted_iota(jnp.int32, (D, HEAD_COLS), 1)
    return (lane == factor_place(head, j)).astype(F32).astype(BF)


def key_columns():
    row = lax.broadcasted_iota(jnp.int32, (HEAD_COLS, LANES), 0)
    lane = lax.broadcasted_iota(jnp.int32, (HEAD_COLS, LANES), 1)
    taken = (row == factor_place(lane % H, lane // H)) & (lane < 2 * RK * H)
    return taken.astype(F32).astype(BF)


def swap_halves(tile):
    lane = lane_iota(tile.shape)
    ahead = pltpu.roll(tile, LANES - HD // 2, 1)
    behind = pltpu.roll(tile, HD // 2, 1)
    return jnp.where(lane % HD < HD // 2, ahead, behind)


def double_left(tile):
    return jnp.where(lane_iota(tile.shape) < HD, tile, pltpu.roll(tile, HD, 1))


def double_right(tile):
    return jnp.where(lane_iota(tile.shape) < HD, pltpu.roll(tile, HD, 1), tile)


def params(**more):
    return pltpu.CompilerParams(vmem_limit_bytes=60 << 20, **more)


def call(body, outs, scratch=(), cost=None):
    return pl.pallas_call(
        body,
        out_shape=outs,
        scratch_shapes=scratch,
        compiler_params=params(),
        cost_estimate=cost,
    )


def cost_of(flops, moved):
    return pl.CostEstimate(flops=int(flops), bytes_accessed=int(moved), transcendentals=0)


MESH = pl.DeviceIdType.MESH
ANY = pl.BlockSpec(memory_space=pl.ANY)


class Mover:
    def __init__(self, send_sem, recv_sem):
        self.send_sem = send_sem
        self.recv_sem = recv_sem
        self.used = 0

    def copy(self, source, target, **place):
        index = self.used
        self.used += 1
        return pltpu.make_async_remote_copy(
            src_ref=source,
            dst_ref=target,
            send_sem=self.send_sem.at[index],
            recv_sem=self.recv_sem.at[index],
            device_id=place,
            device_id_type=MESH,
        )


def greet(partners):
    barrier = pltpu.get_barrier_semaphore()
    count = 0
    for present, place in partners:
        if present is None:
            pl.semaphore_signal(barrier, inc=1, device_id=place, device_id_type=MESH)
            count = count + 1
        else:

            @pl.when(present)
            def _():
                pl.semaphore_signal(barrier, inc=1, device_id=place, device_id_type=MESH)

            count = count + present.astype(jnp.int32)
    pl.semaphore_wait(barrier, count)


def neighbours():
    col = lax.axis_index("col")
    core = col + 1 - 2 * lax.rem(col, 2)
    across = lax.rem(col + 2, 4)
    return col, core, across


def square():
    dp = lax.axis_index("dp")
    x = lax.axis_index("col") // 2
    return dp, (dp * 2 + x, dp * 2 + 1 - x, (1 - dp) * 2 + x, (1 - dp) * 2 + 1 - x)


def comm_params(ident):
    return params(collective_id=ident, has_side_effects=True)


class AttendCopies:
    def __init__(self, cot_ref, rows_ref, near_ref, mixes_ref, send_sem, recv_sem):
        row = lax.axis_index("row")
        col, core, across = neighbours()
        dp, (me, on_x, on_y, _) = square()
        mover = Mover(send_sem, recv_sem)
        self.left = row >= 1
        self.right = row <= 2
        self.both = jnp.logical_and(self.left, self.right)
        self.from_left = row >= 2
        self.from_right = row <= 1
        self.row = row
        cuts = [pl.ds(0, 2), pl.ds(2, 2)]
        lower, upper = rows_ref.at[jnp.maximum(row - 1, 0)], rows_ref.at[jnp.minimum(row + 1, 3)]
        self.pass_right = [mover.copy(lower.at[c], lower.at[c], row=row + 1) for c in cuts]
        self.pass_left = [mover.copy(upper.at[c], upper.at[c], row=row - 1) for c in cuts]
        self.last_right = [mover.copy(rows_ref.at[0, c], rows_ref.at[0, c], row=row + 1) for c in cuts]
        self.last_left = [mover.copy(rows_ref.at[3, c], rows_ref.at[3, c], row=row - 1) for c in cuts]
        half = cot_ref.shape[0] // 2
        top, low = pl.ds(0, half), pl.ds(half, half)
        self.cots = [
            mover.copy(cot_ref.at[low], near_ref.at[me, low], col=across),
            mover.copy(cot_ref.at[top], near_ref.at[me, top], dp=1 - dp),
            mover.copy(cot_ref.at[top], near_ref.at[me, top], col=across),
            mover.copy(cot_ref.at[low], near_ref.at[me, low], dp=1 - dp),
        ]
        self.relays = [
            mover.copy(near_ref.at[on_x, low], near_ref.at[on_x, low], dp=1 - dp),
            mover.copy(near_ref.at[on_y, top], near_ref.at[on_y, top], col=across),
        ]
        self.mixes = []
        for r in range(4):
            for c in (col, across):
                self.mixes.append(mover.copy(mixes_ref.at[r, c], mixes_ref.at[r, c], col=core))

    def first(self):
        for k in range(2):
            pl.when(self.both)(self.pass_right[k].start)
            pl.when(self.both)(self.pass_left[k].start)
        for c in self.cots:
            c.start()

    def early(self):
        self.head_end()
        for c in self.mixes:
            c.start()
        self.hand_on(0)

    def hand_on(self, k):
        pl.when(self.from_left)(self.pass_right[k].wait_recv)
        pl.when(self.from_right)(self.pass_left[k].wait_recv)
        pl.when(self.row == 2)(self.last_right[k].start)
        pl.when(self.row == 1)(self.last_left[k].start)

    def second(self):
        for c in self.cots[:2]:
            c.wait_recv()
        for c in self.relays:
            c.start()
        self.hand_on(1)

    def last(self):
        for k in range(2):
            pl.when(self.both)(self.pass_right[k].wait_send)
            pl.when(self.both)(self.pass_left[k].wait_send)
            pl.when(self.row == 2)(self.last_right[k].wait_send)
            pl.when(self.row == 1)(self.last_left[k].wait_send)
            pl.when(self.row == 3)(self.last_right[k].wait_recv)
            pl.when(self.row == 0)(self.last_left[k].wait_recv)
        for c in self.cots[:2]:
            c.wait_send()
        for c in self.cots[2:] + self.relays + self.mixes:
            c.wait()


class BackCopies:
    def __init__(self, refs, sems):
        (
            self.pair_ref, self.mixed_ref, self.rows_ref, self.g_out_ref, self.hop_ref,
            self.out_ref, self.ends_ref, self.part_ref,
            self.relay_ref, self.diag_ref, self.far_ref, self.send_ref,
            self.right_ref, self.left_ref, self.got_ref,
            self.near_ref, self.side_ref, self.across_ref,
            self.pieces_ref, self.mine_ref, self.rows_in_ref, self.g_in_ref,
        ) = refs
        send_sem, recv_sem, local_sem = sems
        self.row = row = lax.axis_index("row")
        self.col, core, across = col, _, _ = neighbours()
        cross = lax.rem(core + 2, 4)
        self.dp, self.spots = dp, (me, on_x, on_y, on_both) = square()
        mover = Mover(send_sem, recv_sem)
        self.x, self.mine = x, mine = col // 2, lax.rem(col, 2)
        self.partners = [(None, {"col": c}) for c in (core, across, cross)]
        self.partners += [(None, {"dp": 1 - dp})] + [(None, {"row": lax.rem(row + k, 4)}) for k in range(1, 4)]
        half = self.pair_ref.shape[1] // 2
        top, low = pl.ds(0, half), pl.ds(half, half)
        y = 1 - dp
        self.diag = [
            mover.copy(self.pair_ref.at[on_both, top], self.diag_ref.at[0], col=across),
            mover.copy(self.pair_ref.at[on_both, low], self.diag_ref.at[1], dp=y),
        ]
        self.far = [
            mover.copy(self.pair_ref.at[on_x, top], self.far_ref.at[0, top], col=across),
            mover.copy(self.pair_ref.at[on_y, low], self.far_ref.at[1, low], dp=y),
            mover.copy(self.relay_ref.at[0], self.far_ref.at[1, top], dp=y),
            mover.copy(self.relay_ref.at[1], self.far_ref.at[0, low], col=across),
        ]
        self.out = [mover.copy(self.send_ref.at[c], self.out_ref.at[col], col=c) for c in (across, cross, core)]
        self.own = pltpu.make_async_copy(self.send_ref.at[col], self.out_ref.at[col], local_sem.at[0])
        self.hop_right = [
            mover.copy(self.right_ref.at[0], self.got_ref.at[0], row=row + 1),
            mover.copy(self.right_ref.at[1], self.ends_ref.at[0], row=row + 1),
        ]
        self.hop_left = [
            mover.copy(self.left_ref.at[0], self.got_ref.at[1], row=row - 1),
            mover.copy(self.left_ref.at[1], self.ends_ref.at[1], row=row - 1),
        ]
        self.cores = [
            mover.copy(self.g_out_ref.at[r, k * 2 + 1 - mine], self.near_ref.at[k, r], col=core)
            for k in range(2)
            for r in range(4)
        ]
        self.sides = [mover.copy(self.side_ref.at[r], self.across_ref.at[r], col=across) for r in range(4)]
        self.loads = [
            pltpu.make_async_copy(self.pair_ref.at[on_y, top], self.pieces_ref.at[0], local_sem.at[1]),
            pltpu.make_async_copy(self.pair_ref.at[on_x, low], self.pieces_ref.at[1], local_sem.at[2]),
            pltpu.make_async_copy(self.pair_ref.at[me], self.mine_ref, local_sem.at[3]),
        ]
        self.rows_load = pltpu.make_async_copy(self.rows_ref, self.rows_in_ref, local_sem.at[4])
        self.g_loads = [
            pltpu.make_async_copy(
                self.g_out_ref.at[r, lax.rem(x + k, 2) * 2 + mine], self.g_in_ref.at[k, r], local_sem.at[5 + 4 * k + r]
            )
            for k in range(2)
            for r in range(4)
        ]

    def first(self):
        row = self.row
        self.rows_load.start()
        for c in self.loads + self.g_loads:
            c.start()
        greet(self.partners)
        for c in self.diag + self.far[:2] + self.cores:
            c.start()
        self.rows_load.wait()
        hop = self.hop_ref[...].astype(F32)
        ahead = self.rows_in_ref[jnp.minimum(row + 2, 3)].astype(F32)
        self.right_ref[0] = jnp.where(row == 1, ahead + hop, ahead).astype(BF)
        behind = self.rows_in_ref[jnp.maximum(row - 2, 0)].astype(F32)
        self.left_ref[0] = jnp.where(row == 2, behind + hop, behind).astype(BF)
        pl.when(row <= 1)(self.hop_right[0].start)
        pl.when(row >= 2)(self.hop_left[0].start)

    def cross_x(self):
        for c in self.g_loads:
            c.wait()
        for c in self.cores:
            c.wait_recv()
        for r in range(4):
            self.side_ref[r] = (
                self.g_in_ref[1, r].astype(F32) + self.near_ref[1 - self.x, r].astype(F32)
            ).astype(BF)
            self.sides[r].start()

    def second(self):
        row = self.row
        for c in self.loads:
            c.wait()
        for k in range(2):
            self.diag[k].wait_recv()
            self.relay_ref[k] = (self.pieces_ref[k].astype(F32) + self.diag_ref[k].astype(F32)).astype(BF)
            self.far[2 + k].start()

    def last_hop(self):
        row = self.row
        middle = jnp.logical_and(row >= 1, row <= 2)
        pl.when(middle)(self.hop_right[0].wait_recv)
        pl.when(middle)(self.hop_left[0].wait_recv)
        ahead = self.rows_in_ref[jnp.minimum(row + 1, 3)].astype(F32)
        behind = self.rows_in_ref[jnp.maximum(row - 1, 0)].astype(F32)
        self.right_ref[1] = jnp.where(row >= 1, ahead + self.got_ref[0].astype(F32), ahead).astype(BF)
        self.left_ref[1] = jnp.where(row <= 2, behind + self.got_ref[1].astype(F32), behind).astype(BF)
        pl.when(row <= 2)(self.hop_right[1].start)
        pl.when(row >= 1)(self.hop_left[1].start)

    def third(self):
        row = self.row
        for c in self.far:
            c.wait_recv()
        feat = self.send_ref.shape[2]
        for c in range(4):
            lanes = slice(c * feat, (c + 1) * feat)
            self.send_ref[c] = (
                self.mixed_ref[:, lanes]
                + self.mine_ref[:, lanes].astype(F32)
                + self.far_ref[0, :, lanes].astype(F32)
                + self.far_ref[1, :, lanes].astype(F32)
            ).astype(BF)
        for c in self.out:
            c.start()
        self.own.start()

    def last(self):
        row = self.row
        for r in range(4):
            self.sides[r].wait_recv()
            self.part_ref[r] = (
                self.g_in_ref[0, r].astype(F32)
                + self.near_ref[self.x, r].astype(F32)
                + self.across_ref[r].astype(F32)
            ).astype(BF)
        for c in self.out:
            c.wait()
        self.own.wait()
        for c in self.diag + self.far + self.cores + self.sides:
            c.wait_send()
        pl.when(row <= 1)(self.hop_right[0].wait_send)
        pl.when(row >= 2)(self.hop_left[0].wait_send)
        pl.when(row <= 2)(self.hop_right[1].wait_send)
        pl.when(row >= 1)(self.hop_left[1].wait_send)
        pl.when(row >= 1)(self.hop_right[1].wait_recv)
        pl.when(row <= 2)(self.hop_left[1].wait_recv)


def first_norm(x_ref, gain_ref, h_ref):
    parts = x_ref.shape[0]
    feat = x_ref.shape[2]
    xs = [x_ref[c].astype(F32) for c in range(parts)]
    total = sum(jnp.sum(v * v, axis=1, keepdims=True) for v in xs)
    scale = lax.rsqrt(total / D + EPS)
    for c in range(parts):
        lanes = slice(c * feat, (c + 1) * feat)
        h_ref[:, lanes] = (xs[c] * scale * gain_ref[c, :1]).astype(BF)


def place_factor_weights(blocks_ref, w_ref):
    n_row, parts, _, feat = blocks_ref.shape
    ranks_each = RANK_COLS // n_row
    for c in range(parts):
        lanes = slice(c * feat, (c + 1) * feat)
        for r in range(n_row):
            w_ref[r * ranks_each : (r + 1) * ranks_each, lanes] = blocks_ref[r, c, :ranks_each]
            w_ref[RANK_COLS + r * GROUP_COLS : RANK_COLS + (r + 1) * GROUP_COLS, lanes] = blocks_ref[
                r, c, ranks_each:
            ]


def make_factors(h_ref, w_ref, turn_ref, hf_ref, bq_ref, kf_ref):
    both = nt(h_ref[...], w_ref[...])
    heads = both[:, RANK_COLS:]
    hf_ref[...] = heads
    cosine = turn_ref[:, :LANES]
    sine = turn_ref[:, LANES:]
    for tile in range(RANK_COLS // LANES):
        lanes = slice(tile * LANES, (tile + 1) * LANES)
        part = both[:, lanes]
        if tile < 4:
            part = part * cosine + swap_halves(part) * sine
        if tile < 3:
            bq_ref[:, lanes] = part
        else:
            kf_ref[:, (tile - 3) * LANES : (tile - 2) * LANES] = part.astype(BF)
    kf_ref[:, 2 * LANES :] = nn(heads.astype(BF), key_columns()).astype(BF)


def make_queries(hf_ref, bq_ref, q_ref):
    heads = hf_ref[...]
    high = heads.astype(BF)
    low = (heads - high.astype(F32)).astype(BF)
    ranks = []
    for r in range(RQ):
        tile = bq_ref[:, (r // 2) * LANES : (r // 2 + 1) * LANES]
        ranks.append(double_left(tile) if r % 2 == 0 else double_right(tile))
    width = 2 * LANES
    for p in range(D // width):
        lanes = slice(p * width, (p + 1) * width)
        acc = None
        for r in range(RQ):
            pick = head_spread(2 * RK + r, p * (width // HD), width)
            term = (nn(high, pick) + nn(low, pick)) * jnp.concatenate([ranks[r]] * 2, axis=1)
            acc = term if acc is None else acc + term
        q_ref[:, lanes] = (acc / RQ).astype(BF)


def front_body(x_ref, gain_ref, blocks_ref, turn_ref, h_ref, hf_ref, bq_ref, kf_ref, q_ref, w_ref):
    first_norm(x_ref, gain_ref, h_ref)
    place_factor_weights(blocks_ref, w_ref)
    make_factors(h_ref, w_ref, turn_ref, hf_ref, bq_ref, kf_ref)
    make_queries(hf_ref, bq_ref, q_ref)


def front(x_parts, gains, blocks, turn):
    rows = x_parts.shape[1]
    return call(
        front_body,
        (
            jax.ShapeDtypeStruct((rows, D), BF),
            jax.ShapeDtypeStruct((rows, HEAD_COLS), F32),
            jax.ShapeDtypeStruct((rows, RQ * HD), F32),
            jax.ShapeDtypeStruct((rows, 3 * LANES), BF),
            jax.ShapeDtypeStruct((rows, D), BF),
            jax.ShapeDtypeStruct((ALL_COLS, D), BF),
        ),
        cost=cost_of(2 * rows * D * 800 * 3, 6 << 20),
    )(x_parts, gains, blocks, turn)


def head_body(
    tok_ref, ranks_ref, heads_ref, gain_one_ref, gain_two_ref, gate_ref, up_ref, down_ref, mix_ref, seg_all_ref,
    inverse_ref,
    x_ref, gains_ref, parts_ref, mixes_ref, h_ref, hf_ref, bq_ref, q_ref, w_ref, win_ref, seg_ref, turn_ref, rows_ref,
    w_own_ref, gain_ref, ffn_ref, blocks_ref, send_sem, recv_sem, next_copies,
):
    row = lax.axis_index("row")
    col, core, across = neighbours()
    cross = lax.rem(core + 2, 4)
    side = lax.rem(col, 2)
    rows = [lax.rem(row + k, 4) for k in range(4)]
    back = [lax.rem(row + 4 - k, 4) for k in range(4)]
    dp = lax.axis_index("dp")

    rank_rows = ranks_ref.shape[0]
    place = lax.broadcasted_iota(jnp.int32, (GROUP_COLS, FAC * GROUP), 0)
    lane = lax.broadcasted_iota(jnp.int32, (GROUP_COLS, FAC * GROUP), 1)
    factor = lane % FAC
    spot = jnp.where(factor < RQ, factor + 2 * RK, factor - RQ) * GROUP + lane // FAC
    w_own_ref[:rank_rows] = ranks_ref[...]
    w_own_ref[rank_rows:] = nn((place == spot).astype(F32).astype(BF), heads_ref[...]).astype(BF)
    gain_ref[...] = jnp.zeros_like(gain_ref)
    gain_ref[0:1] = gain_one_ref[...]
    gain_ref[1:2] = gain_two_ref[...]
    greet(
        [(None, {"col": c}) for c in (core, across, cross)]
        + [(None, {"row": r}) for r in rows[1:]]
        + [(None, {"dp": 1 - dp})]
    )
    mover = Mover(send_sem, recv_sem)
    started = []

    def go(source, target, **place):
        c = mover.copy(source, target, **place)
        c.start()
        started.append(c)
        return c

    down = [None] + [go(w_own_ref, blocks_ref.at[row, col], row=rows[k]) for k in range(1, 4)]
    sides = [go(w_own_ref, blocks_ref.at[row, col], col=across)]
    cores = [go(w_own_ref, blocks_ref.at[row, col], col=core)]
    toks = []
    rest = []
    for c in (across, cross, core):
        toks.append(go(gain_ref, gains_ref.at[col], col=c))
        toks.append(go(tok_ref.at[c], x_ref.at[col], col=c))
    units = ffn_ref.shape[2]
    hidden = gate_ref.shape[0]
    unit = hidden // 8
    place = lax.broadcasted_iota(jnp.int32, (4 * units, hidden), 0)
    lane = lax.broadcasted_iota(jnp.int32, (4 * units, hidden), 1)
    inside = place % units
    taken = (inside < unit) & (lane == (dp * 4 + place // units) * unit + inside)
    pick = taken.astype(F32).astype(BF)
    for k, source in enumerate((gate_ref, up_ref, down_ref)):
        chosen = nn(pick, source[...]).astype(BF)
        for c in range(4):
            ffn_ref[c, k] = chosen[c * units : (c + 1) * units]
    ffn = [go(ffn_ref.at[c], parts_ref.at[col], col=c) for c in (across, cross, core)]
    part = mix_ref.shape[0] // 2
    half = pl.ds(pl.multiple_of(dp * part, part), part)
    mix_down = [None] + [go(mix_ref.at[half], mixes_ref.at[row, col, half], row=rows[k]) for k in range(1, 4)]
    blocks_ref[row, col] = w_own_ref[...]
    gains_ref[col] = gain_ref[...]
    x_ref[col] = tok_ref[col]
    parts_ref[col] = ffn_ref[col]
    mixes_ref[row, col] = mix_ref[...]
    zero = jnp.zeros(win_ref.shape[1:], BF)
    has_one = row >= 1
    has_two = row >= 2
    for absent, slot in (
        (jnp.logical_not(has_two), 0),
        (jnp.logical_and(jnp.logical_not(has_two), side == 0), 1),
        (jnp.logical_and(jnp.logical_not(has_one), side == 1), 1),
        (jnp.logical_not(has_one), 2),
        (jnp.logical_and(jnp.logical_not(has_one), side == 0), 3),
    ):

        @pl.when(absent)
        def _():
            win_ref[slot] = zero

    keys = seg_ref.shape[1]
    tokens = tok_ref.shape[1]
    block_no = row * 2 + side
    for slot in range(5):
        index = block_no - 4 + slot
        lanes = pl.ds(pl.multiple_of(jnp.maximum(index, 0) * tokens, tokens), tokens)
        seg_ref[:, slot * tokens : (slot + 1) * tokens] = jnp.where(index >= 0, seg_all_ref[col // 2, :, lanes], -1)
    seg_row = seg_ref[...].astype(F32)
    column = jnp.broadcast_to(seg_row, (LANES, keys)).T
    column = jnp.concatenate([column] * (tokens // LANES), axis=1)
    key_idx = lax.broadcasted_iota(jnp.int32, (keys, tokens), 0)
    query_idx = lax.broadcasted_iota(jnp.int32, (keys, tokens), 1) + (keys - tokens)
    before = (column == seg_row[:, keys - tokens :]) & (key_idx < query_idx)
    places = jnp.sum(jnp.where(before, 1.0, 0.0), axis=0, keepdims=True)
    angles = jnp.broadcast_to(places, (LANES, tokens)).T * inverse_ref[...]
    turn_ref[:, :LANES] = jnp.cos(angles)
    sine = jnp.sin(angles)
    turn_ref[:, LANES:] = jnp.where(lane_iota(sine.shape) % HD < HD // 2, -sine, sine)

    for k in range(1, 4):
        down[k].wait_recv()
        block = blocks_ref.at[back[k], col]
        sides.append(go(block, block, col=across))
        cores.append(go(block, block, col=core))
    for c in toks:
        c.wait_recv()
    first_norm(x_ref, gains_ref, h_ref)
    mix_side = []
    for k in range(1, 4):
        mix_down[k].wait_recv()
        block = mixes_ref.at[back[k], col, half]
        mix_side.append(go(block, block, dp=1 - dp))
    for c in ffn:
        c.wait_recv()
    to_right = mover.copy(parts_ref, rows_ref.at[row], row=row + 1)
    to_left = mover.copy(parts_ref, rows_ref.at[row], row=row - 1)
    pl.when(row <= 2)(to_right.start)
    pl.when(row >= 1)(to_left.start)
    passed = []
    for k in range(4):
        sides[k].wait_recv()
        block = blocks_ref.at[back[k], across]
        passed.append(go(block, block, col=core))
    for c in cores + passed:
        c.wait_recv()
    for k in range(4):
        if k > 0:
            mix_side[k - 1].wait_recv()
        block = mixes_ref.at[back[k], col]
        rest.append(go(block, block, col=across))
    place_factor_weights(blocks_ref, w_ref)
    make_factors(h_ref, w_ref, turn_ref, hf_ref, bq_ref, win_ref.at[4])

    own = win_ref.at[4]
    one = mover.copy(own, win_ref.at[2], row=row + 1)
    two = mover.copy(win_ref.at[2], win_ref.at[0], row=row + 1)
    near = mover.copy(own, win_ref.at[3], col=core)
    pass_one = mover.copy(win_ref.at[2], win_ref.at[1 + 2 * side], col=core)
    pass_two = mover.copy(win_ref.at[0], win_ref.at[1], col=core)
    hands_on = jnp.logical_and(has_one, row <= 2)
    sends_two = jnp.logical_and(has_two, side == 1)
    takes_two = jnp.logical_and(has_two, side == 0)
    pl.when(row <= 2)(one.start)
    pl.when(side == 0)(near.start)

    @pl.when(has_one)
    def _():
        one.wait_recv()
        pass_one.start()

    pl.when(hands_on)(two.start)
    pl.when(row >= 1)(to_right.wait_recv)
    pl.when(row <= 2)(to_left.wait_recv)
    next_copies()
    make_queries(hf_ref, bq_ref, q_ref)

    @pl.when(has_two)
    def _():
        two.wait_recv()

    pl.when(sends_two)(pass_two.start)

    @pl.when(has_one)
    def _():
        pass_one.wait_recv()
        pass_one.wait_send()

    pl.when(takes_two)(pass_two.wait_recv)
    pl.when(sends_two)(pass_two.wait_send)
    pl.when(side == 1)(near.wait_recv)
    pl.when(side == 0)(near.wait_send)
    pl.when(row <= 2)(one.wait_send)
    pl.when(hands_on)(two.wait_send)
    pl.when(row <= 2)(to_right.wait_send)
    pl.when(row >= 1)(to_left.wait_send)

    def end():
        for c in rest:
            c.wait_recv()
        for c in started:
            c.wait_send()

    return end


KEPT = (0, 2, 3, 4, 5, 6, 7, 8, 9, 11)


def head_attend_body(*refs):
    head_in, cot_ref = refs[:11], refs[11]
    outs, scratch = refs[12:30], refs[30:]
    kept = dict(zip(KEPT, scratch[10:20]))
    tiles = scratch[20:23]
    keep_sem, tile_sem = scratch[23:]
    head_out = [kept.get(k, outs[k]) for k in range(13)]
    o_out, lse_ref, k_out, v_out, near_ref = outs[13:]
    mixes_ref, q_ref, win_ref, seg_ref, rows_ref = (head_out[k] for k in (3, 7, 9, 10, 12))
    side_work = AttendCopies(cot_ref, rows_ref, near_ref, mixes_ref, *scratch[8:10])
    side_work.head_end = head_body(*head_in, *head_out, *scratch[:6], side_work.first)
    copies = [pltpu.make_async_copy(kept[k], outs[k], keep_sem.at[n]) for n, k in enumerate(KEPT)]
    for k, c in zip(KEPT, copies):
        if k != 3:
            c.start()

    def tile_copies(p):
        lanes = pl.ds(pl.multiple_of(p * LANES, LANES), LANES)
        return [
            pltpu.make_async_copy(source.at[:, lanes], target.at[:, lanes], tile_sem.at[n, p])
            for n, (source, target) in enumerate(zip(tiles, (o_out, k_out, v_out)))
        ]

    def store(p):
        for c in tile_copies(p):
            c.start()

    attend_body(
        True, q_ref, win_ref, seg_ref, tiles[0], lse_ref, tiles[1], tiles[2], *scratch[6:8],
        store=store, side_work=side_work,
    )
    copies[KEPT.index(3)].start()
    for p in range(PAIRS):
        for c in tile_copies(p):
            c.wait()
    for c in copies:
        c.wait()


def head_attend(tok, ranks_t, heads_t, gain_one, gain_two, gate_t, up_t, down, w_out, segments, inverse, cot):
    rows, feat = tok.shape[1:]
    units = -(-gate_t.shape[0] // 8 // 16) * 16
    block = (ranks_t.shape[0] + GROUP_COLS, feat)
    ffn = (4, 3, units, feat)
    count = 3 + 4 + 4 + 6 + 3 + 3 + 3 + 4 + 4 + 2 + 5
    outs = (
        jax.ShapeDtypeStruct(tok.shape, BF),
        jax.ShapeDtypeStruct((4, 8, feat), F32),
        jax.ShapeDtypeStruct(ffn, BF),
        jax.ShapeDtypeStruct((4, 4) + w_out.shape, BF),
        jax.ShapeDtypeStruct((rows, D), BF),
        jax.ShapeDtypeStruct((rows, HEAD_COLS), F32),
        jax.ShapeDtypeStruct((rows, RQ * HD), F32),
        jax.ShapeDtypeStruct((rows, D), BF),
        jax.ShapeDtypeStruct((ALL_COLS, D), BF),
        jax.ShapeDtypeStruct((5, rows, 3 * LANES), BF),
        jax.ShapeDtypeStruct((1, 5 * rows), jnp.int32),
        jax.ShapeDtypeStruct((rows, 2 * LANES), F32),
        jax.ShapeDtypeStruct((4,) + ffn, BF),
        *attend_shapes(rows, 5 * rows),
        jax.ShapeDtypeStruct((4,) + cot.shape, BF),
    )
    out_specs = [VMEM] * 12 + [ANY] + [ANY, VMEM, ANY, ANY] + [ANY]
    for k in KEPT:
        out_specs[k] = ANY
    return pl.pallas_call(
        head_attend_body,
        out_shape=outs,
        in_specs=[VMEM] * 11 + [ANY],
        out_specs=tuple(out_specs),
        scratch_shapes=[
            pltpu.VMEM(block, BF),
            pltpu.VMEM((8, feat), F32),
            pltpu.VMEM(ffn, BF),
            pltpu.VMEM((4, 4) + block, BF),
            pltpu.SemaphoreType.DMA((count,)),
            pltpu.SemaphoreType.DMA((count,)),
            pltpu.VMEM((5 * rows, rows), F32),
            pltpu.VMEM((2 * RK, 5 * rows, LANES), F32),
            pltpu.SemaphoreType.DMA((22,)),
            pltpu.SemaphoreType.DMA((22,)),
        ]
        + [pltpu.VMEM(outs[k].shape, outs[k].dtype) for k in KEPT + (13, 15, 16)]
        + [pltpu.SemaphoreType.DMA((len(KEPT),)), pltpu.SemaphoreType.DMA((3, PAIRS))],
        compiler_params=comm_params(1),
        cost_estimate=cost_of(2 * rows * D * (800 * 3 + 5 * rows * 16), 30 << 20),
    )(tok, ranks_t, heads_t, gain_one, gain_two, gate_t, up_t, down, w_out, segments, inverse, cot)


def window_lanes(ref, lanes):
    value = ref[..., lanes]
    return value.reshape(-1, value.shape[-1])


def mask_bias(seg_ref, keys, rows):
    seg_row = seg_ref[...].astype(F32)
    wide = jnp.broadcast_to(seg_row, (LANES, keys))
    column = wide.T
    column = jnp.concatenate([column] * (rows // LANES), axis=1)
    key_idx = lax.broadcasted_iota(jnp.int32, (keys, rows), 0)
    query_idx = lax.broadcasted_iota(jnp.int32, (keys, rows), 1) + (keys - rows)
    same = column == seg_row[:, keys - rows :]
    return jnp.where(same & (key_idx <= query_idx), 0.0, NEG)


def attend_body(fast, q_ref, kf_ref, seg_ref, *refs, store=None, side_work=None):
    o_ref, lse_ref, k_ref, v_ref, bias_ref, dup_ref = refs
    rows = q_ref.shape[0]
    keys = seg_ref.shape[1]
    bias_ref[...] = mask_bias(seg_ref, keys, rows)
    for s in range(2 * RK):
        tile = window_lanes(kf_ref, slice((s // 2) * LANES, (s // 2 + 1) * LANES)).astype(F32)
        dup_ref[s] = double_left(tile) if s % 2 == 0 else double_right(tile)

    def pair(p, carried):
        if fast:
            pl.when(p == 1)(side_work.early)
            pl.when(p == 3)(side_work.second)
        lanes = pl.ds(pl.multiple_of(p * LANES, LANES), LANES)
        weights = window_lanes(kf_ref, slice(2 * LANES, 3 * LANES))
        made = []
        for kind in range(2):
            acc = None
            for s in range(RK):
                pick = spread(LANES, (kind * RK + s) * H + 2 * p, LANES)
                term = nn(weights, pick) * dup_ref[kind * RK + s]
                acc = term if acc is None else acc + term
            made.append((acc / RK).astype(BF))
        k_tile, v_tile = made
        k_ref[:, lanes] = k_tile
        v_ref[:, lanes] = v_tile
        v_turned = v_tile.astype(F32).T.astype(BF)
        q_turned = (q_ref[:, lanes].astype(F32) * HD**-0.5).T
        half = lax.broadcasted_iota(jnp.int32, q_turned.shape, 0) // HD
        outs = []
        for side in range(2):
            q_side = jnp.where(half == side, q_turned, 0.0).astype(BF)
            scores = nn(k_tile, q_side) + bias_ref[...]
            peak = jnp.max(scores, axis=0, keepdims=True)
            weight = jnp.exp(scores - peak)
            total = jnp.sum(weight, axis=0, keepdims=True)
            probs = (weight * (1.0 / total)).astype(BF)
            outs.append(nn(v_turned[side * HD : (side + 1) * HD], probs))
            lse_ref[2 * p + side] = jnp.broadcast_to(peak + jnp.log(total), (8, rows))
        o_ref[:, lanes] = jnp.concatenate(outs, axis=0).T.astype(BF)
        if fast:
            store(p)
        return carried

    lax.fori_loop(0, PAIRS, pair, 0)
    if fast:
        side_work.last()


def attend_shapes(rows, keys):
    return [
        jax.ShapeDtypeStruct((rows, D), BF),
        jax.ShapeDtypeStruct((H, 8, rows), F32),
        jax.ShapeDtypeStruct((keys, D), BF),
        jax.ShapeDtypeStruct((keys, D), BF),
    ]


def attend(q, kf_window, seg_window):
    rows = q.shape[0]
    keys = kf_window.shape[0]
    return call(
        functools.partial(attend_body, False),
        tuple(attend_shapes(rows, keys)),
        scratch=(pltpu.VMEM((keys, rows), F32), pltpu.VMEM((2 * RK, keys, LANES), F32)),
        cost=cost_of(2 * rows * keys * D * 16, 16 << 20),
    )(q, kf_window, seg_window)


def attend_back_body(fast, q_ref, k_ref, v_ref, do_ref, lse_ref, kf_ref, seg_ref, *refs, load=None):
    if fast:
        dq_ref, dkf_ref = refs[5:7]
        bias_ref, dup_ref, sum_ref, fac_ref = refs[10:14]
        side_work = BackCopies(refs[:5] + refs[7:10] + refs[14:28], refs[28:])
        side_work.first()
    else:
        dq_ref, dkf_ref, bias_ref, dup_ref, sum_ref, fac_ref = refs
    rows = q_ref.shape[0]
    keys = seg_ref.shape[1]
    bias_ref[...] = mask_bias(seg_ref, keys, rows)
    for s in range(2 * RK):
        tile = window_lanes(kf_ref, slice((s // 2) * LANES, (s // 2 + 1) * LANES)).astype(F32)
        dup_ref[s] = double_left(tile) if s % 2 == 0 else double_right(tile)
    sum_ref[...] = jnp.zeros_like(sum_ref)
    fac_ref[...] = jnp.zeros_like(fac_ref)

    def pair(p, carried):
        if fast:
            pl.when(p == 3)(side_work.second)
            pl.when(p == 3)(side_work.cross_x)
            pl.when(p == 4)(side_work.last_hop)
            pl.when(p == 6)(side_work.third)
            load(p)
        lanes = pl.ds(pl.multiple_of(p * LANES, LANES), LANES)
        k_tile = k_ref[:, lanes]
        v_tile = v_ref[:, lanes]
        k_turned = k_tile.astype(F32).T.astype(BF)
        q_tile = q_ref[:, lanes].astype(F32) * HD**-0.5
        do_tile = do_ref[:, lanes].astype(F32)
        q_turned = q_tile.T
        do_turned = do_tile.T
        half = lax.broadcasted_iota(jnp.int32, q_turned.shape, 0) // HD
        lane_half = lax.broadcasted_iota(jnp.int32, q_tile.shape, 1) // HD
        d_k = None
        d_v = None
        d_q = []
        for side in range(2):
            q_side = jnp.where(half == side, q_turned, 0.0).astype(BF)
            do_side = jnp.where(half == side, do_turned, 0.0).astype(BF)
            scores = nn(k_tile, q_side) + bias_ref[...]
            probs = jnp.exp(scores - lse_ref[2 * p + side][:1])
            d_prob = nn(v_tile, do_side)
            delta = jnp.sum(probs * d_prob, axis=0, keepdims=True)
            d_score = (probs * (d_prob - delta)).astype(BF)
            d_q.append(nn(k_turned[side * HD : (side + 1) * HD], d_score))
            q_back = jnp.where(lane_half == side, q_tile, 0.0).astype(BF)
            do_back = jnp.where(lane_half == side, do_tile, 0.0).astype(BF)
            part_k = nn(d_score, q_back)
            part_v = nn(probs.astype(BF), do_back)
            d_k = part_k if d_k is None else d_k + part_k
            d_v = part_v if d_v is None else d_v + part_v
        dq_ref[:, lanes] = jnp.concatenate(d_q, axis=0).T * HD**-0.5
        weights = window_lanes(kf_ref, slice(2 * LANES, 3 * LANES))
        for kind, grad in ((0, d_k), (1, d_v)):
            for s in range(RK):
                slot = kind * RK + s
                pick = spread(LANES, slot * H + 2 * p, LANES)
                sum_ref[slot] += nn(weights, pick) * grad
                product = (grad * dup_ref[slot]).astype(BF)
                fac_ref[...] += nn(product, collect(LANES, LANES, slot * H + 2 * p))
        return carried

    lax.fori_loop(0, PAIRS, pair, 0)
    for tile in range(2):
        first = sum_ref[2 * tile]
        second = sum_ref[2 * tile + 1]
        first = first + pltpu.roll(first, HD, 1)
        second = second + pltpu.roll(second, HD, 1)
        merged = jnp.where(lane_iota(first.shape) < HD, first, second)
        blocks = dkf_ref.shape[:-1] + (LANES,)
        dkf_ref[..., tile * LANES : (tile + 1) * LANES] = (merged / RK).astype(BF).reshape(blocks)
    dkf_ref[..., 2 * LANES :] = (fac_ref[...] / RK).astype(BF).reshape(blocks)
    if fast:
        side_work.last()


def back_scratch(rows, keys):
    return [
        pltpu.VMEM((keys, rows), F32),
        pltpu.VMEM((2 * RK, keys, LANES), F32),
        pltpu.VMEM((2 * RK, keys, LANES), F32),
        pltpu.VMEM((keys, LANES), F32),
    ]


def attend_back(q, k, v, d_heads, lse, kf_window, seg_window):
    rows = q.shape[0]
    keys = kf_window.shape[0]
    return call(
        functools.partial(attend_back_body, False),
        (jax.ShapeDtypeStruct((rows, D), F32), jax.ShapeDtypeStruct(kf_window.shape, BF)),
        scratch=back_scratch(rows, keys),
        cost=cost_of(2 * rows * keys * D * 40, 16 << 20),
    )(q, k, v, d_heads, lse, kf_window, seg_window)


def mixing_body(x_ref, heads_ref, w_out_ref, gain_ref, mixed_ref, h_ref):
    parts, _, feat = x_ref.shape
    rows_of = w_out_ref.shape[0]
    head_rows = w_out_ref.shape[2]
    total = None
    for c in range(parts):
        lanes = slice(c * feat, (c + 1) * feat)
        acc = x_ref[c].astype(F32)
        for r in range(rows_of):
            acc = acc + nn(heads_ref[:, r * head_rows : (r + 1) * head_rows], w_out_ref[r, c])
        mixed_ref[:, lanes] = acc
        part = jnp.sum(acc * acc, axis=1, keepdims=True)
        total = part if total is None else total + part
    scale = lax.rsqrt(total / D + EPS)
    for c in range(parts):
        lanes = slice(c * feat, (c + 1) * feat)
        h_ref[:, lanes] = (mixed_ref[:, lanes] * scale * gain_ref[c, 1:2]).astype(BF)


def mixing(x_parts, heads, w_out, gains):
    rows = heads.shape[0]
    return call(
        mixing_body,
        (jax.ShapeDtypeStruct((rows, D), F32), jax.ShapeDtypeStruct((rows, D), BF)),
        cost=cost_of(2 * rows * D * D, 5 << 20),
    )(x_parts, heads, w_out, gains)


def ffn_steps(blocks, h_at, cot_at, w_ref, hid_ref, dg_ref, du_ref, out_at, back_at):
    def block(t, carried):
        h = h_at(t)[...]
        gate = nt(h, w_ref[0])
        up = nt(h, w_ref[1])
        d_hidden = nt(cot_at(t)[...], w_ref[2])
        sig = 1.0 / (1.0 + jnp.exp(-gate))
        silu = gate * sig
        hidden = (silu * up).astype(BF)
        d_gate = (d_hidden * up * sig * (1.0 + gate * (1.0 - sig))).astype(BF)
        d_up = (d_hidden * silu).astype(BF)
        rows = h.shape[0]
        place = pl.ds(pl.multiple_of(t * rows, rows), rows)
        hid_ref[place] = hidden
        dg_ref[place] = d_gate
        du_ref[place] = d_up
        out_at(t)[...] = nn(hidden, w_ref[2]).astype(BF)
        back_at(t)[...] = (nn(d_gate, w_ref[0]) + nn(d_up, w_ref[1])).astype(BF)
        return carried

    lax.fori_loop(0, blocks, block, 0)


def ffn_body(h_ref, cot_ref, w_ref, out_ref, back_ref, g_ref, hid_ref, dg_ref, du_ref):
    parts, rows, _ = h_ref.shape
    ffn_steps(
        parts, lambda t: h_ref.at[t], lambda t: cot_ref.at[t], w_ref, hid_ref, dg_ref, du_ref,
        lambda t: out_ref.at[t], lambda t: back_ref.at[t],
    )
    h_all = h_ref[...].reshape(parts * rows, D)
    cot_all = cot_ref[...].reshape(parts * rows, D)
    for place, (left, right) in enumerate(((dg_ref, h_all), (du_ref, h_all), (hid_ref, cot_all))):
        g_ref[place] = tn(left[...], right).astype(BF)


def ffn(h_all, cot_all, w):
    parts, rows, _ = h_all.shape
    units = w.shape[1]
    return call(
        ffn_body,
        (
            jax.ShapeDtypeStruct(h_all.shape, BF),
            jax.ShapeDtypeStruct(h_all.shape, BF),
            jax.ShapeDtypeStruct(w.shape, BF),
        ),
        scratch=[pltpu.VMEM((parts * rows, units), BF)] * 3,
        cost=cost_of(2 * parts * rows * 9 * D * units, 20 << 20),
    )(h_all, cot_all, w)


def unmix_math(
    mixed_ref, cot_ref, d_h, heads_ref, w_out_ref, gain_ref, d_mixed_ref, d_heads_ref, g_out_ref, g_gain_ref
):
    rows_of, parts, head_rows, feat = w_out_ref.shape
    mixed = mixed_ref[...]
    scale = lax.rsqrt(jnp.sum(mixed * mixed, axis=1, keepdims=True) / D + EPS)
    normed = mixed * scale
    g_gain_ref[...] = jnp.sum(d_h * normed, axis=0, keepdims=True)
    gain = jnp.concatenate([gain_ref[c, 1:2] for c in range(parts)], axis=1)
    inner = d_h * gain
    dot = jnp.sum(inner * normed, axis=1, keepdims=True) / D
    d_mixed = cot_ref[...].astype(F32) + scale * (inner - normed * dot)
    d_mixed_ref[...] = d_mixed
    low = d_mixed.astype(BF)
    grad = tn(heads_ref[...], low)
    for r in range(rows_of):
        acc = None
        for c in range(parts):
            lanes = slice(c * feat, (c + 1) * feat)
            term = nt(low[:, lanes], w_out_ref[r, c])
            acc = term if acc is None else acc + term
            g_out_ref[r, c] = grad[r * head_rows : (r + 1) * head_rows, lanes].astype(BF)
        d_heads_ref[:, r * head_rows : (r + 1) * head_rows] = acc.astype(BF)


def write_output(mixed_ref, total, out_ref):
    parts, _, feat = out_ref.shape
    for c in range(parts):
        lanes = slice(c * feat, (c + 1) * feat)
        out_ref[c] = (mixed_ref[:, lanes] + total[:, lanes]).astype(BF)


def unmix_body(
    dh_ref, sum_ref, mixed_ref, cot_ref, heads_ref, w_out_ref, gain_ref,
    out_ref, d_mixed_ref, d_heads_ref, g_out_ref, g_gain_ref,
):
    unmix_math(
        mixed_ref, cot_ref, dh_ref[...], heads_ref, w_out_ref, gain_ref,
        d_mixed_ref, d_heads_ref, g_out_ref, g_gain_ref,
    )
    write_output(mixed_ref, sum_ref[...], out_ref)


def middle_body(
    x_ref, heads_ref, w_out_ref, gain_ref, cot_own_ref, cot_in_ref, w_own_ref, rows_ref,
    mixed_out, d_mixed_ref, d_heads_ref, g_out_ref, g_gain_ref, g_hbm, out_pair_hbm, hop_ref,
    w_ref, h_ref, cot_ref, hid_ref, dg_ref, du_ref, back_ref, fwd_ref, back_got_ref, fwd_got_ref,
    pair_ref, diag_ref, far_ref, send_sem, recv_sem, w_sem, cot_sem,
    mixed_ref, g_ref, out_pair_ref, leave_sem,
):
    row = lax.axis_index("row")
    col, core, across = neighbours()
    dp, (me, on_x, on_y, on_both) = square()
    x, mine = col // 2, lax.rem(col, 2)
    y = 1 - dp
    parts, rows, feat = x_ref.shape
    units = rows_ref.shape[3]
    greet(
        [
            (None, {"col": core}),
            (None, {"col": across}),
            (None, {"dp": y}),
            (row <= 2, {"row": row + 1}),
            (row >= 1, {"row": row - 1}),
        ]
    )
    mover = Mover(send_sem, recv_sem)

    def w_place(r, c):
        return w_ref.at[:, pl.ds(pl.multiple_of(r * units, units), units), pl.ds(c * feat, feat)]

    local = []
    for k in range(4):
        r = lax.rem(row + k, 4)
        for c in range(4):
            source = w_own_ref.at[c] if k == 0 else rows_ref.at[r, c]
            copy = pltpu.make_async_copy(source, w_place(r, c), w_sem.at[k, c])
            copy.start()
            local.append(copy)
    cots = []
    for k in range(4):
        from_x = lax.rem(x + k % 2, 2)
        from_dp = lax.rem(dp + k // 2, 2)
        lanes = pl.ds(pl.multiple_of((from_x * 2 + mine) * feat, feat), feat)
        for c in range(4):
            part = pl.ds(c * rows, rows)
            source = cot_own_ref.at[part] if k == 0 else cot_in_ref.at[from_dp * 2 + from_x, part]
            spot = from_dp * 2 + c // 2
            copy = pltpu.make_async_copy(source, cot_ref.at[lax.rem(mine + c, 2), spot, :, lanes], cot_sem.at[k, c])
            copy.start()
            local.append(copy)
            sent = mover.copy(source, cot_ref.at[lax.rem(mine + c + 1, 2), spot, :, lanes], col=core)
            sent.start()
            cots.append(sent)

    total = None
    for c in range(parts):
        lanes = slice(c * feat, (c + 1) * feat)
        acc = x_ref[c].astype(F32)
        for r in range(4):
            acc = acc + nn(heads_ref[:, r * feat : (r + 1) * feat], w_out_ref[r, c])
        mixed_ref[:, lanes] = acc
        part = jnp.sum(acc * acc, axis=1, keepdims=True)
        total = part if total is None else total + part
    scale = lax.rsqrt(total / D + EPS)
    for c in range(parts):
        lanes = slice(c * feat, (c + 1) * feat)
        h_ref[0, me, :, lanes] = (mixed_ref[:, lanes] * scale * gain_ref[c, 1:2]).astype(BF)

    leave = [
        pltpu.make_async_copy(source, target, leave_sem.at[n])
        for n, (source, target) in enumerate(
            ((mixed_ref, mixed_out), (g_ref, g_hbm), (out_pair_ref, out_pair_hbm))
        )
    ]
    leave[0].start()

    half = rows // 2
    top, low = pl.ds(0, half), pl.ds(half, half)

    def h_copy(spot, part=None, side=0, **place):
        source = h_ref.at[0, spot] if part is None else h_ref.at[0, spot, part]
        target = h_ref.at[side, spot] if part is None else h_ref.at[side, spot, part]
        return mover.copy(source, target, **place)

    x_low = h_copy(me, low, col=across)
    y_top = h_copy(me, top, dp=y)
    x_top = h_copy(me, top, col=across)
    y_low = h_copy(me, low, dp=y)
    near = h_copy(me, None, 1, col=core)
    both_low = h_copy(on_x, low, dp=y)
    both_top = h_copy(on_y, top, col=across)
    near_first = [h_copy(on_x, low, 1, col=core), h_copy(on_y, top, 1, col=core)]
    near_second = [h_copy(on_x, top, 1, col=core), h_copy(on_y, low, 1, col=core)]
    near_both = h_copy(on_both, None, 1, col=core)
    for c in (x_low, y_top, near, x_top, y_low):
        c.start()
    steps = (
        ((me, top), (me, low)),
        ((on_x, low), (on_y, top)),
        ((on_x, top), (on_y, low)),
        ((on_both, top), (on_both, low)),
    )
    back_near = [[mover.copy(back_ref.at[1, s, p], back_got_ref.at[s, p], col=core) for s, p in two] for two in steps]
    fwd_near = [[mover.copy(fwd_ref.at[1, s, p], fwd_got_ref.at[s, p], col=core) for s, p in two] for two in steps]
    diag = [
        mover.copy(pair_ref.at[on_both, low], diag_ref.at[0], col=across),
        mover.copy(pair_ref.at[on_both, top], diag_ref.at[1], dp=y),
    ]
    far = [
        mover.copy(pair_ref.at[on_x, low], far_ref.at[0, low], col=across),
        mover.copy(pair_ref.at[on_y, top], far_ref.at[1, top], dp=y),
        mover.copy(pair_ref.at[on_y, low], far_ref.at[1, low], dp=y),
        mover.copy(pair_ref.at[on_x, top], far_ref.at[0, top], col=across),
    ]

    def add_pair(k):
        for (s, p), c in zip(steps[k], back_near[k]):
            c.wait_recv()
            pair_ref[s, p] = (back_ref[0, s, p].astype(F32) + back_got_ref[s, p].astype(F32)).astype(BF)

    for copy in local:
        copy.wait()
    for c in cots:
        c.wait_recv()

    def block(t, carried):
        @pl.when(t == 1)
        def _():
            near.wait_recv()

        @pl.when(t == 2)
        def _():
            x_low.wait_recv()
            both_low.start()
            near_first[0].start()
            y_top.wait_recv()
            both_top.start()
            near_first[1].start()

        @pl.when(t == 3)
        def _():
            for c in near_first:
                c.wait_recv()

        @pl.when(t == 4)
        def _():
            x_top.wait_recv()
            near_second[0].start()
            y_low.wait_recv()
            near_second[1].start()

        @pl.when(t == 5)
        def _():
            for c in near_second:
                c.wait_recv()
            add_pair(1)
            far[0].start()
            far[1].start()

        @pl.when(t == 6)
        def _():
            both_low.wait_recv()
            both_top.wait_recv()
            near_both.start()

        @pl.when(t == 7)
        def _():
            near_both.wait_recv()
            add_pair(2)

        name, side = t // 2, lax.rem(t, 2)
        first_dp = lax.rem(dp + jnp.where(name == 3, 1, 0), 2)
        first_x = lax.rem(x + jnp.where(name >= 1, 1, 0), 2)
        first = first_dp * 2 + first_x
        other_dp = lax.rem(dp + jnp.where(name >= 1, 1, 0), 2)
        other_x = lax.rem(x + jnp.where(name == 3, 1, 0), 2)
        other = other_dp * 2 + other_x
        first_rows = pl.ds(pl.multiple_of(jnp.where(name == 1, half, 0), half), half)
        other_rows = pl.ds(pl.multiple_of(jnp.where(name == 1, 0, half), half), half)
        h = jnp.concatenate([h_ref[side, first, first_rows], h_ref[side, other, other_rows]], axis=0)
        cot = jnp.concatenate([cot_ref[side, first, first_rows], cot_ref[side, other, other_rows]], axis=0)
        gate = nt(h, w_ref[0])
        up = nt(h, w_ref[1])
        d_hidden = nt(cot, w_ref[2])
        sig = 1.0 / (1.0 + jnp.exp(-gate))
        silu = gate * sig
        hidden = (silu * up).astype(BF)
        d_gate = (d_hidden * up * sig * (1.0 + gate * (1.0 - sig))).astype(BF)
        d_up = (d_hidden * silu).astype(BF)
        back = (nn(d_gate, w_ref[0]) + nn(d_up, w_ref[1])).astype(BF)
        fwd = nn(hidden, w_ref[2]).astype(BF)
        for spot, part, cut in ((first, first_rows, slice(0, half)), (other, other_rows, slice(half, rows))):
            start = jnp.where(part.start == 0, 0, half)
            place = pl.ds(pl.multiple_of((side * 4 + spot) * rows + start, half), half)
            hid_ref[place] = hidden[cut]
            dg_ref[place] = d_gate[cut]
            du_ref[place] = d_up[cut]
            back_ref[side, spot, part] = back[cut]
            fwd_ref[side, spot, part] = fwd[cut]
        for k in range(4):

            @pl.when(t == 2 * k + 1)
            def _():
                for c in back_near[k] + fwd_near[k]:
                    c.start()

        return carried

    lax.fori_loop(0, 8, block, 0)
    add_pair(3)
    for c in diag:
        c.start()

    hops = []
    for place in range(3):
        to_right = mover.copy(g_ref.at[3, place], hop_ref.at[place], row=row + 1)
        to_left = mover.copy(g_ref.at[0, place], hop_ref.at[place], row=row - 1)
        hops.append((to_right, to_left))

    def gradient(place, left, right):
        grad = tn(left[...], right[...].reshape(8 * rows, D))
        for r in range(4):
            g_ref[r, place] = grad[r * units : (r + 1) * units].astype(BF)
        pl.when(row == 0)(hops[place][0].start)
        pl.when(row == 3)(hops[place][1].start)

    gradient(0, dg_ref, h_ref)
    gradient(1, du_ref, h_ref)
    for k, (s, part) in enumerate(((on_y, low), (on_x, top))):
        diag[k].wait_recv()
        pair_ref[s, part] = (pair_ref[s, part].astype(F32) + diag_ref[k].astype(F32)).astype(BF)
        far[2 + k].start()
    gradient(2, hid_ref, cot_ref)
    leave[1].start()
    for two, copies in zip(steps, fwd_near):
        for (s, p), c in zip(two, copies):
            c.wait_recv()
            out_pair_ref[s, p] = (fwd_ref[0, s, p].astype(F32) + fwd_got_ref[s, p].astype(F32)).astype(BF)
    leave[2].start()
    add_pair(0)
    for c in far:
        c.wait_recv()
    d_h = pair_ref[me].astype(F32) + far_ref[0].astype(F32) + far_ref[1].astype(F32)
    unmix_math(
        mixed_ref, cot_ref.at[0, me], d_h, heads_ref, w_out_ref, gain_ref,
        d_mixed_ref, d_heads_ref, g_out_ref, g_gain_ref,
    )
    for c in cots + [x_low, y_top, x_top, y_low, near, both_low, both_top, near_both] + near_first + near_second:
        c.wait_send()
    for two in back_near + fwd_near:
        for c in two:
            c.wait_send()
    for c in diag + far:
        c.wait_send()
    for c in leave:
        c.wait()
    for to_right, to_left in hops:
        pl.when(row == 0)(to_right.wait_send)
        pl.when(row == 3)(to_left.wait_send)
        pl.when(row == 1)(to_right.wait_recv)
        pl.when(row == 2)(to_left.wait_recv)


def middle(x_parts, heads, w_out, gains, cot_own, cot_near, w_own, w_rows):
    parts, rows, feat = x_parts.shape
    units = w_rows.shape[3]
    count = 16 + 12 + 16 + 6 + 6
    square_of = pltpu.VMEM((2, 4, rows, D), BF)
    hidden_of = pltpu.VMEM((8 * rows, 4 * units), BF)
    quarter = pltpu.VMEM((4, rows, D), BF)
    return pl.pallas_call(
        middle_body,
        out_shape=(
            jax.ShapeDtypeStruct((rows, D), F32),
            jax.ShapeDtypeStruct((rows, D), F32),
            jax.ShapeDtypeStruct((rows, D), BF),
            jax.ShapeDtypeStruct(w_out.shape, BF),
            jax.ShapeDtypeStruct((1, D), F32),
            jax.ShapeDtypeStruct((4, 3, units, D), BF),
            jax.ShapeDtypeStruct((4, rows, D), BF),
            jax.ShapeDtypeStruct((3, units, D), BF),
        ),
        in_specs=[VMEM] * 4 + [ANY] * 4,
        out_specs=(ANY,) + (VMEM,) * 4 + (ANY,) * 3,
        scratch_shapes=[pltpu.VMEM((3, 4 * units, D), BF), square_of, square_of]
        + [hidden_of] * 3
        + [square_of, square_of, quarter, quarter, quarter]
        + [
            pltpu.VMEM((2, rows // 2, D), BF),
            pltpu.VMEM((2, rows, D), BF),
            pltpu.SemaphoreType.DMA((count,)),
            pltpu.SemaphoreType.DMA((count,)),
            pltpu.SemaphoreType.DMA((4, 4)),
            pltpu.SemaphoreType.DMA((4, 4)),
            pltpu.VMEM((rows, D), F32),
            pltpu.VMEM((4, 3, units, D), BF),
            quarter,
            pltpu.SemaphoreType.DMA((3,)),
        ],
        compiler_params=comm_params(4),
        cost_estimate=cost_of(2 * 8 * rows * 9 * D * 4 * units, 24 << 20),
    )(x_parts, heads, w_out, gains, cot_own, cot_near, w_own, w_rows)


def unmix(dh, out_sum, mixed, cot_own, heads, w_out, gains):
    rows = heads.shape[0]
    parts, feat = w_out.shape[1], w_out.shape[3]
    outs = (
        jax.ShapeDtypeStruct((parts, rows, feat), BF),
        jax.ShapeDtypeStruct((rows, D), F32),
        jax.ShapeDtypeStruct((rows, D), BF),
        jax.ShapeDtypeStruct(w_out.shape, BF),
        jax.ShapeDtypeStruct((1, D), F32),
    )
    return call(unmix_body, outs, cost=cost_of(4 * rows * D * D, 18 << 20))(
        dh, out_sum, mixed, cot_own, heads, w_out, gains
    )


def query_grads(ranks_taken, dq, high, low, bq_ref):
    fac = None
    folded = []
    for r in ranks_taken:
        tile = bq_ref[:, (r // 2) * LANES : (r // 2 + 1) * LANES]
        rank = double_left(tile) if r % 2 == 0 else double_right(tile)
        product = dq * jnp.concatenate([rank] * PAIRS, axis=1)
        term = two_pass(product, head_collect(2 * RK + r))
        fac = term if fac is None else fac + term
        pick = head_spread(2 * RK + r, 0, D)
        terms = (nn(high, pick) + nn(low, pick)) * dq
        acc = terms[:, :LANES]
        for p in range(1, PAIRS):
            acc = acc + terms[:, p * LANES : (p + 1) * LANES]
        folded.append(acc + pltpu.roll(acc, HD, 1))
    return fac, folded


def turned_back(part, turn_ref):
    return part * turn_ref[:, :LANES] - swap_halves(part) * turn_ref[:, LANES:]


def put_query_grads(folded, first, turn_ref, d_ref):
    lane = lane_iota(folded[0].shape)
    for k in range(len(folded) // 2):
        merged = jnp.where(lane < HD, folded[2 * k], folded[2 * k + 1])
        tile = first // 2 + k
        d_ref[:, tile * LANES : (tile + 1) * LANES] = turned_back(merged, turn_ref).astype(BF)


def put_key_grads(dkf, fac, turn_ref, d_ref):
    d_ref[:, 3 * LANES : 4 * LANES] = turned_back(dkf[:, :LANES], turn_ref).astype(BF)
    d_ref[:, 4 * LANES : 5 * LANES] = dkf[:, LANES : 2 * LANES].astype(BF)
    fac = fac.astype(BF).astype(F32) + nt(dkf[:, 2 * LANES :].astype(BF), key_columns())
    d_ref[:, RANK_COLS:] = fac.astype(BF)


def factor_weight_grads(d_ref, h_ref, gains, g_two_ref, g_ref):
    n_row, parts, _, feat = g_ref.shape
    grad = tn(d_ref[...], h_ref[...])
    ranks_each = RANK_COLS // n_row
    used = FAC * GROUP
    for c in range(parts):
        lanes = slice(c * feat, (c + 1) * feat)
        tail = jnp.concatenate(
            [gains[c], g_two_ref[:, lanes], jnp.zeros((GROUP_COLS - used - 2, feat), F32)], axis=0
        )
        for r in range(n_row):
            first = RANK_COLS + r * GROUP_COLS
            g_ref[r, c, :ranks_each] = grad[r * ranks_each : (r + 1) * ranks_each, lanes].astype(BF)
            g_ref[r, c, ranks_each:] = jnp.concatenate([grad[first : first + used, lanes], tail], axis=0).astype(BF)


def first_norm_back(d_h, x_ref, gain_ref, d_mixed_ref, gi_ref):
    parts, _, feat = x_ref.shape
    xs = [x_ref[c].astype(F32) for c in range(parts)]
    total = sum(jnp.sum(v * v, axis=1, keepdims=True) for v in xs)
    scale = lax.rsqrt(total / D + EPS)
    dot = None
    gains = []
    for c in range(parts):
        normed = xs[c] * scale
        grad = d_h[:, c * feat : (c + 1) * feat]
        gains.append(jnp.sum(grad * normed, axis=0, keepdims=True))
        part = jnp.sum(grad * gain_ref[c, :1] * normed, axis=1, keepdims=True)
        dot = part if dot is None else dot + part
    for c in range(parts):
        lanes = slice(c * feat, (c + 1) * feat)
        normed = xs[c] * scale
        total = d_mixed_ref[:, lanes] + scale * (d_h[:, lanes] * gain_ref[c, :1] - normed * (dot / D))
        gi_ref[c] = total.astype(gi_ref.dtype)
    return gains


def back_body(
    dq_ref, dkf_ref, hf_ref, bq_ref, turn_ref, w_ref, h_ref, x_ref, gain_ref, d_mixed_ref, g_two_ref,
    gi_ref, g_ref, d_ref,
):
    heads = hf_ref[...]
    high = heads.astype(BF)
    low = (heads - high.astype(F32)).astype(BF)
    fac, folded = query_grads(range(RQ), dq_ref[...] * (1.0 / RQ), high, low, bq_ref)
    put_query_grads(folded, 0, turn_ref, d_ref)
    put_key_grads(dkf_ref[...].astype(F32), fac, turn_ref, d_ref)
    gains = first_norm_back(nn(d_ref[...], w_ref[...]), x_ref, gain_ref, d_mixed_ref, gi_ref)
    factor_weight_grads(d_ref, h_ref, gains, g_two_ref, g_ref)


def back(dq, dkf, hf, bq, turn, w_rh, h, x_parts, gains, d_mixed, g_two, n_row):
    rows = dq.shape[0]
    parts, _, feat = x_parts.shape
    each = RANK_COLS // n_row + GROUP_COLS
    return call(
        back_body,
        (jax.ShapeDtypeStruct(x_parts.shape, F32), jax.ShapeDtypeStruct((n_row, parts, each, feat), BF)),
        scratch=[pltpu.VMEM((rows, ALL_COLS), BF)],
        cost=cost_of(2 * rows * D * 800 * 6, 12 << 20),
    )(dq, dkf, hf, bq, turn, w_rh, h, x_parts, gains, d_mixed, g_two)


def tail_body(
    win_ref, dq_ref, hf_ref, bq_ref, turn_ref, w_ref, h_ref, x_ref, gain_ref, d_mixed_ref, g_two_ref,
    rows_ref, ends_ref, part_ref,
    grad_ref, gi_all_ref, cols_ref, cols_other_ref, mix_ref, mix_other_ref,
    d_ref, gi_ref, wnear_ref, wsend_ref, wfar_ref, rows_own_ref, cols_send_ref, mix_got_ref,
    g_ref, near_ref, pair_ref, far_ref, side_ref, down_ref, last_ref, end_ref,
    send_sem, recv_sem, local_sem, tail_ref,
):
    row = lax.axis_index("row")
    col, core, across = neighbours()
    cross = lax.rem(core + 2, 4)
    dp = lax.axis_index("dp")
    x, mine = col // 2, lax.rem(col, 2)
    y = 1 - dp
    order = [lax.rem(row + k, 4) for k in (1, 2, 3, 0)]
    mover = Mover(send_sem, recv_sem)
    started = []

    def go(source, target, **place):
        c = mover.copy(source, target, **place)
        c.start()
        started.append(c)
        return c

    rows_own = pltpu.make_async_copy(rows_ref.at[row], rows_own_ref, local_sem.at[1])
    rows_own.start()

    near_one = go(win_ref.at[1], wnear_ref.at[0], col=core)
    near_two = go(win_ref.at[3], wnear_ref.at[1], col=core)
    one = mover.copy(wsend_ref.at[0], wfar_ref.at[0], row=row - 1)
    two = mover.copy(wsend_ref.at[1], wfar_ref.at[1], row=row - 1)
    hands_on = jnp.logical_and(row >= 1, row <= 2)
    left = mine == 0
    heads = hf_ref[...]
    high = heads.astype(BF)
    low = (heads - high.astype(F32)).astype(BF)
    dq = dq_ref[...] * (1.0 / RQ)
    near_one.wait_recv()
    near_two.wait_recv()
    zero = jnp.zeros(wnear_ref.shape[1:], F32)
    from_low = wnear_ref[0].astype(F32)
    from_high = wnear_ref[1].astype(F32)
    wsend_ref[1] = (win_ref[0].astype(F32) + jnp.where(left, zero, from_low)).astype(BF)
    pl.when(row >= 2)(two.start)

    width = x_ref.shape[2]
    rows_own.wait()
    for place in range(3):
        total = rows_own_ref[place].astype(F32)
        total = total + jnp.where(row >= 1, ends_ref[0, place].astype(F32), 0.0)
        total = (total + jnp.where(row <= 2, ends_ref[1, place].astype(F32), 0.0)).astype(BF)
        for c in range(4):
            cols_send_ref[c, place] = total[:, c * width : (c + 1) * width]
    columns = [go(cols_send_ref.at[c], cols_ref.at[col], col=c) for c in (across, cross, core)]
    cols_ref[col] = cols_send_ref[col]
    rest = [go(cols_ref.at[col], cols_other_ref.at[col], dp=y)]

    fac, folded = query_grads(range(0, 4), dq, high, low, bq_ref)
    put_query_grads(folded, 0, turn_ref, d_ref)
    sent_on = win_ref[2].astype(F32) + jnp.where(left, from_low, from_high)
    pl.when(hands_on)(two.wait_recv)
    wsend_ref[0] = jnp.where(hands_on, sent_on + wfar_ref[1].astype(F32), sent_on).astype(BF)
    pl.when(row >= 1)(one.start)

    fac_more, folded = query_grads(range(4, RQ), dq, high, low, bq_ref)
    put_query_grads(folded, 4, turn_ref, d_ref)
    for c, source in zip(columns, (across, cross, core)):
        c.wait_recv()
        rest.append(go(cols_ref.at[source], cols_other_ref.at[source], dp=y))
    split = RQ * HD
    ranks_each = RANK_COLS // 4
    d_h = nn(d_ref[:, :split], w_ref[:split])
    early = tn(d_ref[:, :split], h_ref[...])
    for r in range(2):
        for c in range(4):
            g_ref[r, c, :ranks_each] = early[r * ranks_each : (r + 1) * ranks_each, c * width : (c + 1) * width].astype(BF)
    d_kf = win_ref[4].astype(F32) + jnp.where(left, from_high, zero)
    pl.when(row <= 2)(one.wait_recv)
    d_kf = jnp.where(row <= 2, d_kf + wfar_ref[0].astype(F32), d_kf)
    put_key_grads(d_kf, fac + fac_more, turn_ref, d_ref)
    mixes = [go(part_ref.at[order[k]], mix_got_ref.at[k], row=order[k]) for k in range(3)]
    d_h = d_h + nn(d_ref[:, split:], w_ref[split:])
    gains = first_norm_back(d_h, x_ref, gain_ref, d_mixed_ref, gi_ref)
    for c in range(4):
        tail_ref[0:1, c * width : (c + 1) * width] = gains[c]
    tail_ref[1:2] = g_two_ref[...]
    tail_ref[2:8] = jnp.zeros((6, D), F32)
    start = 2 * LANES
    d_late = d_ref[:, start:]
    used = FAC * GROUP

    def column(c):
        lanes = pl.ds(pl.multiple_of(c * width, width), width)
        grad = tn(d_late, h_ref[:, lanes])
        for r in range(4):
            at = RANK_COLS + r * GROUP_COLS - start
            if r >= 2:
                g_ref[r, c, :ranks_each] = grad[r * ranks_each - start : (r + 1) * ranks_each - start].astype(BF)
            g_ref[r, c, ranks_each:] = jnp.concatenate([grad[at : at + used], tail_ref[:, lanes]], axis=0).astype(BF)

    column((1 - x) * 2 + 1 - mine)
    first = [go(g_ref.at[r, (1 - x) * 2 + 1 - mine], near_ref.at[0, k], col=core) for k, r in enumerate(order)]
    column((1 - x) * 2 + mine)
    column(x * 2 + 1 - mine)
    second = [go(g_ref.at[r, x * 2 + 1 - mine], near_ref.at[1, k], col=core) for k, r in enumerate(order)]
    sides = []
    for k, r in enumerate(order):
        first[k].wait_recv()
        pair_ref[k] = (g_ref[r, (1 - x) * 2 + mine].astype(F32) + near_ref[0, k].astype(F32)).astype(BF)
        sides.append(go(pair_ref.at[k], side_ref.at[k], col=across))
    column(x * 2 + mine)

    total = part_ref[row].astype(F32)
    for k, c in enumerate(mixes):
        c.wait_recv()
        total = total + mix_got_ref[k].astype(F32)
    mix_ref[...] = total.astype(BF)
    rest.append(go(mix_ref, mix_other_ref, dp=y))
    for c in (across, cross, core):
        rest.append(go(gi_ref.at[c], gi_all_ref.at[col], col=c))
    own = pltpu.make_async_copy(gi_ref.at[col], gi_all_ref.at[col], local_sem.at[0])
    own.start()

    downs = []
    for k, r in enumerate(order):
        second[k].wait_recv()
        sides[k].wait_recv()
        far_ref[k] = (
            g_ref[r, x * 2 + mine].astype(F32) + near_ref[1, k].astype(F32) + side_ref[k].astype(F32)
        ).astype(BF)
        if k < 3:
            downs.append(go(far_ref.at[k], down_ref.at[k], row=r))
    total = far_ref[3].astype(F32)
    for k in range(3):
        downs[k].wait_recv()
        total = total + down_ref[k].astype(F32)
    last_ref[...] = total.astype(BF)
    end = go(last_ref, end_ref, dp=y)
    end.wait_recv()
    grad_ref[...] = last_ref[...].astype(F32) + end_ref[...].astype(F32)
    for c in rest:
        c.wait_recv()
    for c in started:
        c.wait_send()
    pl.when(row >= 1)(one.wait_send)
    pl.when(row >= 2)(two.wait_send)
    own.wait()


def back_tail_body(*refs):
    attend_in, side_in, tail_in = refs[:7], refs[7:12], refs[12:21]
    out_ref, *tail_out = refs[21:28]
    scratch = refs[28:]
    dq_ref, dkf_ref, ends_ref, part_ref = scratch[:4]
    gain_ref, g_two_ref = tail_in[6], tail_in[8]
    q_ref, k_hbm, v_hbm, *attend_rest = attend_in
    pair_in, mixed_hbm, *side_rest = side_in
    *scratch, k_ref, v_ref, mixed_ref, hf_ref, bq_ref, turn_ref, w_ref, h_ref, x_ref, d_mixed_ref = scratch[:-2]
    tile_sem, load_sem = refs[-2:]

    def tile_copies(p):
        lanes = pl.ds(pl.multiple_of(p * LANES, LANES), LANES)
        return [
            pltpu.make_async_copy(source.at[:, lanes], target.at[:, lanes], tile_sem.at[n, p])
            for n, (source, target) in enumerate(((k_hbm, k_ref), (v_hbm, v_ref)))
        ]

    for p in range(PAIRS):
        for c in tile_copies(p):
            c.start()
    sources = (mixed_hbm, *(tail_in[k] for k in (0, 1, 2, 3, 4, 5, 7)))
    targets = (mixed_ref, hf_ref, bq_ref, turn_ref, w_ref, h_ref, x_ref, d_mixed_ref)
    loads = [pltpu.make_async_copy(a, b, load_sem.at[n]) for n, (a, b) in enumerate(zip(sources, targets))]
    for c in loads:
        c.start()

    def load(p):
        for c in tile_copies(p):
            c.wait()
        pl.when(p == 5)(loads[0].wait)

    attend_back_body(
        True, q_ref, k_ref, v_ref, *attend_rest, pair_in, mixed_ref, *side_rest, dq_ref, dkf_ref, out_ref, ends_ref,
        part_ref, *scratch[4:25], load=load,
    )
    for c in loads[1:]:
        c.wait()
    tail_body(
        dkf_ref, dq_ref, hf_ref, bq_ref, turn_ref, w_ref, h_ref, x_ref, gain_ref, d_mixed_ref, g_two_ref,
        side_in[2], ends_ref, part_ref, *tail_out, *scratch[25:],
    )


def back_tail(attend_in, side_in, tail_in):
    kf_window, g_rows, g_out = attend_in[5], side_in[2], side_in[3]
    x_parts = tail_in[5]
    parts, rows, feat = x_parts.shape
    units = g_rows.shape[2]
    block = (RANK_COLS // 4 + GROUP_COLS, feat)
    cols = (parts, 3, units, feat)
    mix = g_out.shape[2:]
    wide = g_rows.shape[1:]
    slot = kf_window.shape[1:]
    count = 2 + 2 + 3 + 8 + 4 + 3 + 1 + 1 + 3 + 3 + 3 + 1
    return pl.pallas_call(
        back_tail_body,
        out_shape=(
            jax.ShapeDtypeStruct(x_parts.shape, BF),
            jax.ShapeDtypeStruct(block, F32),
            jax.ShapeDtypeStruct(x_parts.shape, BF),
            jax.ShapeDtypeStruct(cols, BF),
            jax.ShapeDtypeStruct(cols, BF),
            jax.ShapeDtypeStruct(mix, BF),
            jax.ShapeDtypeStruct(mix, BF),
        ),
        in_specs=[VMEM, ANY, ANY] + [VMEM] * 4 + [ANY] * 4 + [VMEM] + [ANY] * 6 + [VMEM, ANY, VMEM],
        out_specs=(ANY, VMEM, ANY, VMEM, ANY, VMEM, ANY),
        scratch_shapes=[
            pltpu.VMEM((rows, D), F32),
            pltpu.VMEM(kf_window.shape, BF),
            pltpu.VMEM((2,) + wide, BF),
            pltpu.VMEM((4,) + mix, BF),
        ]
        + back_scratch(rows, 5 * rows)
        + [
            pltpu.VMEM((2, rows // 2, D), BF),
            pltpu.VMEM((2, rows // 2, D), BF),
            pltpu.VMEM((2, rows, D), BF),
            pltpu.VMEM((parts, rows, feat), BF),
            pltpu.VMEM((2,) + wide, BF),
            pltpu.VMEM((2,) + wide, BF),
            pltpu.VMEM((2,) + wide, BF),
            pltpu.VMEM((2, 4) + mix, BF),
            pltpu.VMEM((4,) + mix, BF),
            pltpu.VMEM((4,) + mix, BF),
            pltpu.VMEM((2, rows // 2, D), BF),
            pltpu.VMEM((rows, D), BF),
            pltpu.VMEM(g_rows.shape, BF),
            pltpu.VMEM((2, 4) + mix, BF),
            pltpu.SemaphoreType.DMA((25,)),
            pltpu.SemaphoreType.DMA((25,)),
            pltpu.SemaphoreType.DMA((13,)),
        ]
        + [
            pltpu.VMEM((rows, ALL_COLS), BF),
            pltpu.VMEM(x_parts.shape, BF),
            pltpu.VMEM((2,) + slot, BF),
            pltpu.VMEM((2,) + slot, BF),
            pltpu.VMEM((2,) + slot, BF),
            pltpu.VMEM(wide, BF),
            pltpu.VMEM(cols, BF),
            pltpu.VMEM((3,) + mix, BF),
            pltpu.VMEM((4, parts) + block, BF),
            pltpu.VMEM((2, 4) + block, BF),
            pltpu.VMEM((4,) + block, BF),
            pltpu.VMEM((4,) + block, BF),
            pltpu.VMEM((4,) + block, BF),
            pltpu.VMEM((3,) + block, BF),
            pltpu.VMEM(block, BF),
            pltpu.VMEM(block, BF),
            pltpu.SemaphoreType.DMA((count,)),
            pltpu.SemaphoreType.DMA((count,)),
            pltpu.SemaphoreType.DMA((2,)),
            pltpu.VMEM((8, D), F32),
        ]
        + [
            pltpu.VMEM(a.shape, a.dtype)
            for a in (attend_in[1], attend_in[2], side_in[1], *(tail_in[k] for k in (0, 1, 2, 3, 4, 5, 7)))
        ]
        + [pltpu.SemaphoreType.DMA((2, PAIRS)), pltpu.SemaphoreType.DMA((8,))],
        compiler_params=comm_params(7),
        cost_estimate=cost_of(2 * rows * 5 * rows * D * 40, 40 << 20),
    )(*attend_in, *side_in, *tail_in)


def layout_body(
    grad_ref, gi_ref, cols_ref, other_ref, mix_ref, mix_other_ref, y_ref,
    y_out_ref, gi_out_ref, gain_ref, gain_two_ref, heads_ref, ranks_ref, out_ref, gate_ref, up_ref, down_ref,
):
    first = lax.axis_index("dp") == 0
    y_out_ref[...] = y_ref[...]
    gi_out_ref[...] = gi_ref[...].astype(F32)
    out_ref[...] = mix_ref[...].astype(F32) + mix_other_ref[...].astype(F32)
    ranks = ranks_ref.shape[0]
    used = heads_ref.shape[0]
    gain_ref[...] = grad_ref[ranks + used : ranks + used + 1]
    gain_two_ref[...] = grad_ref[ranks + used + 1 : ranks + used + 2]
    ranks_ref[...] = grad_ref[:ranks]
    lane = lax.broadcasted_iota(jnp.int32, (used, GROUP_COLS), 1)
    place = lax.broadcasted_iota(jnp.int32, (used, GROUP_COLS), 0)
    factor = place % FAC
    spot = jnp.where(factor < RQ, factor + 2 * RK, factor - RQ) * GROUP + place // FAC
    heads_ref[...] = jnp.dot(
        (lane == spot).astype(F32), grad_ref[ranks:], precision=lax.Precision.HIGHEST, preferred_element_type=F32
    )
    part = down_ref.shape[0] // 8
    for k, target in ((0, gate_ref), (1, up_ref), (2, down_ref)):
        for c in range(4):
            own = cols_ref[c, k].astype(F32)[:part]
            other = other_ref[c, k].astype(F32)[:part]
            target[c * part : (c + 1) * part] = jnp.where(first, own, other)
            target[(4 + c) * part : (5 + c) * part] = jnp.where(first, other, own)


def layout(grad, gi, cols, other, mix, mix_other, y, heads, ranks, hidden):
    feat = grad.shape[1]
    weight = jax.ShapeDtypeStruct((hidden, feat), F32)
    gain = jax.ShapeDtypeStruct((1, feat), F32)
    return call(
        layout_body,
        (
            jax.ShapeDtypeStruct(y.shape, y.dtype),
            jax.ShapeDtypeStruct(gi.shape, F32),
            gain,
            gain,
            jax.ShapeDtypeStruct((heads, feat), F32),
            jax.ShapeDtypeStruct((ranks, feat), F32),
            jax.ShapeDtypeStruct(mix.shape, F32),
            weight,
            weight,
            weight,
        ),
        cost=cost_of(0, 8 << 20),
    )(grad, gi, cols, other, mix, mix_other, y)


def local(
    tokens_in, segments, gain_attn, gain_ffn, w_heads, w_ranks, w_out, w_gate, w_up, w_down, cotangent
):
    n_row = lax.axis_size("row")
    n_col = lax.axis_size("col")
    row = lax.axis_index("row")
    col = lax.axis_index("col")
    micro, row_tokens, feat = tokens_in.shape
    subs = n_col // micro
    rows = row_tokens // subs
    length = row_tokens * n_row
    head_local = w_heads.shape[1] // FAC
    rank_local = w_ranks.shape[1]
    ffn_local = w_gate.shape[1]
    out_local = w_out.shape[0]
    block = row * subs + col % subs
    past = min(-(-(MAX_DOC - 1) // rows), n_row * subs - 1)
    keys = (past + 1) * rows

    dp_count = lax.axis_size("dp")
    fast = n_col == 4 and n_row == 4 and dp_count == 2 and micro == 2 and past == 4

    tokens = tokens_in.reshape(n_col, rows, feat)
    turns = (ROPE ** (-(np.arange(HD // 2) * 2.0 / HD))).astype(np.float32)
    if not fast:
        inverse = ROPE ** (-(jnp.arange(HD // 2, dtype=F32) * 2.0 / HD))
        heads_t = jnp.transpose(w_heads.reshape(feat, head_local, FAC), (2, 1, 0))
        heads_t = heads_t[jnp.array(FAC_ORDER)].reshape(FAC * head_local, feat)
        pad = jnp.zeros((GROUP_COLS - FAC * head_local, feat), BF)
        w_own = jnp.concatenate([w_ranks.T, heads_t, pad], axis=0)
        gains_own = jnp.concatenate([gain_attn[None], gain_ffn[None], jnp.zeros((6, feat), F32)], axis=0)
        part = ffn_local // n_col
        units = part * n_row
        w_ffn = jnp.stack([w_gate.T, w_up.T, w_down]).reshape(3, n_col, part, feat)
        w_ffn = lax.all_to_all(jnp.transpose(w_ffn, (1, 0, 2, 3)), "col", 0, 0, tiled=True)
        w_ffn = jnp.transpose(w_ffn, (1, 2, 0, 3)).reshape(3, part, D)
        w_ffn = jnp.transpose(lax.all_gather(w_ffn, "row", axis=0), (1, 0, 2, 3)).reshape(3, units, D)
        w_blocks = lax.all_gather(w_own, ("row", "col"), axis=0).reshape((n_row, n_col) + w_own.shape)
        gains = lax.all_gather(gains_own, "col", axis=0)
        x_parts = lax.all_to_all(tokens, "col", 0, 0, tiled=True)
        w_out_all = lax.all_gather(w_out, ("row", "col"), axis=0).reshape((n_row, n_col) + w_out.shape)

        seg_row = lax.dynamic_index_in_dim(segments, col // subs, 0, keepdims=False)
        padded = jnp.concatenate([jnp.full((1, past * rows), -1, jnp.int32), seg_row], axis=1)
        seg_window = lax.dynamic_slice_in_dim(padded, block * rows, keys, 1)
        own_seg = seg_window[0, past * rows :]
        key_idx = jnp.arange(keys, dtype=jnp.int32)
        query_idx = jnp.arange(rows, dtype=jnp.int32) + past * rows
        before = (own_seg[:, None] == seg_window) & (key_idx[None, :] < query_idx[:, None])
        places = jnp.sum(before.astype(jnp.int32), axis=1)
        angles = places.astype(F32)[:, None] * inverse[None, :]
        cosine = jnp.cos(angles)
        sine = jnp.sin(angles)
        turn = jnp.concatenate([cosine] * 4 + [-sine, sine, -sine, sine], axis=1)

    groups = [[m * subs + s for s in range(subs)] for m in range(micro)]
    if fast:
        cot_rows = cotangent.reshape(micro * row_tokens, feat)
        (
            x_parts, gains, ffn_parts, mixes, h_one, head_fac, bq_rot, queries, w_rh, kf_window, seg_window, turn, w_rows,
            heads_out, lse, key_all, value_all, cot_near,
        ) = head_attend(
            tokens, w_ranks.T, w_heads.T, gain_attn.reshape(1, feat), gain_ffn.reshape(1, feat), w_gate.T, w_up.T,
            w_down, w_out, segments, np.tile(turns, 4).reshape(1, LANES), cot_rows,
        )
        mixed, d_mixed, d_heads, g_out, g_gain_two, g_rows, out_pair, hop = middle(
            x_parts, heads_out, mixes, gains, cot_rows, cot_near, ffn_parts, w_rows
        )
        output, g_rh, grad_input, g_cols, cols_other, g_out, out_other = back_tail(
            (queries, key_all, value_all, d_heads, lse, kf_window, seg_window),
            (out_pair, mixed, g_rows, g_out, hop),
            (head_fac, bq_rot, turn, w_rh, h_one, x_parts, gains, d_mixed, g_gain_two),
        )
        output, grad_input, g_one, g_two, own_heads, own_ranks, g_out, own_gate, own_up, own_down = layout(
            g_rh, grad_input, g_cols, cols_other, g_out, out_other, output, w_heads.shape[1], w_ranks.shape[1], ffn_local
        )
        return (
            output.reshape(tokens_in.shape),
            grad_input.reshape(tokens_in.shape),
            g_one.reshape(feat),
            g_two.reshape(feat),
            own_heads.T,
            own_ranks.T,
            g_out,
            own_gate.T,
            own_up.T,
            own_down,
        )
    else:
        h_one, head_fac, bq_rot, key_fac, queries, w_rh = front(x_parts, gains, w_blocks, turn)
        gathered = lax.all_gather(key_fac, "row", axis=0)
        gathered = lax.all_gather(gathered, "col", axis=1, axis_index_groups=groups)
        gathered = gathered.reshape(length, key_fac.shape[1])
        padded_kf = jnp.concatenate([jnp.zeros((past * rows, key_fac.shape[1]), BF), gathered], axis=0)
        kf_window = lax.dynamic_slice_in_dim(padded_kf, block * rows, keys, 0)
        heads_out, lse, key_all, value_all = attend(queries, kf_window, seg_window)
        mixed, h_two = mixing(x_parts, heads_out, w_out_all, gains)
        cot_own = lax.all_to_all(cotangent.reshape(n_col, rows, feat), "col", 0, 0, tiled=True)
        cot_own = jnp.transpose(cot_own, (1, 0, 2)).reshape(rows, D)
        cot_all = lax.all_gather(cot_own, "col", axis=0)
        h_all = lax.all_gather(h_two, "col", axis=0)
        out_part, dh_part, g_ffn = ffn(h_all, cot_all, w_ffn)
        dh_sum = lax.psum_scatter(dh_part, "col", scatter_dimension=0, tiled=False).astype(F32)
        out_sum = lax.psum_scatter(out_part, "col", scatter_dimension=0, tiled=False).astype(F32)
        out_parts, d_mixed, d_heads, g_out, g_gain_two = unmix(
            dh_sum, out_sum, mixed, cot_own, heads_out, w_out_all, gains
        )
        d_q, d_kf = attend_back(queries, key_all, value_all, d_heads, lse, kf_window, seg_window)
        spread_kf = jnp.zeros((past * rows + length, d_kf.shape[1]), BF)
        spread_kf = lax.dynamic_update_slice_in_dim(spread_kf, d_kf, block * rows, 0)[past * rows :]
        spread_kf = spread_kf.reshape(n_row, subs, rows, -1)
        own_kf = lax.psum_scatter(spread_kf, "row", scatter_dimension=0, tiled=False)
        own_kf = lax.psum_scatter(own_kf, "col", scatter_dimension=0, tiled=False, axis_index_groups=groups)
        gi_parts, g_rh = back(
            d_q, own_kf, head_fac, bq_rot, turn, w_rh, h_one, x_parts, gains, d_mixed, g_gain_two, n_row
        )
        output = lax.all_to_all(out_parts, "col", 0, 0, tiled=True)
        grad_input = lax.all_to_all(gi_parts, "col", 0, 0, tiled=True)
        g_ffn = lax.psum_scatter(g_ffn.reshape(3, n_row, part, D), "row", scatter_dimension=1, tiled=False)
        g_ffn = jnp.transpose(lax.psum(g_ffn, "dp").reshape(3, part, n_col, feat), (2, 0, 1, 3))
        g_ffn = lax.all_to_all(g_ffn, "col", 0, 0, tiled=True)
        g_ffn = jnp.transpose(g_ffn, (1, 0, 2, 3)).reshape(3, ffn_local, feat).astype(F32)

        def total(values):
            values = values.reshape((n_row * n_col,) + values.shape[2:])
            values = lax.psum_scatter(values, ("row", "col"), scatter_dimension=0, tiled=False)
            return lax.psum(values, "dp").astype(F32)

        g_out = total(g_out)
        g_rh = total(g_rh)

    used = rank_local + FAC * head_local
    own_heads = g_rh[rank_local:used].reshape(FAC, head_local, feat)
    own_heads = jnp.transpose(own_heads[jnp.array(FAC_BACK)], (2, 1, 0)).reshape(w_heads.shape)
    return (
        output.reshape(tokens_in.shape),
        grad_input.reshape(tokens_in.shape),
        g_rh[used],
        g_rh[used + 1],
        own_heads,
        g_rh[:rank_local].T,
        g_out,
        g_ffn[0].T,
        g_ffn[1].T,
        g_ffn[2],
    )


def solution(mesh):
    tokens = P(None, ("dp", "row"), "col")
    both = P("col", "row")
    turned = P("row", "col")
    gain = P("col")
    return jax.shard_map(
        local,
        mesh=mesh,
        in_specs=(tokens, P(None, "dp", None), gain, gain, both, both, turned, both, both, turned, tokens),
        out_specs=(tokens, tokens, gain, gain, both, both, turned, both, both, turned),
        check_vma=False,
    )
```
